32 devices in a mesh: fsdp: 4 (over z), context: 4 (over y, x), tensor: 2 (over core).
Axes of the slice: x: 2, y: 2, z: 4, core: 2. Of those that a mesh axis runs over, the one named last changes fastest.
Arguments:
- tokens: float32 [12, 1408, 1024], P('fsdp', 'context'), may hold values from -6 to 6
- cotangent: float32 [12, 1408, 1024], P('fsdp', 'context'), may hold values from -6 to 6
- gains: float32 [4, 1024], replicated, may hold values from 0.5 to 1.5
- w_qkv: bfloat16 [1024, 3, 1024], P('fsdp', None, 'tensor'), may hold values from -0.1875 to 0.1875
- w_out: bfloat16 [1024, 1024], P('tensor', 'fsdp'), may hold values from -4 to 4
- w_up: bfloat16 [1024, 4096], P('fsdp', 'tensor'), may hold values from -0.1875 to 0.1875
- w_down: bfloat16 [4096, 1024], P('tensor', 'fsdp'), may hold values from -0.09375 to 0.09375
- key_mask: int32 [12, 1408], P('fsdp', 'context'), may hold values from 0 to 1, as said below
- owner: int32 [12], replicated, may hold values from 0 to 11, each once
- stat_left: float32 [12, 2, 512, 1024], P('context', 'tensor', 'fsdp'), may hold values from -120 to 640
- stat_right: float32 [12, 2, 512, 1024], P('context', 'tensor', 'fsdp'), may hold values from -120 to 640
- root_left: float32 [12, 2, 512, 1024], P('context', 'tensor', 'fsdp'), may hold values from -3 to 24
- root_right: float32 [12, 1024, 1024], P('context'), may hold values from -0.3 to 1.6
- master: float32 [12, 2, 512, 1024], P('context', 'tensor', 'fsdp'), may hold values from -6 to 6
- gain_state: float32 [4, 1024], P(None, ('fsdp', 'context')), may hold values from 0.5 to 4
Outputs:
- output: float32 [12, 1408, 1024], P('fsdp', 'context')
- grad_tokens: float32 [12, 1408, 1024], P('fsdp', 'context')
- grad_blocks: float32 [12, 2, 512, 1024], P('context', 'tensor', 'fsdp')
- stat_left_new: float32 [12, 2, 512, 1024], P('context', 'tensor', 'fsdp')
- stat_right_new: float32 [12, 2, 512, 1024], P('context', 'tensor', 'fsdp')
- weight_new: float32 [12, 2, 512, 1024], P('context', 'tensor', 'fsdp')
- gain_grad: float32 [4, 1024], P(None, ('fsdp', 'context'))
- gain_state_new: float32 [4, 1024], P(None, ('fsdp', 'context'))
- gain_new: float32 [4, 1024], P(None, ('fsdp', 'context'))
The draws below stay inside these ranges and needn't reach their ends.
Inputs may be any that keep to these rules, and one draw needn't show every extreme that they name: `key_mask`: each image's real tokens are its first p * p + 1 positions, for a whole p from 28 to 37; some image has p = 37.
All inputs are finite; a program needn't handle non-finite values.
Results may differ from the reference program's by a relative error of at most 0.012.
Values may be sent and summed in bfloat16 or wider, within the bound.
A program may use at most 256 MiB of HBM per device.

```python
import math
import jax
import jax.numpy as jnp
from jax import lax

D = 1024
HEADS = 16
HD = 64
FF = 4096
SEQ = 1408
PATCH = 37
IMAGES = 12
HALF = 512
NBLK = 12
N_TENSOR = 2


def symmetric_set(key, count, low_mult, high_mult):
    key_noise, key_mult = jax.random.split(key)
    noise = jax.random.truncated_normal(key_noise, -4.0, 4.0, (count, D, D), jnp.float32)
    noise = (noise + jnp.swapaxes(noise, 1, 2)) * (0.3 / math.sqrt(2.0 * D))
    multiple = jnp.exp(jax.random.uniform(key_mult, (count, 1, 1), jnp.float32, math.log(low_mult), math.log(high_mult)))
    return multiple * (jnp.eye(D, dtype=jnp.float32) + noise)


def draw_stat_left(key, part):
    return symmetric_set(jax.random.fold_in(key, 11), NBLK, 8.0, 512.0).reshape(NBLK, D // HALF, HALF, D)


def draw_stat_right(key, part):
    return symmetric_set(jax.random.fold_in(key, 23), NBLK, 8.0, 512.0).reshape(NBLK, D // HALF, HALF, D)


def draw_root_left(key, part):
    base = symmetric_set(jax.random.fold_in(key, 37), NBLK, 0.8, 1.25)
    rising = jnp.exp(jnp.arange(D, dtype=jnp.float32) * (math.log(4.0) / (D - 1)))
    scaled = base * rising[None, :, None] * rising[None, None, :]
    return scaled.reshape(NBLK, D // HALF, HALF, D)


def draw_root_right(key, part):
    return symmetric_set(jax.random.fold_in(key, 41), NBLK, 0.8, 1.25)


def draw_key_mask(key, part):
    key_side, key_pick = jax.random.split(jax.random.fold_in(key, 5))
    side_len = jax.random.randint(key_side, (IMAGES,), PATCH - PATCH // 4, PATCH + 1)
    chosen = jax.random.randint(key_pick, (), 0, IMAGES)
    side_len = jnp.where(jnp.arange(IMAGES) == chosen, PATCH, side_len)
    real_count = side_len * side_len + 1
    return (jnp.arange(SEQ)[None, :] < real_count[:, None]).astype(jnp.int32)


def shard_levels(rng, extent, cuts, smallest, top_value):
    def one(dim, shards_of):
        draws = jax.random.uniform(jax.random.fold_in(jax.random.fold_in(rng, 6), dim), (shards_of,), jnp.float32, smallest / len(cuts), top_value / len(cuts))
        return jnp.repeat(jnp.exp(draws), extent[dim] // shards_of).reshape((-1,) + (1,) * (len(extent) - dim - 1))

    factor_of = one(*cuts[0])
    for cut in cuts[1:]:
        factor_of = factor_of * one(*cut)
    return factor_of


def gaussian(key, dims, width, bound, pieces=(), kind=jnp.bfloat16):
    gain = shard_levels(key, dims, pieces, -0.22, 0.18) if pieces else 1.0
    result = jax.random.normal(key, dims, jnp.float32) * width * gain
    return jnp.minimum(jnp.maximum(result, -bound), bound).astype(kind)


def setup_inputs(seed: int = 0) -> dict:
    streams_of = jax.random.split(jax.random.key(seed), 16)
    tokens = gaussian(streams_of[0], (IMAGES, SEQ, D), 1.0, 6.0, ((0, 4), (1, 4)), jnp.float32)
    cotangent = gaussian(streams_of[1], (IMAGES, SEQ, D), 1.0, 6.0, ((0, 4), (1, 4)), jnp.float32)
    gains = jnp.clip(1.0 + 0.1 * jax.random.normal(streams_of[2], (4, D), jnp.float32), 0.5, 1.5)
    w_qkv = gaussian(streams_of[3], (D, 3, D), D ** -0.5, 0.1875, ((0, 4), (2, 2)))
    w_out = gaussian(streams_of[4], (D, D), (max(1, 3 * D // SEQ)) ** -0.5, 4.0, ((0, 2), (1, 4)))
    w_up = gaussian(streams_of[5], (D, FF), D ** -0.5, 0.1875, ((0, 4), (1, 2)))
    w_down = gaussian(streams_of[6], (FF, D), FF ** -0.5, 0.09375, ((0, 2), (1, 4)))
    key_mask = draw_key_mask(jax.random.fold_in(streams_of[15], 71), 0)
    owner = jax.random.permutation(streams_of[8], NBLK).astype(jnp.int32)
    stat_left = draw_stat_left(jax.random.fold_in(streams_of[15], 71), 0)
    stat_right = draw_stat_right(jax.random.fold_in(streams_of[15], 71), 0)
    root_left = draw_root_left(jax.random.fold_in(streams_of[15], 71), 0)
    root_right = draw_root_right(jax.random.fold_in(streams_of[15], 71), 0)
    master = gaussian(streams_of[13], (NBLK, D // HALF, HALF, D), 1.0, 6.0, ((0, 4), (1, 2), (2, 4)), jnp.float32)
    gain_state = jnp.clip(jnp.exp(math.log(4.0) - 2.0794415 * jax.random.uniform(streams_of[14], (4, D), jnp.float32) ** shard_levels(streams_of[14], (4, D), ((1, 16),), -0.2, 0.2)), 0.5, 4.0)
    return {"tokens": tokens, "cotangent": cotangent, "gains": gains, "w_qkv": w_qkv, "w_out": w_out, "w_up": w_up, "w_down": w_down, "key_mask": key_mask, "owner": owner, "stat_left": stat_left, "stat_right": stat_right, "root_left": root_left, "root_right": root_right, "master": master, "gain_state": gain_state}


@jax.custom_vjp
def low(v):
    return lax.optimization_barrier(v.astype(jnp.bfloat16)).astype(jnp.float32)

@jax.custom_vjp
def low_back(v):
    return v

def low_keep(v):
    return (low(v), None)

def low_pass(kept, grad):
    return (grad,)

def back_keep(v):
    return (v, None)

def back_low(kept, grad):
    return (low(grad),)
low.defvjp(low_keep, low_pass)
low_back.defvjp(back_keep, back_low)

def layer_norm(field_in, gain_vec):
    centred = field_in - lax.optimization_barrier(jnp.mean(field_in, axis=-1, keepdims=True))
    inv_std = lax.rsqrt(lax.optimization_barrier(jnp.mean(centred * centred, axis=-1, keepdims=True)) + 1e-06)
    return centred * inv_std * gain_vec

def attend(operands):
    queries, key_rows, value_rows, mask_row = operands
    seq_len = queries.shape[0]
    queries = queries.reshape(seq_len, HEADS, HD)
    key_rows = key_rows.reshape(seq_len, HEADS, HD)
    value_rows = value_rows.reshape(seq_len, HEADS, HD)
    scores = jnp.einsum('qhd,khd->hqk', queries, key_rows, precision=lax.Precision.HIGHEST) * HD ** (-0.5)
    scores = low_back(scores)
    scores = jnp.where(mask_row[None, None, :] > 0, scores, -1e+30)
    peak_val = lax.optimization_barrier(jnp.max(scores, axis=-1, keepdims=True))
    expo_val = jnp.exp(scores - peak_val)
    prob_low = low(expo_val / lax.optimization_barrier(jnp.sum(expo_val, axis=-1, keepdims=True)))
    mixed = jnp.einsum('hqk,khd->qhd', prob_low, value_rows, precision=lax.Precision.HIGHEST)
    return mixed.reshape(seq_len, HEADS * HD)

def reference(tokens, cotangent, gains, w_qkv, w_out, w_up, w_down, key_mask, owner, stat_left, stat_right, root_left, root_right, master, gain_state):
    highest = lax.Precision.HIGHEST

    def forward(field_in, qkv_w, out_w, up_w, down_w, gain_set):
        normed1 = low(layer_norm(field_in, gain_set[0]))
        qkv = jnp.einsum('isd,djh->isjh', normed1, qkv_w, precision=highest)
        qkv = low_back(low(qkv))
        attended = lax.map(jax.checkpoint(attend), (qkv[:, :, 0], qkv[:, :, 1], qkv[:, :, 2], key_mask))
        attended = low_back(low(attended))
        branch_attn = low_back(jnp.einsum('isd,de->ise', attended, out_w, precision=highest))
        middle = field_in + gain_set[2] * branch_attn
        normed2 = low(layer_norm(middle, gain_set[1]))
        pre_act = low_back(jnp.einsum('isd,df->isf', normed2, up_w, precision=highest))
        act_low = low(jax.nn.gelu(pre_act, approximate=False))
        branch_mlp = low_back(jnp.einsum('isf,fd->isd', act_low, down_w, precision=highest))
        return middle + gain_set[3] * branch_mlp
    primal_in = (tokens, w_qkv.astype(jnp.float32), w_out.astype(jnp.float32), w_up.astype(jnp.float32), w_down.astype(jnp.float32), gains)
    output, pull_back = jax.vjp(forward, *primal_in)
    grad_tokens, grad_qkv, grad_out, grad_up, grad_down, gain_grad = pull_back(cotangent)
    half_width = D // N_TENSOR
    up_blocks = FF // D
    blocks = jnp.concatenate([jnp.transpose(grad_qkv, (1, 2, 0)), grad_out[None], grad_up.T.reshape(N_TENSOR, up_blocks, half_width, D).transpose(1, 0, 2, 3).reshape(up_blocks, D, D), grad_down.reshape(N_TENSOR, up_blocks, half_width, D).transpose(1, 0, 2, 3).reshape(up_blocks, D, D)], axis=0)
    block_of = jnp.zeros((NBLK,), jnp.int32).at[owner].set(jnp.arange(NBLK, dtype=jnp.int32))
    grads = blocks[block_of]
    tokens_all = IMAGES * SEQ
    state_shape = stat_left.shape
    left_old = stat_left.reshape(NBLK, D, D)
    right_old = stat_right.reshape(NBLK, D, D)
    left_root = root_left.reshape(NBLK, D, D)
    left_new = 0.5 * left_old + 0.5 / tokens_all * jnp.einsum('sab,scb->sac', grads, grads, precision=highest)
    right_new = 0.5 * right_old + 0.5 / tokens_all * jnp.einsum('sba,sbc->sac', grads, grads, precision=highest)
    inner_prod = jnp.einsum('sab,sbc->sac', left_root, grads, precision=highest)
    update = jnp.einsum('sab,sbc->sac', inner_prod, root_right, precision=highest)
    square_sum = lax.optimization_barrier(jnp.sum(update * update, axis=(1, 2)))
    factor = 1.0 * lax.rsqrt(square_sum / (D * D) + 1e-06)
    weight_new = master.reshape(NBLK, D, D) - factor[:, None, None] * update
    state_new = 0.5 * gain_state + 0.5 * gain_grad * gain_grad / tokens_all
    gain_new = gains - 0.1 * gain_grad * lax.rsqrt(tokens_all * state_new)
    return (output, grad_tokens, grads.reshape(state_shape), left_new.reshape(state_shape), right_new.reshape(state_shape), weight_new.reshape(state_shape), gain_grad, state_new, gain_new)
```

```python
import functools

import jax
import jax.numpy as jnp
from jax import lax
from jax.experimental import pallas as pl
from jax.experimental.pallas import tpu as pltpu
from jax.sharding import PartitionSpec as P

D = 1024
HD = 64
SEQ = 1408
NBLK = 12
LATE = 3
EARLY = NBLK - LATE
BF = jnp.bfloat16
F32 = jnp.float32
SCALE = HD ** (-0.5)


def norm_fwd(field_in, gain_vec):
    centred = field_in - jnp.mean(field_in, axis=-1, keepdims=True)
    inv_std = lax.rsqrt(jnp.mean(centred * centred, axis=-1, keepdims=True) + 1e-06)
    normed = centred * inv_std
    return (normed, inv_std, normed * gain_vec)


def norm_back(grad_out, gain_vec, normed, inv_std):
    scaled = grad_out * gain_vec
    inner_sum = (
        scaled
        - jnp.mean(scaled, axis=-1, keepdims=True)
        - normed * jnp.mean(scaled * normed, axis=-1, keepdims=True)
    )
    return (inner_sum * inv_std, jnp.sum(grad_out * normed, axis=(0, 1)))


def gelu_parts(field_in):
    normal_cdf = 0.5 * (1.0 + lax.erf(field_in * 0.7071067811865476))
    normal_pdf = jnp.exp(-0.5 * field_in * field_in) * 0.3989422804014327
    return (field_in * normal_cdf, normal_cdf + field_in * normal_pdf)


def dot_nt(a, b):
    return lax.dot_general(a, b, (((1,), (1,)), ((), ())), preferred_element_type=F32)


def dot_tn(a, b):
    return lax.dot_general(a, b, (((0,), (0,)), ((), ())), preferred_element_type=F32)


def dot_nn(a, b):
    return lax.dot_general(a, b, (((1,), (0,)), ((), ())), preferred_element_type=F32)


def attn_fwd_kernel(q_ref, k_ref, v_ref, bias_ref, o_ref, lse_ref):
    q = q_ref[...] * SCALE
    k = k_ref[...]
    v = v_ref[...]
    bias = bias_ref[...]
    first = lax.broadcasted_iota(jnp.int32, q.shape, 1) < HD
    outs, sums = [], []
    for head in range(2):
        mask = first if head == 0 else jnp.logical_not(first)
        scores = dot_nt(jnp.where(mask, q, jnp.zeros_like(q)), k) + bias
        peak = jnp.max(scores, axis=-1, keepdims=True)
        expo = jnp.exp(scores - peak)
        total = jnp.sum(expo, axis=-1, keepdims=True)
        outs.append(dot_nn(expo.astype(BF), v) / total)
        sums.append(peak + jnp.log(total))
    o_ref[...] = jnp.where(first, outs[0], outs[1]).astype(BF)
    lse_ref[...] = jnp.where(first, sums[0], sums[1])


def attn_fwd(qkv, bias_row):
    rows = qkv.shape[0]
    bq = rows // 4
    return pl.pallas_call(
        attn_fwd_kernel,
        grid=(rows // bq,),
        out_shape=(
            jax.ShapeDtypeStruct((rows, 128), BF),
            jax.ShapeDtypeStruct((rows, 128), F32),
        ),
        in_specs=[
            pl.BlockSpec((bq, 128), lambda i: (i, 0)),
            pl.BlockSpec((rows, 128), lambda i: (0, 1)),
            pl.BlockSpec((rows, 128), lambda i: (0, 2)),
            pl.BlockSpec((1, rows), lambda i: (0, 0)),
        ],
        out_specs=(
            pl.BlockSpec((bq, 128), lambda i: (i, 0)),
            pl.BlockSpec((bq, 128), lambda i: (i, 0)),
        ),
        compiler_params=pltpu.CompilerParams(vmem_limit_bytes=40 << 20),
        cost_estimate=pl.CostEstimate(
            flops=4 * rows * rows * 512, bytes_accessed=rows * 2048, transcendentals=2 * rows * rows
        ),
        name="attn_fwd",
    )(qkv, qkv, qkv, bias_row)


def attn_bwd_kernel(q_ref, k_ref, v_ref, do_ref, o_ref, lse_ref, live_ref, out_ref, dq_ref, row_ref):
    step = pl.program_id(0)
    chunk = k_ref.shape[0]

    @pl.when(step == 0)
    def _():
        row_ref[0:128, :] = lse_ref[...].T
        prod = do_ref[...].astype(F32) * o_ref[...].astype(F32)
        prod_t = prod.T
        row_ref[128:136, :] = jnp.broadcast_to(
            jnp.sum(prod_t[0:HD], axis=0, keepdims=True), (8, prod_t.shape[1])
        )
        row_ref[136:144, :] = jnp.broadcast_to(
            jnp.sum(prod_t[HD:128], axis=0, keepdims=True), (8, prod_t.shape[1])
        )
        dq_ref[...] = jnp.zeros_like(dq_ref)

    q = q_ref[...]
    k = k_ref[...] * SCALE
    v = v_ref[...]
    do = do_ref[...]
    live = live_ref[:, 0:1] > 0
    first = lax.broadcasted_iota(jnp.int32, k.shape, 1) < HD
    dks, dvs = [], []
    for head in range(2):
        mask = first if head == 0 else jnp.logical_not(first)
        kh = jnp.where(mask, k, jnp.zeros_like(k))
        vh = jnp.where(mask, v, jnp.zeros_like(v))
        lse = row_ref[64 * head : 64 * head + 1, :]
        delta = row_ref[128 + 8 * head : 129 + 8 * head, :]
        prob = jnp.where(live, jnp.exp(dot_nt(kh, q) - lse), 0.0)
        ds = (prob * (dot_nt(vh, do) - delta)).astype(BF)
        dvs.append(dot_nn(prob.astype(BF), do))
        dks.append(dot_nn(ds, q) * SCALE)
        dq_ref[...] += dot_tn(ds, kh)
    at = pl.ds(pl.multiple_of(step * chunk, chunk), chunk)
    out_ref[at, 128:256] = jnp.where(first, dks[0], dks[1]).astype(BF)
    out_ref[at, 256:384] = jnp.where(first, dvs[0], dvs[1]).astype(BF)

    @pl.when(step == pl.num_programs(0) - 1)
    def _():
        out_ref[:, 0:128] = dq_ref[...].astype(BF)


def attn_bwd(qkv, grad, out, lse, live_col):
    rows = qkv.shape[0]
    chunk = rows // 4
    return pl.pallas_call(
        attn_bwd_kernel,
        grid=(rows // chunk,),
        out_shape=jax.ShapeDtypeStruct((rows, 384), BF),
        in_specs=[
            pl.BlockSpec((rows, 128), lambda i: (0, 0)),
            pl.BlockSpec((chunk, 128), lambda i: (i, 1)),
            pl.BlockSpec((chunk, 128), lambda i: (i, 2)),
            pl.BlockSpec((rows, 128), lambda i: (0, 0)),
            pl.BlockSpec((rows, 128), lambda i: (0, 0)),
            pl.BlockSpec((rows, 128), lambda i: (0, 0)),
            pl.BlockSpec((chunk, 128), lambda i: (i, 0)),
        ],
        out_specs=pl.BlockSpec((rows, 384), lambda i: (0, 0)),
        scratch_shapes=[pltpu.VMEM((rows, 128), F32), pltpu.VMEM((144, rows), F32)],
        compiler_params=pltpu.CompilerParams(vmem_limit_bytes=50 << 20),
        cost_estimate=pl.CostEstimate(
            flops=10 * rows * rows * 512, bytes_accessed=rows * 4096, transcendentals=2 * rows * rows
        ),
        name="attn_bwd",
    )(qkv, qkv, qkv, grad, out, lse, live_col)


def xor_permute(value, axis, step):
    size = lax.axis_size(axis)
    return lax.ppermute(value, axis, [(j, j ^ step) for j in range(size)])


def xor_order(pieces, index):
    bit = 1
    while bit < len(pieces):
        odd = (index & bit) > 0
        pieces = [jnp.where(odd, pieces[j ^ bit], pieces[j]) for j in range(len(pieces))]
        bit *= 2
    return pieces


def sum_tensor(value):
    low = lax.optimization_barrier(value.astype(BF))
    return low.astype(F32) + xor_permute(low, "tensor", 1).astype(F32)


def gather_fsdp(value):
    size = lax.axis_size("fsdp")
    if size > 4:
        return lax.all_gather(value, "fsdp", axis=0, tiled=False)
    pieces = [value] + [
        lax.ppermute(value, "fsdp", [(j, (j - k) % size) for j in range(size)])
        for k in range(1, size)
    ]
    doubled = jnp.stack(pieces + pieces[:-1])
    start = lax.rem(size - lax.axis_index("fsdp"), size)
    return lax.dynamic_slice_in_dim(doubled, start, size, 0)


def sum_fsdp(value):
    size = lax.axis_size("fsdp")
    if size > 4:
        return lax.psum(value, "fsdp")
    total = value
    for k in range(1, size):
        total = total + lax.ppermute(value, "fsdp", [(j, (j - k) % size) for j in range(size)])
    return total


def per_device(
    tokens,
    cotangent,
    gains,
    w_qkv,
    w_out,
    w_up,
    w_down,
    key_mask,
    owner,
    stat_left,
    stat_right,
    root_left,
    root_right,
    master,
    gain_state,
):
    images, local_len = tokens.shape[:2]
    tok_rows = images * local_len
    nz, nc, nt = (lax.axis_size(a) for a in ("fsdp", "context", "tensor"))
    me_z, me_c, me_t = (lax.axis_index(a) for a in ("fsdp", "context", "tensor"))
    half_width = w_qkv.shape[2]
    hidden = w_up.shape[1]
    up_blocks = hidden // half_width
    cols = half_width // nc
    half_len = local_len // nt

    wq_part = lax.dynamic_slice_in_dim(w_qkv, me_c * cols, cols, 2)
    wq = gather_fsdp(wq_part).reshape(D, 3 * cols)

    def two_stage(weight, member_axis, fsdp_axis):
        width = weight.shape[member_axis] // nc
        part = lax.dynamic_slice_in_dim(weight, me_c * width, width, member_axis)
        part = lax.all_gather(part, "fsdp", axis=fsdp_axis, tiled=True)
        return lax.all_gather(part, "context", axis=member_axis, tiled=True)

    out_full = two_stage(w_out, 0, 1)
    up_full = two_stage(w_up, 1, 0)
    down_full = two_stage(w_down, 0, 1)

    counts = jnp.sum(key_mask, axis=1)
    real = counts
    for k in range(1, nc):
        real = real + xor_permute(counts, "context", k)
    position = (
        (me_c ^ jnp.arange(nc))[:, None, None] * local_len
        + (me_t ^ jnp.arange(nt))[None, :, None] * half_len
        + jnp.arange(half_len)[None, None, :]
    ).reshape(-1)
    live = position[None, :] < real[:, None]
    bias = jnp.where(live, 0.0, -1e30).astype(F32)
    live_col = jnp.broadcast_to(live[:, :, None].astype(F32), (images, SEQ, 128))

    normed1, inv_std1, pre_norm1 = norm_fwd(tokens, gains[0])
    normed1_low = pre_norm1.astype(BF)

    def to_natural(value):
        parts = value.reshape((nt, half_len) + value.shape[1:])
        return jnp.where(me_t > 0, parts[::-1], parts).reshape(value.shape)

    x_all, qkv, out_heads, log_sums, attended = [], [], [], [], []
    for i in range(images):
        mine = lax.dynamic_slice_in_dim(normed1_low[i], me_t * half_len, half_len, 0)
        held = jnp.stack([mine] + [xor_permute(mine, "context", k) for k in range(1, nc)])
        other = xor_permute(held, "tensor", 1)
        x_i = jnp.stack([held, other], axis=1).reshape(SEQ, D)
        qkv_i = dot_nn(x_i, wq).astype(BF)
        o_i, lse_i = attn_fwd(qkv_i, bias[i][None])
        chunks = o_i.reshape(nc, local_len, 2 * HD)
        moved = [to_natural(chunks[0])] + [
            to_natural(xor_permute(chunks[k], "context", k)) for k in range(1, nc)
        ]
        attended.append(jnp.concatenate(xor_order(moved, me_c), axis=-1))
        x_all.append(x_i)
        qkv.append(qkv_i)
        out_heads.append(o_i)
        log_sums.append(lse_i)
    attended = jnp.stack(attended)

    branch_attn = sum_tensor(
        jnp.einsum("ish,hd->isd", attended, out_full, preferred_element_type=F32)
    )
    middle = tokens + gains[2] * branch_attn
    normed2, inv_std2, pre_norm2 = norm_fwd(middle, gains[1])
    normed2_low = pre_norm2.astype(BF)
    pre_act = jnp.einsum("isd,df->isf", normed2_low, up_full, preferred_element_type=F32)
    act_val, act_slope = gelu_parts(pre_act)
    act_low = act_val.astype(BF)
    branch_mlp = sum_tensor(
        jnp.einsum("isf,fd->isd", act_low, down_full, preferred_element_type=F32)
    )
    output = middle + gains[3] * branch_mlp

    grad_mlp = (gains[3] * cotangent).astype(BF)
    grad_hidden = jnp.einsum("isd,fd->isf", grad_mlp, down_full, preferred_element_type=F32)
    grad_pre = (grad_hidden * act_slope).astype(BF)
    grad_n2 = sum_tensor(
        jnp.einsum("isf,df->isd", grad_pre, up_full, preferred_element_type=F32)
    )
    middle_part, grad_gain2 = norm_back(grad_n2, gains[1], normed2, inv_std2)
    grad_middle = cotangent + middle_part
    grad_branch = (gains[2] * grad_middle).astype(BF)
    grad_att = jnp.einsum(
        "isd,hd->ish", grad_branch, out_full, preferred_element_type=F32
    ).astype(BF)

    term_qkv = None
    grad_tok = []
    for i in range(images):
        pieces = [grad_att[i, :, j * cols : (j + 1) * cols] for j in range(nc)]
        pieces = [to_natural(p) for p in xor_order(pieces, me_c)]
        grad_i = jnp.concatenate(
            [pieces[0]] + [xor_permute(pieces[k], "context", k) for k in range(1, nc)]
        )
        g_i = attn_bwd(qkv[i], grad_i, out_heads[i], log_sums[i], live_col[i])
        chunks = g_i.reshape(nc, local_len, 3 * cols)
        moved = [to_natural(chunks[0])] + [
            to_natural(xor_permute(chunks[k], "context", k)) for k in range(1, nc)
        ]
        grad_tok.append(jnp.stack(xor_order(moved, me_c), axis=1))
        term = dot_tn(g_i, x_all[i])
        term_qkv = term if term_qkv is None else term_qkv + term
    grad_tok = jnp.stack(grad_tok)
    wq_all = lax.all_gather(wq, "context", axis=0, tiled=False)
    grad_n1 = sum_tensor(
        jnp.einsum("isjc,jdc->isd", grad_tok, wq_all, preferred_element_type=F32)
    )
    input_part, grad_gain1 = norm_back(grad_n1, gains[0], normed1, inv_std1)
    grad_tokens = grad_middle + input_part
    grad_gain3 = jnp.sum(grad_middle * branch_attn, axis=(0, 1))
    grad_gain4 = jnp.sum(cotangent * branch_mlp, axis=(0, 1))
    gain_terms = jnp.stack([grad_gain1, grad_gain2, grad_gain3, grad_gain4], axis=0)

    def early_terms(left, right):
        term = dot_tn(left.reshape(tok_rows, -1), right.reshape(tok_rows, D)).astype(BF)
        term = jnp.swapaxes(term.reshape(-1, nc, half_width // nc, D), 0, 1)
        return lax.psum_scatter(
            term.reshape(-1, D), "context", scatter_dimension=0, tiled=True
        ).reshape(-1, half_width // nc, D)

    early = jnp.concatenate(
        [
            early_terms(attended, grad_branch),
            early_terms(grad_pre, normed2_low),
            early_terms(act_low, grad_mlp),
        ],
        axis=0,
    )
    sub = half_width // nc // nz
    early = lax.psum_scatter(
        jnp.swapaxes(early.reshape(EARLY, nz, sub, D), 0, 1).reshape(-1, D),
        "fsdp",
        scatter_dimension=0,
        tiled=True,
    ).reshape(EARLY, sub, D)
    onehot = (owner[:, None] == jnp.arange(NBLK, dtype=jnp.int32)[None, :]).astype(jnp.int32)
    block_of = jnp.sum(onehot * jnp.arange(NBLK, dtype=jnp.int32)[:, None], axis=0)
    slot_count = NBLK // nc
    slots_of = block_of.reshape(nc, slot_count)

    def slots_for(k):
        blocks = lax.dynamic_index_in_dim(slots_of, me_c ^ k, 0, keepdims=False)
        return early[jnp.clip(blocks - LATE, 0, EARLY - 1)]

    placed = [slots_for(0)] + [xor_permute(slots_for(k), "context", k) for k in range(1, nc)]
    placed = jnp.stack(xor_order(placed, me_c), axis=1)
    placed = lax.all_gather(placed, "fsdp", axis=2, tiled=False)
    placed = placed.reshape(slot_count, half_width, D)
    placed_other = xor_permute(placed, "tensor", 1)
    both = jnp.stack([placed, placed_other], axis=1)
    early_full = jnp.where(me_t > 0, both[:, ::-1], both).reshape(slot_count, D, D)

    late = jnp.swapaxes(term_qkv.astype(BF).reshape(LATE, nz, sub, D), 0, 1).reshape(-1, D)
    late = lax.psum_scatter(late, "fsdp", scatter_dimension=0, tiled=True)
    late = lax.all_gather(late, ("context", "fsdp"), axis=0, tiled=True)
    late = jnp.swapaxes(late.reshape(nc * nz, LATE, sub, D), 0, 1).reshape(LATE, half_width, D)
    late_other = xor_permute(late, "tensor", 1)
    both = jnp.stack([late, late_other], axis=1)
    late_full = jnp.where(me_t > 0, both[:, ::-1], both).reshape(LATE, D, D)

    mine = lax.dynamic_index_in_dim(slots_of, me_c, 0, keepdims=False)
    grad_full = jnp.where(
        (mine < LATE)[:, None, None], late_full[jnp.clip(mine, 0, LATE - 1)], early_full
    )

    row_count = half_width // nz
    row_offset = me_t * half_width + me_z * row_count
    tokens_all = images * nz * SEQ
    grad_mine = lax.dynamic_slice_in_dim(grad_full, row_offset, row_count, 1)
    left_new = 0.5 * stat_left[:, 0] + 0.5 / tokens_all * jnp.einsum(
        "sra,sba->srb", grad_mine, grad_full, preferred_element_type=F32
    )
    grad_cols = lax.dynamic_slice_in_dim(grad_full, row_offset, row_count, 2)
    right_new = 0.5 * stat_right[:, 0] + 0.5 / tokens_all * jnp.einsum(
        "sar,sab->srb", grad_cols, grad_full, preferred_element_type=F32
    )
    inner_prod = jnp.einsum(
        "sra,sab->srb", root_left[:, 0].astype(BF), grad_full, preferred_element_type=F32
    ).astype(BF)
    update = jnp.einsum(
        "srb,sbc->src", inner_prod, root_right.astype(BF), preferred_element_type=F32
    )
    square_sum = jnp.sum(update * update, axis=(1, 2))
    square_sum = sum_fsdp(square_sum + xor_permute(square_sum, "tensor", 1))
    factor = lax.rsqrt(square_sum / (D * D) + 1e-06)
    weight_new = master[:, 0] - factor[:, None, None] * update

    gain_sum = gain_terms
    step = 1
    while step < nc:
        gain_sum = gain_sum + xor_permute(gain_sum, "context", step)
        step *= 2
    gain_sum = sum_fsdp(gain_sum)
    share_width = gain_state.shape[1]
    gain_index = lax.axis_index(("fsdp", "context"))
    gain_grad = lax.dynamic_slice_in_dim(gain_sum, gain_index * share_width, share_width, 1)
    gain_mine = lax.dynamic_slice_in_dim(gains, gain_index * share_width, share_width, 1)
    state_new = 0.5 * gain_state + 0.5 * gain_grad * gain_grad / tokens_all
    gain_new = gain_mine - 0.1 * gain_grad * lax.rsqrt(tokens_all * state_new)
    return (
        output,
        grad_tokens,
        grad_mine.astype(F32)[:, None],
        left_new[:, None],
        right_new[:, None],
        weight_new[:, None],
        gain_grad,
        state_new,
        gain_new,
    )


def solution(mesh):
    return jax.shard_map(
        per_device,
        mesh=mesh,
        in_specs=(
            P("fsdp", "context", None),
            P("fsdp", "context", None),
            P(),
            P("fsdp", None, "tensor"),
            P("tensor", "fsdp"),
            P("fsdp", "tensor"),
            P("tensor", "fsdp"),
            P("fsdp", "context"),
            P(),
            P("context", "tensor", "fsdp", None),
            P("context", "tensor", "fsdp", None),
            P("context", "tensor", "fsdp", None),
            P("context", None, None),
            P("context", "tensor", "fsdp", None),
            P(None, ("fsdp", "context")),
        ),
        out_specs=(
            P("fsdp", "context", None),
            P("fsdp", "context", None),
            P("context", "tensor", "fsdp", None),
            P("context", "tensor", "fsdp", None),
            P("context", "tensor", "fsdp", None),
            P("context", "tensor", "fsdp", None),
            P(None, ("fsdp", "context")),
            P(None, ("fsdp", "context")),
            P(None, ("fsdp", "context")),
        ),
        check_vma=False,
    )
```

```python
import functools

import jax
import jax.numpy as jnp
from jax import lax
from jax.experimental import pallas as pl
from jax.experimental.pallas import tpu as pltpu
from jax.sharding import PartitionSpec as P

D = 1024
HD = 64
SEQ = 1408
NBLK = 12
LATE = 3
EARLY = NBLK - LATE
BF = jnp.bfloat16
F32 = jnp.float32
SCALE = HD ** (-0.5)


def norm_fwd(field_in, gain_vec):
    centred = field_in - jnp.mean(field_in, axis=-1, keepdims=True)
    inv_std = lax.rsqrt(jnp.mean(centred * centred, axis=-1, keepdims=True) + 1e-06)
    normed = centred * inv_std
    return (normed, inv_std, normed * gain_vec)


def norm_back(grad_out, gain_vec, normed, inv_std):
    scaled = grad_out * gain_vec
    inner_sum = (
        scaled
        - jnp.mean(scaled, axis=-1, keepdims=True)
        - normed * jnp.mean(scaled * normed, axis=-1, keepdims=True)
    )
    return (inner_sum * inv_std, jnp.sum(grad_out * normed, axis=(0, 1)))


def gelu_parts(field_in):
    normal_cdf = 0.5 * (1.0 + lax.erf(field_in * 0.7071067811865476))
    normal_pdf = jnp.exp(-0.5 * field_in * field_in) * 0.3989422804014327
    return (field_in * normal_cdf, normal_cdf + field_in * normal_pdf)


def dot_nt(a, b):
    return lax.dot_general(a, b, (((1,), (1,)), ((), ())), preferred_element_type=F32)


def dot_tn(a, b):
    return lax.dot_general(a, b, (((0,), (0,)), ((), ())), preferred_element_type=F32)


def dot_nn(a, b):
    return lax.dot_general(a, b, (((1,), (0,)), ((), ())), preferred_element_type=F32)


def attn_fwd_kernel(q_ref, k_ref, v_ref, bias_ref, o_ref, lse_ref):
    q = q_ref[...] * SCALE
    k = k_ref[...]
    v = v_ref[...]
    bias = bias_ref[...]
    first = lax.broadcasted_iota(jnp.int32, q.shape, 1) < HD
    outs, sums = [], []
    for head in range(2):
        mask = first if head == 0 else jnp.logical_not(first)
        scores = dot_nt(jnp.where(mask, q, jnp.zeros_like(q)), k) + bias
        peak = jnp.max(scores, axis=-1, keepdims=True)
        expo = jnp.exp(scores - peak)
        total = jnp.sum(expo, axis=-1, keepdims=True)
        outs.append(dot_nn(expo.astype(BF), v) / total)
        sums.append(peak + jnp.log(total))
    o_ref[...] = jnp.where(first, outs[0], outs[1]).astype(BF)
    lse_ref[...] = jnp.where(first, sums[0], sums[1])


def attn_fwd(qkv, bias_row):
    rows = qkv.shape[0]
    bq = rows // 4
    return pl.pallas_call(
        attn_fwd_kernel,
        grid=(rows // bq,),
        out_shape=(
            jax.ShapeDtypeStruct((rows, 128), BF),
            jax.ShapeDtypeStruct((rows, 128), F32),
        ),
        in_specs=[
            pl.BlockSpec((bq, 128), lambda i: (i, 0)),
            pl.BlockSpec((rows, 128), lambda i: (0, 1)),
            pl.BlockSpec((rows, 128), lambda i: (0, 2)),
            pl.BlockSpec((1, rows), lambda i: (0, 0)),
        ],
        out_specs=(
            pl.BlockSpec((bq, 128), lambda i: (i, 0)),
            pl.BlockSpec((bq, 128), lambda i: (i, 0)),
        ),
        compiler_params=pltpu.CompilerParams(vmem_limit_bytes=40 << 20),
        cost_estimate=pl.CostEstimate(
            flops=4 * rows * rows * 512, bytes_accessed=rows * 2048, transcendentals=2 * rows * rows
        ),
        name="attn_fwd",
    )(qkv, qkv, qkv, bias_row)


def attn_bwd_kernel(q_ref, k_ref, v_ref, do_ref, o_ref, lse_ref, live_ref, out_ref, dq_ref, row_ref):
    step = pl.program_id(0)
    chunk = k_ref.shape[0]

    @pl.when(step == 0)
    def _():
        row_ref[0:128, :] = lse_ref[...].T
        prod = do_ref[...].astype(F32) * o_ref[...].astype(F32)
        prod_t = prod.T
        row_ref[128:136, :] = jnp.broadcast_to(
            jnp.sum(prod_t[0:HD], axis=0, keepdims=True), (8, prod_t.shape[1])
        )
        row_ref[136:144, :] = jnp.broadcast_to(
            jnp.sum(prod_t[HD:128], axis=0, keepdims=True), (8, prod_t.shape[1])
        )
        dq_ref[...] = jnp.zeros_like(dq_ref)

    q = q_ref[...]
    k = k_ref[...] * SCALE
    v = v_ref[...]
    do = do_ref[...]
    live = live_ref[:, 0:1] > 0
    first = lax.broadcasted_iota(jnp.int32, k.shape, 1) < HD
    dks, dvs = [], []
    for head in range(2):
        mask = first if head == 0 else jnp.logical_not(first)
        kh = jnp.where(mask, k, jnp.zeros_like(k))
        vh = jnp.where(mask, v, jnp.zeros_like(v))
        lse = row_ref[64 * head : 64 * head + 1, :]
        delta = row_ref[128 + 8 * head : 129 + 8 * head, :]
        prob = jnp.where(live, jnp.exp(dot_nt(kh, q) - lse), 0.0)
        ds = (prob * (dot_nt(vh, do) - delta)).astype(BF)
        dvs.append(dot_nn(prob.astype(BF), do))
        dks.append(dot_nn(ds, q) * SCALE)
        dq_ref[...] += dot_tn(ds, kh)
    at = pl.ds(pl.multiple_of(step * chunk, chunk), chunk)
    out_ref[at, 128:256] = jnp.where(first, dks[0], dks[1]).astype(BF)
    out_ref[at, 256:384] = jnp.where(first, dvs[0], dvs[1]).astype(BF)

    @pl.when(step == pl.num_programs(0) - 1)
    def _():
        out_ref[:, 0:128] = dq_ref[...].astype(BF)


def attn_bwd(qkv, grad, out, lse, live_col):
    rows = qkv.shape[0]
    chunk = rows // 4
    return pl.pallas_call(
        attn_bwd_kernel,
        grid=(rows // chunk,),
        out_shape=jax.ShapeDtypeStruct((rows, 384), BF),
        in_specs=[
            pl.BlockSpec((rows, 128), lambda i: (0, 0)),
            pl.BlockSpec((chunk, 128), lambda i: (i, 1)),
            pl.BlockSpec((chunk, 128), lambda i: (i, 2)),
            pl.BlockSpec((rows, 128), lambda i: (0, 0)),
            pl.BlockSpec((rows, 128), lambda i: (0, 0)),
            pl.BlockSpec((rows, 128), lambda i: (0, 0)),
            pl.BlockSpec((chunk, 128), lambda i: (i, 0)),
        ],
        out_specs=pl.BlockSpec((rows, 384), lambda i: (0, 0)),
        scratch_shapes=[pltpu.VMEM((rows, 128), F32), pltpu.VMEM((144, rows), F32)],
        compiler_params=pltpu.CompilerParams(vmem_limit_bytes=50 << 20),
        cost_estimate=pl.CostEstimate(
            flops=10 * rows * rows * 512, bytes_accessed=rows * 4096, transcendentals=2 * rows * rows
        ),
        name="attn_bwd",
    )(qkv, qkv, qkv, grad, out, lse, live_col)


class Moves:
    def __init__(self, send_sems, recv_sems):
        self.send_sems, self.recv_sems, self.count = send_sems, recv_sems, 0

    def make(self, src, dst, device, cond=None, recv_cond=None):
        index = self.count
        self.count += 1
        return Move(self, index, src, dst, device, cond, recv_cond)


class Move:
    def __init__(self, moves, index, src, dst, device, cond, recv_cond):
        self.args = (src, dst, moves.send_sems.at[index], moves.recv_sems.at[index])
        self.device, self.cond, self.recv_cond = device, cond, recv_cond

    def copy(self):
        return pltpu.make_async_remote_copy(
            *self.args, device_id=self.device, device_id_type=pl.DeviceIdType.MESH
        )

    def when(self, cond, act):
        if cond is None:
            act()
        else:
            pl.when(cond)(act)

    def start(self):
        self.when(self.cond, lambda: self.copy().start())

    def wait_recv(self):
        self.when(self.recv_cond, lambda: self.copy().wait_recv())

    def wait_send(self):
        self.when(self.cond, lambda: self.copy().wait_send())


def greet(devices):
    barrier = pltpu.get_barrier_semaphore()
    for device in devices:
        pl.semaphore_signal(
            barrier, inc=1, device_id=device, device_id_type=pl.DeviceIdType.MESH
        )
    pl.semaphore_wait(barrier, len(devices))


def grad_gather_kernel(
    nz, nc, slot_blocks, early_ref, late_ref, out_ref, g_ref, l_ref, place_ref, part_ref, send, recv
):
    me_z, me_c, me_t = (lax.axis_index(a) for a in ("fsdp", "context", "tensor"))
    slots = out_ref.shape[0]
    core = {"tensor": 1 - me_t}
    x_near, y_near = {"context": me_c ^ 1}, {"context": me_c ^ 2}
    above, below = {"fsdp": me_z + 1}, {"fsdp": me_z - 1}
    z_peers = [{"fsdp": lax.rem(me_z + k, nz)} for k in range(1, nz)]
    c_peers = [{"context": me_c ^ k} for k in range(1, nc)]
    greet(z_peers + c_peers + [core])
    moves = Moves(send, recv)
    sent = []

    def go(*args, **kw):
        move = moves.make(*args, **kw)
        move.start()
        sent.append(move)
        return move

    late_in = [
        go(late_ref.at[lax.rem(me_z + k, nz)], part_ref.at[k - 1], z_peers[k - 1])
        for k in range(1, nz)
    ]
    for slot in range(NBLK):
        block = jnp.clip(slot_blocks[slot] - LATE, 0, EARLY - 1)
        place_ref[slot] = early_ref[block]
    placed = []
    for k in range(1, nc):
        theirs = place_ref.at[pl.ds((me_c ^ k) * slots, slots)]
        placed.append(go(theirs, g_ref.at[:, me_t, me_c, me_z], c_peers[k - 1]))
    for slot in range(slots):
        g_ref[slot, me_t, me_c, me_z] = place_ref[me_c * slots + slot]

    def along_fsdp(ref, member, ready):
        ready()
        own = ref.at[:, me_t, member, me_z]
        up = go(own, own, above, cond=me_z < nz - 1, recv_cond=me_z > 0)
        down = go(own, own, below, cond=me_z > 0, recv_cond=me_z < nz - 1)
        return [up, down]

    def onward(ref, member, last, hop):
        up_in, down_in = last
        up_z, down_z = me_z - hop, me_z + hop
        up_in.wait_recv()
        up = down = None
        if hop < nz - 1:
            piece = ref.at[:, me_t, member, up_z]
            up = go(
                piece,
                piece,
                above,
                cond=jnp.logical_and(me_z < nz - 1, up_z >= 0),
                recv_cond=up_z - 1 >= 0,
            )
        down_in.wait_recv()
        if hop < nz - 1:
            piece = ref.at[:, me_t, member, down_z]
            down = go(
                piece,
                piece,
                below,
                cond=jnp.logical_and(me_z > 0, down_z <= nz - 1),
                recv_cond=down_z + 1 <= nz - 1,
            )
        return [up, down], [(up_z, up_z >= 0), (down_z, down_z <= nz - 1)]

    swapped = []

    def swap(ref, member, z, cond=None, columns=None):
        piece = ref.at[:, me_t, member, z]
        if columns is not None:
            piece = ref.at[:, me_t, member, z, :, columns]
        swapped.append(go(piece, piece, core, cond=cond, recv_cond=cond))

    lines = {}
    for k in range(nc):
        member = me_c ^ k
        lines[k] = along_fsdp(
            g_ref, member, (lambda: None) if k == 0 else placed[k - 1].wait_recv
        )
        swap(g_ref, member, me_z)

    total = late_ref[me_z].astype(F32)
    for k in range(1, nz):
        late_in[k - 1].wait_recv()
        total = total + part_ref[k - 1].astype(F32)
    l_ref[:, me_t, me_c, me_z] = total.astype(BF)
    late_line = along_fsdp(l_ref, me_c, lambda: None)
    left, right = pl.ds(0, D // 2), pl.ds(D // 2, D // 2)
    near = []

    def spread(z, cond=None):
        piece = l_ref.at[:, me_t, me_c, z]
        near.append(
            (
                z,
                cond,
                go(piece, piece, x_near, cond=cond, recv_cond=cond),
                go(piece, piece, y_near, cond=cond, recv_cond=cond),
            )
        )
        swap(l_ref, me_c, z, cond)

    spread(me_z)
    far = []
    done = 0

    def spread_on():
        nonlocal done
        for z, cond, x_in, y_in in near[done:]:
            x_in.wait_recv()
            piece = l_ref.at[:, me_t, me_c ^ 1, z, :, left]
            far.append((z, cond, left, go(piece, piece, y_near, cond=cond, recv_cond=cond)))
            swap(l_ref, me_c ^ 1, z, cond)
            y_in.wait_recv()
            piece = l_ref.at[:, me_t, me_c ^ 2, z, :, right]
            far.append((z, cond, right, go(piece, piece, x_near, cond=cond, recv_cond=cond)))
            swap(l_ref, me_c ^ 2, z, cond)
        done = len(near)

    for hop in range(1, nz):
        before = late_line
        late_line, here = onward(l_ref, me_c, before, hop)
        for z, cond in here:
            spread(z, cond)
        for k in range(nc):
            member = me_c ^ k
            lines[k], here = onward(g_ref, member, lines[k], hop)
            for z, cond in here:
                swap(g_ref, member, z, cond)
        spread_on()
    for z, cond, columns, move in far:
        move.wait_recv()
        swap(l_ref, me_c ^ 3, z, cond, columns)
    for move in swapped:
        move.wait_recv()
    for slot in range(slots):
        block = slot_blocks[me_c * slots + slot]
        late = l_ref[jnp.clip(block, 0, LATE - 1)]
        out_ref[slot] = jnp.where(block < LATE, late, g_ref[slot])
    for move in sent:
        move.wait_send()


def grad_gather(block_of, early, late, nz, nc, nt):
    sub = early.shape[1]
    slots = NBLK // nc
    shape = (slots, nt, nc, nz, sub, D)
    count = 192
    vmem = pl.BlockSpec(memory_space=pltpu.VMEM)
    out = pl.pallas_call(
        functools.partial(grad_gather_kernel, nz, nc),
        out_shape=jax.ShapeDtypeStruct(shape, BF),
        in_specs=[pl.BlockSpec(memory_space=pltpu.SMEM), vmem, vmem],
        out_specs=vmem,
        scratch_shapes=[
            pltpu.VMEM(shape, BF),
            pltpu.VMEM((LATE, nt, nc, nz, sub, D), BF),
            pltpu.VMEM((NBLK, sub, D), BF),
            pltpu.VMEM((nz - 1, LATE, sub, D), BF),
            pltpu.SemaphoreType.DMA((count,)),
            pltpu.SemaphoreType.DMA((count,)),
        ],
        compiler_params=pltpu.CompilerParams(
            collective_id=0, has_side_effects=True, vmem_limit_bytes=40 << 20
        ),
        name="grad_gather",
    )(block_of, early, late)
    return out.reshape(slots, D, D)


def xor_permute(value, axis, step):
    size = lax.axis_size(axis)
    return lax.ppermute(value, axis, [(j, j ^ step) for j in range(size)])


def xor_order(pieces, index):
    bit = 1
    while bit < len(pieces):
        odd = (index & bit) > 0
        pieces = [jnp.where(odd, pieces[j ^ bit], pieces[j]) for j in range(len(pieces))]
        bit *= 2
    return pieces


def sum_tensor(value):
    low = lax.optimization_barrier(value.astype(BF))
    return low.astype(F32) + xor_permute(low, "tensor", 1).astype(F32)


def gather_fsdp(value):
    size = lax.axis_size("fsdp")
    if size > 4:
        return lax.all_gather(value, "fsdp", axis=0, tiled=False)
    pieces = [value] + [
        lax.ppermute(value, "fsdp", [(j, (j - k) % size) for j in range(size)])
        for k in range(1, size)
    ]
    doubled = jnp.stack(pieces + pieces[:-1])
    start = lax.rem(size - lax.axis_index("fsdp"), size)
    return lax.dynamic_slice_in_dim(doubled, start, size, 0)


def sum_fsdp(value):
    size = lax.axis_size("fsdp")
    if size > 4:
        return lax.psum(value, "fsdp")
    total = value
    for k in range(1, size):
        total = total + lax.ppermute(value, "fsdp", [(j, (j - k) % size) for j in range(size)])
    return total


def grad_gather_plain(block_of, early, late, nz, nc):
    me_c, me_t = (lax.axis_index(a) for a in ("context", "tensor"))
    sub = early.shape[1]
    half_width = nc * nz * sub
    slot_count = NBLK // nc
    slots_of = block_of.reshape(nc, slot_count)

    def slots_for(k):
        blocks = lax.dynamic_index_in_dim(slots_of, me_c ^ k, 0, keepdims=False)
        return early[jnp.clip(blocks - LATE, 0, EARLY - 1)]

    placed = [slots_for(0)] + [xor_permute(slots_for(k), "context", k) for k in range(1, nc)]
    placed = jnp.stack(xor_order(placed, me_c), axis=1)
    placed = lax.all_gather(placed, "fsdp", axis=2, tiled=False)
    placed = placed.reshape(slot_count, half_width, D)
    placed_other = xor_permute(placed, "tensor", 1)
    both = jnp.stack([placed, placed_other], axis=1)
    early_full = jnp.where(me_t > 0, both[:, ::-1], both).reshape(slot_count, D, D)

    late = late.reshape(-1, D)
    late = lax.psum_scatter(late, "fsdp", scatter_dimension=0, tiled=True)
    late = lax.all_gather(late, ("context", "fsdp"), axis=0, tiled=True)
    late = jnp.swapaxes(late.reshape(nc * nz, LATE, sub, D), 0, 1).reshape(LATE, half_width, D)
    late_other = xor_permute(late, "tensor", 1)
    both = jnp.stack([late, late_other], axis=1)
    late_full = jnp.where(me_t > 0, both[:, ::-1], both).reshape(LATE, D, D)

    mine = lax.dynamic_index_in_dim(slots_of, me_c, 0, keepdims=False)
    return jnp.where(
        (mine < LATE)[:, None, None], late_full[jnp.clip(mine, 0, LATE - 1)], early_full
    )


def per_device(
    tokens,
    cotangent,
    gains,
    w_qkv,
    w_out,
    w_up,
    w_down,
    key_mask,
    owner,
    stat_left,
    stat_right,
    root_left,
    root_right,
    master,
    gain_state,
):
    images, local_len = tokens.shape[:2]
    tok_rows = images * local_len
    nz, nc, nt = (lax.axis_size(a) for a in ("fsdp", "context", "tensor"))
    me_z, me_c, me_t = (lax.axis_index(a) for a in ("fsdp", "context", "tensor"))
    half_width = w_qkv.shape[2]
    hidden = w_up.shape[1]
    up_blocks = hidden // half_width
    cols = half_width // nc
    half_len = local_len // nt

    wq_part = lax.dynamic_slice_in_dim(w_qkv, me_c * cols, cols, 2)
    wq = gather_fsdp(wq_part).reshape(D, 3 * cols)

    def two_stage(weight, member_axis, fsdp_axis):
        width = weight.shape[member_axis] // nc
        part = lax.dynamic_slice_in_dim(weight, me_c * width, width, member_axis)
        part = lax.all_gather(part, "fsdp", axis=fsdp_axis, tiled=True)
        return lax.all_gather(part, "context", axis=member_axis, tiled=True)

    out_full = two_stage(w_out, 0, 1)
    up_full = two_stage(w_up, 1, 0)
    down_full = two_stage(w_down, 0, 1)

    counts = jnp.sum(key_mask, axis=1)
    real = counts
    for k in range(1, nc):
        real = real + xor_permute(counts, "context", k)
    position = (
        (me_c ^ jnp.arange(nc))[:, None, None] * local_len
        + (me_t ^ jnp.arange(nt))[None, :, None] * half_len
        + jnp.arange(half_len)[None, None, :]
    ).reshape(-1)
    live = position[None, :] < real[:, None]
    bias = jnp.where(live, 0.0, -1e30).astype(F32)
    live_col = jnp.broadcast_to(live[:, :, None].astype(F32), (images, SEQ, 128))

    normed1, inv_std1, pre_norm1 = norm_fwd(tokens, gains[0])
    normed1_low = pre_norm1.astype(BF)

    def to_natural(value):
        parts = value.reshape((nt, half_len) + value.shape[1:])
        return jnp.where(me_t > 0, parts[::-1], parts).reshape(value.shape)

    x_all, qkv, out_heads, log_sums, attended = [], [], [], [], []
    for i in range(images):
        mine = lax.dynamic_slice_in_dim(normed1_low[i], me_t * half_len, half_len, 0)
        held = jnp.stack([mine] + [xor_permute(mine, "context", k) for k in range(1, nc)])
        other = xor_permute(held, "tensor", 1)
        x_i = jnp.stack([held, other], axis=1).reshape(SEQ, D)
        qkv_i = dot_nn(x_i, wq).astype(BF)
        o_i, lse_i = attn_fwd(qkv_i, bias[i][None])
        chunks = o_i.reshape(nc, local_len, 2 * HD)
        moved = [to_natural(chunks[0])] + [
            to_natural(xor_permute(chunks[k], "context", k)) for k in range(1, nc)
        ]
        attended.append(jnp.concatenate(xor_order(moved, me_c), axis=-1))
        x_all.append(x_i)
        qkv.append(qkv_i)
        out_heads.append(o_i)
        log_sums.append(lse_i)
    attended = jnp.stack(attended)

    branch_attn = sum_tensor(
        jnp.einsum("ish,hd->isd", attended, out_full, preferred_element_type=F32)
    )
    middle = tokens + gains[2] * branch_attn
    normed2, inv_std2, pre_norm2 = norm_fwd(middle, gains[1])
    normed2_low = pre_norm2.astype(BF)
    pre_act = jnp.einsum("isd,df->isf", normed2_low, up_full, preferred_element_type=F32)
    act_val, act_slope = gelu_parts(pre_act)
    act_low = act_val.astype(BF)
    branch_mlp = sum_tensor(
        jnp.einsum("isf,fd->isd", act_low, down_full, preferred_element_type=F32)
    )
    output = middle + gains[3] * branch_mlp

    grad_mlp = (gains[3] * cotangent).astype(BF)
    grad_hidden = jnp.einsum("isd,fd->isf", grad_mlp, down_full, preferred_element_type=F32)
    grad_pre = (grad_hidden * act_slope).astype(BF)
    grad_n2 = sum_tensor(
        jnp.einsum("isf,df->isd", grad_pre, up_full, preferred_element_type=F32)
    )
    middle_part, grad_gain2 = norm_back(grad_n2, gains[1], normed2, inv_std2)
    grad_middle = cotangent + middle_part
    grad_branch = (gains[2] * grad_middle).astype(BF)
    grad_att = jnp.einsum(
        "isd,hd->ish", grad_branch, out_full, preferred_element_type=F32
    ).astype(BF)

    term_qkv = None
    grad_tok = []
    for i in range(images):
        pieces = [grad_att[i, :, j * cols : (j + 1) * cols] for j in range(nc)]
        pieces = [to_natural(p) for p in xor_order(pieces, me_c)]
        grad_i = jnp.concatenate(
            [pieces[0]] + [xor_permute(pieces[k], "context", k) for k in range(1, nc)]
        )
        g_i = attn_bwd(qkv[i], grad_i, out_heads[i], log_sums[i], live_col[i])
        chunks = g_i.reshape(nc, local_len, 3 * cols)
        moved = [to_natural(chunks[0])] + [
            to_natural(xor_permute(chunks[k], "context", k)) for k in range(1, nc)
        ]
        grad_tok.append(jnp.stack(xor_order(moved, me_c), axis=1))
        term = dot_tn(g_i, x_all[i])
        term_qkv = term if term_qkv is None else term_qkv + term
    grad_tok = jnp.stack(grad_tok)
    wq_all = lax.all_gather(wq, "context", axis=0, tiled=False)
    grad_n1 = sum_tensor(
        jnp.einsum("isjc,jdc->isd", grad_tok, wq_all, preferred_element_type=F32)
    )
    input_part, grad_gain1 = norm_back(grad_n1, gains[0], normed1, inv_std1)
    grad_tokens = grad_middle + input_part
    grad_gain3 = jnp.sum(grad_middle * branch_attn, axis=(0, 1))
    grad_gain4 = jnp.sum(cotangent * branch_mlp, axis=(0, 1))
    gain_terms = jnp.stack([grad_gain1, grad_gain2, grad_gain3, grad_gain4], axis=0)

    def early_terms(left, right):
        term = dot_tn(left.reshape(tok_rows, -1), right.reshape(tok_rows, D)).astype(BF)
        term = jnp.swapaxes(term.reshape(-1, nc, half_width // nc, D), 0, 1)
        return lax.psum_scatter(
            term.reshape(-1, D), "context", scatter_dimension=0, tiled=True
        ).reshape(-1, half_width // nc, D)

    early = jnp.concatenate(
        [
            early_terms(attended, grad_branch),
            early_terms(grad_pre, normed2_low),
            early_terms(act_low, grad_mlp),
        ],
        axis=0,
    )
    sub = half_width // nc // nz
    early = lax.psum_scatter(
        jnp.swapaxes(early.reshape(EARLY, nz, sub, D), 0, 1).reshape(-1, D),
        "fsdp",
        scatter_dimension=0,
        tiled=True,
    ).reshape(EARLY, sub, D)
    onehot = (owner[:, None] == jnp.arange(NBLK, dtype=jnp.int32)[None, :]).astype(jnp.int32)
    block_of = jnp.sum(onehot * jnp.arange(NBLK, dtype=jnp.int32)[:, None], axis=0)

    late = jnp.swapaxes(term_qkv.astype(BF).reshape(LATE, nz, sub, D), 0, 1)
    if nz == 4 and nc == 4:
        grad_full = grad_gather(block_of, early, late, nz, nc, nt)
    else:
        grad_full = grad_gather_plain(block_of, early, late, nz, nc)

    row_count = half_width // nz
    row_offset = me_t * half_width + me_z * row_count
    tokens_all = images * nz * SEQ
    grad_mine = lax.dynamic_slice_in_dim(grad_full, row_offset, row_count, 1)
    left_new = 0.5 * stat_left[:, 0] + 0.5 / tokens_all * jnp.einsum(
        "sra,sba->srb", grad_mine, grad_full, preferred_element_type=F32
    )
    grad_cols = lax.dynamic_slice_in_dim(grad_full, row_offset, row_count, 2)
    right_new = 0.5 * stat_right[:, 0] + 0.5 / tokens_all * jnp.einsum(
        "sar,sab->srb", grad_cols, grad_full, preferred_element_type=F32
    )
    inner_prod = jnp.einsum(
        "sra,sab->srb", root_left[:, 0].astype(BF), grad_full, preferred_element_type=F32
    ).astype(BF)
    update = jnp.einsum(
        "srb,sbc->src", inner_prod, root_right.astype(BF), preferred_element_type=F32
    )
    square_sum = jnp.sum(update * update, axis=(1, 2))
    square_sum = sum_fsdp(square_sum + xor_permute(square_sum, "tensor", 1))
    factor = lax.rsqrt(square_sum / (D * D) + 1e-06)
    weight_new = master[:, 0] - factor[:, None, None] * update

    gain_sum = gain_terms
    step = 1
    while step < nc:
        gain_sum = gain_sum + xor_permute(gain_sum, "context", step)
        step *= 2
    gain_sum = sum_fsdp(gain_sum)
    share_width = gain_state.shape[1]
    gain_index = lax.axis_index(("fsdp", "context"))
    gain_grad = lax.dynamic_slice_in_dim(gain_sum, gain_index * share_width, share_width, 1)
    gain_mine = lax.dynamic_slice_in_dim(gains, gain_index * share_width, share_width, 1)
    state_new = 0.5 * gain_state + 0.5 * gain_grad * gain_grad / tokens_all
    gain_new = gain_mine - 0.1 * gain_grad * lax.rsqrt(tokens_all * state_new)
    return (
        output,
        grad_tokens,
        grad_mine.astype(F32)[:, None],
        left_new[:, None],
        right_new[:, None],
        weight_new[:, None],
        gain_grad,
        state_new,
        gain_new,
    )


def solution(mesh):
    return jax.shard_map(
        per_device,
        mesh=mesh,
        in_specs=(
            P("fsdp", "context", None),
            P("fsdp", "context", None),
            P(),
            P("fsdp", None, "tensor"),
            P("tensor", "fsdp"),
            P("fsdp", "tensor"),
            P("tensor", "fsdp"),
            P("fsdp", "context"),
            P(),
            P("context", "tensor", "fsdp", None),
            P("context", "tensor", "fsdp", None),
            P("context", "tensor", "fsdp", None),
            P("context", None, None),
            P("context", "tensor", "fsdp", None),
            P(None, ("fsdp", "context")),
        ),
        out_specs=(
            P("fsdp", "context", None),
            P("fsdp", "context", None),
            P("context", "tensor", "fsdp", None),
            P("context", "tensor", "fsdp", None),
            P("context", "tensor", "fsdp", None),
            P("context", "tensor", "fsdp", None),
            P(None, ("fsdp", "context")),
            P(None, ("fsdp", "context")),
            P(None, ("fsdp", "context")),
        ),
        check_vma=False,
    )
```

```python
import functools

import jax
import jax.numpy as jnp
from jax import lax
from jax.experimental import pallas as pl
from jax.experimental.pallas import tpu as pltpu
from jax.sharding import PartitionSpec as P

D = 1024
HD = 64
SEQ = 1408
NBLK = 12
LATE = 3
EARLY = NBLK - LATE
BF = jnp.bfloat16
F32 = jnp.float32
SCALE = HD ** (-0.5)


def norm_fwd(field_in, gain_vec):
    centred = field_in - jnp.mean(field_in, axis=-1, keepdims=True)
    inv_std = lax.rsqrt(jnp.mean(centred * centred, axis=-1, keepdims=True) + 1e-06)
    normed = centred * inv_std
    return (normed, inv_std, normed * gain_vec)


def norm_back(grad_out, gain_vec, normed, inv_std):
    scaled = grad_out * gain_vec
    inner_sum = (
        scaled
        - jnp.mean(scaled, axis=-1, keepdims=True)
        - normed * jnp.mean(scaled * normed, axis=-1, keepdims=True)
    )
    return (inner_sum * inv_std, jnp.sum(grad_out * normed, axis=(0, 1)))


def gelu_parts(field_in):
    normal_cdf = 0.5 * (1.0 + lax.erf(field_in * 0.7071067811865476))
    normal_pdf = jnp.exp(-0.5 * field_in * field_in) * 0.3989422804014327
    return (field_in * normal_cdf, normal_cdf + field_in * normal_pdf)


def dot_nt(a, b):
    return lax.dot_general(a, b, (((1,), (1,)), ((), ())), preferred_element_type=F32)


def dot_tn(a, b):
    return lax.dot_general(a, b, (((0,), (0,)), ((), ())), preferred_element_type=F32)


def dot_nn(a, b):
    return lax.dot_general(a, b, (((1,), (0,)), ((), ())), preferred_element_type=F32)


def attn_fwd_kernel(q_ref, k_ref, v_ref, bias_ref, o_ref, lse_ref):
    q = q_ref[...] * SCALE
    k = k_ref[...]
    v = v_ref[...]
    bias = bias_ref[...]
    first = lax.broadcasted_iota(jnp.int32, q.shape, 1) < HD
    outs, sums = [], []
    for head in range(2):
        mask = first if head == 0 else jnp.logical_not(first)
        scores = dot_nt(jnp.where(mask, q, jnp.zeros_like(q)), k) + bias
        peak = jnp.max(scores, axis=-1, keepdims=True)
        expo = jnp.exp(scores - peak)
        total = jnp.sum(expo, axis=-1, keepdims=True)
        outs.append(dot_nn(expo.astype(BF), v) / total)
        sums.append(peak + jnp.log(total))
    o_ref[...] = jnp.where(first, outs[0], outs[1]).astype(BF)
    lse_ref[...] = jnp.where(first, sums[0], sums[1])


def attn_fwd(qkv, bias_row):
    rows = qkv.shape[0]
    bq = rows // 4
    return pl.pallas_call(
        attn_fwd_kernel,
        grid=(rows // bq,),
        out_shape=(
            jax.ShapeDtypeStruct((rows, 128), BF),
            jax.ShapeDtypeStruct((rows, 128), F32),
        ),
        in_specs=[
            pl.BlockSpec((bq, 128), lambda i: (i, 0)),
            pl.BlockSpec((rows, 128), lambda i: (0, 1)),
            pl.BlockSpec((rows, 128), lambda i: (0, 2)),
            pl.BlockSpec((1, rows), lambda i: (0, 0)),
        ],
        out_specs=(
            pl.BlockSpec((bq, 128), lambda i: (i, 0)),
            pl.BlockSpec((bq, 128), lambda i: (i, 0)),
        ),
        compiler_params=pltpu.CompilerParams(vmem_limit_bytes=40 << 20),
        cost_estimate=pl.CostEstimate(
            flops=4 * rows * rows * 512, bytes_accessed=rows * 2048, transcendentals=2 * rows * rows
        ),
        name="attn_fwd",
    )(qkv, qkv, qkv, bias_row)


def attn_bwd_kernel(q_ref, k_ref, v_ref, do_ref, o_ref, lse_ref, live_ref, out_ref, dq_ref, row_ref):
    step = pl.program_id(0)
    chunk = k_ref.shape[0]

    @pl.when(step == 0)
    def _():
        row_ref[0:128, :] = lse_ref[...].T
        prod = do_ref[...].astype(F32) * o_ref[...].astype(F32)
        prod_t = prod.T
        row_ref[128:136, :] = jnp.broadcast_to(
            jnp.sum(prod_t[0:HD], axis=0, keepdims=True), (8, prod_t.shape[1])
        )
        row_ref[136:144, :] = jnp.broadcast_to(
            jnp.sum(prod_t[HD:128], axis=0, keepdims=True), (8, prod_t.shape[1])
        )
        dq_ref[...] = jnp.zeros_like(dq_ref)

    q = q_ref[...]
    k = k_ref[...] * SCALE
    v = v_ref[...]
    do = do_ref[...]
    live = live_ref[:, 0:1] > 0
    first = lax.broadcasted_iota(jnp.int32, k.shape, 1) < HD
    dks, dvs = [], []
    for head in range(2):
        mask = first if head == 0 else jnp.logical_not(first)
        kh = jnp.where(mask, k, jnp.zeros_like(k))
        vh = jnp.where(mask, v, jnp.zeros_like(v))
        lse = row_ref[64 * head : 64 * head + 1, :]
        delta = row_ref[128 + 8 * head : 129 + 8 * head, :]
        prob = jnp.where(live, jnp.exp(dot_nt(kh, q) - lse), 0.0)
        ds = (prob * (dot_nt(vh, do) - delta)).astype(BF)
        dvs.append(dot_nn(prob.astype(BF), do))
        dks.append(dot_nn(ds, q) * SCALE)
        dq_ref[...] += dot_tn(ds, kh)
    at = pl.ds(pl.multiple_of(step * chunk, chunk), chunk)
    out_ref[at, 128:256] = jnp.where(first, dks[0], dks[1]).astype(BF)
    out_ref[at, 256:384] = jnp.where(first, dvs[0], dvs[1]).astype(BF)

    @pl.when(step == pl.num_programs(0) - 1)
    def _():
        out_ref[:, 0:128] = dq_ref[...].astype(BF)


def attn_bwd(qkv, grad, out, lse, live_col):
    rows = qkv.shape[0]
    chunk = rows // 4
    return pl.pallas_call(
        attn_bwd_kernel,
        grid=(rows // chunk,),
        out_shape=jax.ShapeDtypeStruct((rows, 384), BF),
        in_specs=[
            pl.BlockSpec((rows, 128), lambda i: (0, 0)),
            pl.BlockSpec((chunk, 128), lambda i: (i, 1)),
            pl.BlockSpec((chunk, 128), lambda i: (i, 2)),
            pl.BlockSpec((rows, 128), lambda i: (0, 0)),
            pl.BlockSpec((rows, 128), lambda i: (0, 0)),
            pl.BlockSpec((rows, 128), lambda i: (0, 0)),
            pl.BlockSpec((chunk, 128), lambda i: (i, 0)),
        ],
        out_specs=pl.BlockSpec((rows, 384), lambda i: (0, 0)),
        scratch_shapes=[pltpu.VMEM((rows, 128), F32), pltpu.VMEM((144, rows), F32)],
        compiler_params=pltpu.CompilerParams(vmem_limit_bytes=50 << 20),
        cost_estimate=pl.CostEstimate(
            flops=10 * rows * rows * 512, bytes_accessed=rows * 4096, transcendentals=2 * rows * rows
        ),
        name="attn_bwd",
    )(qkv, qkv, qkv, grad, out, lse, live_col)


class Moves:
    def __init__(self, send_sems, recv_sems):
        self.send_sems, self.recv_sems, self.count = send_sems, recv_sems, 0

    def make(self, src, dst, device, cond=None, recv_cond=None):
        index = self.count
        self.count += 1
        return Move(self, index, src, dst, device, cond, recv_cond)


class Move:
    def __init__(self, moves, index, src, dst, device, cond, recv_cond):
        self.args = (src, dst, moves.send_sems.at[index], moves.recv_sems.at[index])
        self.device, self.cond, self.recv_cond = device, cond, recv_cond

    def copy(self):
        return pltpu.make_async_remote_copy(
            *self.args, device_id=self.device, device_id_type=pl.DeviceIdType.MESH
        )

    def when(self, cond, act):
        if cond is None:
            act()
        else:
            pl.when(cond)(act)

    def start(self):
        self.when(self.cond, lambda: self.copy().start())

    def wait_recv(self):
        self.when(self.recv_cond, lambda: self.copy().wait_recv())

    def wait_send(self):
        self.when(self.cond, lambda: self.copy().wait_send())


def greet(devices):
    barrier = pltpu.get_barrier_semaphore()
    for device in devices:
        pl.semaphore_signal(
            barrier, inc=1, device_id=device, device_id_type=pl.DeviceIdType.MESH
        )
    pl.semaphore_wait(barrier, len(devices))


def span(start, size):
    return pl.ds(pl.multiple_of(start, size & -size), size)


class Local:
    def __init__(self, sems):
        self.sems, self.count, self.open = sems, 0, []

    def start(self, src, dst):
        copy = pltpu.make_async_copy(src, dst, self.sems.at[self.count])
        self.count += 1
        copy.start()
        self.open.append(copy)
        return copy

    def wait(self, copy):
        copy.wait()
        self.open = [c for c in self.open if c is not copy]

    def finish(self):
        for copy in self.open:
            copy.wait()
        self.open = []


def spread_plane(go, ref_of, me_c, cond=None):
    own = ref_of(me_c, None)
    return [go(own, own, {"context": me_c ^ 1}), go(own, own, {"context": me_c ^ 2})]


def spread_plane_on(go, ref_of, me_c, near):
    near[0].wait_recv()
    piece = ref_of(me_c ^ 1, 0)
    first = go(piece, piece, {"context": me_c ^ 2})
    near[1].wait_recv()
    piece = ref_of(me_c ^ 2, 1)
    second = go(piece, piece, {"context": me_c ^ 1})
    return [first, second]


def forward_kernel(
    nz,
    nc,
    tokens_ref,
    gain_ref,
    count_ref,
    wq_ref,
    wout_ref,
    wup_ref,
    wdown_ref,
    x_out,
    qkv_out,
    o_out,
    lse_out,
    att_out,
    cnt_out,
    wq_out,
    out_full,
    up_full,
    down_part,
    tok,
    x_all,
    qkv,
    o_all,
    lse_all,
    wq,
    counts,
    send,
    recv,
    local_sems,
):
    me_z, me_c, me_t = (lax.axis_index(a) for a in ("fsdp", "context", "tensor"))
    images, local_len = att_out.shape[:2]
    half = local_len // 2
    seq = x_all.shape[1]
    core = {"tensor": 1 - me_t}
    z_peers = [{"fsdp": lax.rem(me_z + k, nz)} for k in range(1, nz)]
    c_peers = [{"context": me_c ^ k} for k in range(1, nc)]
    local = Local(local_sems)
    token_in = [
        local.start(tokens_ref.at[i, span(me_t * half, half)], tok.at[i]) for i in range(images)
    ]
    depth = wq_ref.shape[0]
    wq_own = local.start(wq_ref, wq.at[span(me_z * depth, depth)])
    greet(z_peers + c_peers + [core])
    moves = Moves(send, recv)
    sent = []

    def go(*args, **kw):
        move = moves.make(*args, **kw)
        move.start()
        sent.append(move)
        return move

    wq_in = [go(wq_ref, wq.at[span(me_z * depth, depth)], peer) for peer in z_peers]
    counts[me_c] = count_ref[...]
    count_in = [go(count_ref, counts.at[me_c], peer) for peer in c_peers]

    def to_line(src, dst):
        local_copy = local.start(src, dst)
        return [local_copy] + [go(src, dst, peer) for peer in z_peers]

    cols, hid, depth_o = wout_ref.shape[0] // nc, wup_ref.shape[1] // nc, wout_ref.shape[1]
    out_in = to_line(
        wout_ref.at[span(me_c * cols, cols)],
        out_full.at[span(me_c * cols, cols), span(me_z * depth_o, depth_o)],
    )
    up_in = to_line(
        wup_ref.at[:, span(me_c * hid, hid)],
        up_full.at[span(me_z * depth, depth), span(me_c * hid, hid)],
    )
    down_in = to_line(
        wdown_ref.at[span(me_c * hid, hid)], down_part.at[:, span(me_z * depth_o, depth_o)]
    )

    def x_piece(i):
        def at(member, part):
            rows = span(member * local_len + me_t * half, half)
            if part is None:
                return x_all.at[i, rows]
            return x_all.at[i, rows, pl.ds(part * (D // 2), D // 2)]

        return at

    swaps = [[] for _ in range(images)]

    def swap(i, member, part=None):
        piece = x_piece(i)(member, part)
        swaps[i].append(go(piece, piece, core))

    near = []
    for i in range(images):
        local.wait(token_in[i])
        value = tok[i]
        centred = value - jnp.mean(value, axis=-1, keepdims=True)
        inv_std = lax.rsqrt(jnp.mean(centred * centred, axis=-1, keepdims=True) + 1e-06)
        x_all[i, span(me_c * local_len + me_t * half, half)] = (
            centred * inv_std * gain_ref[...]
        ).astype(BF)
        near.append(spread_plane(go, x_piece(i), me_c))
        swap(i, me_c)
    far = []
    for i in range(images):
        far.append(spread_plane_on(go, x_piece(i), me_c, near[i]))
        swap(i, me_c ^ 1)
        swap(i, me_c ^ 2)

    local.wait(wq_own)
    for move in wq_in:
        move.wait_recv()
    local.start(wq, wq_out)
    for move in count_in:
        move.wait_recv()
    total = counts[0]
    for k in range(1, nc):
        total = total + counts[k]
    cnt_out[...] = total

    first = lax.broadcasted_iota(jnp.int32, (local_len, 128), 1) < HD
    place = lax.broadcasted_iota(jnp.int32, (1, seq), 1)

    def weight_plane(move_in, ref_of):
        local.wait(move_in[0])
        for move in move_in[1:]:
            move.wait_recv()
        return spread_plane(go, ref_of, me_c)

    def out_piece(member, part):
        rows = span(member * cols, cols)
        return out_full.at[rows] if part is None else out_full.at[rows, pl.ds(part * (D // 2), D // 2)]

    def up_piece(member, part):
        at = span(member * hid, hid)
        return up_full.at[:, at] if part is None else up_full.at[pl.ds(part * (D // 2), D // 2), at]

    att_in = []
    for i in range(images):
        for part in range(2):
            far[i][part].wait_recv()
            swap(i, me_c ^ 3, part)
        for move in swaps[i]:
            move.wait_recv()
        local.start(x_all.at[i], x_out.at[i])

        @pl.loop(0, nc)
        def _(chunk):
            rows = span(chunk * local_len, local_len)
            qkv[i, rows] = dot_nn(x_all[i, rows], wq[...]).astype(BF)

        local.start(qkv.at[i], qkv_out.at[i])
        bias = jnp.where(place < cnt_out[i : i + 1, 0:1], 0.0, -1e30)

        @pl.loop(0, nc)
        def _(chunk):
            rows = span(chunk * local_len, local_len)
            q = qkv[i, rows, 0:128] * SCALE
            k = qkv[i, :, 128:256]
            v = qkv[i, :, 256:384]
            outs, sums = [], []
            for head in range(2):
                mask = first if head == 0 else jnp.logical_not(first)
                scores = dot_nt(jnp.where(mask, q, jnp.zeros_like(q)), k) + bias
                peak = jnp.max(scores, axis=-1, keepdims=True)
                expo = jnp.exp(scores - peak)
                norm = jnp.sum(expo, axis=-1, keepdims=True)
                outs.append(dot_nn(expo.astype(BF), v) / norm)
                sums.append(peak + jnp.log(norm))
            o_all[i, rows] = jnp.where(first, outs[0], outs[1]).astype(BF)
            lse_all[rows] = jnp.where(first, sums[0], sums[1])

        mine = att_out.at[i, :, span(me_c * 128, 128)]
        for k in range(1, nc):
            att_in.append(
                go(o_all.at[i, span((me_c ^ k) * local_len, local_len)], mine, c_peers[k - 1])
            )
        local.start(o_all.at[i, span(me_c * local_len, local_len)], mine)
        local.start(o_all.at[i], o_out.at[i])
        sums_t = lse_all[...].T
        for head in range(2):
            lse_out[i, 8 * head : 8 * head + 8, :] = jnp.broadcast_to(
                sums_t[HD * head : HD * head + 1], (8, seq)
            )
        if i == 0:
            out_near = weight_plane(out_in, out_piece)
        if i == images - 1:
            up_near = weight_plane(up_in, up_piece)
            out_far = spread_plane_on(go, out_piece, me_c, out_near)
    up_far = spread_plane_on(go, up_piece, me_c, up_near)
    for move in att_in + out_far + up_far + down_in[1:]:
        move.wait_recv()
    local.finish()
    for move in sent:
        move.wait_send()


def forward_attention(tokens, gain, counts, wq_part, w_out, w_up, w_down, nz, nc):
    images, local_len = tokens.shape[:2]
    seq = nc * local_len
    cols, hid = w_out.shape[0], w_up.shape[1]
    any_ = pl.BlockSpec(memory_space=pl.ANY)
    vmem = pl.BlockSpec(memory_space=pltpu.VMEM)
    return pl.pallas_call(
        functools.partial(forward_kernel, nz, nc),
        out_shape=(
            jax.ShapeDtypeStruct((images, seq, D), BF),
            jax.ShapeDtypeStruct((images, seq, 384), BF),
            jax.ShapeDtypeStruct((images, seq, 128), BF),
            jax.ShapeDtypeStruct((images, 16, seq), F32),
            jax.ShapeDtypeStruct((images, local_len, cols), BF),
            jax.ShapeDtypeStruct((8, 128), jnp.int32),
            jax.ShapeDtypeStruct((D, 384), BF),
            jax.ShapeDtypeStruct((cols, D), BF),
            jax.ShapeDtypeStruct((D, hid), BF),
            jax.ShapeDtypeStruct((hid // nc, D), BF),
        ),
        in_specs=[any_, vmem, vmem, any_, any_, any_, any_],
        out_specs=(any_, any_, any_, vmem, any_, vmem, any_, any_, any_, any_),
        scratch_shapes=[
            pltpu.VMEM((images, local_len // 2, D), F32),
            pltpu.VMEM((images, seq, D), BF),
            pltpu.VMEM((images, seq, 384), BF),
            pltpu.VMEM((images, seq, 128), BF),
            pltpu.VMEM((seq, 128), F32),
            pltpu.VMEM((D, 384), BF),
            pltpu.VMEM((nc, 8, 128), jnp.int32),
            pltpu.SemaphoreType.DMA((96,)),
            pltpu.SemaphoreType.DMA((96,)),
            pltpu.SemaphoreType.DMA((32,)),
        ],
        compiler_params=pltpu.CompilerParams(
            collective_id=1, has_side_effects=True, vmem_limit_bytes=56 << 20
        ),
        name="forward_attention",
    )(tokens, gain, counts, wq_part, w_out, w_up, w_down)


def backward_kernel(
    nz,
    nc,
    slot_blocks,
    qkv_ref,
    o_ref,
    lse_ref,
    att_ref,
    cnt_ref,
    term_out_ref,
    term_up_ref,
    down_ref,
    x_ref,
    wq_ref,
    out_ref,
    tok_out,
    wq_out,
    grad,
    heads,
    qkv,
    o_all,
    x_all,
    dq_ref,
    row_ref,
    weight_ref,
    own_ref,
    far_y,
    far_x,
    near_in,
    far_in,
    mine_ref,
    zpart_ref,
    early_ref,
    late_ref,
    lpart_ref,
    place_ref,
    g_ref,
    l_ref,
    send,
    recv,
    local_sems,
):
    me_z, me_c, me_t = (lax.axis_index(a) for a in ("fsdp", "context", "tensor"))
    images, local_len = att_ref.shape[:2]
    slots = out_ref.shape[0]
    x_c, y_c, far_c = me_c ^ 1, me_c ^ 2, me_c ^ 3
    core, x_near, y_near = {"tensor": 1 - me_t}, {"context": x_c}, {"context": y_c}
    above, below = {"fsdp": me_z + 1}, {"fsdp": me_z - 1}
    z_peers = [{"fsdp": lax.rem(me_z + k, nz)} for k in range(1, nz)]
    c_peers = [{"context": me_c ^ k} for k in range(1, nc)]
    left, right = pl.ds(0, D // 2), pl.ds(D // 2, D // 2)
    ups, downs = term_up_ref.shape[0], down_ref.shape[0]
    terms = [(term_out_ref, 0)] + [(term_up_ref, j) for j in range(ups)]
    local = Local(local_sems)
    held = [
        [local.start(a.at[i], b.at[i]) for a, b in ((qkv_ref, qkv), (o_ref, o_all))]
        for i in range(images)
    ]
    x_in = [local.start(x_ref.at[i], x_all.at[i % 2]) for i in range(2)]
    own_in, far_own = [], []
    for index, (ref, block) in enumerate(terms):
        own_in.append(local.start(ref.at[block, me_c], own_ref.at[index]))
        far_own.append(local.start(ref.at[block, y_c, :, :, left], far_y.at[index]))
        far_own.append(local.start(ref.at[block, x_c, :, :, right], far_x.at[index]))
    mine_in = local.start(down_ref.at[:, me_z], mine_ref)
    greet(z_peers + c_peers + [core])
    moves = Moves(send, recv)
    sent = []

    def go(*args, **kw):
        move = moves.make(*args, **kw)
        move.start()
        sent.append(move)
        return move

    grad_in = []
    for i in range(images):
        here = grad.at[i, span(me_c * local_len, local_len)]
        grad_in.append(
            [local.start(att_ref.at[i, :, span(me_c * 128, 128)], here)]
            + [
                go(att_ref.at[i, :, span((me_c ^ k) * 128, 128)], here, c_peers[k - 1])
                for k in range(1, nc)
            ]
        )
    near = []
    for index, (ref, block) in enumerate(terms):
        near.append(
            [
                go(ref.at[block, x_c, :, :, left], near_in.at[index, 0], x_near),
                go(ref.at[block, far_c, :, :, left], near_in.at[index, 1], x_near),
                go(ref.at[block, y_c, :, :, right], near_in.at[index, 2], y_near),
                go(ref.at[block, far_c, :, :, right], near_in.at[index, 3], y_near),
            ]
        )
    down_in = [
        go(
            down_ref.at[:, lax.rem(me_z + k, nz)],
            zpart_ref.at[k - 1, pl.ds(len(terms), downs)],
            z_peers[k - 1],
        )
        for k in range(1, nz)
    ]
    width = wq_ref.shape[1]

    def wq_piece(member, part):
        at = span(member * width, width)
        return wq_out.at[:, at] if part is None else wq_out.at[pl.ds(part * (D // 2), D // 2), at]

    wq_own = local.start(wq_ref, wq_piece(me_c, None))
    first = lax.broadcasted_iota(jnp.int32, (local_len, 128), 1) < HD
    place = lax.broadcasted_iota(jnp.int32, (local_len, 128), 0)
    weight_ref[...] = jnp.zeros_like(weight_ref)
    far_moves = []

    def sum_step(index):
        for move in near[index]:
            move.wait_recv()
        local.wait(own_in[index])
        local.wait(far_own[2 * index])
        local.wait(far_own[2 * index + 1])
        far_y[index] += near_in[index, 1]
        first_far = go(far_y.at[index], far_in.at[index, 0], y_near)
        far_x[index] += near_in[index, 3]
        far_moves.append((first_far, go(far_x.at[index], far_in.at[index, 1], x_near)))

    for i in range(images):
        for copy in held[i]:
            local.wait(copy)
        local.wait(grad_in[i][0])
        for move in grad_in[i][1:]:
            move.wait_recv()
        prod = (grad[i].astype(F32) * o_all[i].astype(F32)).T
        for head in range(2):
            row_ref[8 * head : 8 * head + 8, :] = jnp.broadcast_to(
                jnp.sum(prod[HD * head : HD * (head + 1)], axis=0, keepdims=True),
                (8, prod.shape[1]),
            )
        dq_ref[...] = jnp.zeros_like(dq_ref)
        real = cnt_ref[i : i + 1, :]

        @pl.loop(0, nc)
        def _(chunk):
            rows = span(chunk * local_len, local_len)
            q = qkv[i, :, 0:128]
            k = qkv[i, rows, 128:256] * SCALE
            v = qkv[i, rows, 256:384]
            do = grad[i]
            live = (place + chunk * local_len < real)[:, 0:1]
            dks, dvs = [], []
            for head in range(2):
                mask = first if head == 0 else jnp.logical_not(first)
                kh = jnp.where(mask, k, jnp.zeros_like(k))
                vh = jnp.where(mask, v, jnp.zeros_like(v))
                lse = lse_ref[i, 8 * head : 8 * head + 1, :]
                delta = row_ref[8 * head : 8 * head + 1, :]
                prob = jnp.where(live, jnp.exp(dot_nt(kh, q) - lse), 0.0)
                ds = (prob * (dot_nt(vh, do) - delta)).astype(BF)
                dvs.append(dot_nn(prob.astype(BF), do))
                dks.append(dot_nn(ds, q) * SCALE)
                dq_ref[...] += dot_tn(ds, kh)
            heads[i, rows, 128:256] = jnp.where(first, dks[0], dks[1]).astype(BF)
            heads[i, rows, 256:384] = jnp.where(first, dvs[0], dvs[1]).astype(BF)

        heads[i, :, 0:128] = dq_ref[...].astype(BF)
        local.wait(x_in[i])

        @pl.loop(0, nc)
        def _(chunk):
            rows = span(chunk * local_len, local_len)
            weight_ref[...] += dot_tn(heads[i, rows], x_all[i % 2, rows])

        if i + 2 < images:
            x_in.append(local.start(x_ref.at[i + 2], x_all.at[i % 2]))
        if i == 1:
            for index in range(3):
                sum_step(index)
    sub = late_ref.shape[2]
    for z in range(nz):
        for j in range(LATE):
            late_ref[z, j] = weight_ref[pl.ds(j * 128 + z * sub, sub)].astype(BF)
    late_in = [
        go(late_ref.at[lax.rem(me_z + k, nz)], lpart_ref.at[k - 1], z_peers[k - 1])
        for k in range(1, nz)
    ]
    for index in range(3, len(terms)):
        sum_step(index)
    for index in range(len(terms)):
        for move in far_moves[index]:
            move.wait_recv()
        own_ref[index, :, :, left] += near_in[index, 0] + far_in[index, 0]
        own_ref[index, :, :, right] += near_in[index, 2] + far_in[index, 1]
    zterm_in = [
        go(
            own_ref.at[:, lax.rem(me_z + k, nz)],
            zpart_ref.at[k - 1, pl.ds(0, len(terms))],
            z_peers[k - 1],
        )
        for k in range(1, nz)
    ]

    swapped = []

    def swap(ref, member, z, cond=None, columns=None):
        piece = ref.at[:, me_t, member, z]
        if columns is not None:
            piece = ref.at[:, me_t, member, z, :, columns]
        swapped.append(go(piece, piece, core, cond=cond, recv_cond=cond))

    def along_fsdp(ref, member):
        own = ref.at[:, me_t, member, me_z]
        return [
            go(own, own, above, cond=me_z < nz - 1, recv_cond=me_z > 0),
            go(own, own, below, cond=me_z > 0, recv_cond=me_z < nz - 1),
        ]

    def onward(ref, member, last, hop):
        up_z, down_z = me_z - hop, me_z + hop
        last[0].wait_recv()
        up = down = None
        if hop < nz - 1:
            piece = ref.at[:, me_t, member, up_z]
            cond = jnp.logical_and(me_z < nz - 1, up_z >= 0)
            up = go(piece, piece, above, cond=cond, recv_cond=up_z - 1 >= 0)
        last[1].wait_recv()
        if hop < nz - 1:
            piece = ref.at[:, me_t, member, down_z]
            cond = jnp.logical_and(me_z > 0, down_z <= nz - 1)
            down = go(piece, piece, below, cond=cond, recv_cond=down_z + 1 <= nz - 1)
        return [up, down], [(up_z, up_z >= 0), (down_z, down_z <= nz - 1)]

    total = late_ref[me_z].astype(F32)
    for k in range(1, nz):
        late_in[k - 1].wait_recv()
        total = total + lpart_ref[k - 1].astype(F32)
    l_ref[:, me_t, me_c, me_z] = total.astype(BF)
    late_line = along_fsdp(l_ref, me_c)
    near = []

    def spread(z, cond=None):
        piece = l_ref.at[:, me_t, me_c, z]
        near.append(
            (
                z,
                cond,
                go(piece, piece, x_near, cond=cond, recv_cond=cond),
                go(piece, piece, y_near, cond=cond, recv_cond=cond),
            )
        )
        swap(l_ref, me_c, z, cond)

    for move in down_in + zterm_in:
        move.wait_recv()
    local.wait(mine_in)
    for block in range(EARLY):
        if block < len(terms):
            total = own_ref[block, me_z].astype(F32)
        else:
            total = mine_ref[block - len(terms)].astype(F32)
        for k in range(1, nz):
            total = total + zpart_ref[k - 1, block].astype(F32)
        early_ref[block] = total.astype(BF)
    for slot in range(NBLK):
        block = jnp.clip(slot_blocks[slot] - LATE, 0, EARLY - 1)
        place_ref[slot] = early_ref[block]
    placed = []
    for k in range(1, nc):
        theirs = place_ref.at[pl.ds((me_c ^ k) * slots, slots)]
        placed.append(go(theirs, g_ref.at[:, me_t, me_c, me_z], c_peers[k - 1]))
    for slot in range(slots):
        g_ref[slot, me_t, me_c, me_z] = place_ref[me_c * slots + slot]
    lines = {}
    for k in range(nc):
        member = me_c ^ k
        if k > 0:
            placed[k - 1].wait_recv()
        lines[k] = along_fsdp(g_ref, member)
        swap(g_ref, member, me_z)
    tok_in = []
    for i in range(images):
        there = tok_out.at[i, :, span(me_c * 384, 384)]
        for k in range(1, nc):
            tok_in.append(
                go(heads.at[i, span((me_c ^ k) * local_len, local_len)], there, c_peers[k - 1])
            )
        local.start(heads.at[i, span(me_c * local_len, local_len)], there)
    spread(me_z)
    local.wait(wq_own)
    wq_near = spread_plane(go, wq_piece, me_c)
    far = []
    done = 0

    def spread_on():
        nonlocal done
        for z, cond, x_move, y_move in near[done:]:
            x_move.wait_recv()
            piece = l_ref.at[:, me_t, x_c, z, :, left]
            far.append((z, cond, left, go(piece, piece, y_near, cond=cond, recv_cond=cond)))
            swap(l_ref, x_c, z, cond)
            y_move.wait_recv()
            piece = l_ref.at[:, me_t, y_c, z, :, right]
            far.append((z, cond, right, go(piece, piece, x_near, cond=cond, recv_cond=cond)))
            swap(l_ref, y_c, z, cond)
        done = len(near)

    for hop in range(1, nz):
        late_line, here = onward(l_ref, me_c, late_line, hop)
        for z, cond in here:
            spread(z, cond)
        for k in range(nc):
            member = me_c ^ k
            lines[k], here = onward(g_ref, member, lines[k], hop)
            for z, cond in here:
                swap(g_ref, member, z, cond)
        spread_on()
    wq_far = spread_plane_on(go, wq_piece, me_c, wq_near)
    for z, cond, columns, move in far:
        move.wait_recv()
        swap(l_ref, far_c, z, cond, columns)
    for move in swapped:
        move.wait_recv()
    for move in tok_in + wq_far:
        move.wait_recv()
    for move in sent:
        move.wait_send()
    for slot in range(slots):
        block = slot_blocks[me_c * slots + slot]
        late = l_ref[jnp.clip(block, 0, LATE - 1)]
        g_ref[slot] = jnp.where(block < LATE, late, g_ref[slot])
        local.start(g_ref.at[slot], out_ref.at[slot])
    local.finish()


def backward_attention(
    block_of, qkv, o_heads, lse, grad_att, counts, term_out, term_up, down, x_all, wq, nz, nc, nt
):
    images, seq = qkv.shape[:2]
    local_len = seq // nc
    sub = term_up.shape[3]
    slots = NBLK // nc
    terms = 1 + term_up.shape[0]
    any_ = pl.BlockSpec(memory_space=pl.ANY)
    vmem = pl.BlockSpec(memory_space=pltpu.VMEM)
    shape = (slots, nt, nc, nz, sub, D)
    out, tok, wq_all = pl.pallas_call(
        functools.partial(backward_kernel, nz, nc),
        out_shape=(
            jax.ShapeDtypeStruct(shape, BF),
            jax.ShapeDtypeStruct((images, local_len, nc * 384), BF),
            jax.ShapeDtypeStruct((D, nc * 384), BF),
        ),
        in_specs=[
            pl.BlockSpec(memory_space=pltpu.SMEM),
            any_,
            any_,
            vmem,
            any_,
            vmem,
            any_,
            any_,
            any_,
            any_,
            any_,
        ],
        out_specs=(any_, any_, any_),
        scratch_shapes=[
            pltpu.VMEM((images, seq, 128), BF),
            pltpu.VMEM((images, seq, 384), BF),
            pltpu.VMEM((images, seq, 384), BF),
            pltpu.VMEM((images, seq, 128), BF),
            pltpu.VMEM((2, seq, D), BF),
            pltpu.VMEM((seq, 128), F32),
            pltpu.VMEM((16, seq), F32),
            pltpu.VMEM((384, D), F32),
            pltpu.VMEM((terms, nz, sub, D), BF),
            pltpu.VMEM((terms, nz, sub, D // 2), BF),
            pltpu.VMEM((terms, nz, sub, D // 2), BF),
            pltpu.VMEM((terms, 4, nz, sub, D // 2), BF),
            pltpu.VMEM((terms, 2, nz, sub, D // 2), BF),
            pltpu.VMEM((EARLY - terms, sub, D), BF),
            pltpu.VMEM((nz - 1, EARLY, sub, D), BF),
            pltpu.VMEM((EARLY, sub, D), BF),
            pltpu.VMEM((nz, LATE, sub, D), BF),
            pltpu.VMEM((nz - 1, LATE, sub, D), BF),
            pltpu.VMEM((NBLK, sub, D), BF),
            pltpu.VMEM(shape, BF),
            pltpu.VMEM((LATE, nt, nc, nz, sub, D), BF),
            pltpu.SemaphoreType.DMA((256,)),
            pltpu.SemaphoreType.DMA((256,)),
            pltpu.SemaphoreType.DMA((64,)),
        ],
        compiler_params=pltpu.CompilerParams(
            collective_id=2, has_side_effects=True, vmem_limit_bytes=61 << 20
        ),
        name="backward_attention",
    )(
        block_of,
        qkv,
        o_heads,
        lse,
        grad_att,
        counts,
        term_out,
        term_up,
        down,
        x_all,
        wq,
    )
    return out.reshape(slots, D, D), tok, wq_all


def xor_permute(value, axis, step):
    size = lax.axis_size(axis)
    return lax.ppermute(value, axis, [(j, j ^ step) for j in range(size)])


def xor_order(pieces, index):
    bit = 1
    while bit < len(pieces):
        odd = (index & bit) > 0
        pieces = [jnp.where(odd, pieces[j ^ bit], pieces[j]) for j in range(len(pieces))]
        bit *= 2
    return pieces


def sum_tensor(value):
    low = lax.optimization_barrier(value.astype(BF))
    return low.astype(F32) + xor_permute(low, "tensor", 1).astype(F32)


def gather_fsdp(value):
    size = lax.axis_size("fsdp")
    if size > 4:
        return lax.all_gather(value, "fsdp", axis=0, tiled=False)
    pieces = [value] + [
        lax.ppermute(value, "fsdp", [(j, (j - k) % size) for j in range(size)])
        for k in range(1, size)
    ]
    doubled = jnp.stack(pieces + pieces[:-1])
    start = lax.rem(size - lax.axis_index("fsdp"), size)
    return lax.dynamic_slice_in_dim(doubled, start, size, 0)


def sum_fsdp(value):
    size = lax.axis_size("fsdp")
    if size > 4:
        return lax.psum(value, "fsdp")
    total = value
    for k in range(1, size):
        total = total + lax.ppermute(value, "fsdp", [(j, (j - k) % size) for j in range(size)])
    return total


def grad_gather_plain(block_of, early, late, nz, nc):
    me_c, me_t = (lax.axis_index(a) for a in ("context", "tensor"))
    sub = early.shape[1]
    half_width = nc * nz * sub
    slot_count = NBLK // nc
    slots_of = block_of.reshape(nc, slot_count)

    def slots_for(k):
        blocks = lax.dynamic_index_in_dim(slots_of, me_c ^ k, 0, keepdims=False)
        return early[jnp.clip(blocks - LATE, 0, EARLY - 1)]

    placed = [slots_for(0)] + [xor_permute(slots_for(k), "context", k) for k in range(1, nc)]
    placed = jnp.stack(xor_order(placed, me_c), axis=1)
    placed = lax.all_gather(placed, "fsdp", axis=2, tiled=False)
    placed = placed.reshape(slot_count, half_width, D)
    placed_other = xor_permute(placed, "tensor", 1)
    both = jnp.stack([placed, placed_other], axis=1)
    early_full = jnp.where(me_t > 0, both[:, ::-1], both).reshape(slot_count, D, D)

    late = late.reshape(-1, D)
    late = lax.psum_scatter(late, "fsdp", scatter_dimension=0, tiled=True)
    late = lax.all_gather(late, ("context", "fsdp"), axis=0, tiled=True)
    late = jnp.swapaxes(late.reshape(nc * nz, LATE, sub, D), 0, 1).reshape(LATE, half_width, D)
    late_other = xor_permute(late, "tensor", 1)
    both = jnp.stack([late, late_other], axis=1)
    late_full = jnp.where(me_t > 0, both[:, ::-1], both).reshape(LATE, D, D)

    mine = lax.dynamic_index_in_dim(slots_of, me_c, 0, keepdims=False)
    return jnp.where(
        (mine < LATE)[:, None, None], late_full[jnp.clip(mine, 0, LATE - 1)], early_full
    )


def to_natural(value, me_t, half_len):
    parts = value.reshape((-1, half_len) + value.shape[1:])
    return jnp.where(me_t > 0, parts[::-1], parts).reshape(value.shape)


def forward_plain(tokens, gain, key_mask, w_qkv, w_out, w_up, w_down):
    images, local_len = tokens.shape[:2]
    nc, nt = (lax.axis_size(a) for a in ("context", "tensor"))
    me_c, me_t = (lax.axis_index(a) for a in ("context", "tensor"))
    cols = w_qkv.shape[2] // nc
    half_len = local_len // nt
    wq_part = lax.dynamic_slice_in_dim(w_qkv, me_c * cols, cols, 2)
    wq = gather_fsdp(wq_part).reshape(D, 3 * cols)

    def two_stage(weight, member_axis, fsdp_axis):
        width = weight.shape[member_axis] // nc
        part = lax.dynamic_slice_in_dim(weight, me_c * width, width, member_axis)
        part = lax.all_gather(part, "fsdp", axis=fsdp_axis, tiled=True)
        return lax.all_gather(part, "context", axis=member_axis, tiled=True)

    out_full = two_stage(w_out, 0, 1)
    up_full = two_stage(w_up, 1, 0)
    down_full = two_stage(w_down, 0, 1)

    counts = jnp.sum(key_mask, axis=1)
    real = counts
    for k in range(1, nc):
        real = real + xor_permute(counts, "context", k)
    position = (
        (me_c ^ jnp.arange(nc))[:, None, None] * local_len
        + (me_t ^ jnp.arange(nt))[None, :, None] * half_len
        + jnp.arange(half_len)[None, None, :]
    ).reshape(-1)
    live = position[None, :] < real[:, None]
    bias = jnp.where(live, 0.0, -1e30).astype(F32)
    live_col = jnp.broadcast_to(live[:, :, None].astype(F32), (images, SEQ, 128))

    normed1, inv_std1, pre_norm1 = norm_fwd(tokens, gain)
    normed1_low = pre_norm1.astype(BF)

    x_all, qkv, out_heads, log_sums, attended = [], [], [], [], []
    for i in range(images):
        mine = lax.dynamic_slice_in_dim(normed1_low[i], me_t * half_len, half_len, 0)
        held = jnp.stack([mine] + [xor_permute(mine, "context", k) for k in range(1, nc)])
        other = xor_permute(held, "tensor", 1)
        x_i = jnp.stack([held, other], axis=1).reshape(SEQ, D)
        qkv_i = dot_nn(x_i, wq).astype(BF)
        o_i, lse_i = attn_fwd(qkv_i, bias[i][None])
        chunks = o_i.reshape(nc, local_len, 2 * HD)
        moved = [to_natural(chunks[0], me_t, half_len)] + [
            to_natural(xor_permute(chunks[k], "context", k), me_t, half_len) for k in range(1, nc)
        ]
        attended.append(jnp.concatenate(xor_order(moved, me_c), axis=-1))
        x_all.append(x_i)
        qkv.append(qkv_i)
        out_heads.append(o_i)
        log_sums.append(lse_i)
    attended = jnp.stack(attended)
    return (
        jnp.stack(x_all),
        jnp.stack(qkv),
        jnp.stack(out_heads),
        jnp.stack(log_sums),
        attended,
        live_col,
        wq,
        out_full,
        up_full,
        down_full,
        normed1,
        inv_std1,
    )


def backward_plain(qkv, out_heads, log_sums, grad_att, live_col, early, wq):
    images, local_len = grad_att.shape[:2]
    nz, nc, nt = (lax.axis_size(a) for a in ("fsdp", "context", "tensor"))
    me_c, me_t = (lax.axis_index(a) for a in ("context", "tensor"))
    cols = grad_att.shape[2] // nc
    half_len = local_len // nt
    sub = early.shape[2]
    grad_heads = []
    grad_tok = []
    for i in range(images):
        pieces = [grad_att[i, :, j * cols : (j + 1) * cols] for j in range(nc)]
        pieces = [to_natural(p, me_t, half_len) for p in xor_order(pieces, me_c)]
        grad_i = jnp.concatenate(
            [pieces[0]] + [xor_permute(pieces[k], "context", k) for k in range(1, nc)]
        )
        g_i = attn_bwd(qkv[i], grad_i, out_heads[i], log_sums[i], live_col[i])
        chunks = g_i.reshape(nc, local_len, 3 * cols)
        moved = [to_natural(chunks[0], me_t, half_len)] + [
            to_natural(xor_permute(chunks[k], "context", k), me_t, half_len) for k in range(1, nc)
        ]
        grad_tok.append(jnp.stack(xor_order(moved, me_c), axis=1))
        grad_heads.append(g_i)
    grad_tok = jnp.stack(grad_tok)
    wq_all = lax.all_gather(wq, "context", axis=0, tiled=False)
    grad_n1 = sum_tensor(
        jnp.einsum("isjc,jdc->isd", grad_tok, wq_all, preferred_element_type=F32)
    )
    early = lax.psum_scatter(
        jnp.swapaxes(early, 0, 1).reshape(-1, D),
        "fsdp",
        scatter_dimension=0,
        tiled=True,
    ).reshape(EARLY, sub, D)
    return jnp.stack(grad_heads), grad_n1, early


def per_device(
    tokens,
    cotangent,
    gains,
    w_qkv,
    w_out,
    w_up,
    w_down,
    key_mask,
    owner,
    stat_left,
    stat_right,
    root_left,
    root_right,
    master,
    gain_state,
):
    images, local_len = tokens.shape[:2]
    tok_rows = images * local_len
    nz, nc, nt = (lax.axis_size(a) for a in ("fsdp", "context", "tensor"))
    me_z, me_c, me_t = (lax.axis_index(a) for a in ("fsdp", "context", "tensor"))
    half_width = w_qkv.shape[2]
    hidden = w_up.shape[1]
    up_blocks = hidden // half_width
    cols = half_width // nc
    fast = nz == 4 and nc == 4
    if fast:
        wq_part = lax.dynamic_slice_in_dim(w_qkv, me_c * cols, cols, 2).reshape(-1, 3 * cols)
        counts = jnp.pad(jnp.sum(key_mask, axis=1), (0, 8 - images))
        counts = jnp.broadcast_to(counts[:, None], (8, 128))
        (
            x_all,
            qkv,
            out_heads,
            log_sums,
            attended,
            counts,
            wq,
            out_full,
            up_full,
            down_part,
        ) = forward_attention(
            tokens, gains[0:1], counts, wq_part, w_out, w_up, w_down, nz, nc
        )
        down_full = lax.all_gather(down_part, "context", axis=0, tiled=True)
        normed1, inv_std1, _ = norm_fwd(tokens, gains[0])
    else:
        (
            x_all,
            qkv,
            out_heads,
            log_sums,
            attended,
            live_col,
            wq,
            out_full,
            up_full,
            down_full,
            normed1,
            inv_std1,
        ) = forward_plain(tokens, gains[0], key_mask, w_qkv, w_out, w_up, w_down)

    branch_attn = sum_tensor(
        jnp.einsum("ish,hd->isd", attended, out_full, preferred_element_type=F32)
    )
    middle = tokens + gains[2] * branch_attn
    normed2, inv_std2, pre_norm2 = norm_fwd(middle, gains[1])
    normed2_low = pre_norm2.astype(BF)
    pre_act = jnp.einsum("isd,df->isf", normed2_low, up_full, preferred_element_type=F32)
    act_val, act_slope = gelu_parts(pre_act)
    act_low = act_val.astype(BF)
    branch_mlp = sum_tensor(
        jnp.einsum("isf,fd->isd", act_low, down_full, preferred_element_type=F32)
    )
    output = middle + gains[3] * branch_mlp

    grad_mlp = (gains[3] * cotangent).astype(BF)
    grad_hidden = jnp.einsum("isd,fd->isf", grad_mlp, down_full, preferred_element_type=F32)
    grad_pre = (grad_hidden * act_slope).astype(BF)
    grad_n2 = sum_tensor(
        jnp.einsum("isf,df->isd", grad_pre, up_full, preferred_element_type=F32)
    )
    middle_part, grad_gain2 = norm_back(grad_n2, gains[1], normed2, inv_std2)
    grad_middle = cotangent + middle_part
    grad_branch = (gains[2] * grad_middle).astype(BF)
    grad_att = jnp.einsum(
        "isd,hd->ish", grad_branch, out_full, preferred_element_type=F32
    ).astype(BF)

    sub = half_width // nc // nz
    onehot = (owner[:, None] == jnp.arange(NBLK, dtype=jnp.int32)[None, :]).astype(jnp.int32)
    block_of = jnp.sum(onehot * jnp.arange(NBLK, dtype=jnp.int32)[:, None], axis=0)

    def early_term(left, right):
        term = dot_tn(left.reshape(tok_rows, -1), right.reshape(tok_rows, D)).astype(BF)
        return term.reshape(-1, nc, nz, sub, D)

    def early_sum(term):
        return lax.psum_scatter(
            jnp.swapaxes(term, 0, 1).reshape(-1, D), "context", scatter_dimension=0, tiled=True
        ).reshape(-1, nz, sub, D)

    term_out = early_term(attended, grad_branch)
    term_up = early_term(grad_pre, normed2_low)
    down = early_sum(early_term(act_low, grad_mlp))
    if fast:
        grad_full, grad_tok, wq_all = backward_attention(
            block_of,
            qkv,
            out_heads,
            log_sums,
            grad_att,
            counts,
            term_out,
            term_up,
            down,
            x_all,
            wq,
            nz,
            nc,
            nt,
        )
        grad_n1 = sum_tensor(
            lax.dot_general(
                grad_tok, wq_all, (((2,), (1,)), ((), ())), preferred_element_type=F32
            )
        )
    else:
        early = jnp.concatenate([early_sum(term_out), early_sum(term_up), down], axis=0)
        grad_heads, grad_n1, early = backward_plain(
            qkv, out_heads, log_sums, grad_att, live_col, early, wq
        )
        term_qkv = jnp.einsum("isk,isd->kd", grad_heads, x_all, preferred_element_type=F32)
        late = jnp.swapaxes(term_qkv.astype(BF).reshape(LATE, nz, sub, D), 0, 1)
        grad_full = grad_gather_plain(block_of, early, late, nz, nc)
    input_part, grad_gain1 = norm_back(grad_n1, gains[0], normed1, inv_std1)
    grad_tokens = grad_middle + input_part
    grad_gain3 = jnp.sum(grad_middle * branch_attn, axis=(0, 1))
    grad_gain4 = jnp.sum(cotangent * branch_mlp, axis=(0, 1))
    gain_terms = jnp.stack([grad_gain1, grad_gain2, grad_gain3, grad_gain4], axis=0)

    row_count = half_width // nz
    row_offset = me_t * half_width + me_z * row_count
    tokens_all = images * nz * SEQ
    grad_mine = lax.dynamic_slice_in_dim(grad_full, row_offset, row_count, 1)
    left_new = 0.5 * stat_left[:, 0] + 0.5 / tokens_all * jnp.einsum(
        "sra,sba->srb", grad_mine, grad_full, preferred_element_type=F32
    )
    grad_cols = lax.dynamic_slice_in_dim(grad_full, row_offset, row_count, 2)
    right_new = 0.5 * stat_right[:, 0] + 0.5 / tokens_all * jnp.einsum(
        "sar,sab->srb", grad_cols, grad_full, preferred_element_type=F32
    )
    inner_prod = jnp.einsum(
        "sra,sab->srb", root_left[:, 0].astype(BF), grad_full, preferred_element_type=F32
    ).astype(BF)
    update = jnp.einsum(
        "srb,sbc->src", inner_prod, root_right.astype(BF), preferred_element_type=F32
    )
    square_sum = jnp.sum(update * update, axis=(1, 2))
    square_sum = sum_fsdp(square_sum + xor_permute(square_sum, "tensor", 1))
    factor = lax.rsqrt(square_sum / (D * D) + 1e-06)
    weight_new = master[:, 0] - factor[:, None, None] * update

    gain_sum = gain_terms
    step = 1
    while step < nc:
        gain_sum = gain_sum + xor_permute(gain_sum, "context", step)
        step *= 2
    gain_sum = sum_fsdp(gain_sum)
    share_width = gain_state.shape[1]
    gain_index = lax.axis_index(("fsdp", "context"))
    gain_grad = lax.dynamic_slice_in_dim(gain_sum, gain_index * share_width, share_width, 1)
    gain_mine = lax.dynamic_slice_in_dim(gains, gain_index * share_width, share_width, 1)
    state_new = 0.5 * gain_state + 0.5 * gain_grad * gain_grad / tokens_all
    gain_new = gain_mine - 0.1 * gain_grad * lax.rsqrt(tokens_all * state_new)
    return (
        output,
        grad_tokens,
        grad_mine.astype(F32)[:, None],
        left_new[:, None],
        right_new[:, None],
        weight_new[:, None],
        gain_grad,
        state_new,
        gain_new,
    )


def solution(mesh):
    return jax.shard_map(
        per_device,
        mesh=mesh,
        in_specs=(
            P("fsdp", "context", None),
            P("fsdp", "context", None),
            P(),
            P("fsdp", None, "tensor"),
            P("tensor", "fsdp"),
            P("fsdp", "tensor"),
            P("tensor", "fsdp"),
            P("fsdp", "context"),
            P(),
            P("context", "tensor", "fsdp", None),
            P("context", "tensor", "fsdp", None),
            P("context", "tensor", "fsdp", None),
            P("context", None, None),
            P("context", "tensor", "fsdp", None),
            P(None, ("fsdp", "context")),
        ),
        out_specs=(
            P("fsdp", "context", None),
            P("fsdp", "context", None),
            P("context", "tensor", "fsdp", None),
            P("context", "tensor", "fsdp", None),
            P("context", "tensor", "fsdp", None),
            P("context", "tensor", "fsdp", None),
            P(None, ("fsdp", "context")),
            P(None, ("fsdp", "context")),
            P(None, ("fsdp", "context")),
        ),
        check_vma=False,
    )
```

```python
import functools

import jax
import jax.numpy as jnp
from jax import lax
from jax.experimental import pallas as pl
from jax.experimental.pallas import tpu as pltpu
from jax.sharding import PartitionSpec as P

D = 1024
HD = 64
SEQ = 1408
NBLK = 12
LATE = 3
EARLY = NBLK - LATE
BF = jnp.bfloat16
F32 = jnp.float32
SCALE = HD ** (-0.5)


def norm_fwd(field_in, gain_vec):
    centred = field_in - jnp.mean(field_in, axis=-1, keepdims=True)
    inv_std = lax.rsqrt(jnp.mean(centred * centred, axis=-1, keepdims=True) + 1e-06)
    normed = centred * inv_std
    return (normed, inv_std, normed * gain_vec)


def norm_back(grad_out, gain_vec, normed, inv_std):
    scaled = grad_out * gain_vec
    inner_sum = (
        scaled
        - jnp.mean(scaled, axis=-1, keepdims=True)
        - normed * jnp.mean(scaled * normed, axis=-1, keepdims=True)
    )
    return (inner_sum * inv_std, jnp.sum(grad_out * normed, axis=(0, 1)))


def gelu_parts(field_in):
    normal_cdf = 0.5 * (1.0 + lax.erf(field_in * 0.7071067811865476))
    normal_pdf = jnp.exp(-0.5 * field_in * field_in) * 0.3989422804014327
    return (field_in * normal_cdf, normal_cdf + field_in * normal_pdf)


def dot_nt(a, b):
    return lax.dot_general(a, b, (((1,), (1,)), ((), ())), preferred_element_type=F32)


def dot_tn(a, b):
    return lax.dot_general(a, b, (((0,), (0,)), ((), ())), preferred_element_type=F32)


def dot_nn(a, b):
    return lax.dot_general(a, b, (((1,), (0,)), ((), ())), preferred_element_type=F32)


def attn_fwd_kernel(q_ref, k_ref, v_ref, bias_ref, o_ref, lse_ref):
    q = q_ref[...] * SCALE
    k = k_ref[...]
    v = v_ref[...]
    bias = bias_ref[...]
    first = lax.broadcasted_iota(jnp.int32, q.shape, 1) < HD
    outs, sums = [], []
    for head in range(2):
        mask = first if head == 0 else jnp.logical_not(first)
        scores = dot_nt(jnp.where(mask, q, jnp.zeros_like(q)), k) + bias
        peak = jnp.max(scores, axis=-1, keepdims=True)
        expo = jnp.exp(scores - peak)
        total = jnp.sum(expo, axis=-1, keepdims=True)
        outs.append(dot_nn(expo.astype(BF), v) / total)
        sums.append(peak + jnp.log(total))
    o_ref[...] = jnp.where(first, outs[0], outs[1]).astype(BF)
    lse_ref[...] = jnp.where(first, sums[0], sums[1])


def attn_fwd(qkv, bias_row):
    rows = qkv.shape[0]
    bq = rows // 4
    return pl.pallas_call(
        attn_fwd_kernel,
        grid=(rows // bq,),
        out_shape=(
            jax.ShapeDtypeStruct((rows, 128), BF),
            jax.ShapeDtypeStruct((rows, 128), F32),
        ),
        in_specs=[
            pl.BlockSpec((bq, 128), lambda i: (i, 0)),
            pl.BlockSpec((rows, 128), lambda i: (0, 1)),
            pl.BlockSpec((rows, 128), lambda i: (0, 2)),
            pl.BlockSpec((1, rows), lambda i: (0, 0)),
        ],
        out_specs=(
            pl.BlockSpec((bq, 128), lambda i: (i, 0)),
            pl.BlockSpec((bq, 128), lambda i: (i, 0)),
        ),
        compiler_params=pltpu.CompilerParams(vmem_limit_bytes=40 << 20),
        cost_estimate=pl.CostEstimate(
            flops=4 * rows * rows * 512, bytes_accessed=rows * 2048, transcendentals=2 * rows * rows
        ),
        name="attn_fwd",
    )(qkv, qkv, qkv, bias_row)


def attn_bwd_kernel(q_ref, k_ref, v_ref, do_ref, o_ref, lse_ref, live_ref, out_ref, dq_ref, row_ref):
    step = pl.program_id(0)
    chunk = k_ref.shape[0]

    @pl.when(step == 0)
    def _():
        row_ref[0:128, :] = lse_ref[...].T
        prod = do_ref[...].astype(F32) * o_ref[...].astype(F32)
        prod_t = prod.T
        row_ref[128:136, :] = jnp.broadcast_to(
            jnp.sum(prod_t[0:HD], axis=0, keepdims=True), (8, prod_t.shape[1])
        )
        row_ref[136:144, :] = jnp.broadcast_to(
            jnp.sum(prod_t[HD:128], axis=0, keepdims=True), (8, prod_t.shape[1])
        )
        dq_ref[...] = jnp.zeros_like(dq_ref)

    q = q_ref[...]
    k = k_ref[...] * SCALE
    v = v_ref[...]
    do = do_ref[...]
    live = live_ref[:, 0:1] > 0
    first = lax.broadcasted_iota(jnp.int32, k.shape, 1) < HD
    dks, dvs = [], []
    for head in range(2):
        mask = first if head == 0 else jnp.logical_not(first)
        kh = jnp.where(mask, k, jnp.zeros_like(k))
        vh = jnp.where(mask, v, jnp.zeros_like(v))
        lse = row_ref[64 * head : 64 * head + 1, :]
        delta = row_ref[128 + 8 * head : 129 + 8 * head, :]
        prob = jnp.where(live, jnp.exp(dot_nt(kh, q) - lse), 0.0)
        ds = (prob * (dot_nt(vh, do) - delta)).astype(BF)
        dvs.append(dot_nn(prob.astype(BF), do))
        dks.append(dot_nn(ds, q) * SCALE)
        dq_ref[...] += dot_tn(ds, kh)
    at = pl.ds(pl.multiple_of(step * chunk, chunk), chunk)
    out_ref[at, 128:256] = jnp.where(first, dks[0], dks[1]).astype(BF)
    out_ref[at, 256:384] = jnp.where(first, dvs[0], dvs[1]).astype(BF)

    @pl.when(step == pl.num_programs(0) - 1)
    def _():
        out_ref[:, 0:128] = dq_ref[...].astype(BF)


def attn_bwd(qkv, grad, out, lse, live_col):
    rows = qkv.shape[0]
    chunk = rows // 4
    return pl.pallas_call(
        attn_bwd_kernel,
        grid=(rows // chunk,),
        out_shape=jax.ShapeDtypeStruct((rows, 384), BF),
        in_specs=[
            pl.BlockSpec((rows, 128), lambda i: (0, 0)),
            pl.BlockSpec((chunk, 128), lambda i: (i, 1)),
            pl.BlockSpec((chunk, 128), lambda i: (i, 2)),
            pl.BlockSpec((rows, 128), lambda i: (0, 0)),
            pl.BlockSpec((rows, 128), lambda i: (0, 0)),
            pl.BlockSpec((rows, 128), lambda i: (0, 0)),
            pl.BlockSpec((chunk, 128), lambda i: (i, 0)),
        ],
        out_specs=pl.BlockSpec((rows, 384), lambda i: (0, 0)),
        scratch_shapes=[pltpu.VMEM((rows, 128), F32), pltpu.VMEM((144, rows), F32)],
        compiler_params=pltpu.CompilerParams(vmem_limit_bytes=50 << 20),
        cost_estimate=pl.CostEstimate(
            flops=10 * rows * rows * 512, bytes_accessed=rows * 4096, transcendentals=2 * rows * rows
        ),
        name="attn_bwd",
    )(qkv, qkv, qkv, grad, out, lse, live_col)


class Moves:
    def __init__(self, send_sems, recv_sems):
        self.send_sems, self.recv_sems, self.count = send_sems, recv_sems, 0

    def make(self, src, dst, device, cond=None, recv_cond=None):
        index = self.count
        self.count += 1
        return Move(self, index, src, dst, device, cond, recv_cond)


class Move:
    def __init__(self, moves, index, src, dst, device, cond, recv_cond):
        self.args = (src, dst, moves.send_sems.at[index], moves.recv_sems.at[index])
        self.device, self.cond, self.recv_cond = device, cond, recv_cond

    def copy(self):
        return pltpu.make_async_remote_copy(
            *self.args, device_id=self.device, device_id_type=pl.DeviceIdType.MESH
        )

    def when(self, cond, act):
        if cond is None:
            act()
        else:
            pl.when(cond)(act)

    def start(self):
        self.when(self.cond, lambda: self.copy().start())

    def wait_recv(self):
        self.when(self.recv_cond, lambda: self.copy().wait_recv())

    def wait_send(self):
        self.when(self.cond, lambda: self.copy().wait_send())


def greet(devices):
    barrier = pltpu.get_barrier_semaphore()
    for device in devices:
        pl.semaphore_signal(
            barrier, inc=1, device_id=device, device_id_type=pl.DeviceIdType.MESH
        )
    pl.semaphore_wait(barrier, len(devices))


def span(start, size):
    return pl.ds(pl.multiple_of(start, size & -size), size)


class Local:
    def __init__(self, sems):
        self.sems, self.count, self.open = sems, 0, []

    def start(self, src, dst):
        copy = pltpu.make_async_copy(src, dst, self.sems.at[self.count])
        self.count += 1
        copy.start()
        self.open.append(copy)
        return copy

    def wait(self, copy):
        copy.wait()
        self.open = [c for c in self.open if c is not copy]

    def finish(self):
        for copy in self.open:
            copy.wait()
        self.open = []


def spread_plane(go, ref_of, me_c, cond=None):
    own = ref_of(me_c, None)
    return [go(own, own, {"context": me_c ^ 1}), go(own, own, {"context": me_c ^ 2})]


def spread_plane_on(go, ref_of, me_c, near):
    near[0].wait_recv()
    piece = ref_of(me_c ^ 1, 0)
    first = go(piece, piece, {"context": me_c ^ 2})
    near[1].wait_recv()
    piece = ref_of(me_c ^ 2, 1)
    second = go(piece, piece, {"context": me_c ^ 1})
    return [first, second]


def forward_kernel(
    nz,
    nc,
    tokens_ref,
    gain_ref,
    count_ref,
    wq_ref,
    wout_ref,
    wup_ref,
    wdown_ref,
    x_out,
    qkv_out,
    o_out,
    lse_out,
    att_out,
    cnt_out,
    wq_out,
    out_full,
    up_full,
    down_part,
    tok,
    x_all,
    qkv,
    o_all,
    lse_all,
    wq,
    counts,
    send,
    recv,
    local_sems,
):
    me_z, me_c, me_t = (lax.axis_index(a) for a in ("fsdp", "context", "tensor"))
    images, local_len = att_out.shape[:2]
    half = local_len // 2
    seq = x_all.shape[1]
    core = {"tensor": 1 - me_t}
    z_peers = [{"fsdp": lax.rem(me_z + k, nz)} for k in range(1, nz)]
    c_peers = [{"context": me_c ^ k} for k in range(1, nc)]
    local = Local(local_sems)
    token_in = [
        local.start(tokens_ref.at[i, span(me_t * half, half)], tok.at[i]) for i in range(images)
    ]
    depth = wq_ref.shape[0]
    wq_own = local.start(wq_ref, wq.at[span(me_z * depth, depth)])
    greet(z_peers + c_peers + [core])
    moves = Moves(send, recv)
    sent = []

    def go(*args, **kw):
        move = moves.make(*args, **kw)
        move.start()
        sent.append(move)
        return move

    wq_in = [go(wq_ref, wq.at[span(me_z * depth, depth)], peer) for peer in z_peers]
    counts[me_c] = count_ref[...]
    count_in = [go(count_ref, counts.at[me_c], peer) for peer in c_peers]

    def to_line(src, dst):
        local_copy = local.start(src, dst)
        return [local_copy] + [go(src, dst, peer) for peer in z_peers]

    cols, hid, depth_o = wout_ref.shape[0] // nc, wup_ref.shape[1] // nc, wout_ref.shape[1]

    def x_piece(i):
        def at(member, part):
            rows = span(member * local_len + me_t * half, half)
            if part is None:
                return x_all.at[i, rows]
            return x_all.at[i, rows, pl.ds(part * (D // 2), D // 2)]

        return at

    swaps = [[] for _ in range(images)]
    near, far = [], []

    def swap(i, member, part=None):
        piece = x_piece(i)(member, part)
        swaps[i].append(go(piece, piece, core))

    def normalize(i):
        local.wait(token_in[i])
        value = tok[i]
        centred = value - jnp.mean(value, axis=-1, keepdims=True)
        inv_std = lax.rsqrt(jnp.mean(centred * centred, axis=-1, keepdims=True) + 1e-06)
        x_all[i, span(me_c * local_len + me_t * half, half)] = (
            centred * inv_std * gain_ref[...]
        ).astype(BF)

    def send_near(i):
        near.append(spread_plane(go, x_piece(i), me_c))
        swap(i, me_c)

    def send_far(i):
        far.append(spread_plane_on(go, x_piece(i), me_c, near[i]))
        swap(i, me_c ^ 1)
        swap(i, me_c ^ 2)

    normalize(0)
    send_near(0)
    out_in = to_line(
        wout_ref.at[span(me_c * cols, cols)],
        out_full.at[span(me_c * cols, cols), span(me_z * depth_o, depth_o)],
    )
    up_in = to_line(
        wup_ref.at[:, span(me_c * hid, hid)],
        up_full.at[span(me_z * depth, depth), span(me_c * hid, hid)],
    )
    down_in = to_line(
        wdown_ref.at[span(me_c * hid, hid)],
        down_part.at[:, span(me_z * depth_o, depth_o)],
    )
    normalize(1)
    send_near(1)
    normalize(2)
    send_far(0)
    send_near(2)
    local.wait(wq_own)
    for move in wq_in:
        move.wait_recv()
    local.start(wq, wq_out)
    for move in count_in:
        move.wait_recv()
    total = counts[0]
    for k in range(1, nc):
        total = total + counts[k]
    cnt_out[...] = total

    first = lax.broadcasted_iota(jnp.int32, (local_len, 128), 1) < HD
    place = lax.broadcasted_iota(jnp.int32, (1, seq), 1)

    def weight_plane(move_in, ref_of):
        local.wait(move_in[0])
        for move in move_in[1:]:
            move.wait_recv()
        return spread_plane(go, ref_of, me_c)

    def out_piece(member, part):
        rows = span(member * cols, cols)
        return out_full.at[rows] if part is None else out_full.at[rows, pl.ds(part * (D // 2), D // 2)]

    def up_piece(member, part):
        at = span(member * hid, hid)
        return up_full.at[:, at] if part is None else up_full.at[pl.ds(part * (D // 2), D // 2), at]

    att_in = []
    for i in range(images):
        for part in range(2):
            far[i][part].wait_recv()
            swap(i, me_c ^ 3, part)
        for move in swaps[i]:
            move.wait_recv()
        local.start(x_all.at[i], x_out.at[i])

        @pl.loop(0, nc)
        def _(chunk):
            rows = span(chunk * local_len, local_len)
            qkv[i, rows] = dot_nn(x_all[i, rows], wq[...]).astype(BF)

        local.start(qkv.at[i], qkv_out.at[i])
        if i == 0:
            send_far(1)
        bias = jnp.where(place < cnt_out[i : i + 1, 0:1], 0.0, -1e30)
        def attend(chunk):
            rows = span(chunk * local_len, local_len)
            q = qkv[i, rows, 0:128] * SCALE
            k = qkv[i, :, 128:256]
            v = qkv[i, :, 256:384]
            outs, sums = [], []
            for head in range(2):
                mask = first if head == 0 else jnp.logical_not(first)
                scores = dot_nt(jnp.where(mask, q, jnp.zeros_like(q)), k) + bias
                peak = jnp.max(scores, axis=-1, keepdims=True)
                expo = jnp.exp(scores - peak)
                norm = jnp.sum(expo, axis=-1, keepdims=True)
                outs.append(dot_nn(expo.astype(BF), v) / norm)
                sums.append(peak + jnp.log(norm))
            o_all[i, rows] = jnp.where(first, outs[0], outs[1]).astype(BF)
            lse_all[rows] = jnp.where(first, sums[0], sums[1])

        pl.loop(0, nc // 2)(attend)
        if i == 0:
            send_far(2)
            out_near = weight_plane(out_in, out_piece)
        if i == images - 1:
            out_far = spread_plane_on(go, out_piece, me_c, out_near)
        pl.loop(nc // 2, nc)(attend)

        mine = att_out.at[i, :, span(me_c * 128, 128)]
        for k in range(1, nc):
            att_in.append(
                go(o_all.at[i, span((me_c ^ k) * local_len, local_len)], mine, c_peers[k - 1])
            )
        local.start(o_all.at[i, span(me_c * local_len, local_len)], mine)
        local.start(o_all.at[i], o_out.at[i])
        sums_t = lse_all[...].T
        for head in range(2):
            lse_out[i, 8 * head : 8 * head + 8, :] = jnp.broadcast_to(
                sums_t[HD * head : HD * head + 1], (8, seq)
            )
        if i == 1:
            up_near = weight_plane(up_in, up_piece)
    up_far = spread_plane_on(go, up_piece, me_c, up_near)
    for move in att_in + out_far + up_far + down_in[1:]:
        move.wait_recv()
    local.finish()
    for move in sent:
        move.wait_send()


def forward_attention(tokens, gain, counts, wq_part, w_out, w_up, w_down, nz, nc):
    images, local_len = tokens.shape[:2]
    seq = nc * local_len
    cols, hid = w_out.shape[0], w_up.shape[1]
    any_ = pl.BlockSpec(memory_space=pl.ANY)
    vmem = pl.BlockSpec(memory_space=pltpu.VMEM)
    return pl.pallas_call(
        functools.partial(forward_kernel, nz, nc),
        out_shape=(
            jax.ShapeDtypeStruct((images, seq, D), BF),
            jax.ShapeDtypeStruct((images, seq, 384), BF),
            jax.ShapeDtypeStruct((images, seq, 128), BF),
            jax.ShapeDtypeStruct((images, 16, seq), F32),
            jax.ShapeDtypeStruct((images, local_len, cols), BF),
            jax.ShapeDtypeStruct((8, 128), jnp.int32),
            jax.ShapeDtypeStruct((D, 384), BF),
            jax.ShapeDtypeStruct((cols, D), BF),
            jax.ShapeDtypeStruct((D, hid), BF),
            jax.ShapeDtypeStruct((hid // nc, D), BF),
        ),
        in_specs=[any_, vmem, vmem, any_, any_, any_, any_],
        out_specs=(any_, any_, any_, vmem, any_, vmem, any_, any_, any_, any_),
        scratch_shapes=[
            pltpu.VMEM((images, local_len // 2, D), F32),
            pltpu.VMEM((images, seq, D), BF),
            pltpu.VMEM((images, seq, 384), BF),
            pltpu.VMEM((images, seq, 128), BF),
            pltpu.VMEM((seq, 128), F32),
            pltpu.VMEM((D, 384), BF),
            pltpu.VMEM((nc, 8, 128), jnp.int32),
            pltpu.SemaphoreType.DMA((96,)),
            pltpu.SemaphoreType.DMA((96,)),
            pltpu.SemaphoreType.DMA((32,)),
        ],
        compiler_params=pltpu.CompilerParams(
            collective_id=1, has_side_effects=True, vmem_limit_bytes=56 << 20
        ),
        name="forward_attention",
    )(tokens, gain, counts, wq_part, w_out, w_up, w_down)


def backward_kernel(
    nz,
    nc,
    qkv_ref,
    o_ref,
    lse_ref,
    att_ref,
    cnt_ref,
    term_out_ref,
    term_up_ref,
    down_ref,
    x_ref,
    wq_ref,
    early_ref,
    late_out,
    heads_out,
    wq_out,
    grad,
    heads,
    qkv,
    o_all,
    x_all,
    dq_ref,
    row_ref,
    weight_ref,
    own_ref,
    far_y,
    far_x,
    near_in,
    far_in,
    mine_ref,
    zpart_ref,
    zsend_ref,
    znext_ref,
    late_ref,
    lpart_ref,
    lsend_ref,
    lnext_ref,
    send,
    recv,
    local_sems,
):
    me_z, me_c, me_t = (lax.axis_index(a) for a in ("fsdp", "context", "tensor"))
    images, local_len = att_ref.shape[:2]
    x_c, y_c, far_c = me_c ^ 1, me_c ^ 2, me_c ^ 3
    x_near, y_near = {"context": x_c}, {"context": y_c}
    z_peers = [{"fsdp": lax.rem(me_z + k, nz)} for k in range(1, nz)]
    c_peers = [{"context": me_c ^ k} for k in range(1, nc)]
    left, right = pl.ds(0, D // 2), pl.ds(D // 2, D // 2)
    ups, downs = term_up_ref.shape[0], down_ref.shape[0]
    terms = [(term_out_ref, 0)] + [(term_up_ref, j) for j in range(ups)]
    local = Local(local_sems)
    held = [
        [local.start(a.at[i], b.at[i]) for a, b in ((qkv_ref, qkv), (o_ref, o_all))]
        for i in range(images)
    ]
    x_in = [local.start(x_ref.at[i], x_all.at[i % 2]) for i in range(2)]
    own_in, far_own = [], []
    for index, (ref, block) in enumerate(terms):
        own_in.append(local.start(ref.at[block, me_c], own_ref.at[index]))
        far_own.append(local.start(ref.at[block, y_c, :, :, left], far_y.at[index]))
        far_own.append(local.start(ref.at[block, x_c, :, :, right], far_x.at[index]))
    mine_in = [
        local.start(down_ref.at[:, me_z], mine_ref.at[0]),
        local.start(down_ref.at[:, me_z ^ 2], mine_ref.at[1]),
    ]
    greet(z_peers + c_peers)
    moves = Moves(send, recv)
    sent = []

    def go(*args, **kw):
        move = moves.make(*args, **kw)
        move.start()
        sent.append(move)
        return move

    grad_in = []

    def send_grad(i):
        here = grad.at[i, span(me_c * local_len, local_len)]
        grad_in.append(
            [local.start(att_ref.at[i, :, span(me_c * 128, 128)], here)]
            + [
                go(att_ref.at[i, :, span((me_c ^ k) * 128, 128)], here, c_peers[k - 1])
                for k in range(1, nc)
            ]
        )

    near = []

    def send_term(index):
        ref, block = terms[index]
        near.append(
            [
                go(ref.at[block, x_c, :, :, left], near_in.at[index, 0], x_near),
                go(ref.at[block, far_c, :, :, left], near_in.at[index, 1], x_near),
                go(ref.at[block, y_c, :, :, right], near_in.at[index, 2], y_near),
                go(ref.at[block, far_c, :, :, right], near_in.at[index, 3], y_near),
            ]
        )

    send_grad(0)
    send_term(0)
    send_term(1)
    send_grad(1)
    width = wq_ref.shape[1]
    wq_here = wq_out.at[:, span(me_c * width, width)]
    local.start(wq_ref, wq_here)
    z_pair, z_next = {"fsdp": me_z ^ 1}, {"fsdp": me_z ^ 2}

    def halve(ref, low, count, at):
        blocks = pl.ds(low, count)
        return [
            go(ref.at[blocks, me_z ^ 1], zpart_ref.at[0, pl.ds(at, count)], z_pair),
            go(ref.at[blocks, me_z ^ 3], zpart_ref.at[1, pl.ds(at, count)], z_pair),
        ]

    def halve_on(moves_in, own, count, at):
        for move in moves_in:
            move.wait_recv()
        for block in range(count):
            zsend_ref[at + block] = own(block) + zpart_ref[1, at + block]
        blocks = pl.ds(at, count)
        return go(zsend_ref.at[blocks], znext_ref.at[blocks], z_next)

    down_in = halve(down_ref, 0, downs, len(terms))
    first = lax.broadcasted_iota(jnp.int32, (local_len, 128), 1) < HD
    place = lax.broadcasted_iota(jnp.int32, (local_len, 128), 0)
    weight_ref[...] = jnp.zeros_like(weight_ref)
    far_moves = []

    def sum_step(index):
        for move in near[index]:
            move.wait_recv()
        local.wait(own_in[index])
        local.wait(far_own[2 * index])
        local.wait(far_own[2 * index + 1])
        far_y[index] += near_in[index, 1]
        first_far = go(far_y.at[index], far_in.at[index, 0], y_near)
        far_x[index] += near_in[index, 3]
        far_moves.append((first_far, go(far_x.at[index], far_in.at[index, 1], x_near)))

    def sum_end(index):
        for move in far_moves[index]:
            move.wait_recv()
        own_ref[index, :, :, left] += near_in[index, 0] + far_in[index, 0]
        own_ref[index, :, :, right] += near_in[index, 2] + far_in[index, 1]

    for i in range(images):
        for copy in held[i]:
            local.wait(copy)
        local.wait(grad_in[i][0])
        for move in grad_in[i][1:]:
            move.wait_recv()
        prod = (grad[i].astype(F32) * o_all[i].astype(F32)).T
        for head in range(2):
            row_ref[8 * head : 8 * head + 8, :] = jnp.broadcast_to(
                jnp.sum(prod[HD * head : HD * (head + 1)], axis=0, keepdims=True),
                (8, prod.shape[1]),
            )
        dq_ref[...] = jnp.zeros_like(dq_ref)
        real = cnt_ref[i : i + 1, :]

        def attend(chunk):
            rows = span(chunk * local_len, local_len)
            q = qkv[i, :, 0:128]
            k = qkv[i, rows, 128:256] * SCALE
            v = qkv[i, rows, 256:384]
            do = grad[i]
            live = (place + chunk * local_len < real)[:, 0:1]
            dks, dvs = [], []
            for head in range(2):
                mask = first if head == 0 else jnp.logical_not(first)
                kh = jnp.where(mask, k, jnp.zeros_like(k))
                vh = jnp.where(mask, v, jnp.zeros_like(v))
                lse = lse_ref[i, 8 * head : 8 * head + 1, :]
                delta = row_ref[8 * head : 8 * head + 1, :]
                prob = jnp.where(live, jnp.exp(dot_nt(kh, q) - lse), 0.0)
                ds = (prob * (dot_nt(vh, do) - delta)).astype(BF)
                dvs.append(dot_nn(prob.astype(BF), do))
                dks.append(dot_nn(ds, q) * SCALE)
                dq_ref[...] += dot_tn(ds, kh)
            heads[i, rows, 128:256] = jnp.where(first, dks[0], dks[1]).astype(BF)
            heads[i, rows, 256:384] = jnp.where(first, dvs[0], dvs[1]).astype(BF)

        pl.loop(0, nc // 2)(attend)
        if i == 0:
            sum_step(0)
            send_term(2)
        if i == 1:
            sum_step(2)
            send_term(4)
        if i == 2:
            sum_step(3)
            for index in range(3):
                sum_end(index)
            group_a = halve(own_ref, 0, 3, 0)
        pl.loop(nc // 2, nc)(attend)
        heads[i, :, 0:128] = dq_ref[...].astype(BF)
        local.wait(x_in[i])

        @pl.loop(0, nc)
        def _(chunk):
            rows = span(chunk * local_len, local_len)
            weight_ref[...] += dot_tn(heads[i, rows], x_all[i % 2, rows])

        local.start(heads.at[i], heads_out.at[i])
        if i + 2 < images:
            x_in.append(local.start(x_ref.at[i + 2], x_all.at[i % 2]))
        if i == 0:
            for copy in mine_in:
                local.wait(copy)
            down_next = halve_on(down_in, lambda b: mine_ref[1, b], downs, len(terms))
            sum_step(1)
            send_grad(2)
            send_term(3)
    sub = late_ref.shape[2]
    for z in range(nz):
        for j in range(LATE):
            late_ref[z, j] = weight_ref[pl.ds(j * 128 + z * sub, sub)].astype(BF)
    late_in = [
        go(late_ref.at[me_z ^ 1], lpart_ref.at[0], z_pair),
        go(late_ref.at[me_z ^ 3], lpart_ref.at[1], z_pair),
    ]
    sum_step(4)
    wq_in = [go(wq_ref, wq_here, x_near), go(wq_ref, wq_here, y_near)]
    next_in = [down_next, halve_on(group_a, lambda b: own_ref[b, me_z ^ 2], 3, 0)]
    for index in range(3, len(terms)):
        sum_end(index)
    group_b = halve(own_ref, 3, len(terms) - 3, 3)
    for move in late_in:
        move.wait_recv()
    lsend_ref[...] = late_ref[me_z ^ 2] + lpart_ref[1]
    late_next = go(lsend_ref, lnext_ref, z_next)
    next_in.append(
        halve_on(group_b, lambda b: own_ref[3 + b, me_z ^ 2], len(terms) - 3, 3)
    )
    late_next.wait_recv()
    total = late_ref[me_z].astype(F32) + lpart_ref[0].astype(F32) + lnext_ref[...].astype(F32)
    late_out[...] = total.astype(BF)
    for move in next_in:
        move.wait_recv()
    for block in range(EARLY):
        if block < len(terms):
            total = own_ref[block, me_z].astype(F32)
        else:
            total = mine_ref[0, block - len(terms)].astype(F32)
        total = total + zpart_ref[0, block].astype(F32) + znext_ref[block].astype(F32)
        early_ref[block] = total.astype(BF)
    for move in wq_in:
        move.wait_recv()
    local.finish()
    for move in sent:
        move.wait_send()


def backward_attention(
    qkv, o_heads, lse, grad_att, counts, term_out, term_up, down, x_all, wq, nz, nc
):
    images, seq = qkv.shape[:2]
    local_len = seq // nc
    sub = term_up.shape[3]
    terms = 1 + term_up.shape[0]
    any_ = pl.BlockSpec(memory_space=pl.ANY)
    vmem = pl.BlockSpec(memory_space=pltpu.VMEM)
    return pl.pallas_call(
        functools.partial(backward_kernel, nz, nc),
        out_shape=(
            jax.ShapeDtypeStruct((EARLY, sub, D), BF),
            jax.ShapeDtypeStruct((LATE, sub, D), BF),
            jax.ShapeDtypeStruct((images, seq, 384), BF),
            jax.ShapeDtypeStruct((D, nc * 384), BF),
        ),
        in_specs=[
            any_,
            any_,
            vmem,
            any_,
            vmem,
            any_,
            any_,
            any_,
            any_,
            any_,
        ],
        out_specs=(vmem, vmem, any_, any_),
        scratch_shapes=[
            pltpu.VMEM((images, seq, 128), BF),
            pltpu.VMEM((images, seq, 384), BF),
            pltpu.VMEM((images, seq, 384), BF),
            pltpu.VMEM((images, seq, 128), BF),
            pltpu.VMEM((2, seq, D), BF),
            pltpu.VMEM((seq, 128), F32),
            pltpu.VMEM((16, seq), F32),
            pltpu.VMEM((384, D), F32),
            pltpu.VMEM((terms, nz, sub, D), BF),
            pltpu.VMEM((terms, nz, sub, D // 2), BF),
            pltpu.VMEM((terms, nz, sub, D // 2), BF),
            pltpu.VMEM((terms, 4, nz, sub, D // 2), BF),
            pltpu.VMEM((terms, 2, nz, sub, D // 2), BF),
            pltpu.VMEM((2, EARLY - terms, sub, D), BF),
            pltpu.VMEM((2, EARLY, sub, D), BF),
            pltpu.VMEM((EARLY, sub, D), BF),
            pltpu.VMEM((EARLY, sub, D), BF),
            pltpu.VMEM((nz, LATE, sub, D), BF),
            pltpu.VMEM((2, LATE, sub, D), BF),
            pltpu.VMEM((LATE, sub, D), BF),
            pltpu.VMEM((LATE, sub, D), BF),
            pltpu.SemaphoreType.DMA((256,)),
            pltpu.SemaphoreType.DMA((256,)),
            pltpu.SemaphoreType.DMA((64,)),
        ],
        compiler_params=pltpu.CompilerParams(
            collective_id=2, has_side_effects=True, vmem_limit_bytes=61 << 20
        ),
        name="backward_attention",
    )(
        qkv,
        o_heads,
        lse,
        grad_att,
        counts,
        term_out,
        term_up,
        down,
        x_all,
        wq,
    )


def tail_kernel(
    nz,
    nc,
    token_count,
    slot_blocks,
    early_ref,
    late_ref,
    heads_ref,
    wq_ref,
    tokens_ref,
    mid_ref,
    gain_ref,
    gains_ref,
    rl_ref,
    rr_ref,
    sl_ref,
    sr_ref,
    ms_ref,
    tokens_out,
    gain_out,
    grad_out,
    left_out,
    right_out,
    weight_out,
    tok,
    wq,
    x_buf,
    mid_buf,
    part,
    part_in,
    rl,
    rr,
    sl,
    sr,
    ms,
    update,
    square,
    square_in,
    gain_sum,
    gain_in,
    place_ref,
    g_ref,
    l_ref,
    g_all,
    send,
    recv,
    local_sems,
):
    me_z, me_c, me_t = (lax.axis_index(a) for a in ("fsdp", "context", "tensor"))
    images, local_len = tokens_ref.shape[:2]
    slots = g_ref.shape[0]
    x_c, y_c, far_c = me_c ^ 1, me_c ^ 2, me_c ^ 3
    core, x_near, y_near = {"tensor": 1 - me_t}, {"context": x_c}, {"context": y_c}
    above, below = {"fsdp": me_z + 1}, {"fsdp": me_z - 1}
    c_peers = [{"context": me_c ^ k} for k in range(1, nc)]
    group = [
        {"fsdp": me_z ^ (k // 2), "tensor": me_t ^ (k % 2)} for k in range(1, 2 * nz)
    ]
    rows_group = [(me_z ^ (k // nc), me_c ^ (k % nc)) for k in range(1, nz * nc)]
    others = [{"fsdp": z, "context": c} for z, c in rows_group[nc - 1 :] ]
    diagonal = [d for k, d in enumerate(others) if (k + nc) % nc]
    left, right = pl.ds(0, D // 2), pl.ds(D // 2, D // 2)
    local = Local(local_sems)
    width = wq.shape[1] // nc
    wq_in = [
        local.start(wq_ref.at[:, span(m * width, width)], wq.at[:, span(m * width, width)])
        for m in (me_c, x_c, y_c)
    ]
    x_in = [local.start(tokens_ref.at[i], x_buf.at[i]) for i in range(images)]
    mid_in = [local.start(mid_ref.at[i], mid_buf.at[i]) for i in range(images)]
    state_in = [
        local.start(a, b) for a, b in ((rl_ref, rl), (sl_ref, sl), (sr_ref, sr), (ms_ref, ms))
    ]
    rr_in = [local.start(rr_ref.at[0], rr)]
    for slot in range(NBLK):
        block = jnp.clip(slot_blocks[slot] - LATE, 0, EARLY - 1)
        place_ref[slot] = early_ref[block]
    l_ref[:, me_t, me_c, me_z] = late_ref[...]
    for slot in range(slots):
        g_ref[slot, me_t, me_c, me_z] = place_ref[me_c * slots + slot]
    greet(group + c_peers + diagonal)
    moves = Moves(send, recv)
    sent = []

    def go(*args, **kw):
        move = moves.make(*args, **kw)
        move.start()
        sent.append(move)
        return move

    placed = []
    for k in range(1, nc):
        theirs = place_ref.at[pl.ds((me_c ^ k) * slots, slots)]
        placed.append(go(theirs, g_ref.at[:, me_t, me_c, me_z], c_peers[k - 1]))

    swapped = []

    def swap(piece, cond=None):
        swapped.append(go(piece, piece, core, cond=cond, recv_cond=cond))

    def along_fsdp(at):
        own = at(me_z)
        return [
            go(own, own, above, cond=me_z < nz - 1, recv_cond=me_z > 0),
            go(own, own, below, cond=me_z > 0, recv_cond=me_z < nz - 1),
        ]

    def onward(at, last, hop):
        up_z, down_z = me_z - hop, me_z + hop
        last[0].wait_recv()
        up = down = None
        if hop < nz - 1:
            piece = at(up_z)
            cond = jnp.logical_and(me_z < nz - 1, up_z >= 0)
            up = go(piece, piece, above, cond=cond, recv_cond=up_z - 1 >= 0)
        last[1].wait_recv()
        if hop < nz - 1:
            piece = at(down_z)
            cond = jnp.logical_and(me_z > 0, down_z <= nz - 1)
            down = go(piece, piece, below, cond=cond, recv_cond=down_z + 1 <= nz - 1)
        return [up, down], [(up_z, up_z >= 0), (down_z, down_z <= nz - 1)]

    def late_at(member):
        return lambda z: l_ref.at[:, me_t, member, z]

    def slot_at(slot):
        return lambda z: g_ref.at[slot, me_t, :, z]

    late_line = along_fsdp(late_at(me_c))
    near, far = [], []

    def spread(z, cond=None):
        piece = late_at(me_c)(z)
        near.append(
            (
                z,
                cond,
                go(piece, piece, x_near, cond=cond, recv_cond=cond),
                go(piece, piece, y_near, cond=cond, recv_cond=cond),
            )
        )
        swap(piece, cond)

    def spread_on(entry):
        z, cond, x_move, y_move = entry
        x_move.wait_recv()
        piece = l_ref.at[:, me_t, x_c, z, :, left]
        first = go(piece, piece, y_near, cond=cond, recv_cond=cond)
        swap(late_at(x_c)(z), cond)
        y_move.wait_recv()
        piece = l_ref.at[:, me_t, y_c, z, :, right]
        second = go(piece, piece, x_near, cond=cond, recv_cond=cond)
        swap(late_at(y_c)(z), cond)
        far.append((z, cond, left, first))
        far.append((z, cond, right, second))

    spread(me_z)
    tok_in = []

    def send_tok(i):
        there = tok.at[i, :, span(me_c * 384, 384)]
        tok_in.append(
            [local.start(heads_ref.at[i, span(me_c * local_len, local_len)], there)]
            + [
                go(
                    heads_ref.at[i, span((me_c ^ k) * local_len, local_len)],
                    there,
                    c_peers[k - 1],
                )
                for k in range(1, nc)
            ]
        )
    lines = []

    def slot_line(slot):
        lines.append(along_fsdp(slot_at(slot)))
        swap(slot_at(slot)(me_z))

    def late_on(hop):
        nonlocal late_line
        late_line, here = onward(late_at(me_c), late_line, hop)
        for z, cond in here:
            spread(z, cond)

    half_rows = D // 2
    for copy in wq_in[1:]:
        local.wait(copy)
    late_on(1)
    for move in placed:
        move.wait_recv()
    slot_line(0)
    spread_on(near[0])
    late_on(2)
    slot_line(1)
    slot_line(2)
    for entry in near[1:3]:
        spread_on(entry)
    send_tok(0)
    late_on(3)
    for entry in near[3:5]:
        spread_on(entry)
    x_rows = wq.at[pl.ds(0, half_rows), span(x_c * width, width)]
    y_rows = wq.at[pl.ds(half_rows, half_rows), span(y_c * width, width)]
    wq_far = [go(x_rows, x_rows, y_near), go(y_rows, y_rows, x_near)]

    part_moves = []
    gain_out[...] = jnp.zeros_like(gain_out)
    square[...] = jnp.zeros_like(square)

    def project(i):
        local.wait(tok_in[i][0])
        for move in tok_in[i][1:]:
            move.wait_recv()
        part[i] = dot_nt(tok[i], wq[...]).astype(BF)
        part_moves.append(go(part.at[i], part_in.at[i], core))

    def norm_backward(i):
        part_moves[i].wait_recv()
        local.wait(x_in[i])
        local.wait(mid_in[i])

        @pl.loop(0, 2)
        def _(step):
            rows = span(step * (local_len // 2), local_len // 2)
            value = x_buf[i, rows]
            centred = value - jnp.mean(value, axis=-1, keepdims=True)
            inv_std = lax.rsqrt(jnp.mean(centred * centred, axis=-1, keepdims=True) + 1e-06)
            normed = centred * inv_std
            grad = part[i, rows].astype(F32) + part_in[i, rows].astype(F32)
            scaled = grad * gain_ref[...]
            inner = (
                scaled
                - jnp.mean(scaled, axis=-1, keepdims=True)
                - normed * jnp.mean(scaled * normed, axis=-1, keepdims=True)
            )
            mid_buf[i, rows] += inner * inv_std
            gain_out[0:1, :] += jnp.sum(grad * normed, axis=0, keepdims=True)

        local.start(mid_buf.at[i], tokens_out.at[i])

    def slots_on(hop):
        for slot in range(slots):
            lines[slot], here = onward(slot_at(slot), lines[slot], hop)
            for z, cond in here:
                swap(slot_at(slot)(z), cond)

    slots_on(1)
    for entry in near[5:]:
        spread_on(entry)
    for i in range(1, images):
        send_tok(i)
    for z, cond, columns, move in far:
        move.wait_recv()
        swap(l_ref.at[:, me_t, far_c, z, :, columns], cond)
    local.wait(wq_in[0])
    for move in wq_far:
        move.wait_recv()
    project(0)
    slots_on(2)
    for i in range(1, images):
        project(i)
    for i in range(images):
        norm_backward(i)
    gain_sum[...] = gains_ref[...]
    gain_sum[0:1, :] = gain_out[0:1, :]
    gain_moves = []
    for k, (z, c) in enumerate(rows_group):
        theirs = span((z * nc + c) // 2 * 128, 128)
        gain_moves.append(
            go(gain_sum.at[:, theirs], gain_in.at[k], {"fsdp": z, "context": c})
        )
    slots_on(3)
    for move in swapped:
        move.wait_recv()
    for copy in state_in:
        local.wait(copy)
    offset = me_t * (D // 2) + me_z * rl.shape[1]
    mine = span(offset, rl.shape[1])
    for slot in range(slots):
        block = slot_blocks[me_c * slots + slot]
        late = l_ref[jnp.clip(block, 0, LATE - 1)]
        g_all[...] = jnp.where(block < LATE, late, g_ref[slot]).reshape(D, D)
        rows = g_all[mine, :]
        grad_out[slot] = rows.astype(F32)
        left_out[slot] = 0.5 * sl[slot] + 0.5 / token_count * dot_nt(rows, g_all[...])
        right_out[slot] = 0.5 * sr[slot] + 0.5 / token_count * dot_tn(g_all[:, mine], g_all[...])
        inner = dot_nn(rl[slot].astype(BF), g_all[...]).astype(BF)
        local.wait(rr_in[slot])
        update[slot] = dot_nn(inner, rr[...].astype(BF))
        if slot + 1 < slots:
            rr_in.append(local.start(rr_ref.at[slot + 1], rr))
        total = jnp.sum(update[slot] * update[slot], axis=0, keepdims=True)
        total = jnp.sum(total, axis=1, keepdims=True)
        square[slot : slot + 1, :] = jnp.broadcast_to(total, (1, 128))
    square_moves = [
        go(square, square_in.at[k], group[k]) for k in range(len(group))
    ]
    for move in square_moves:
        move.wait_recv()
    for slot in range(slots):
        total = square[slot : slot + 1, 0:1]
        for k in range(len(group)):
            total = total + square_in[k, slot : slot + 1, 0:1]
        weight_out[slot] = ms[slot] - lax.rsqrt(total / (D * D) + 1e-06) * update[slot]
    total = gain_sum[:, span((me_z * nc + me_c) // 2 * 128, 128)]
    for k, move in enumerate(gain_moves):
        move.wait_recv()
        total = total + gain_in[k]
    gain_out[:, 0:128] = total
    local.finish()
    for move in sent:
        move.wait_send()


def tail(
    block_of,
    early,
    late,
    grad_heads,
    wq_all,
    tokens,
    grad_middle,
    gain,
    gain_terms,
    root_left,
    root_right,
    stat_left,
    stat_right,
    master,
    token_count,
    nz,
    nc,
    nt,
):
    images, local_len = tokens.shape[:2]
    sub = early.shape[1]
    slots, row_count = root_left.shape[:2]
    any_ = pl.BlockSpec(memory_space=pl.ANY)
    vmem = pl.BlockSpec(memory_space=pltpu.VMEM)
    state = jax.ShapeDtypeStruct((slots, row_count, D), F32)
    shape = (slots, nt, nc, nz, sub, D)
    return pl.pallas_call(
        functools.partial(tail_kernel, nz, nc, token_count),
        out_shape=(
            jax.ShapeDtypeStruct((images, local_len, D), F32),
            jax.ShapeDtypeStruct((8, D), F32),
            state,
            state,
            state,
            state,
        ),
        in_specs=[pl.BlockSpec(memory_space=pltpu.SMEM), vmem, vmem]
        + [any_] * 4
        + [vmem, vmem]
        + [any_] * 5,
        out_specs=(any_, vmem, vmem, vmem, vmem, vmem),
        scratch_shapes=[
            pltpu.VMEM((images, local_len, nc * 384), BF),
            pltpu.VMEM((D, nc * 384), BF),
            pltpu.VMEM((images, local_len, D), F32),
            pltpu.VMEM((images, local_len, D), F32),
            pltpu.VMEM((images, local_len, D), BF),
            pltpu.VMEM((images, local_len, D), BF),
            pltpu.VMEM((slots, row_count, D), F32),
            pltpu.VMEM((D, D), F32),
            pltpu.VMEM((slots, row_count, D), F32),
            pltpu.VMEM((slots, row_count, D), F32),
            pltpu.VMEM((slots, row_count, D), F32),
            pltpu.VMEM((slots, row_count, D), F32),
            pltpu.VMEM((8, 128), F32),
            pltpu.VMEM((2 * nz - 1, 8, 128), F32),
            pltpu.VMEM((8, D), F32),
            pltpu.VMEM((nz * nc - 1, 8, 128), F32),
            pltpu.VMEM((NBLK, sub, D), BF),
            pltpu.VMEM(shape, BF),
            pltpu.VMEM((LATE, nt, nc, nz, sub, D), BF),
            pltpu.VMEM((D, D), BF),
            pltpu.SemaphoreType.DMA((160,)),
            pltpu.SemaphoreType.DMA((160,)),
            pltpu.SemaphoreType.DMA((32,)),
        ],
        compiler_params=pltpu.CompilerParams(
            collective_id=3, has_side_effects=True, vmem_limit_bytes=61 << 20
        ),
        name="tail",
    )(
        block_of,
        early,
        late,
        grad_heads,
        wq_all,
        tokens,
        grad_middle,
        gain,
        gain_terms,
        root_left,
        root_right,
        stat_left,
        stat_right,
        master,
    )


def xor_permute(value, axis, step):
    size = lax.axis_size(axis)
    return lax.ppermute(value, axis, [(j, j ^ step) for j in range(size)])


def xor_order(pieces, index):
    bit = 1
    while bit < len(pieces):
        odd = (index & bit) > 0
        pieces = [jnp.where(odd, pieces[j ^ bit], pieces[j]) for j in range(len(pieces))]
        bit *= 2
    return pieces


def sum_tensor(value):
    low = lax.optimization_barrier(value.astype(BF))
    return low.astype(F32) + xor_permute(low, "tensor", 1).astype(F32)


def gather_fsdp(value):
    size = lax.axis_size("fsdp")
    if size > 4:
        return lax.all_gather(value, "fsdp", axis=0, tiled=False)
    pieces = [value] + [
        lax.ppermute(value, "fsdp", [(j, (j - k) % size) for j in range(size)])
        for k in range(1, size)
    ]
    doubled = jnp.stack(pieces + pieces[:-1])
    start = lax.rem(size - lax.axis_index("fsdp"), size)
    return lax.dynamic_slice_in_dim(doubled, start, size, 0)


def sum_fsdp(value):
    size = lax.axis_size("fsdp")
    if size > 4:
        return lax.psum(value, "fsdp")
    total = value
    for k in range(1, size):
        total = total + lax.ppermute(value, "fsdp", [(j, (j - k) % size) for j in range(size)])
    return total


def grad_gather_plain(block_of, early, late, nz, nc):
    me_c, me_t = (lax.axis_index(a) for a in ("context", "tensor"))
    sub = early.shape[1]
    half_width = nc * nz * sub
    slot_count = NBLK // nc
    slots_of = block_of.reshape(nc, slot_count)

    def slots_for(k):
        blocks = lax.dynamic_index_in_dim(slots_of, me_c ^ k, 0, keepdims=False)
        return early[jnp.clip(blocks - LATE, 0, EARLY - 1)]

    placed = [slots_for(0)] + [xor_permute(slots_for(k), "context", k) for k in range(1, nc)]
    placed = jnp.stack(xor_order(placed, me_c), axis=1)
    placed = lax.all_gather(placed, "fsdp", axis=2, tiled=False)
    placed = placed.reshape(slot_count, half_width, D)
    placed_other = xor_permute(placed, "tensor", 1)
    both = jnp.stack([placed, placed_other], axis=1)
    early_full = jnp.where(me_t > 0, both[:, ::-1], both).reshape(slot_count, D, D)

    late = late.reshape(-1, D)
    late = lax.psum_scatter(late, "fsdp", scatter_dimension=0, tiled=True)
    late = lax.all_gather(late, ("context", "fsdp"), axis=0, tiled=True)
    late = jnp.swapaxes(late.reshape(nc * nz, LATE, sub, D), 0, 1).reshape(LATE, half_width, D)
    late_other = xor_permute(late, "tensor", 1)
    both = jnp.stack([late, late_other], axis=1)
    late_full = jnp.where(me_t > 0, both[:, ::-1], both).reshape(LATE, D, D)

    mine = lax.dynamic_index_in_dim(slots_of, me_c, 0, keepdims=False)
    return jnp.where(
        (mine < LATE)[:, None, None], late_full[jnp.clip(mine, 0, LATE - 1)], early_full
    )


def to_natural(value, me_t, half_len):
    parts = value.reshape((-1, half_len) + value.shape[1:])
    return jnp.where(me_t > 0, parts[::-1], parts).reshape(value.shape)


def forward_plain(tokens, gain, key_mask, w_qkv, w_out, w_up, w_down):
    images, local_len = tokens.shape[:2]
    nc, nt = (lax.axis_size(a) for a in ("context", "tensor"))
    me_c, me_t = (lax.axis_index(a) for a in ("context", "tensor"))
    cols = w_qkv.shape[2] // nc
    half_len = local_len // nt
    wq_part = lax.dynamic_slice_in_dim(w_qkv, me_c * cols, cols, 2)
    wq = gather_fsdp(wq_part).reshape(D, 3 * cols)

    def two_stage(weight, member_axis, fsdp_axis):
        width = weight.shape[member_axis] // nc
        part = lax.dynamic_slice_in_dim(weight, me_c * width, width, member_axis)
        part = lax.all_gather(part, "fsdp", axis=fsdp_axis, tiled=True)
        return lax.all_gather(part, "context", axis=member_axis, tiled=True)

    out_full = two_stage(w_out, 0, 1)
    up_full = two_stage(w_up, 1, 0)
    down_full = two_stage(w_down, 0, 1)

    counts = jnp.sum(key_mask, axis=1)
    real = counts
    for k in range(1, nc):
        real = real + xor_permute(counts, "context", k)
    position = (
        (me_c ^ jnp.arange(nc))[:, None, None] * local_len
        + (me_t ^ jnp.arange(nt))[None, :, None] * half_len
        + jnp.arange(half_len)[None, None, :]
    ).reshape(-1)
    live = position[None, :] < real[:, None]
    bias = jnp.where(live, 0.0, -1e30).astype(F32)
    live_col = jnp.broadcast_to(live[:, :, None].astype(F32), (images, SEQ, 128))

    normed1, inv_std1, pre_norm1 = norm_fwd(tokens, gain)
    normed1_low = pre_norm1.astype(BF)

    x_all, qkv, out_heads, log_sums, attended = [], [], [], [], []
    for i in range(images):
        mine = lax.dynamic_slice_in_dim(normed1_low[i], me_t * half_len, half_len, 0)
        held = jnp.stack([mine] + [xor_permute(mine, "context", k) for k in range(1, nc)])
        other = xor_permute(held, "tensor", 1)
        x_i = jnp.stack([held, other], axis=1).reshape(SEQ, D)
        qkv_i = dot_nn(x_i, wq).astype(BF)
        o_i, lse_i = attn_fwd(qkv_i, bias[i][None])
        chunks = o_i.reshape(nc, local_len, 2 * HD)
        moved = [to_natural(chunks[0], me_t, half_len)] + [
            to_natural(xor_permute(chunks[k], "context", k), me_t, half_len) for k in range(1, nc)
        ]
        attended.append(jnp.concatenate(xor_order(moved, me_c), axis=-1))
        x_all.append(x_i)
        qkv.append(qkv_i)
        out_heads.append(o_i)
        log_sums.append(lse_i)
    attended = jnp.stack(attended)
    return (
        jnp.stack(x_all),
        jnp.stack(qkv),
        jnp.stack(out_heads),
        jnp.stack(log_sums),
        attended,
        live_col,
        wq,
        out_full,
        up_full,
        down_full,
        normed1,
        inv_std1,
    )


def backward_plain(qkv, out_heads, log_sums, grad_att, live_col, early, wq):
    images, local_len = grad_att.shape[:2]
    nz, nc, nt = (lax.axis_size(a) for a in ("fsdp", "context", "tensor"))
    me_c, me_t = (lax.axis_index(a) for a in ("context", "tensor"))
    cols = grad_att.shape[2] // nc
    half_len = local_len // nt
    sub = early.shape[2]
    grad_heads = []
    grad_tok = []
    for i in range(images):
        pieces = [grad_att[i, :, j * cols : (j + 1) * cols] for j in range(nc)]
        pieces = [to_natural(p, me_t, half_len) for p in xor_order(pieces, me_c)]
        grad_i = jnp.concatenate(
            [pieces[0]] + [xor_permute(pieces[k], "context", k) for k in range(1, nc)]
        )
        g_i = attn_bwd(qkv[i], grad_i, out_heads[i], log_sums[i], live_col[i])
        chunks = g_i.reshape(nc, local_len, 3 * cols)
        moved = [to_natural(chunks[0], me_t, half_len)] + [
            to_natural(xor_permute(chunks[k], "context", k), me_t, half_len) for k in range(1, nc)
        ]
        grad_tok.append(jnp.stack(xor_order(moved, me_c), axis=1))
        grad_heads.append(g_i)
    grad_tok = jnp.stack(grad_tok)
    wq_all = lax.all_gather(wq, "context", axis=0, tiled=False)
    grad_n1 = sum_tensor(
        jnp.einsum("isjc,jdc->isd", grad_tok, wq_all, preferred_element_type=F32)
    )
    early = lax.psum_scatter(
        jnp.swapaxes(early, 0, 1).reshape(-1, D),
        "fsdp",
        scatter_dimension=0,
        tiled=True,
    ).reshape(EARLY, sub, D)
    return jnp.stack(grad_heads), grad_n1, early


def per_device(
    tokens,
    cotangent,
    gains,
    w_qkv,
    w_out,
    w_up,
    w_down,
    key_mask,
    owner,
    stat_left,
    stat_right,
    root_left,
    root_right,
    master,
    gain_state,
):
    images, local_len = tokens.shape[:2]
    tok_rows = images * local_len
    nz, nc, nt = (lax.axis_size(a) for a in ("fsdp", "context", "tensor"))
    me_z, me_c, me_t = (lax.axis_index(a) for a in ("fsdp", "context", "tensor"))
    half_width = w_qkv.shape[2]
    hidden = w_up.shape[1]
    up_blocks = hidden // half_width
    cols = half_width // nc
    fast = nz == 4 and nc == 4 and nt == 2 and images == 3
    if fast:
        wq_part = lax.dynamic_slice_in_dim(w_qkv, me_c * cols, cols, 2).reshape(-1, 3 * cols)
        counts = jnp.pad(jnp.sum(key_mask, axis=1), (0, 8 - images))
        counts = jnp.broadcast_to(counts[:, None], (8, 128))
        (
            x_all,
            qkv,
            out_heads,
            log_sums,
            attended,
            counts,
            wq,
            out_full,
            up_full,
            down_part,
        ) = forward_attention(
            tokens, gains[0:1], counts, wq_part, w_out, w_up, w_down, nz, nc
        )
        down_full = lax.all_gather(down_part, "context", axis=0, tiled=True)
        normed1, inv_std1, _ = norm_fwd(tokens, gains[0])
    else:
        (
            x_all,
            qkv,
            out_heads,
            log_sums,
            attended,
            live_col,
            wq,
            out_full,
            up_full,
            down_full,
            normed1,
            inv_std1,
        ) = forward_plain(tokens, gains[0], key_mask, w_qkv, w_out, w_up, w_down)

    branch_attn = sum_tensor(
        jnp.einsum("ish,hd->isd", attended, out_full, preferred_element_type=F32)
    )
    middle = tokens + gains[2] * branch_attn
    normed2, inv_std2, pre_norm2 = norm_fwd(middle, gains[1])
    normed2_low = pre_norm2.astype(BF)
    pre_act = jnp.einsum("isd,df->isf", normed2_low, up_full, preferred_element_type=F32)
    act_val, act_slope = gelu_parts(pre_act)
    act_low = act_val.astype(BF)
    branch_mlp = sum_tensor(
        jnp.einsum("isf,fd->isd", act_low, down_full, preferred_element_type=F32)
    )
    output = middle + gains[3] * branch_mlp

    grad_mlp = (gains[3] * cotangent).astype(BF)
    grad_hidden = jnp.einsum("isd,fd->isf", grad_mlp, down_full, preferred_element_type=F32)
    grad_pre = (grad_hidden * act_slope).astype(BF)
    grad_n2 = sum_tensor(
        jnp.einsum("isf,df->isd", grad_pre, up_full, preferred_element_type=F32)
    )
    middle_part, grad_gain2 = norm_back(grad_n2, gains[1], normed2, inv_std2)
    grad_middle = cotangent + middle_part
    grad_branch = (gains[2] * grad_middle).astype(BF)
    grad_att = jnp.einsum(
        "isd,hd->ish", grad_branch, out_full, preferred_element_type=F32
    ).astype(BF)

    sub = half_width // nc // nz
    onehot = (owner[:, None] == jnp.arange(NBLK, dtype=jnp.int32)[None, :]).astype(jnp.int32)
    block_of = jnp.sum(onehot * jnp.arange(NBLK, dtype=jnp.int32)[:, None], axis=0)

    def early_term(left, right):
        term = dot_tn(left.reshape(tok_rows, -1), right.reshape(tok_rows, D)).astype(BF)
        return term.reshape(-1, nc, nz, sub, D)

    def early_sum(term):
        return lax.psum_scatter(
            jnp.swapaxes(term, 0, 1).reshape(-1, D), "context", scatter_dimension=0, tiled=True
        ).reshape(-1, nz, sub, D)

    term_out = early_term(attended, grad_branch)
    term_up = early_term(grad_pre, normed2_low)
    down = early_sum(early_term(act_low, grad_mlp))
    tokens_all = images * nz * SEQ
    grad_gain3 = jnp.sum(grad_middle * branch_attn, axis=(0, 1))
    grad_gain4 = jnp.sum(cotangent * branch_mlp, axis=(0, 1))
    blank = jnp.zeros_like(grad_gain2)
    gain_terms = jnp.stack([blank, grad_gain2, grad_gain3, grad_gain4] + [blank] * 4, axis=0)
    if fast:
        early, late, grad_heads, wq_all = backward_attention(
            qkv, out_heads, log_sums, grad_att, counts, term_out, term_up, down, x_all, wq, nz, nc
        )
        grad_tokens, gain_sum, grad_mine, left_new, right_new, weight_new = tail(
            block_of,
            early,
            late,
            grad_heads,
            wq_all,
            tokens,
            grad_middle,
            gains[0:1],
            gain_terms,
            root_left[:, 0],
            root_right,
            stat_left[:, 0],
            stat_right[:, 0],
            master[:, 0],
            tokens_all,
            nz,
            nc,
            nt,
        )
    else:
        early = jnp.concatenate([early_sum(term_out), early_sum(term_up), down], axis=0)
        grad_heads, grad_n1, early = backward_plain(
            qkv, out_heads, log_sums, grad_att, live_col, early, wq
        )
        term_qkv = jnp.einsum("isk,isd->kd", grad_heads, x_all, preferred_element_type=F32)
        late = jnp.swapaxes(term_qkv.astype(BF).reshape(LATE, nz, sub, D), 0, 1)
        grad_full = grad_gather_plain(block_of, early, late, nz, nc)
        input_part, grad_gain1 = norm_back(grad_n1, gains[0], normed1, inv_std1)
        grad_tokens = grad_middle + input_part
        row_count = half_width // nz
        row_offset = me_t * half_width + me_z * row_count
        grad_mine = lax.dynamic_slice_in_dim(grad_full, row_offset, row_count, 1)
        left_new = 0.5 * stat_left[:, 0] + 0.5 / tokens_all * jnp.einsum(
            "sra,sba->srb", grad_mine, grad_full, preferred_element_type=F32
        )
        grad_cols = lax.dynamic_slice_in_dim(grad_full, row_offset, row_count, 2)
        right_new = 0.5 * stat_right[:, 0] + 0.5 / tokens_all * jnp.einsum(
            "sar,sab->srb", grad_cols, grad_full, preferred_element_type=F32
        )
        inner_prod = jnp.einsum(
            "sra,sab->srb", root_left[:, 0].astype(BF), grad_full, preferred_element_type=F32
        ).astype(BF)
        update = jnp.einsum(
            "srb,sbc->src", inner_prod, root_right.astype(BF), preferred_element_type=F32
        )
        square_sum = jnp.sum(update * update, axis=(1, 2))
        square_sum = sum_fsdp(square_sum + xor_permute(square_sum, "tensor", 1))
        factor = lax.rsqrt(square_sum / (D * D) + 1e-06)
        weight_new = master[:, 0] - factor[:, None, None] * update

        gain_terms = gain_terms[:4].at[0].set(grad_gain1)
        gain_sum = gain_terms
        step = 1
        while step < nc:
            gain_sum = gain_sum + xor_permute(gain_sum, "context", step)
            step *= 2
        gain_sum = sum_fsdp(gain_sum)

    share_width = gain_state.shape[1]
    gain_index = lax.axis_index(("fsdp", "context"))
    if fast:
        at = lax.rem(gain_index * share_width, 128)
        gain_grad = lax.dynamic_slice(gain_sum, (0, at), (4, share_width))
    else:
        gain_grad = lax.dynamic_slice_in_dim(
            gain_sum, gain_index * share_width, share_width, 1
        )
    gain_mine = lax.dynamic_slice_in_dim(gains, gain_index * share_width, share_width, 1)
    state_new = 0.5 * gain_state + 0.5 * gain_grad * gain_grad / tokens_all
    gain_new = gain_mine - 0.1 * gain_grad * lax.rsqrt(tokens_all * state_new)
    return (
        output,
        grad_tokens,
        grad_mine.astype(F32)[:, None],
        left_new[:, None],
        right_new[:, None],
        weight_new[:, None],
        gain_grad,
        state_new,
        gain_new,
    )


def solution(mesh):
    return jax.shard_map(
        per_device,
        mesh=mesh,
        in_specs=(
            P("fsdp", "context", None),
            P("fsdp", "context", None),
            P(),
            P("fsdp", None, "tensor"),
            P("tensor", "fsdp"),
            P("fsdp", "tensor"),
            P("tensor", "fsdp"),
            P("fsdp", "context"),
            P(),
            P("context", "tensor", "fsdp", None),
            P("context", "tensor", "fsdp", None),
            P("context", "tensor", "fsdp", None),
            P("context", None, None),
            P("context", "tensor", "fsdp", None),
            P(None, ("fsdp", "context")),
        ),
        out_specs=(
            P("fsdp", "context", None),
            P("fsdp", "context", None),
            P("context", "tensor", "fsdp", None),
            P("context", "tensor", "fsdp", None),
            P("context", "tensor", "fsdp", None),
            P("context", "tensor", "fsdp", None),
            P(None, ("fsdp", "context")),
            P(None, ("fsdp", "context")),
            P(None, ("fsdp", "context")),
        ),
        check_vma=False,
    )
```

```python
import functools

import jax
import jax.numpy as jnp
from jax import lax
from jax.experimental import pallas as pl
from jax.experimental.pallas import tpu as pltpu
from jax.sharding import PartitionSpec as P

D = 1024
HD = 64
SEQ = 1408
NBLK = 12
LATE = 3
EARLY = NBLK - LATE
BF = jnp.bfloat16
F32 = jnp.float32
SCALE = HD ** (-0.5)


def norm_fwd(field_in, gain_vec):
    centred = field_in - jnp.mean(field_in, axis=-1, keepdims=True)
    inv_std = lax.rsqrt(jnp.mean(centred * centred, axis=-1, keepdims=True) + 1e-06)
    normed = centred * inv_std
    return (normed, inv_std, normed * gain_vec)


def norm_back(grad_out, gain_vec, normed, inv_std):
    scaled = grad_out * gain_vec
    inner_sum = (
        scaled
        - jnp.mean(scaled, axis=-1, keepdims=True)
        - normed * jnp.mean(scaled * normed, axis=-1, keepdims=True)
    )
    return (inner_sum * inv_std, jnp.sum(grad_out * normed, axis=(0, 1)))


def gelu_parts(field_in):
    normal_cdf = 0.5 * (1.0 + lax.erf(field_in * 0.7071067811865476))
    normal_pdf = jnp.exp(-0.5 * field_in * field_in) * 0.3989422804014327
    return (field_in * normal_cdf, normal_cdf + field_in * normal_pdf)


def dot_nt(a, b):
    return lax.dot_general(a, b, (((1,), (1,)), ((), ())), preferred_element_type=F32)


def dot_tn(a, b):
    return lax.dot_general(a, b, (((0,), (0,)), ((), ())), preferred_element_type=F32)


def dot_nn(a, b):
    return lax.dot_general(a, b, (((1,), (0,)), ((), ())), preferred_element_type=F32)


def attn_fwd_kernel(q_ref, k_ref, v_ref, bias_ref, o_ref, lse_ref):
    q = q_ref[...] * SCALE
    k = k_ref[...]
    v = v_ref[...]
    bias = bias_ref[...]
    first = lax.broadcasted_iota(jnp.int32, q.shape, 1) < HD
    outs, sums = [], []
    for head in range(2):
        mask = first if head == 0 else jnp.logical_not(first)
        scores = dot_nt(jnp.where(mask, q, jnp.zeros_like(q)), k) + bias
        peak = jnp.max(scores, axis=-1, keepdims=True)
        expo = jnp.exp(scores - peak)
        total = jnp.sum(expo, axis=-1, keepdims=True)
        outs.append(dot_nn(expo.astype(BF), v) / total)
        sums.append(peak + jnp.log(total))
    o_ref[...] = jnp.where(first, outs[0], outs[1]).astype(BF)
    lse_ref[...] = jnp.where(first, sums[0], sums[1])


def attn_fwd(qkv, bias_row):
    rows = qkv.shape[0]
    bq = rows // 4
    return pl.pallas_call(
        attn_fwd_kernel,
        grid=(rows // bq,),
        out_shape=(
            jax.ShapeDtypeStruct((rows, 128), BF),
            jax.ShapeDtypeStruct((rows, 128), F32),
        ),
        in_specs=[
            pl.BlockSpec((bq, 128), lambda i: (i, 0)),
            pl.BlockSpec((rows, 128), lambda i: (0, 1)),
            pl.BlockSpec((rows, 128), lambda i: (0, 2)),
            pl.BlockSpec((1, rows), lambda i: (0, 0)),
        ],
        out_specs=(
            pl.BlockSpec((bq, 128), lambda i: (i, 0)),
            pl.BlockSpec((bq, 128), lambda i: (i, 0)),
        ),
        compiler_params=pltpu.CompilerParams(vmem_limit_bytes=40 << 20),
        cost_estimate=pl.CostEstimate(
            flops=4 * rows * rows * 512, bytes_accessed=rows * 2048, transcendentals=2 * rows * rows
        ),
        name="attn_fwd",
    )(qkv, qkv, qkv, bias_row)


def attn_bwd_kernel(q_ref, k_ref, v_ref, do_ref, o_ref, lse_ref, live_ref, out_ref, dq_ref, row_ref):
    step = pl.program_id(0)
    chunk = k_ref.shape[0]

    @pl.when(step == 0)
    def _():
        row_ref[0:128, :] = lse_ref[...].T
        prod = do_ref[...].astype(F32) * o_ref[...].astype(F32)
        prod_t = prod.T
        row_ref[128:136, :] = jnp.broadcast_to(
            jnp.sum(prod_t[0:HD], axis=0, keepdims=True), (8, prod_t.shape[1])
        )
        row_ref[136:144, :] = jnp.broadcast_to(
            jnp.sum(prod_t[HD:128], axis=0, keepdims=True), (8, prod_t.shape[1])
        )
        dq_ref[...] = jnp.zeros_like(dq_ref)

    q = q_ref[...]
    k = k_ref[...] * SCALE
    v = v_ref[...]
    do = do_ref[...]
    live = live_ref[:, 0:1] > 0
    first = lax.broadcasted_iota(jnp.int32, k.shape, 1) < HD
    dks, dvs = [], []
    for head in range(2):
        mask = first if head == 0 else jnp.logical_not(first)
        kh = jnp.where(mask, k, jnp.zeros_like(k))
        vh = jnp.where(mask, v, jnp.zeros_like(v))
        lse = row_ref[64 * head : 64 * head + 1, :]
        delta = row_ref[128 + 8 * head : 129 + 8 * head, :]
        prob = jnp.where(live, jnp.exp(dot_nt(kh, q) - lse), 0.0)
        ds = (prob * (dot_nt(vh, do) - delta)).astype(BF)
        dvs.append(dot_nn(prob.astype(BF), do))
        dks.append(dot_nn(ds, q) * SCALE)
        dq_ref[...] += dot_tn(ds, kh)
    at = pl.ds(pl.multiple_of(step * chunk, chunk), chunk)
    out_ref[at, 128:256] = jnp.where(first, dks[0], dks[1]).astype(BF)
    out_ref[at, 256:384] = jnp.where(first, dvs[0], dvs[1]).astype(BF)

    @pl.when(step == pl.num_programs(0) - 1)
    def _():
        out_ref[:, 0:128] = dq_ref[...].astype(BF)


def attn_bwd(qkv, grad, out, lse, live_col):
    rows = qkv.shape[0]
    chunk = rows // 4
    return pl.pallas_call(
        attn_bwd_kernel,
        grid=(rows // chunk,),
        out_shape=jax.ShapeDtypeStruct((rows, 384), BF),
        in_specs=[
            pl.BlockSpec((rows, 128), lambda i: (0, 0)),
            pl.BlockSpec((chunk, 128), lambda i: (i, 1)),
            pl.BlockSpec((chunk, 128), lambda i: (i, 2)),
            pl.BlockSpec((rows, 128), lambda i: (0, 0)),
            pl.BlockSpec((rows, 128), lambda i: (0, 0)),
            pl.BlockSpec((rows, 128), lambda i: (0, 0)),
            pl.BlockSpec((chunk, 128), lambda i: (i, 0)),
        ],
        out_specs=pl.BlockSpec((rows, 384), lambda i: (0, 0)),
        scratch_shapes=[pltpu.VMEM((rows, 128), F32), pltpu.VMEM((144, rows), F32)],
        compiler_params=pltpu.CompilerParams(vmem_limit_bytes=50 << 20),
        cost_estimate=pl.CostEstimate(
            flops=10 * rows * rows * 512, bytes_accessed=rows * 4096, transcendentals=2 * rows * rows
        ),
        name="attn_bwd",
    )(qkv, qkv, qkv, grad, out, lse, live_col)


class Moves:
    def __init__(self, send_sems, recv_sems):
        self.send_sems, self.recv_sems, self.count = send_sems, recv_sems, 0

    def make(self, src, dst, device, cond=None, recv_cond=None):
        index = self.count
        self.count += 1
        return Move(self, index, src, dst, device, cond, recv_cond)


class Move:
    def __init__(self, moves, index, src, dst, device, cond, recv_cond):
        self.args = (src, dst, moves.send_sems.at[index], moves.recv_sems.at[index])
        self.device, self.cond, self.recv_cond = device, cond, recv_cond

    def copy(self):
        return pltpu.make_async_remote_copy(
            *self.args, device_id=self.device, device_id_type=pl.DeviceIdType.MESH
        )

    def when(self, cond, act):
        if cond is None:
            act()
        else:
            pl.when(cond)(act)

    def start(self):
        self.when(self.cond, lambda: self.copy().start())

    def wait_recv(self):
        self.when(self.recv_cond, lambda: self.copy().wait_recv())

    def wait_send(self):
        self.when(self.cond, lambda: self.copy().wait_send())


def greet(devices):
    barrier = pltpu.get_barrier_semaphore()
    for device in devices:
        pl.semaphore_signal(
            barrier, inc=1, device_id=device, device_id_type=pl.DeviceIdType.MESH
        )
    pl.semaphore_wait(barrier, len(devices))


def span(start, size):
    return pl.ds(pl.multiple_of(start, size & -size), size)


class Local:
    def __init__(self, sems):
        self.sems, self.count, self.open = sems, 0, []

    def start(self, src, dst):
        copy = pltpu.make_async_copy(src, dst, self.sems.at[self.count])
        self.count += 1
        copy.start()
        self.open.append(copy)
        return copy

    def wait(self, copy):
        copy.wait()
        self.open = [c for c in self.open if c is not copy]

    def finish(self):
        for copy in self.open:
            copy.wait()
        self.open = []


def spread_plane(go, ref_of, me_c, cond=None):
    own = ref_of(me_c, None)
    return [go(own, own, {"context": me_c ^ 1}), go(own, own, {"context": me_c ^ 2})]


def spread_plane_on(go, ref_of, me_c, near):
    near[0].wait_recv()
    piece = ref_of(me_c ^ 1, 0)
    first = go(piece, piece, {"context": me_c ^ 2})
    near[1].wait_recv()
    piece = ref_of(me_c ^ 2, 1)
    second = go(piece, piece, {"context": me_c ^ 1})
    return [first, second]


def forward_kernel(
    nz,
    nc,
    tokens_ref,
    gain_ref,
    count_ref,
    wq_ref,
    wout_ref,
    wup_ref,
    wdown_ref,
    x_out,
    qkv_out,
    o_out,
    lse_out,
    att_out,
    cnt_out,
    wq_out,
    out_full,
    up_full,
    down_part,
    tok,
    x_all,
    qkv,
    o_all,
    lse_all,
    wq,
    counts,
    send,
    recv,
    local_sems,
):
    me_z, me_c, me_t = (lax.axis_index(a) for a in ("fsdp", "context", "tensor"))
    images, local_len = att_out.shape[:2]
    half = local_len // 2
    seq = x_all.shape[1]
    core = {"tensor": 1 - me_t}
    z_peers = [{"fsdp": lax.rem(me_z + k, nz)} for k in range(1, nz)]
    c_peers = [{"context": me_c ^ k} for k in range(1, nc)]
    local = Local(local_sems)
    token_in = [
        local.start(tokens_ref.at[i, span(me_t * half, half)], tok.at[i]) for i in range(images)
    ]
    depth = wq_ref.shape[0]
    wq_own = local.start(wq_ref, wq.at[span(me_z * depth, depth)])
    greet(z_peers + c_peers + [core])
    moves = Moves(send, recv)
    sent = []

    def go(*args, **kw):
        move = moves.make(*args, **kw)
        move.start()
        sent.append(move)
        return move

    wq_in = [go(wq_ref, wq.at[span(me_z * depth, depth)], peer) for peer in z_peers]
    counts[me_c] = count_ref[...]
    count_in = [go(count_ref, counts.at[me_c], peer) for peer in c_peers]

    def to_line(src, dst):
        local_copy = local.start(src, dst)
        return [local_copy] + [go(src, dst, peer) for peer in z_peers]

    cols, hid, depth_o = wout_ref.shape[0] // nc, wup_ref.shape[1] // nc, wout_ref.shape[1]

    def x_piece(i):
        def at(member, part):
            rows = span(member * local_len + me_t * half, half)
            if part is None:
                return x_all.at[i, rows]
            return x_all.at[i, rows, pl.ds(part * (D // 2), D // 2)]

        return at

    swaps = [[] for _ in range(images)]
    near, far = [], []

    def swap(i, member, part=None):
        piece = x_piece(i)(member, part)
        swaps[i].append(go(piece, piece, core))

    def normalize(i):
        local.wait(token_in[i])
        value = tok[i]
        centred = value - jnp.mean(value, axis=-1, keepdims=True)
        inv_std = lax.rsqrt(jnp.mean(centred * centred, axis=-1, keepdims=True) + 1e-06)
        x_all[i, span(me_c * local_len + me_t * half, half)] = (
            centred * inv_std * gain_ref[...]
        ).astype(BF)

    def send_near(i):
        near.append(spread_plane(go, x_piece(i), me_c))
        swap(i, me_c)

    def send_far(i):
        far.append(spread_plane_on(go, x_piece(i), me_c, near[i]))
        swap(i, me_c ^ 1)
        swap(i, me_c ^ 2)

    normalize(0)
    send_near(0)
    out_in = to_line(
        wout_ref.at[span(me_c * cols, cols)],
        out_full.at[span(me_c * cols, cols), span(me_z * depth_o, depth_o)],
    )
    up_in = to_line(
        wup_ref.at[:, span(me_c * hid, hid)],
        up_full.at[span(me_z * depth, depth), span(me_c * hid, hid)],
    )
    down_in = to_line(
        wdown_ref.at[span(me_c * hid, hid)],
        down_part.at[:, span(me_z * depth_o, depth_o)],
    )
    normalize(1)
    send_near(1)
    normalize(2)
    send_far(0)
    send_near(2)
    local.wait(wq_own)
    for move in wq_in:
        move.wait_recv()
    local.start(wq, wq_out)
    for move in count_in:
        move.wait_recv()
    total = counts[0]
    for k in range(1, nc):
        total = total + counts[k]
    cnt_out[...] = total

    first = lax.broadcasted_iota(jnp.int32, (local_len, 128), 1) < HD
    place = lax.broadcasted_iota(jnp.int32, (1, seq), 1)

    def weight_plane(move_in, ref_of):
        local.wait(move_in[0])
        for move in move_in[1:]:
            move.wait_recv()
        return spread_plane(go, ref_of, me_c)

    def out_piece(member, part):
        rows = span(member * cols, cols)
        return out_full.at[rows] if part is None else out_full.at[rows, pl.ds(part * (D // 2), D // 2)]

    def up_piece(member, part):
        at = span(member * hid, hid)
        return up_full.at[:, at] if part is None else up_full.at[pl.ds(part * (D // 2), D // 2), at]

    att_in = []
    for i in range(images):
        for part in range(2):
            far[i][part].wait_recv()
            swap(i, me_c ^ 3, part)
        for move in swaps[i]:
            move.wait_recv()
        local.start(x_all.at[i], x_out.at[i])

        @pl.loop(0, nc)
        def _(chunk):
            rows = span(chunk * local_len, local_len)
            qkv[i, rows] = dot_nn(x_all[i, rows], wq[...]).astype(BF)

        local.start(qkv.at[i], qkv_out.at[i])
        if i == 0:
            send_far(1)
        bias = jnp.where(place < cnt_out[i : i + 1, 0:1], 0.0, -1e30)
        def attend(chunk):
            rows = span(chunk * local_len, local_len)
            q = qkv[i, rows, 0:128] * SCALE
            k = qkv[i, :, 128:256]
            v = qkv[i, :, 256:384]
            outs, sums = [], []
            for head in range(2):
                mask = first if head == 0 else jnp.logical_not(first)
                scores = dot_nt(jnp.where(mask, q, jnp.zeros_like(q)), k) + bias
                peak = jnp.max(scores, axis=-1, keepdims=True)
                expo = jnp.exp(scores - peak)
                norm = jnp.sum(expo, axis=-1, keepdims=True)
                outs.append(dot_nn(expo.astype(BF), v) / norm)
                sums.append(peak + jnp.log(norm))
            o_all[i, rows] = jnp.where(first, outs[0], outs[1]).astype(BF)
            lse_all[rows] = jnp.where(first, sums[0], sums[1])

        pl.loop(0, nc // 2)(attend)
        if i == 0:
            send_far(2)
            out_near = weight_plane(out_in, out_piece)
        if i == images - 1:
            out_far = spread_plane_on(go, out_piece, me_c, out_near)
        pl.loop(nc // 2, nc)(attend)

        mine = att_out.at[i, :, span(me_c * 128, 128)]
        for k in range(1, nc):
            att_in.append(
                go(o_all.at[i, span((me_c ^ k) * local_len, local_len)], mine, c_peers[k - 1])
            )
        local.start(o_all.at[i, span(me_c * local_len, local_len)], mine)
        local.start(o_all.at[i], o_out.at[i])
        sums_t = lse_all[...].T
        for head in range(2):
            lse_out[i, 8 * head : 8 * head + 8, :] = jnp.broadcast_to(
                sums_t[HD * head : HD * head + 1], (8, seq)
            )
        if i == 1:
            up_near = weight_plane(up_in, up_piece)
    up_far = spread_plane_on(go, up_piece, me_c, up_near)
    for move in att_in + out_far + up_far + down_in[1:]:
        move.wait_recv()
    local.finish()
    for move in sent:
        move.wait_send()


def forward_attention(tokens, gain, counts, wq_part, w_out, w_up, w_down, nz, nc):
    images, local_len = tokens.shape[:2]
    seq = nc * local_len
    cols, hid = w_out.shape[0], w_up.shape[1]
    any_ = pl.BlockSpec(memory_space=pl.ANY)
    vmem = pl.BlockSpec(memory_space=pltpu.VMEM)
    return pl.pallas_call(
        functools.partial(forward_kernel, nz, nc),
        out_shape=(
            jax.ShapeDtypeStruct((images, seq, D), BF),
            jax.ShapeDtypeStruct((images, seq, 384), BF),
            jax.ShapeDtypeStruct((images, seq, 128), BF),
            jax.ShapeDtypeStruct((images, 16, seq), F32),
            jax.ShapeDtypeStruct((images, local_len, cols), BF),
            jax.ShapeDtypeStruct((8, 128), jnp.int32),
            jax.ShapeDtypeStruct((D, 384), BF),
            jax.ShapeDtypeStruct((cols, D), BF),
            jax.ShapeDtypeStruct((D, hid), BF),
            jax.ShapeDtypeStruct((hid // nc, D), BF),
        ),
        in_specs=[any_, vmem, vmem, any_, any_, any_, any_],
        out_specs=(any_, any_, any_, vmem, any_, vmem, any_, any_, any_, any_),
        scratch_shapes=[
            pltpu.VMEM((images, local_len // 2, D), F32),
            pltpu.VMEM((images, seq, D), BF),
            pltpu.VMEM((images, seq, 384), BF),
            pltpu.VMEM((images, seq, 128), BF),
            pltpu.VMEM((seq, 128), F32),
            pltpu.VMEM((D, 384), BF),
            pltpu.VMEM((nc, 8, 128), jnp.int32),
            pltpu.SemaphoreType.DMA((96,)),
            pltpu.SemaphoreType.DMA((96,)),
            pltpu.SemaphoreType.DMA((32,)),
        ],
        compiler_params=pltpu.CompilerParams(
            collective_id=1, has_side_effects=True, vmem_limit_bytes=56 << 20
        ),
        name="forward_attention",
    )(tokens, gain, counts, wq_part, w_out, w_up, w_down)


def feed_forward_kernel(
    nc,
    att_ref,
    wout_ref,
    wup_ref,
    wdown_ref,
    tokens_ref,
    cot_ref,
    gains_ref,
    output_out,
    mid_out,
    gatt_out,
    tout_out,
    tup_out,
    own_out,
    fary_out,
    farx_out,
    gain_out,
    att,
    wout,
    wup,
    wdown,
    tok,
    cot,
    normed_low,
    act,
    slope,
    low,
    first_own,
    first_in,
    second_own,
    second_in,
    third_in,
    stage,
    term,
    near_in,
    gatt,
    send,
    recv,
    local_sems,
):
    me_c, me_t = (lax.axis_index(a) for a in ("context", "tensor"))
    images, local_len = tok.shape[:2]
    hid = wdown_ref.shape[0]
    x_c, y_c, far_c = me_c ^ 1, me_c ^ 2, me_c ^ 3
    core, x_near, y_near = {"tensor": 1 - me_t}, {"context": x_c}, {"context": y_c}
    left, right = pl.ds(0, D // 2), pl.ds(D // 2, D // 2)
    half = local_len // 2
    local = Local(local_sems)
    att_in = [local.start(att_ref, att), local.start(wout_ref, wout)]
    cot_in = local.start(cot_ref, cot)
    tok_in = local.start(tokens_ref, tok)
    up_in = local.start(wup_ref, wup)

    def down_piece(member, part):
        rows = span(member * hid, hid)
        return wdown.at[rows] if part is None else wdown.at[rows, pl.ds(part * (D // 2), D // 2)]

    down_own = local.start(wdown_ref, down_piece(me_c, None))
    greet([core, x_near, y_near])
    moves = Moves(send, recv)
    sent = []

    def go(*args, **kw):
        move = moves.make(*args, **kw)
        move.start()
        sent.append(move)
        return move

    down_near = [
        go(wdown_ref, down_piece(me_c, None), x_near),
        go(wdown_ref, down_piece(me_c, None), y_near),
    ]
    for copy in att_in:
        local.wait(copy)

    @pl.loop(0, images)
    def _(i):
        first_own[i] = dot_nn(att[i], wout[...]).astype(BF)

    first = go(first_own, first_in, core)
    local.wait(cot_in)

    @pl.loop(0, images)
    def _(i):
        low[i] = (gains_ref[3:4, :] * cot[i]).astype(BF)

    local.wait(tok_in)
    first.wait_recv()

    @pl.loop(0, 2 * images)
    def _(step):
        i, rows = step // 2, span(lax.rem(step, 2) * half, half)
        branch = first_own[i, rows].astype(F32) + first_in[i, rows].astype(F32)
        value = tok[i, rows] + gains_ref[2:3, :] * branch
        tok[i, rows] = value
        centred = value - jnp.mean(value, axis=-1, keepdims=True)
        inv_std = lax.rsqrt(jnp.mean(centred * centred, axis=-1, keepdims=True) + 1e-06)
        normed_low[i, rows] = (centred * inv_std * gains_ref[1:2, :]).astype(BF)

    local.wait(up_in)
    width = 512

    @pl.loop(0, images)
    def _(i):
        @pl.loop(0, wup.shape[1] // width)
        def _(step):
            cols = span(step * width, width)
            value = dot_nn(normed_low[i], wup[:, cols])
            cdf = 0.5 * (1.0 + lax.erf(value * 0.7071067811865476))
            pdf = jnp.exp(-0.5 * value * value) * 0.3989422804014327
            act[i, :, cols] = (value * cdf).astype(BF)
            slope[i, :, cols] = (cdf + value * pdf).astype(BF)

    down_far = spread_plane_on(go, down_piece, me_c, down_near)
    blocks = term.shape[0]
    chunk_rows = term.shape[2]

    @pl.loop(0, blocks)
    def _(j):
        cols = span(j * width, width)
        total = jnp.zeros((width, D), F32)
        for i in range(images):
            total += dot_tn(act[i, :, cols], low[i])
        for c in range(nc):
            term[j, c] = total[c * chunk_rows : (c + 1) * chunk_rows].astype(BF)

    near = [
        go(term.at[:, x_c, :, left], near_in.at[0], x_near),
        go(term.at[:, far_c, :, left], near_in.at[1], x_near),
        go(term.at[:, y_c, :, right], near_in.at[2], y_near),
        go(term.at[:, far_c, :, right], near_in.at[3], y_near),
    ]
    local.wait(down_own)
    for move in down_far:
        move.wait_recv()

    @pl.loop(0, images)
    def _(i):
        second_own[i] = dot_nn(act[i], wdown[...]).astype(BF)

    second = go(second_own, second_in, core)

    @pl.loop(0, images)
    def _(i):
        @pl.loop(0, wup.shape[1] // width)
        def _(step):
            cols = span(step * width, width)
            value = dot_nt(low[i], wdown[cols, :]) * slope[i, :, cols].astype(F32)
            slope[i, :, cols] = value.astype(BF)

    first.wait_send()
    sent.remove(first)
    second.wait_recv()
    gain_out[...] = jnp.zeros_like(gain_out)

    @pl.loop(0, 2 * images)
    def _(step):
        i, rows = step // 2, span(lax.rem(step, 2) * half, half)
        branch = first_own[i, rows].astype(F32) + first_in[i, rows].astype(F32)
        first_in[i, rows] = branch.astype(BF)

    @pl.loop(0, images)
    def _(i):
        first_own[i] = dot_nt(slope[i], wup[...]).astype(BF)

    third = go(first_own, third_in, core)

    def up_term(j, at):
        cols = span(j * width, width)
        total = jnp.zeros((width, D), F32)
        for i in range(images):
            total += dot_tn(slope[i, :, cols], normed_low[i])
        stage[at] = total.astype(BF)

    copies = []
    for j in range(blocks):
        if j >= 2:
            local.wait(copies[j - 2])
        up_term(j, j % 2)
        copies.append(local.start(stage.at[j % 2], tup_out.at[pl.ds(j * width, width)]))
    third.wait_recv()

    @pl.loop(0, 2 * images)
    def _(step):
        i, rows = step // 2, span(lax.rem(step, 2) * half, half)
        value = tok[i, rows]
        centred = value - jnp.mean(value, axis=-1, keepdims=True)
        inv_std = lax.rsqrt(jnp.mean(centred * centred, axis=-1, keepdims=True) + 1e-06)
        normed = centred * inv_std
        branch = second_own[i, rows].astype(F32) + second_in[i, rows].astype(F32)
        tok[i, rows] = value + gains_ref[3:4, :] * branch
        cotangent = cot[i, rows]
        gain_out[3:4, :] += jnp.sum(cotangent * branch, axis=0, keepdims=True)
        grad = first_own[i, rows].astype(F32) + third_in[i, rows].astype(F32)
        gain_out[1:2, :] += jnp.sum(grad * normed, axis=0, keepdims=True)
        scaled = grad * gains_ref[1:2, :]
        inner = (
            scaled
            - jnp.mean(scaled, axis=-1, keepdims=True)
            - normed * jnp.mean(scaled * normed, axis=-1, keepdims=True)
        )
        grad = cotangent + inner * inv_std
        cot[i, rows] = grad
        gain_out[2:3, :] += jnp.sum(grad * first_in[i, rows].astype(F32), axis=0, keepdims=True)
        low[i, rows] = (gains_ref[2:3, :] * grad).astype(BF)

    local.start(tok, output_out)
    local.start(cot, mid_out)

    @pl.loop(0, images)
    def _(i):
        gatt[i] = dot_nt(low[i], wout[...]).astype(BF)

    local.start(gatt, gatt_out)
    total = jnp.zeros((att.shape[2], D), F32)
    for i in range(images):
        total += dot_tn(att[i], low[i])
    for copy in copies[-2:]:
        local.wait(copy)
    stage[0] = total.astype(BF)
    local.start(stage.at[0], tout_out)
    for move in near:
        move.wait_recv()
    for move in near:
        move.wait_send()
        sent.remove(move)
    term[:, me_c, :, left] += near_in[0]
    term[:, me_c, :, right] += near_in[2]
    term[:, y_c, :, left] += near_in[1]
    term[:, x_c, :, right] += near_in[3]
    local.start(term.at[:, me_c], own_out)
    local.start(term.at[:, y_c, :, left], fary_out)
    local.start(term.at[:, x_c, :, right], farx_out)
    local.finish()
    for move in sent:
        move.wait_send()


def feed_forward(attended, out_full, up_full, down_part, tokens, cotangent, gains, nc):
    images, local_len = tokens.shape[:2]
    cols, hid = out_full.shape[0], up_full.shape[1]
    blocks = hid // 512
    piece = (blocks, 512 // nc)
    any_ = pl.BlockSpec(memory_space=pl.ANY)
    vmem = pl.BlockSpec(memory_space=pltpu.VMEM)
    rows = (images, local_len)
    return pl.pallas_call(
        functools.partial(feed_forward_kernel, nc),
        out_shape=(
            jax.ShapeDtypeStruct(rows + (D,), F32),
            jax.ShapeDtypeStruct(rows + (D,), F32),
            jax.ShapeDtypeStruct(rows + (cols,), BF),
            jax.ShapeDtypeStruct((cols, D), BF),
            jax.ShapeDtypeStruct((hid, D), BF),
            jax.ShapeDtypeStruct(piece + (D,), BF),
            jax.ShapeDtypeStruct(piece + (D // 2,), BF),
            jax.ShapeDtypeStruct(piece + (D // 2,), BF),
            jax.ShapeDtypeStruct((8, D), F32),
        ),
        in_specs=[any_] * 6 + [vmem],
        out_specs=(any_,) * 8 + (vmem,),
        scratch_shapes=[
            pltpu.VMEM(rows + (cols,), BF),
            pltpu.VMEM((cols, D), BF),
            pltpu.VMEM((D, hid), BF),
            pltpu.VMEM((hid, D), BF),
            pltpu.VMEM(rows + (D,), F32),
            pltpu.VMEM(rows + (D,), F32),
            pltpu.VMEM(rows + (D,), BF),
            pltpu.VMEM(rows + (hid,), BF),
            pltpu.VMEM(rows + (hid,), BF),
            pltpu.VMEM(rows + (D,), BF),
            pltpu.VMEM(rows + (D,), BF),
            pltpu.VMEM(rows + (D,), BF),
            pltpu.VMEM(rows + (D,), BF),
            pltpu.VMEM(rows + (D,), BF),
            pltpu.VMEM(rows + (D,), BF),
            pltpu.VMEM((2, 512, D), BF),
            pltpu.VMEM((blocks, nc, 512 // nc, D), BF),
            pltpu.VMEM((4, blocks, 512 // nc, D // 2), BF),
            pltpu.VMEM(rows + (cols,), BF),
            pltpu.SemaphoreType.DMA((16,)),
            pltpu.SemaphoreType.DMA((16,)),
            pltpu.SemaphoreType.DMA((24,)),
        ],
        compiler_params=pltpu.CompilerParams(
            collective_id=4, has_side_effects=True, vmem_limit_bytes=62 << 20
        ),
        name="feed_forward",
    )(attended, out_full, up_full, down_part, tokens, cotangent, gains)


def backward_kernel(
    nz,
    nc,
    qkv_ref,
    o_ref,
    lse_ref,
    att_ref,
    cnt_ref,
    term_out_ref,
    term_up_ref,
    down_ref,
    down_y_ref,
    down_x_ref,
    x_ref,
    wq_ref,
    early_ref,
    late_out,
    heads_out,
    wq_out,
    grad,
    heads,
    qkv,
    o_all,
    x_all,
    dq_ref,
    row_ref,
    weight_ref,
    own_ref,
    far_y,
    far_x,
    near_in,
    far_in,
    mine_ref,
    mine_in_ref,
    zpart_ref,
    zsend_ref,
    znext_ref,
    late_ref,
    lpart_ref,
    lsend_ref,
    lnext_ref,
    send,
    recv,
    local_sems,
):
    me_z, me_c, me_t = (lax.axis_index(a) for a in ("fsdp", "context", "tensor"))
    images, local_len = att_ref.shape[:2]
    x_c, y_c, far_c = me_c ^ 1, me_c ^ 2, me_c ^ 3
    x_near, y_near = {"context": x_c}, {"context": y_c}
    z_peers = [{"fsdp": lax.rem(me_z + k, nz)} for k in range(1, nz)]
    c_peers = [{"context": me_c ^ k} for k in range(1, nc)]
    left, right = pl.ds(0, D // 2), pl.ds(D // 2, D // 2)
    ups, downs = term_up_ref.shape[0], down_ref.shape[0]
    terms = [(term_out_ref, 0)] + [(term_up_ref, j) for j in range(ups)]
    local = Local(local_sems)
    held = [
        [local.start(a.at[i], b.at[i]) for a, b in ((qkv_ref, qkv), (o_ref, o_all))]
        for i in range(images)
    ]
    x_in = [local.start(x_ref.at[i], x_all.at[i % 2]) for i in range(2)]
    own_in, far_own = [], []
    for index, (ref, block) in enumerate(terms):
        own_in.append(local.start(ref.at[block, me_c], own_ref.at[index]))
        far_own.append(local.start(ref.at[block, y_c, :, :, left], far_y.at[index]))
        far_own.append(local.start(ref.at[block, x_c, :, :, right], far_x.at[index]))
    mine_in = local.start(down_ref, mine_ref)
    greet(z_peers + c_peers)
    moves = Moves(send, recv)
    sent = []

    def go(*args, **kw):
        move = moves.make(*args, **kw)
        move.start()
        sent.append(move)
        return move

    grad_in = []

    def send_grad(i):
        here = grad.at[i, span(me_c * local_len, local_len)]
        grad_in.append(
            [local.start(att_ref.at[i, :, span(me_c * 128, 128)], here)]
            + [
                go(att_ref.at[i, :, span((me_c ^ k) * 128, 128)], here, c_peers[k - 1])
                for k in range(1, nc)
            ]
        )

    near = []

    def send_term(index):
        ref, block = terms[index]
        near.append(
            [
                go(ref.at[block, x_c, :, :, left], near_in.at[index, 0], x_near),
                go(ref.at[block, far_c, :, :, left], near_in.at[index, 1], x_near),
                go(ref.at[block, y_c, :, :, right], near_in.at[index, 2], y_near),
                go(ref.at[block, far_c, :, :, right], near_in.at[index, 3], y_near),
            ]
        )

    send_grad(0)
    down_far = [
        go(down_y_ref, mine_in_ref.at[0], y_near),
        go(down_x_ref, mine_in_ref.at[1], x_near),
    ]
    send_term(0)
    send_term(1)
    send_grad(1)
    width = wq_ref.shape[1]
    wq_here = wq_out.at[:, span(me_c * width, width)]
    local.start(wq_ref, wq_here)
    z_pair, z_next = {"fsdp": me_z ^ 1}, {"fsdp": me_z ^ 2}

    def halve(ref, low, count, at):
        blocks = pl.ds(low, count)
        return [
            go(ref.at[blocks, me_z ^ 1], zpart_ref.at[0, pl.ds(at, count)], z_pair),
            go(ref.at[blocks, me_z ^ 3], zpart_ref.at[1, pl.ds(at, count)], z_pair),
        ]

    def halve_on(moves_in, own, count, at):
        for move in moves_in:
            move.wait_recv()
        for block in range(count):
            zsend_ref[at + block] = own(block) + zpart_ref[1, at + block]
        blocks = pl.ds(at, count)
        return go(zsend_ref.at[blocks], znext_ref.at[blocks], z_next)

    first = lax.broadcasted_iota(jnp.int32, (local_len, 128), 1) < HD
    place = lax.broadcasted_iota(jnp.int32, (local_len, 128), 0)
    weight_ref[...] = jnp.zeros_like(weight_ref)
    far_moves = []

    def sum_step(index):
        for move in near[index]:
            move.wait_recv()
        local.wait(own_in[index])
        local.wait(far_own[2 * index])
        local.wait(far_own[2 * index + 1])
        far_y[index] += near_in[index, 1]
        first_far = go(far_y.at[index], far_in.at[index, 0], y_near)
        far_x[index] += near_in[index, 3]
        far_moves.append((first_far, go(far_x.at[index], far_in.at[index, 1], x_near)))

    def sum_end(index):
        for move in far_moves[index]:
            move.wait_recv()
        own_ref[index, :, :, left] += near_in[index, 0] + far_in[index, 0]
        own_ref[index, :, :, right] += near_in[index, 2] + far_in[index, 1]

    for i in range(images):
        for copy in held[i]:
            local.wait(copy)
        local.wait(grad_in[i][0])
        for move in grad_in[i][1:]:
            move.wait_recv()
        prod = (grad[i].astype(F32) * o_all[i].astype(F32)).T
        for head in range(2):
            row_ref[8 * head : 8 * head + 8, :] = jnp.broadcast_to(
                jnp.sum(prod[HD * head : HD * (head + 1)], axis=0, keepdims=True),
                (8, prod.shape[1]),
            )
        dq_ref[...] = jnp.zeros_like(dq_ref)
        real = cnt_ref[i : i + 1, :]

        def attend(chunk):
            rows = span(chunk * local_len, local_len)
            q = qkv[i, :, 0:128]
            k = qkv[i, rows, 128:256] * SCALE
            v = qkv[i, rows, 256:384]
            do = grad[i]
            live = (place + chunk * local_len < real)[:, 0:1]
            dks, dvs = [], []
            for head in range(2):
                mask = first if head == 0 else jnp.logical_not(first)
                kh = jnp.where(mask, k, jnp.zeros_like(k))
                vh = jnp.where(mask, v, jnp.zeros_like(v))
                lse = lse_ref[i, 8 * head : 8 * head + 1, :]
                delta = row_ref[8 * head : 8 * head + 1, :]
                prob = jnp.where(live, jnp.exp(dot_nt(kh, q) - lse), 0.0)
                ds = (prob * (dot_nt(vh, do) - delta)).astype(BF)
                dvs.append(dot_nn(prob.astype(BF), do))
                dks.append(dot_nn(ds, q) * SCALE)
                dq_ref[...] += dot_tn(ds, kh)
            heads[i, rows, 128:256] = jnp.where(first, dks[0], dks[1]).astype(BF)
            heads[i, rows, 256:384] = jnp.where(first, dvs[0], dvs[1]).astype(BF)

        pl.loop(0, nc // 2)(attend)
        if i == 0:
            sum_step(0)
            send_term(2)
            local.wait(mine_in)
            for move in down_far:
                move.wait_recv()
            mine_ref[:, :, :, left] += mine_in_ref[0]
            mine_ref[:, :, :, right] += mine_in_ref[1]
            down_in = halve(mine_ref, 0, downs, len(terms))
        if i == 1:
            down_next = halve_on(down_in, lambda b: mine_ref[b, me_z ^ 2], downs, len(terms))
            sum_step(2)
            send_term(4)
        if i == 2:
            sum_step(3)
            for index in range(3):
                sum_end(index)
            group_a = halve(own_ref, 0, 3, 0)
        pl.loop(nc // 2, nc)(attend)
        heads[i, :, 0:128] = dq_ref[...].astype(BF)
        local.wait(x_in[i])

        @pl.loop(0, nc)
        def _(chunk):
            rows = span(chunk * local_len, local_len)
            weight_ref[...] += dot_tn(heads[i, rows], x_all[i % 2, rows])

        local.start(heads.at[i], heads_out.at[i])
        if i + 2 < images:
            x_in.append(local.start(x_ref.at[i + 2], x_all.at[i % 2]))
        if i == 0:
            sum_step(1)
            send_grad(2)
            send_term(3)
    sub = late_ref.shape[2]
    for z in range(nz):
        for j in range(LATE):
            late_ref[z, j] = weight_ref[pl.ds(j * 128 + z * sub, sub)].astype(BF)
    late_in = [
        go(late_ref.at[me_z ^ 1], lpart_ref.at[0], z_pair),
        go(late_ref.at[me_z ^ 3], lpart_ref.at[1], z_pair),
    ]
    sum_step(4)
    wq_in = [go(wq_ref, wq_here, x_near), go(wq_ref, wq_here, y_near)]
    next_in = [down_next, halve_on(group_a, lambda b: own_ref[b, me_z ^ 2], 3, 0)]
    for index in range(3, len(terms)):
        sum_end(index)
    group_b = halve(own_ref, 3, len(terms) - 3, 3)
    for move in late_in:
        move.wait_recv()
    lsend_ref[...] = late_ref[me_z ^ 2] + lpart_ref[1]
    late_next = go(lsend_ref, lnext_ref, z_next)
    next_in.append(
        halve_on(group_b, lambda b: own_ref[3 + b, me_z ^ 2], len(terms) - 3, 3)
    )
    late_next.wait_recv()
    total = late_ref[me_z].astype(F32) + lpart_ref[0].astype(F32) + lnext_ref[...].astype(F32)
    late_out[...] = total.astype(BF)
    for move in next_in:
        move.wait_recv()
    for block in range(EARLY):
        if block < len(terms):
            total = own_ref[block, me_z].astype(F32)
        else:
            total = mine_ref[block - len(terms), me_z].astype(F32)
        total = total + zpart_ref[0, block].astype(F32) + znext_ref[block].astype(F32)
        early_ref[block] = total.astype(BF)
    for move in wq_in:
        move.wait_recv()
    local.finish()
    for move in sent:
        move.wait_send()


def backward_attention(
    qkv, o_heads, lse, grad_att, counts, term_out, term_up, down, down_y, down_x, x_all, wq, nz, nc
):
    images, seq = qkv.shape[:2]
    local_len = seq // nc
    sub = term_up.shape[3]
    terms = 1 + term_up.shape[0]
    any_ = pl.BlockSpec(memory_space=pl.ANY)
    vmem = pl.BlockSpec(memory_space=pltpu.VMEM)
    return pl.pallas_call(
        functools.partial(backward_kernel, nz, nc),
        out_shape=(
            jax.ShapeDtypeStruct((EARLY, sub, D), BF),
            jax.ShapeDtypeStruct((LATE, sub, D), BF),
            jax.ShapeDtypeStruct((images, seq, 384), BF),
            jax.ShapeDtypeStruct((D, nc * 384), BF),
        ),
        in_specs=[
            any_,
            any_,
            vmem,
            any_,
            vmem,
            any_,
            any_,
            any_,
            any_,
            any_,
            any_,
            any_,
        ],
        out_specs=(vmem, vmem, any_, any_),
        scratch_shapes=[
            pltpu.VMEM((images, seq, 128), BF),
            pltpu.VMEM((images, seq, 384), BF),
            pltpu.VMEM((images, seq, 384), BF),
            pltpu.VMEM((images, seq, 128), BF),
            pltpu.VMEM((2, seq, D), BF),
            pltpu.VMEM((seq, 128), F32),
            pltpu.VMEM((16, seq), F32),
            pltpu.VMEM((384, D), F32),
            pltpu.VMEM((terms, nz, sub, D), BF),
            pltpu.VMEM((terms, nz, sub, D // 2), BF),
            pltpu.VMEM((terms, nz, sub, D // 2), BF),
            pltpu.VMEM((terms, 4, nz, sub, D // 2), BF),
            pltpu.VMEM((terms, 2, nz, sub, D // 2), BF),
            pltpu.VMEM((EARLY - terms, nz, sub, D), BF),
            pltpu.VMEM((2, EARLY - terms, nz, sub, D // 2), BF),
            pltpu.VMEM((2, EARLY, sub, D), BF),
            pltpu.VMEM((EARLY, sub, D), BF),
            pltpu.VMEM((EARLY, sub, D), BF),
            pltpu.VMEM((nz, LATE, sub, D), BF),
            pltpu.VMEM((2, LATE, sub, D), BF),
            pltpu.VMEM((LATE, sub, D), BF),
            pltpu.VMEM((LATE, sub, D), BF),
            pltpu.SemaphoreType.DMA((256,)),
            pltpu.SemaphoreType.DMA((256,)),
            pltpu.SemaphoreType.DMA((64,)),
        ],
        compiler_params=pltpu.CompilerParams(
            collective_id=2, has_side_effects=True, vmem_limit_bytes=61 << 20
        ),
        name="backward_attention",
    )(
        qkv,
        o_heads,
        lse,
        grad_att,
        counts,
        term_out,
        term_up,
        down,
        down_y,
        down_x,
        x_all,
        wq,
    )


def tail_kernel(
    nz,
    nc,
    token_count,
    slot_blocks,
    early_ref,
    late_ref,
    heads_ref,
    wq_ref,
    tokens_ref,
    mid_ref,
    gain_ref,
    gains_ref,
    rl_ref,
    rr_ref,
    sl_ref,
    sr_ref,
    ms_ref,
    tokens_out,
    gain_out,
    grad_out,
    left_out,
    right_out,
    weight_out,
    tok,
    wq,
    x_buf,
    mid_buf,
    part,
    part_in,
    rl,
    rr,
    sl,
    sr,
    ms,
    update,
    square,
    square_in,
    gain_sum,
    gain_in,
    place_ref,
    g_ref,
    l_ref,
    g_all,
    send,
    recv,
    local_sems,
):
    me_z, me_c, me_t = (lax.axis_index(a) for a in ("fsdp", "context", "tensor"))
    images, local_len = tokens_ref.shape[:2]
    slots = g_ref.shape[0]
    x_c, y_c, far_c = me_c ^ 1, me_c ^ 2, me_c ^ 3
    core, x_near, y_near = {"tensor": 1 - me_t}, {"context": x_c}, {"context": y_c}
    above, below = {"fsdp": me_z + 1}, {"fsdp": me_z - 1}
    c_peers = [{"context": me_c ^ k} for k in range(1, nc)]
    group = [
        {"fsdp": me_z ^ (k // 2), "tensor": me_t ^ (k % 2)} for k in range(1, 2 * nz)
    ]
    rows_group = [(me_z ^ (k // nc), me_c ^ (k % nc)) for k in range(1, nz * nc)]
    others = [{"fsdp": z, "context": c} for z, c in rows_group[nc - 1 :] ]
    diagonal = [d for k, d in enumerate(others) if (k + nc) % nc]
    left, right = pl.ds(0, D // 2), pl.ds(D // 2, D // 2)
    local = Local(local_sems)
    width = wq.shape[1] // nc
    wq_in = [
        local.start(wq_ref.at[:, span(m * width, width)], wq.at[:, span(m * width, width)])
        for m in (me_c, x_c, y_c)
    ]
    x_in = [local.start(tokens_ref.at[i], x_buf.at[i]) for i in range(images)]
    mid_in = [local.start(mid_ref.at[i], mid_buf.at[i]) for i in range(images)]
    state_in = [
        local.start(a, b) for a, b in ((rl_ref, rl), (sl_ref, sl), (sr_ref, sr), (ms_ref, ms))
    ]
    rr_in = [local.start(rr_ref.at[0], rr)]
    for slot in range(NBLK):
        block = jnp.clip(slot_blocks[slot] - LATE, 0, EARLY - 1)
        place_ref[slot] = early_ref[block]
    l_ref[:, me_t, me_c, me_z] = late_ref[...]
    for slot in range(slots):
        g_ref[slot, me_t, me_c, me_z] = place_ref[me_c * slots + slot]
    greet(group + c_peers + diagonal)
    moves = Moves(send, recv)
    sent = []

    def go(*args, **kw):
        move = moves.make(*args, **kw)
        move.start()
        sent.append(move)
        return move

    placed = []
    for k in range(1, nc):
        theirs = place_ref.at[pl.ds((me_c ^ k) * slots, slots)]
        placed.append(go(theirs, g_ref.at[:, me_t, me_c, me_z], c_peers[k - 1]))

    swapped = []

    def swap(piece, cond=None):
        swapped.append(go(piece, piece, core, cond=cond, recv_cond=cond))

    def along_fsdp(at):
        own = at(me_z)
        return [
            go(own, own, above, cond=me_z < nz - 1, recv_cond=me_z > 0),
            go(own, own, below, cond=me_z > 0, recv_cond=me_z < nz - 1),
        ]

    def onward(at, last, hop):
        up_z, down_z = me_z - hop, me_z + hop
        last[0].wait_recv()
        up = down = None
        if hop < nz - 1:
            piece = at(up_z)
            cond = jnp.logical_and(me_z < nz - 1, up_z >= 0)
            up = go(piece, piece, above, cond=cond, recv_cond=up_z - 1 >= 0)
        last[1].wait_recv()
        if hop < nz - 1:
            piece = at(down_z)
            cond = jnp.logical_and(me_z > 0, down_z <= nz - 1)
            down = go(piece, piece, below, cond=cond, recv_cond=down_z + 1 <= nz - 1)
        return [up, down], [(up_z, up_z >= 0), (down_z, down_z <= nz - 1)]

    def late_at(member):
        return lambda z: l_ref.at[:, me_t, member, z]

    def slot_at(slot):
        return lambda z: g_ref.at[slot, me_t, :, z]

    late_line = along_fsdp(late_at(me_c))
    tok_in = []

    def send_tok(i):
        there = tok.at[i, :, span(me_c * 384, 384)]
        tok_in.append(
            [local.start(heads_ref.at[i, span(me_c * local_len, local_len)], there)]
            + [
                go(
                    heads_ref.at[i, span((me_c ^ k) * local_len, local_len)],
                    there,
                    c_peers[k - 1],
                )
                for k in range(1, nc)
            ]
        )
    lines = []

    def slot_line(slot):
        lines.append(along_fsdp(slot_at(slot)))

    def late_on(hop):
        nonlocal late_line
        late_line, _ = onward(late_at(me_c), late_line, hop)

    half_rows = D // 2
    for copy in wq_in[1:]:
        local.wait(copy)
    send_tok(0)
    late_on(1)
    for move in placed:
        move.wait_recv()
    slot_line(0)
    late_on(2)
    slot_line(1)
    slot_line(2)
    swap(g_ref.at[:, me_t, :, me_z])
    late_on(3)
    late_own = l_ref.at[:, me_t, me_c]
    near = [go(late_own, late_own, x_near), go(late_own, late_own, y_near)]
    swap(late_own)
    x_rows = wq.at[pl.ds(0, half_rows), span(x_c * width, width)]
    y_rows = wq.at[pl.ds(half_rows, half_rows), span(y_c * width, width)]
    wq_far = [go(x_rows, x_rows, y_near), go(y_rows, y_rows, x_near)]

    part_moves = []
    gain_out[...] = jnp.zeros_like(gain_out)
    square[...] = jnp.zeros_like(square)

    def project(i):
        local.wait(tok_in[i][0])
        for move in tok_in[i][1:]:
            move.wait_recv()
        part[i] = dot_nt(tok[i], wq[...]).astype(BF)
        part_moves.append(go(part.at[i], part_in.at[i], core))

    def norm_backward(i):
        part_moves[i].wait_recv()
        local.wait(x_in[i])
        local.wait(mid_in[i])

        @pl.loop(0, 2)
        def _(step):
            rows = span(step * (local_len // 2), local_len // 2)
            value = x_buf[i, rows]
            centred = value - jnp.mean(value, axis=-1, keepdims=True)
            inv_std = lax.rsqrt(jnp.mean(centred * centred, axis=-1, keepdims=True) + 1e-06)
            normed = centred * inv_std
            grad = part[i, rows].astype(F32) + part_in[i, rows].astype(F32)
            scaled = grad * gain_ref[...]
            inner = (
                scaled
                - jnp.mean(scaled, axis=-1, keepdims=True)
                - normed * jnp.mean(scaled * normed, axis=-1, keepdims=True)
            )
            mid_buf[i, rows] += inner * inv_std
            gain_out[0:1, :] += jnp.sum(grad * normed, axis=0, keepdims=True)

        local.start(mid_buf.at[i], tokens_out.at[i])

    def slots_on(hop):
        for slot in range(slots):
            lines[slot], here = onward(slot_at(slot), lines[slot], hop)
        for z, cond in here:
            swap(g_ref.at[:, me_t, :, z], cond)

    slots_on(1)
    near[0].wait_recv()
    piece = l_ref.at[:, me_t, x_c, :, :, left]
    far = [go(piece, piece, y_near)]
    near[1].wait_recv()
    piece = l_ref.at[:, me_t, y_c, :, :, right]
    far.append(go(piece, piece, x_near))
    swap(l_ref.at[:, me_t, x_c])
    swap(l_ref.at[:, me_t, y_c])
    for i in range(1, images):
        send_tok(i)
    local.wait(wq_in[0])
    for move in wq_far:
        move.wait_recv()
    project(0)
    slots_on(2)
    for i in range(1, images):
        project(i)
    for i in range(images):
        norm_backward(i)
    for move in far:
        move.wait_recv()
    swap(l_ref.at[:, me_t, far_c])
    gain_sum[...] = gains_ref[...]
    gain_sum[0:1, :] = gain_out[0:1, :]
    gain_moves = []
    for k, (z, c) in enumerate(rows_group):
        theirs = span((z * nc + c) // 2 * 128, 128)
        gain_moves.append(
            go(gain_sum.at[:, theirs], gain_in.at[k], {"fsdp": z, "context": c})
        )
    slots_on(3)
    for move in swapped:
        move.wait_recv()
    for copy in state_in:
        local.wait(copy)
    offset = me_t * (D // 2) + me_z * rl.shape[1]
    mine = span(offset, rl.shape[1])
    for slot in range(slots):
        block = slot_blocks[me_c * slots + slot]
        late = l_ref[jnp.clip(block, 0, LATE - 1)]
        g_all[...] = jnp.where(block < LATE, late, g_ref[slot]).reshape(D, D)
        rows = g_all[mine, :]
        grad_out[slot] = rows.astype(F32)
        left_out[slot] = 0.5 * sl[slot] + 0.5 / token_count * dot_nt(rows, g_all[...])
        right_out[slot] = 0.5 * sr[slot] + 0.5 / token_count * dot_tn(g_all[:, mine], g_all[...])
        inner = dot_nn(rl[slot].astype(BF), g_all[...]).astype(BF)
        local.wait(rr_in[slot])
        update[slot] = dot_nn(inner, rr[...].astype(BF))
        if slot + 1 < slots:
            rr_in.append(local.start(rr_ref.at[slot + 1], rr))
        total = jnp.sum(update[slot] * update[slot], axis=0, keepdims=True)
        total = jnp.sum(total, axis=1, keepdims=True)
        square[slot : slot + 1, :] = jnp.broadcast_to(total, (1, 128))
    square_moves = [
        go(square, square_in.at[k], group[k]) for k in range(len(group))
    ]
    for move in square_moves:
        move.wait_recv()
    for slot in range(slots):
        total = square[slot : slot + 1, 0:1]
        for k in range(len(group)):
            total = total + square_in[k, slot : slot + 1, 0:1]
        weight_out[slot] = ms[slot] - lax.rsqrt(total / (D * D) + 1e-06) * update[slot]
    total = gain_sum[:, span((me_z * nc + me_c) // 2 * 128, 128)]
    for k, move in enumerate(gain_moves):
        move.wait_recv()
        total = total + gain_in[k]
    gain_out[:, 0:128] = total
    local.finish()
    for move in sent:
        move.wait_send()


def tail(
    block_of,
    early,
    late,
    grad_heads,
    wq_all,
    tokens,
    grad_middle,
    gain,
    gain_terms,
    root_left,
    root_right,
    stat_left,
    stat_right,
    master,
    token_count,
    nz,
    nc,
    nt,
):
    images, local_len = tokens.shape[:2]
    sub = early.shape[1]
    slots, row_count = root_left.shape[:2]
    any_ = pl.BlockSpec(memory_space=pl.ANY)
    vmem = pl.BlockSpec(memory_space=pltpu.VMEM)
    state = jax.ShapeDtypeStruct((slots, row_count, D), F32)
    shape = (slots, nt, nc, nz, sub, D)
    return pl.pallas_call(
        functools.partial(tail_kernel, nz, nc, token_count),
        out_shape=(
            jax.ShapeDtypeStruct((images, local_len, D), F32),
            jax.ShapeDtypeStruct((8, D), F32),
            state,
            state,
            state,
            state,
        ),
        in_specs=[pl.BlockSpec(memory_space=pltpu.SMEM), vmem, vmem]
        + [any_] * 4
        + [vmem, vmem]
        + [any_] * 5,
        out_specs=(any_, vmem, vmem, vmem, vmem, vmem),
        scratch_shapes=[
            pltpu.VMEM((images, local_len, nc * 384), BF),
            pltpu.VMEM((D, nc * 384), BF),
            pltpu.VMEM((images, local_len, D), F32),
            pltpu.VMEM((images, local_len, D), F32),
            pltpu.VMEM((images, local_len, D), BF),
            pltpu.VMEM((images, local_len, D), BF),
            pltpu.VMEM((slots, row_count, D), F32),
            pltpu.VMEM((D, D), F32),
            pltpu.VMEM((slots, row_count, D), F32),
            pltpu.VMEM((slots, row_count, D), F32),
            pltpu.VMEM((slots, row_count, D), F32),
            pltpu.VMEM((slots, row_count, D), F32),
            pltpu.VMEM((8, 128), F32),
            pltpu.VMEM((2 * nz - 1, 8, 128), F32),
            pltpu.VMEM((8, D), F32),
            pltpu.VMEM((nz * nc - 1, 8, 128), F32),
            pltpu.VMEM((NBLK, sub, D), BF),
            pltpu.VMEM(shape, BF),
            pltpu.VMEM((LATE, nt, nc, nz, sub, D), BF),
            pltpu.VMEM((D, D), BF),
            pltpu.SemaphoreType.DMA((160,)),
            pltpu.SemaphoreType.DMA((160,)),
            pltpu.SemaphoreType.DMA((32,)),
        ],
        compiler_params=pltpu.CompilerParams(
            collective_id=3, has_side_effects=True, vmem_limit_bytes=61 << 20
        ),
        name="tail",
    )(
        block_of,
        early,
        late,
        grad_heads,
        wq_all,
        tokens,
        grad_middle,
        gain,
        gain_terms,
        root_left,
        root_right,
        stat_left,
        stat_right,
        master,
    )


def xor_permute(value, axis, step):
    size = lax.axis_size(axis)
    return lax.ppermute(value, axis, [(j, j ^ step) for j in range(size)])


def xor_order(pieces, index):
    bit = 1
    while bit < len(pieces):
        odd = (index & bit) > 0
        pieces = [jnp.where(odd, pieces[j ^ bit], pieces[j]) for j in range(len(pieces))]
        bit *= 2
    return pieces


def sum_tensor(value):
    low = lax.optimization_barrier(value.astype(BF))
    return low.astype(F32) + xor_permute(low, "tensor", 1).astype(F32)


def gather_fsdp(value):
    size = lax.axis_size("fsdp")
    if size > 4:
        return lax.all_gather(value, "fsdp", axis=0, tiled=False)
    pieces = [value] + [
        lax.ppermute(value, "fsdp", [(j, (j - k) % size) for j in range(size)])
        for k in range(1, size)
    ]
    doubled = jnp.stack(pieces + pieces[:-1])
    start = lax.rem(size - lax.axis_index("fsdp"), size)
    return lax.dynamic_slice_in_dim(doubled, start, size, 0)


def sum_fsdp(value):
    size = lax.axis_size("fsdp")
    if size > 4:
        return lax.psum(value, "fsdp")
    total = value
    for k in range(1, size):
        total = total + lax.ppermute(value, "fsdp", [(j, (j - k) % size) for j in range(size)])
    return total


def grad_gather_plain(block_of, early, late, nz, nc):
    me_c, me_t = (lax.axis_index(a) for a in ("context", "tensor"))
    sub = early.shape[1]
    half_width = nc * nz * sub
    slot_count = NBLK // nc
    slots_of = block_of.reshape(nc, slot_count)

    def slots_for(k):
        blocks = lax.dynamic_index_in_dim(slots_of, me_c ^ k, 0, keepdims=False)
        return early[jnp.clip(blocks - LATE, 0, EARLY - 1)]

    placed = [slots_for(0)] + [xor_permute(slots_for(k), "context", k) for k in range(1, nc)]
    placed = jnp.stack(xor_order(placed, me_c), axis=1)
    placed = lax.all_gather(placed, "fsdp", axis=2, tiled=False)
    placed = placed.reshape(slot_count, half_width, D)
    placed_other = xor_permute(placed, "tensor", 1)
    both = jnp.stack([placed, placed_other], axis=1)
    early_full = jnp.where(me_t > 0, both[:, ::-1], both).reshape(slot_count, D, D)

    late = late.reshape(-1, D)
    late = lax.psum_scatter(late, "fsdp", scatter_dimension=0, tiled=True)
    late = lax.all_gather(late, ("context", "fsdp"), axis=0, tiled=True)
    late = jnp.swapaxes(late.reshape(nc * nz, LATE, sub, D), 0, 1).reshape(LATE, half_width, D)
    late_other = xor_permute(late, "tensor", 1)
    both = jnp.stack([late, late_other], axis=1)
    late_full = jnp.where(me_t > 0, both[:, ::-1], both).reshape(LATE, D, D)

    mine = lax.dynamic_index_in_dim(slots_of, me_c, 0, keepdims=False)
    return jnp.where(
        (mine < LATE)[:, None, None], late_full[jnp.clip(mine, 0, LATE - 1)], early_full
    )


def to_natural(value, me_t, half_len):
    parts = value.reshape((-1, half_len) + value.shape[1:])
    return jnp.where(me_t > 0, parts[::-1], parts).reshape(value.shape)


def forward_plain(tokens, gain, key_mask, w_qkv, w_out, w_up, w_down):
    images, local_len = tokens.shape[:2]
    nc, nt = (lax.axis_size(a) for a in ("context", "tensor"))
    me_c, me_t = (lax.axis_index(a) for a in ("context", "tensor"))
    cols = w_qkv.shape[2] // nc
    half_len = local_len // nt
    wq_part = lax.dynamic_slice_in_dim(w_qkv, me_c * cols, cols, 2)
    wq = gather_fsdp(wq_part).reshape(D, 3 * cols)

    def two_stage(weight, member_axis, fsdp_axis):
        width = weight.shape[member_axis] // nc
        part = lax.dynamic_slice_in_dim(weight, me_c * width, width, member_axis)
        part = lax.all_gather(part, "fsdp", axis=fsdp_axis, tiled=True)
        return lax.all_gather(part, "context", axis=member_axis, tiled=True)

    out_full = two_stage(w_out, 0, 1)
    up_full = two_stage(w_up, 1, 0)
    down_full = two_stage(w_down, 0, 1)

    counts = jnp.sum(key_mask, axis=1)
    real = counts
    for k in range(1, nc):
        real = real + xor_permute(counts, "context", k)
    position = (
        (me_c ^ jnp.arange(nc))[:, None, None] * local_len
        + (me_t ^ jnp.arange(nt))[None, :, None] * half_len
        + jnp.arange(half_len)[None, None, :]
    ).reshape(-1)
    live = position[None, :] < real[:, None]
    bias = jnp.where(live, 0.0, -1e30).astype(F32)
    live_col = jnp.broadcast_to(live[:, :, None].astype(F32), (images, SEQ, 128))

    normed1, inv_std1, pre_norm1 = norm_fwd(tokens, gain)
    normed1_low = pre_norm1.astype(BF)

    x_all, qkv, out_heads, log_sums, attended = [], [], [], [], []
    for i in range(images):
        mine = lax.dynamic_slice_in_dim(normed1_low[i], me_t * half_len, half_len, 0)
        held = jnp.stack([mine] + [xor_permute(mine, "context", k) for k in range(1, nc)])
        other = xor_permute(held, "tensor", 1)
        x_i = jnp.stack([held, other], axis=1).reshape(SEQ, D)
        qkv_i = dot_nn(x_i, wq).astype(BF)
        o_i, lse_i = attn_fwd(qkv_i, bias[i][None])
        chunks = o_i.reshape(nc, local_len, 2 * HD)
        moved = [to_natural(chunks[0], me_t, half_len)] + [
            to_natural(xor_permute(chunks[k], "context", k), me_t, half_len) for k in range(1, nc)
        ]
        attended.append(jnp.concatenate(xor_order(moved, me_c), axis=-1))
        x_all.append(x_i)
        qkv.append(qkv_i)
        out_heads.append(o_i)
        log_sums.append(lse_i)
    attended = jnp.stack(attended)
    return (
        jnp.stack(x_all),
        jnp.stack(qkv),
        jnp.stack(out_heads),
        jnp.stack(log_sums),
        attended,
        live_col,
        wq,
        out_full,
        up_full,
        down_full,
        normed1,
        inv_std1,
    )


def backward_plain(qkv, out_heads, log_sums, grad_att, live_col, early, wq):
    images, local_len = grad_att.shape[:2]
    nz, nc, nt = (lax.axis_size(a) for a in ("fsdp", "context", "tensor"))
    me_c, me_t = (lax.axis_index(a) for a in ("context", "tensor"))
    cols = grad_att.shape[2] // nc
    half_len = local_len // nt
    sub = early.shape[2]
    grad_heads = []
    grad_tok = []
    for i in range(images):
        pieces = [grad_att[i, :, j * cols : (j + 1) * cols] for j in range(nc)]
        pieces = [to_natural(p, me_t, half_len) for p in xor_order(pieces, me_c)]
        grad_i = jnp.concatenate(
            [pieces[0]] + [xor_permute(pieces[k], "context", k) for k in range(1, nc)]
        )
        g_i = attn_bwd(qkv[i], grad_i, out_heads[i], log_sums[i], live_col[i])
        chunks = g_i.reshape(nc, local_len, 3 * cols)
        moved = [to_natural(chunks[0], me_t, half_len)] + [
            to_natural(xor_permute(chunks[k], "context", k), me_t, half_len) for k in range(1, nc)
        ]
        grad_tok.append(jnp.stack(xor_order(moved, me_c), axis=1))
        grad_heads.append(g_i)
    grad_tok = jnp.stack(grad_tok)
    wq_all = lax.all_gather(wq, "context", axis=0, tiled=False)
    grad_n1 = sum_tensor(
        jnp.einsum("isjc,jdc->isd", grad_tok, wq_all, preferred_element_type=F32)
    )
    early = lax.psum_scatter(
        jnp.swapaxes(early, 0, 1).reshape(-1, D),
        "fsdp",
        scatter_dimension=0,
        tiled=True,
    ).reshape(EARLY, sub, D)
    return jnp.stack(grad_heads), grad_n1, early


def per_device(
    tokens,
    cotangent,
    gains,
    w_qkv,
    w_out,
    w_up,
    w_down,
    key_mask,
    owner,
    stat_left,
    stat_right,
    root_left,
    root_right,
    master,
    gain_state,
):
    images, local_len = tokens.shape[:2]
    tok_rows = images * local_len
    nz, nc, nt = (lax.axis_size(a) for a in ("fsdp", "context", "tensor"))
    me_z, me_c, me_t = (lax.axis_index(a) for a in ("fsdp", "context", "tensor"))
    half_width = w_qkv.shape[2]
    hidden = w_up.shape[1]
    up_blocks = hidden // half_width
    cols = half_width // nc
    fast = nz == 4 and nc == 4 and nt == 2 and images == 3
    if fast:
        wq_part = lax.dynamic_slice_in_dim(w_qkv, me_c * cols, cols, 2).reshape(-1, 3 * cols)
        counts = jnp.pad(jnp.sum(key_mask, axis=1), (0, 8 - images))
        counts = jnp.broadcast_to(counts[:, None], (8, 128))
        (
            x_all,
            qkv,
            out_heads,
            log_sums,
            attended,
            counts,
            wq,
            out_full,
            up_full,
            down_part,
        ) = forward_attention(
            tokens, gains[0:1], counts, wq_part, w_out, w_up, w_down, nz, nc
        )
    else:
        (
            x_all,
            qkv,
            out_heads,
            log_sums,
            attended,
            live_col,
            wq,
            out_full,
            up_full,
            down_full,
            normed1,
            inv_std1,
        ) = forward_plain(tokens, gains[0], key_mask, w_qkv, w_out, w_up, w_down)

    sub = half_width // nc // nz
    onehot = (owner[:, None] == jnp.arange(NBLK, dtype=jnp.int32)[None, :]).astype(jnp.int32)
    block_of = jnp.sum(onehot * jnp.arange(NBLK, dtype=jnp.int32)[:, None], axis=0)

    if fast:
        output, grad_middle, grad_att, term_out, term_up, down, down_y, down_x, gain_terms = (
            feed_forward(attended, out_full, up_full, down_part, tokens, cotangent, gains, nc)
        )
        term_out = term_out.reshape(1, nc, nz, sub, D)
        term_up = term_up.reshape(-1, nc, nz, sub, D)
        down = down.reshape(-1, nz, sub, D)
        down_y = down_y.reshape(-1, nz, sub, D // 2)
        down_x = down_x.reshape(-1, nz, sub, D // 2)
    else:
        branch_attn = sum_tensor(
            jnp.einsum("ish,hd->isd", attended, out_full, preferred_element_type=F32)
        )
        middle = tokens + gains[2] * branch_attn
        normed2, inv_std2, pre_norm2 = norm_fwd(middle, gains[1])
        normed2_low = pre_norm2.astype(BF)
        pre_act = jnp.einsum("isd,df->isf", normed2_low, up_full, preferred_element_type=F32)
        act_val, act_slope = gelu_parts(pre_act)
        act_low = act_val.astype(BF)
        branch_mlp = sum_tensor(
            jnp.einsum("isf,fd->isd", act_low, down_full, preferred_element_type=F32)
        )
        output = middle + gains[3] * branch_mlp

        grad_mlp = (gains[3] * cotangent).astype(BF)
        grad_hidden = jnp.einsum("isd,fd->isf", grad_mlp, down_full, preferred_element_type=F32)
        grad_pre = (grad_hidden * act_slope).astype(BF)
        grad_n2 = sum_tensor(
            jnp.einsum("isf,df->isd", grad_pre, up_full, preferred_element_type=F32)
        )
        middle_part, grad_gain2 = norm_back(grad_n2, gains[1], normed2, inv_std2)
        grad_middle = cotangent + middle_part
        grad_branch = (gains[2] * grad_middle).astype(BF)
        grad_att = jnp.einsum(
            "isd,hd->ish", grad_branch, out_full, preferred_element_type=F32
        ).astype(BF)

        def early_term(left, right):
            term = dot_tn(left.reshape(tok_rows, -1), right.reshape(tok_rows, D)).astype(BF)
            return term.reshape(-1, nc, nz, sub, D)

        def early_sum(term):
            return lax.psum_scatter(
                jnp.swapaxes(term, 0, 1).reshape(-1, D), "context", scatter_dimension=0, tiled=True
            ).reshape(-1, nz, sub, D)

        term_out = early_term(attended, grad_branch)
        term_up = early_term(grad_pre, normed2_low)
        down = early_sum(early_term(act_low, grad_mlp))
        grad_gain3 = jnp.sum(grad_middle * branch_attn, axis=(0, 1))
        grad_gain4 = jnp.sum(cotangent * branch_mlp, axis=(0, 1))
        blank = jnp.zeros_like(grad_gain2)
        gain_terms = jnp.stack([blank, grad_gain2, grad_gain3, grad_gain4] + [blank] * 4, axis=0)
    tokens_all = images * nz * SEQ
    if fast:
        early, late, grad_heads, wq_all = backward_attention(
            qkv, out_heads, log_sums, grad_att, counts, term_out, term_up, down, down_y, down_x, x_all, wq, nz, nc
        )
        grad_tokens, gain_sum, grad_mine, left_new, right_new, weight_new = tail(
            block_of,
            early,
            late,
            grad_heads,
            wq_all,
            tokens,
            grad_middle,
            gains[0:1],
            gain_terms,
            root_left[:, 0],
            root_right,
            stat_left[:, 0],
            stat_right[:, 0],
            master[:, 0],
            tokens_all,
            nz,
            nc,
            nt,
        )
    else:
        early = jnp.concatenate([early_sum(term_out), early_sum(term_up), down], axis=0)
        grad_heads, grad_n1, early = backward_plain(
            qkv, out_heads, log_sums, grad_att, live_col, early, wq
        )
        term_qkv = jnp.einsum("isk,isd->kd", grad_heads, x_all, preferred_element_type=F32)
        late = jnp.swapaxes(term_qkv.astype(BF).reshape(LATE, nz, sub, D), 0, 1)
        grad_full = grad_gather_plain(block_of, early, late, nz, nc)
        input_part, grad_gain1 = norm_back(grad_n1, gains[0], normed1, inv_std1)
        grad_tokens = grad_middle + input_part
        row_count = half_width // nz
        row_offset = me_t * half_width + me_z * row_count
        grad_mine = lax.dynamic_slice_in_dim(grad_full, row_offset, row_count, 1)
        left_new = 0.5 * stat_left[:, 0] + 0.5 / tokens_all * jnp.einsum(
            "sra,sba->srb", grad_mine, grad_full, preferred_element_type=F32
        )
        grad_cols = lax.dynamic_slice_in_dim(grad_full, row_offset, row_count, 2)
        right_new = 0.5 * stat_right[:, 0] + 0.5 / tokens_all * jnp.einsum(
            "sar,sab->srb", grad_cols, grad_full, preferred_element_type=F32
        )
        inner_prod = jnp.einsum(
            "sra,sab->srb", root_left[:, 0].astype(BF), grad_full, preferred_element_type=F32
        ).astype(BF)
        update = jnp.einsum(
            "srb,sbc->src", inner_prod, root_right.astype(BF), preferred_element_type=F32
        )
        square_sum = jnp.sum(update * update, axis=(1, 2))
        square_sum = sum_fsdp(square_sum + xor_permute(square_sum, "tensor", 1))
        factor = lax.rsqrt(square_sum / (D * D) + 1e-06)
        weight_new = master[:, 0] - factor[:, None, None] * update

        gain_terms = gain_terms[:4].at[0].set(grad_gain1)
        gain_sum = gain_terms
        step = 1
        while step < nc:
            gain_sum = gain_sum + xor_permute(gain_sum, "context", step)
            step *= 2
        gain_sum = sum_fsdp(gain_sum)

    share_width = gain_state.shape[1]
    gain_index = lax.axis_index(("fsdp", "context"))
    if fast:
        at = lax.rem(gain_index * share_width, 128)
        gain_grad = lax.dynamic_slice(gain_sum, (0, at), (4, share_width))
    else:
        gain_grad = lax.dynamic_slice_in_dim(
            gain_sum, gain_index * share_width, share_width, 1
        )
    gain_mine = lax.dynamic_slice_in_dim(gains, gain_index * share_width, share_width, 1)
    state_new = 0.5 * gain_state + 0.5 * gain_grad * gain_grad / tokens_all
    gain_new = gain_mine - 0.1 * gain_grad * lax.rsqrt(tokens_all * state_new)
    return (
        output,
        grad_tokens,
        grad_mine.astype(F32)[:, None],
        left_new[:, None],
        right_new[:, None],
        weight_new[:, None],
        gain_grad,
        state_new,
        gain_new,
    )


def solution(mesh):
    return jax.shard_map(
        per_device,
        mesh=mesh,
        in_specs=(
            P("fsdp", "context", None),
            P("fsdp", "context", None),
            P(),
            P("fsdp", None, "tensor"),
            P("tensor", "fsdp"),
            P("fsdp", "tensor"),
            P("tensor", "fsdp"),
            P("fsdp", "context"),
            P(),
            P("context", "tensor", "fsdp", None),
            P("context", "tensor", "fsdp", None),
            P("context", "tensor", "fsdp", None),
            P("context", None, None),
            P("context", "tensor", "fsdp", None),
            P(None, ("fsdp", "context")),
        ),
        out_specs=(
            P("fsdp", "context", None),
            P("fsdp", "context", None),
            P("context", "tensor", "fsdp", None),
            P("context", "tensor", "fsdp", None),
            P("context", "tensor", "fsdp", None),
            P("context", "tensor", "fsdp", None),
            P(None, ("fsdp", "context")),
            P(None, ("fsdp", "context")),
            P(None, ("fsdp", "context")),
        ),
        check_vma=False,
    )
```

```python
import functools

import jax
import jax.numpy as jnp
from jax import lax
from jax.experimental import pallas as pl
from jax.experimental.pallas import tpu as pltpu
from jax.sharding import PartitionSpec as P

D = 1024
HD = 64
SEQ = 1408
NBLK = 12
LATE = 3
EARLY = NBLK - LATE
BF = jnp.bfloat16
F32 = jnp.float32
SCALE = HD ** (-0.5)


def norm_fwd(field_in, gain_vec):
    centred = field_in - jnp.mean(field_in, axis=-1, keepdims=True)
    inv_std = lax.rsqrt(jnp.mean(centred * centred, axis=-1, keepdims=True) + 1e-06)
    normed = centred * inv_std
    return (normed, inv_std, normed * gain_vec)


def norm_back(grad_out, gain_vec, normed, inv_std):
    scaled = grad_out * gain_vec
    inner_sum = (
        scaled
        - jnp.mean(scaled, axis=-1, keepdims=True)
        - normed * jnp.mean(scaled * normed, axis=-1, keepdims=True)
    )
    return (inner_sum * inv_std, jnp.sum(grad_out * normed, axis=(0, 1)))


def gelu_parts(field_in):
    normal_cdf = 0.5 * (1.0 + lax.erf(field_in * 0.7071067811865476))
    normal_pdf = jnp.exp(-0.5 * field_in * field_in) * 0.3989422804014327
    return (field_in * normal_cdf, normal_cdf + field_in * normal_pdf)


def dot_nt(a, b):
    return lax.dot_general(a, b, (((1,), (1,)), ((), ())), preferred_element_type=F32)


def dot_tn(a, b):
    return lax.dot_general(a, b, (((0,), (0,)), ((), ())), preferred_element_type=F32)


def dot_nn(a, b):
    return lax.dot_general(a, b, (((1,), (0,)), ((), ())), preferred_element_type=F32)


def attn_fwd_kernel(q_ref, k_ref, v_ref, bias_ref, o_ref, lse_ref):
    q = q_ref[...] * SCALE
    k = k_ref[...]
    v = v_ref[...]
    bias = bias_ref[...]
    first = lax.broadcasted_iota(jnp.int32, q.shape, 1) < HD
    outs, sums = [], []
    for head in range(2):
        mask = first if head == 0 else jnp.logical_not(first)
        scores = dot_nt(jnp.where(mask, q, jnp.zeros_like(q)), k) + bias
        peak = jnp.max(scores, axis=-1, keepdims=True)
        expo = jnp.exp(scores - peak)
        total = jnp.sum(expo, axis=-1, keepdims=True)
        outs.append(dot_nn(expo.astype(BF), v) / total)
        sums.append(peak + jnp.log(total))
    o_ref[...] = jnp.where(first, outs[0], outs[1]).astype(BF)
    lse_ref[...] = jnp.where(first, sums[0], sums[1])


def attn_fwd(qkv, bias_row):
    rows = qkv.shape[0]
    bq = rows // 4
    return pl.pallas_call(
        attn_fwd_kernel,
        grid=(rows // bq,),
        out_shape=(
            jax.ShapeDtypeStruct((rows, 128), BF),
            jax.ShapeDtypeStruct((rows, 128), F32),
        ),
        in_specs=[
            pl.BlockSpec((bq, 128), lambda i: (i, 0)),
            pl.BlockSpec((rows, 128), lambda i: (0, 1)),
            pl.BlockSpec((rows, 128), lambda i: (0, 2)),
            pl.BlockSpec((1, rows), lambda i: (0, 0)),
        ],
        out_specs=(
            pl.BlockSpec((bq, 128), lambda i: (i, 0)),
            pl.BlockSpec((bq, 128), lambda i: (i, 0)),
        ),
        compiler_params=pltpu.CompilerParams(vmem_limit_bytes=40 << 20),
        cost_estimate=pl.CostEstimate(
            flops=4 * rows * rows * 512, bytes_accessed=rows * 2048, transcendentals=2 * rows * rows
        ),
        name="attn_fwd",
    )(qkv, qkv, qkv, bias_row)


def attn_bwd_kernel(q_ref, k_ref, v_ref, do_ref, o_ref, lse_ref, live_ref, out_ref, dq_ref, row_ref):
    step = pl.program_id(0)
    chunk = k_ref.shape[0]

    @pl.when(step == 0)
    def _():
        row_ref[0:128, :] = lse_ref[...].T
        prod = do_ref[...].astype(F32) * o_ref[...].astype(F32)
        prod_t = prod.T
        row_ref[128:136, :] = jnp.broadcast_to(
            jnp.sum(prod_t[0:HD], axis=0, keepdims=True), (8, prod_t.shape[1])
        )
        row_ref[136:144, :] = jnp.broadcast_to(
            jnp.sum(prod_t[HD:128], axis=0, keepdims=True), (8, prod_t.shape[1])
        )
        dq_ref[...] = jnp.zeros_like(dq_ref)

    q = q_ref[...]
    k = k_ref[...] * SCALE
    v = v_ref[...]
    do = do_ref[...]
    live = live_ref[:, 0:1] > 0
    first = lax.broadcasted_iota(jnp.int32, k.shape, 1) < HD
    dks, dvs = [], []
    for head in range(2):
        mask = first if head == 0 else jnp.logical_not(first)
        kh = jnp.where(mask, k, jnp.zeros_like(k))
        vh = jnp.where(mask, v, jnp.zeros_like(v))
        lse = row_ref[64 * head : 64 * head + 1, :]
        delta = row_ref[128 + 8 * head : 129 + 8 * head, :]
        prob = jnp.where(live, jnp.exp(dot_nt(kh, q) - lse), 0.0)
        ds = (prob * (dot_nt(vh, do) - delta)).astype(BF)
        dvs.append(dot_nn(prob.astype(BF), do))
        dks.append(dot_nn(ds, q) * SCALE)
        dq_ref[...] += dot_tn(ds, kh)
    at = pl.ds(pl.multiple_of(step * chunk, chunk), chunk)
    out_ref[at, 128:256] = jnp.where(first, dks[0], dks[1]).astype(BF)
    out_ref[at, 256:384] = jnp.where(first, dvs[0], dvs[1]).astype(BF)

    @pl.when(step == pl.num_programs(0) - 1)
    def _():
        out_ref[:, 0:128] = dq_ref[...].astype(BF)


def attn_bwd(qkv, grad, out, lse, live_col):
    rows = qkv.shape[0]
    chunk = rows // 4
    return pl.pallas_call(
        attn_bwd_kernel,
        grid=(rows // chunk,),
        out_shape=jax.ShapeDtypeStruct((rows, 384), BF),
        in_specs=[
            pl.BlockSpec((rows, 128), lambda i: (0, 0)),
            pl.BlockSpec((chunk, 128), lambda i: (i, 1)),
            pl.BlockSpec((chunk, 128), lambda i: (i, 2)),
            pl.BlockSpec((rows, 128), lambda i: (0, 0)),
            pl.BlockSpec((rows, 128), lambda i: (0, 0)),
            pl.BlockSpec((rows, 128), lambda i: (0, 0)),
            pl.BlockSpec((chunk, 128), lambda i: (i, 0)),
        ],
        out_specs=pl.BlockSpec((rows, 384), lambda i: (0, 0)),
        scratch_shapes=[pltpu.VMEM((rows, 128), F32), pltpu.VMEM((144, rows), F32)],
        compiler_params=pltpu.CompilerParams(vmem_limit_bytes=50 << 20),
        cost_estimate=pl.CostEstimate(
            flops=10 * rows * rows * 512, bytes_accessed=rows * 4096, transcendentals=2 * rows * rows
        ),
        name="attn_bwd",
    )(qkv, qkv, qkv, grad, out, lse, live_col)


class Moves:
    def __init__(self, send_sems, recv_sems):
        self.send_sems, self.recv_sems, self.count = send_sems, recv_sems, 0

    def make(self, src, dst, device, cond=None, recv_cond=None):
        index = self.count
        self.count += 1
        return Move(self, index, src, dst, device, cond, recv_cond)


class Move:
    def __init__(self, moves, index, src, dst, device, cond, recv_cond):
        self.args = (src, dst, moves.send_sems.at[index], moves.recv_sems.at[index])
        self.device, self.cond, self.recv_cond = device, cond, recv_cond

    def copy(self):
        return pltpu.make_async_remote_copy(
            *self.args, device_id=self.device, device_id_type=pl.DeviceIdType.MESH
        )

    def when(self, cond, act):
        if cond is None:
            act()
        else:
            pl.when(cond)(act)

    def start(self):
        self.when(self.cond, lambda: self.copy().start())

    def wait_recv(self):
        self.when(self.recv_cond, lambda: self.copy().wait_recv())

    def wait_send(self):
        self.when(self.cond, lambda: self.copy().wait_send())


def greet(devices):
    barrier = pltpu.get_barrier_semaphore()
    for device in devices:
        pl.semaphore_signal(
            barrier, inc=1, device_id=device, device_id_type=pl.DeviceIdType.MESH
        )
    pl.semaphore_wait(barrier, len(devices))


def span(start, size):
    return pl.ds(pl.multiple_of(start, size & -size), size)


class Local:
    def __init__(self, sems):
        self.sems, self.count, self.open = sems, 0, []

    def start(self, src, dst):
        copy = pltpu.make_async_copy(src, dst, self.sems.at[self.count])
        self.count += 1
        copy.start()
        self.open.append(copy)
        return copy

    def wait(self, copy):
        copy.wait()
        self.open = [c for c in self.open if c is not copy]

    def finish(self):
        for copy in self.open:
            copy.wait()
        self.open = []


def spread_plane(go, ref_of, me_c, cond=None):
    own = ref_of(me_c, None)
    return [go(own, own, {"context": me_c ^ 1}), go(own, own, {"context": me_c ^ 2})]


def spread_plane_on(go, ref_of, me_c, near):
    near[0].wait_recv()
    piece = ref_of(me_c ^ 1, 0)
    first = go(piece, piece, {"context": me_c ^ 2})
    near[1].wait_recv()
    piece = ref_of(me_c ^ 2, 1)
    second = go(piece, piece, {"context": me_c ^ 1})
    return [first, second]


def forward_kernel(
    nz,
    nc,
    tokens_ref,
    gain_ref,
    count_ref,
    wq_ref,
    wout_ref,
    wup_ref,
    wdown_ref,
    x_out,
    qkv_out,
    o_out,
    lse_out,
    att_out,
    cnt_out,
    wq_out,
    out_full,
    up_full,
    down_part,
    tok,
    x_all,
    qkv,
    o_all,
    lse_all,
    wq,
    counts,
    send,
    recv,
    local_sems,
):
    me_z, me_c, me_t = (lax.axis_index(a) for a in ("fsdp", "context", "tensor"))
    images, local_len = att_out.shape[:2]
    half = local_len // 2
    seq = x_all.shape[1]
    core = {"tensor": 1 - me_t}
    z_peers = [{"fsdp": lax.rem(me_z + k, nz)} for k in range(1, nz)]
    c_peers = [{"context": me_c ^ k} for k in range(1, nc)]
    local = Local(local_sems)
    token_in = [
        local.start(tokens_ref.at[i, span(me_t * half, half)], tok.at[i]) for i in range(images)
    ]
    depth = wq_ref.shape[0]
    wq_part = wq_ref.at[:, span(me_c * 384, 384)]
    wq_own = local.start(wq_part, wq.at[span(me_z * depth, depth)])
    greet(z_peers + c_peers + [core])
    moves = Moves(send, recv)
    sent = []

    def go(*args, **kw):
        move = moves.make(*args, **kw)
        move.start()
        sent.append(move)
        return move

    wq_in = [go(wq_part, wq.at[span(me_z * depth, depth)], peer) for peer in z_peers]
    counts[me_c] = count_ref[...]
    count_in = [go(count_ref, counts.at[me_c], peer) for peer in c_peers]

    def to_line(src, dst):
        local_copy = local.start(src, dst)
        return [local_copy] + [go(src, dst, peer) for peer in z_peers]

    hid, depth_o = wup_ref.shape[1] // nc, wout_ref.shape[1]

    def x_piece(i):
        def at(member, part):
            rows = span(member * local_len + me_t * half, half)
            if part is None:
                return x_all.at[i, rows]
            return x_all.at[i, rows, pl.ds(part * (D // 2), D // 2)]

        return at

    swaps = [[] for _ in range(images)]
    near, far = [], []

    def swap(i, member, part=None):
        piece = x_piece(i)(member, part)
        swaps[i].append(go(piece, piece, core))

    def normalize(i):
        local.wait(token_in[i])
        value = tok[i]
        centred = value - jnp.mean(value, axis=-1, keepdims=True)
        inv_std = lax.rsqrt(jnp.mean(centred * centred, axis=-1, keepdims=True) + 1e-06)
        x_all[i, span(me_c * local_len + me_t * half, half)] = (
            centred * inv_std * gain_ref[...]
        ).astype(BF)

    def send_near(i):
        near.append(spread_plane(go, x_piece(i), me_c))
        swap(i, me_c)

    def send_far(i):
        far.append(spread_plane_on(go, x_piece(i), me_c, near[i]))
        swap(i, me_c ^ 1)
        swap(i, me_c ^ 2)

    normalize(0)
    send_near(0)
    normalize(1)
    send_near(1)
    normalize(2)
    send_far(0)
    send_near(2)
    local.wait(wq_own)
    for move in wq_in:
        move.wait_recv()
    up_in = to_line(
        wup_ref.at[:, span(me_c * hid, hid)],
        up_full.at[span(me_z * depth, depth), span(me_c * hid, hid)],
    )
    out_in = to_line(wout_ref, out_full.at[:, span(me_z * depth_o, depth_o)])
    local.start(wq, wq_out)
    for move in count_in:
        move.wait_recv()
    total = counts[0]
    for k in range(1, nc):
        total = total + counts[k]
    cnt_out[...] = total

    first = lax.broadcasted_iota(jnp.int32, (local_len, 128), 1) < HD
    place = lax.broadcasted_iota(jnp.int32, (1, seq), 1)

    def up_piece(k):
        start = lax.rem(me_z - k + nz, nz) * depth

        def at(member, part):
            columns = span(member * hid, hid)
            if part is None:
                return up_full.at[span(start, depth), columns]
            return up_full.at[span(start + part * (depth // 2), depth // 2), columns]

        return at

    up_near, up_far = [], []

    def up_step(k):
        if k == 0:
            local.wait(up_in[0])
        else:
            up_in[k].wait_recv()
        up_near.append(spread_plane(go, up_piece(k), me_c))

    def up_step_on(k):
        up_far.extend(spread_plane_on(go, up_piece(k), me_c, up_near[k]))

    att_in = []
    for i in range(images):
        for part in range(2):
            far[i][part].wait_recv()
            swap(i, me_c ^ 3, part)
        for move in swaps[i]:
            move.wait_recv()
        local.start(x_all.at[i], x_out.at[i])

        @pl.loop(0, nc)
        def _(chunk):
            rows = span(chunk * local_len, local_len)
            qkv[i, rows] = dot_nn(x_all[i, rows], wq[...]).astype(BF)

        local.start(qkv.at[i], qkv_out.at[i])
        if i == 0:
            send_far(1)
        bias = jnp.where(place < cnt_out[i : i + 1, 0:1], 0.0, -1e30)
        def attend(chunk):
            rows = span(chunk * local_len, local_len)
            q = qkv[i, rows, 0:128] * SCALE
            k = qkv[i, :, 128:256]
            v = qkv[i, :, 256:384]
            outs, sums = [], []
            for head in range(2):
                mask = first if head == 0 else jnp.logical_not(first)
                scores = dot_nt(jnp.where(mask, q, jnp.zeros_like(q)), k) + bias
                peak = jnp.max(scores, axis=-1, keepdims=True)
                expo = jnp.exp(scores - peak)
                norm = jnp.sum(expo, axis=-1, keepdims=True)
                outs.append(dot_nn(expo.astype(BF), v) / norm)
                sums.append(peak + jnp.log(norm))
            o_all[i, rows] = jnp.where(first, outs[0], outs[1]).astype(BF)
            lse_all[rows] = jnp.where(first, sums[0], sums[1])

        pl.loop(0, nc // 2)(attend)
        if i == 0:
            send_far(2)
            up_step(0)
        if i == 1:
            up_step(2)
        if i == 2:
            up_step_on(0)
            up_step_on(1)
        pl.loop(nc // 2, nc)(attend)

        mine = att_out.at[i, :, span(me_c * 128, 128)]
        for k in range(1, nc):
            att_in.append(
                go(o_all.at[i, span((me_c ^ k) * local_len, local_len)], mine, c_peers[k - 1])
            )
        local.start(o_all.at[i, span(me_c * local_len, local_len)], mine)
        local.start(o_all.at[i], o_out.at[i])
        sums_t = lse_all[...].T
        for head in range(2):
            lse_out[i, 8 * head : 8 * head + 8, :] = jnp.broadcast_to(
                sums_t[HD * head : HD * head + 1], (8, seq)
            )
        if i == 0:
            up_step(1)
        if i == 1:
            up_step(3)
            down_in = to_line(
                wdown_ref.at[span(me_c * hid, hid)],
                down_part.at[:, span(me_z * depth_o, depth_o)],
            )
    up_step_on(2)
    up_step_on(3)
    for move in up_far:
        move.wait_recv()
    for move in att_in:
        move.wait_recv()
    for move in out_in[1:] + down_in[1:]:
        move.wait_recv()
    local.finish()
    for move in sent:
        move.wait_send()


def forward_attention(tokens, gain, counts, wq_part, w_out, w_up, w_down, nz, nc):
    images, local_len = tokens.shape[:2]
    seq = nc * local_len
    cols, hid = w_out.shape[0], w_up.shape[1]
    any_ = pl.BlockSpec(memory_space=pl.ANY)
    vmem = pl.BlockSpec(memory_space=pltpu.VMEM)
    return pl.pallas_call(
        functools.partial(forward_kernel, nz, nc),
        out_shape=(
            jax.ShapeDtypeStruct((images, seq, D), BF),
            jax.ShapeDtypeStruct((images, seq, 384), BF),
            jax.ShapeDtypeStruct((images, seq, 128), BF),
            jax.ShapeDtypeStruct((images, 16, seq), F32),
            jax.ShapeDtypeStruct((images, local_len, cols), BF),
            jax.ShapeDtypeStruct((8, 128), jnp.int32),
            jax.ShapeDtypeStruct((D, 384), BF),
            jax.ShapeDtypeStruct((cols, D), BF),
            jax.ShapeDtypeStruct((D, hid), BF),
            jax.ShapeDtypeStruct((hid // nc, D), BF),
        ),
        in_specs=[any_, vmem, vmem, any_, any_, any_, any_],
        out_specs=(any_, any_, any_, vmem, any_, vmem, any_, any_, any_, any_),
        scratch_shapes=[
            pltpu.VMEM((images, local_len // 2, D), F32),
            pltpu.VMEM((images, seq, D), BF),
            pltpu.VMEM((images, seq, 384), BF),
            pltpu.VMEM((images, seq, 128), BF),
            pltpu.VMEM((seq, 128), F32),
            pltpu.VMEM((D, 384), BF),
            pltpu.VMEM((nc, 8, 128), jnp.int32),
            pltpu.SemaphoreType.DMA((96,)),
            pltpu.SemaphoreType.DMA((96,)),
            pltpu.SemaphoreType.DMA((32,)),
        ],
        compiler_params=pltpu.CompilerParams(
            collective_id=1, has_side_effects=True, vmem_limit_bytes=56 << 20
        ),
        name="forward_attention",
    )(tokens, gain, counts, wq_part, w_out, w_up, w_down)


def feed_forward_kernel(
    nz,
    nc,
    att_ref,
    wout_ref,
    wup_ref,
    wdown_ref,
    tokens_ref,
    cot_ref,
    gains_ref,
    wq_ref,
    output_out,
    mid_out,
    gatt_out,
    tout_out,
    tup_out,
    own_out,
    fary_out,
    farx_out,
    wq_out,
    gain_out,
    att,
    wout,
    wup,
    wdown,
    tok,
    cot,
    normed_low,
    act,
    slope,
    low,
    first_own,
    first_in,
    second_own,
    second_in,
    third_in,
    stage,
    term,
    near_in,
    gatt,
    send,
    recv,
    local_sems,
):
    me_z, me_c, me_t = (lax.axis_index(a) for a in ("fsdp", "context", "tensor"))
    z_peers = [{"fsdp": lax.rem(me_z + k, nz)} for k in range(1, nz)]
    images, local_len = tok.shape[:2]
    hid = wdown_ref.shape[0]
    x_c, y_c, far_c = me_c ^ 1, me_c ^ 2, me_c ^ 3
    core, x_near, y_near = {"tensor": 1 - me_t}, {"context": x_c}, {"context": y_c}
    left, right = pl.ds(0, D // 2), pl.ds(D // 2, D // 2)
    half = local_len // 2
    local = Local(local_sems)
    att_in = [local.start(att_ref, att), local.start(wout_ref, wout)]
    cot_in = local.start(cot_ref, cot)
    tok_in = local.start(tokens_ref, tok)
    up_in = local.start(wup_ref, wup)

    def down_piece(member, part):
        rows = span(member * hid, hid)
        return wdown.at[rows] if part is None else wdown.at[rows, pl.ds(part * (D // 2), D // 2)]

    down_own = local.start(wdown_ref, down_piece(me_c, None))
    greet([core, x_near, y_near] + z_peers)
    moves = Moves(send, recv)
    sent = []

    def go(*args, **kw):
        move = moves.make(*args, **kw)
        move.start()
        sent.append(move)
        return move

    down_near = [
        go(wdown_ref.at[:, columns], down_piece(me_c, part), device)
        for part, columns, device in (
            (0, left, x_near),
            (1, right, y_near),
            (1, right, x_near),
            (0, left, y_near),
        )
    ]
    depth = wq_ref.shape[0]
    wq_in = []
    for k in range(1, nc):
        columns = span((me_c ^ k) * 384, 384)
        there = wq_out.at[span(me_z * depth, depth), columns]
        local.start(wq_ref.at[:, columns], there)
        wq_in += [go(wq_ref.at[:, columns], there, peer) for peer in z_peers]
    for copy in att_in:
        local.wait(copy)

    @pl.loop(0, images)
    def _(i):
        first_own[i] = dot_nn(att[i], wout[...]).astype(BF)

    first = go(first_own, first_in, core)
    local.wait(cot_in)

    @pl.loop(0, images)
    def _(i):
        low[i] = (gains_ref[3:4, :] * cot[i]).astype(BF)

    local.wait(tok_in)
    first.wait_recv()

    @pl.loop(0, 2 * images)
    def _(step):
        i, rows = step // 2, span(lax.rem(step, 2) * half, half)
        branch = first_own[i, rows].astype(F32) + first_in[i, rows].astype(F32)
        value = tok[i, rows] + gains_ref[2:3, :] * branch
        tok[i, rows] = value
        centred = value - jnp.mean(value, axis=-1, keepdims=True)
        inv_std = lax.rsqrt(jnp.mean(centred * centred, axis=-1, keepdims=True) + 1e-06)
        normed_low[i, rows] = (centred * inv_std * gains_ref[1:2, :]).astype(BF)

    local.wait(up_in)
    width = 512

    @pl.loop(0, images)
    def _(i):
        @pl.loop(0, wup.shape[1] // width)
        def _(step):
            cols = span(step * width, width)
            value = dot_nn(normed_low[i], wup[:, cols])
            cdf = 0.5 * (1.0 + lax.erf(value * 0.7071067811865476))
            pdf = jnp.exp(-0.5 * value * value) * 0.3989422804014327
            act[i, :, cols] = (value * cdf).astype(BF)
            slope[i, :, cols] = (cdf + value * pdf).astype(BF)

    down_near[0].wait_recv()
    x_piece = down_piece(x_c, 0)
    down_far = [go(x_piece, x_piece, y_near)]
    down_near[1].wait_recv()
    y_piece = down_piece(y_c, 1)
    down_far.append(go(y_piece, y_piece, x_near))
    blocks = term.shape[0]
    chunk_rows = term.shape[2]

    @pl.loop(0, blocks)
    def _(j):
        cols = span(j * width, width)
        total = jnp.zeros((width, D), F32)
        for i in range(images):
            total += dot_tn(act[i, :, cols], low[i])
        for c in range(nc):
            term[j, c] = total[c * chunk_rows : (c + 1) * chunk_rows].astype(BF)

    near = [
        go(term.at[:, x_c, :, left], near_in.at[0], x_near),
        go(term.at[:, far_c, :, left], near_in.at[1], x_near),
        go(term.at[:, y_c, :, right], near_in.at[2], y_near),
        go(term.at[:, far_c, :, right], near_in.at[3], y_near),
    ]
    local.wait(down_own)
    for move in down_near[2:]:
        move.wait_recv()

    def back_down(member):
        columns = span(member * hid, hid)

        @pl.loop(0, images)
        def _(i):
            value = dot_nt(low[i], wdown[columns, :]) * slope[i, :, columns].astype(F32)
            slope[i, :, columns] = value.astype(BF)

    @pl.loop(0, 3)
    def _(k):
        back_down(me_c ^ k)

    for move in down_far:
        move.wait_recv()
    back_down(far_c)

    @pl.loop(0, images)
    def _(i):
        second_own[i] = dot_nn(act[i], wdown[...]).astype(BF)

    second = go(second_own, second_in, core)
    first.wait_send()
    sent.remove(first)
    gain_out[...] = jnp.zeros_like(gain_out)

    @pl.loop(0, 2 * images)
    def _(step):
        i, rows = step // 2, span(lax.rem(step, 2) * half, half)
        branch = first_own[i, rows].astype(F32) + first_in[i, rows].astype(F32)
        first_in[i, rows] = branch.astype(BF)

    @pl.loop(0, images)
    def _(i):
        first_own[i] = dot_nt(slope[i], wup[...]).astype(BF)

    third = go(first_own, third_in, core)

    def up_term(j, at):
        cols = span(j * width, width)
        total = jnp.zeros((width, D), F32)
        for i in range(images):
            total += dot_tn(slope[i, :, cols], normed_low[i])
        stage[at] = total.astype(BF)

    copies = []
    for j in range(blocks):
        if j >= 2:
            local.wait(copies[j - 2])
        up_term(j, j % 2)
        copies.append(local.start(stage.at[j % 2], tup_out.at[pl.ds(j * width, width)]))
    second.wait_recv()
    third.wait_recv()

    @pl.loop(0, 2 * images)
    def _(step):
        i, rows = step // 2, span(lax.rem(step, 2) * half, half)
        value = tok[i, rows]
        centred = value - jnp.mean(value, axis=-1, keepdims=True)
        inv_std = lax.rsqrt(jnp.mean(centred * centred, axis=-1, keepdims=True) + 1e-06)
        normed = centred * inv_std
        branch = second_own[i, rows].astype(F32) + second_in[i, rows].astype(F32)
        tok[i, rows] = value + gains_ref[3:4, :] * branch
        cotangent = cot[i, rows]
        gain_out[3:4, :] += jnp.sum(cotangent * branch, axis=0, keepdims=True)
        grad = first_own[i, rows].astype(F32) + third_in[i, rows].astype(F32)
        gain_out[1:2, :] += jnp.sum(grad * normed, axis=0, keepdims=True)
        scaled = grad * gains_ref[1:2, :]
        inner = (
            scaled
            - jnp.mean(scaled, axis=-1, keepdims=True)
            - normed * jnp.mean(scaled * normed, axis=-1, keepdims=True)
        )
        grad = cotangent + inner * inv_std
        cot[i, rows] = grad
        gain_out[2:3, :] += jnp.sum(grad * first_in[i, rows].astype(F32), axis=0, keepdims=True)
        low[i, rows] = (gains_ref[2:3, :] * grad).astype(BF)

    local.start(tok, output_out)
    local.start(cot, mid_out)

    @pl.loop(0, images)
    def _(i):
        gatt[i] = dot_nt(low[i], wout[...]).astype(BF)

    local.start(gatt, gatt_out)
    total = jnp.zeros((att.shape[2], D), F32)
    for i in range(images):
        total += dot_tn(att[i], low[i])
    for copy in copies[-2:]:
        local.wait(copy)
    stage[0] = total.astype(BF)
    local.start(stage.at[0], tout_out)
    for move in near:
        move.wait_recv()
    for move in near:
        move.wait_send()
        sent.remove(move)
    term[:, me_c, :, left] += near_in[0]
    term[:, me_c, :, right] += near_in[2]
    term[:, y_c, :, left] += near_in[1]
    term[:, x_c, :, right] += near_in[3]
    for move in wq_in:
        move.wait_recv()
    local.start(term.at[:, me_c], own_out)
    local.start(term.at[:, y_c, :, left], fary_out)
    local.start(term.at[:, x_c, :, right], farx_out)
    local.finish()
    for move in sent:
        move.wait_send()


def feed_forward(attended, out_full, up_full, down_part, tokens, cotangent, gains, wq_rows, nz, nc):
    images, local_len = tokens.shape[:2]
    cols, hid = out_full.shape[0], up_full.shape[1]
    blocks = hid // 512
    piece = (blocks, 512 // nc)
    any_ = pl.BlockSpec(memory_space=pl.ANY)
    vmem = pl.BlockSpec(memory_space=pltpu.VMEM)
    rows = (images, local_len)
    return pl.pallas_call(
        functools.partial(feed_forward_kernel, nz, nc),
        out_shape=(
            jax.ShapeDtypeStruct(rows + (D,), F32),
            jax.ShapeDtypeStruct(rows + (D,), F32),
            jax.ShapeDtypeStruct(rows + (cols,), BF),
            jax.ShapeDtypeStruct((cols, D), BF),
            jax.ShapeDtypeStruct((hid, D), BF),
            jax.ShapeDtypeStruct(piece + (D,), BF),
            jax.ShapeDtypeStruct(piece + (D // 2,), BF),
            jax.ShapeDtypeStruct(piece + (D // 2,), BF),
            jax.ShapeDtypeStruct((D, nc * 384), BF),
            jax.ShapeDtypeStruct((8, D), F32),
        ),
        in_specs=[any_] * 6 + [vmem, any_],
        out_specs=(any_,) * 9 + (vmem,),
        scratch_shapes=[
            pltpu.VMEM(rows + (cols,), BF),
            pltpu.VMEM((cols, D), BF),
            pltpu.VMEM((D, hid), BF),
            pltpu.VMEM((hid, D), BF),
            pltpu.VMEM(rows + (D,), F32),
            pltpu.VMEM(rows + (D,), F32),
            pltpu.VMEM(rows + (D,), BF),
            pltpu.VMEM(rows + (hid,), BF),
            pltpu.VMEM(rows + (hid,), BF),
            pltpu.VMEM(rows + (D,), BF),
            pltpu.VMEM(rows + (D,), BF),
            pltpu.VMEM(rows + (D,), BF),
            pltpu.VMEM(rows + (D,), BF),
            pltpu.VMEM(rows + (D,), BF),
            pltpu.VMEM(rows + (D,), BF),
            pltpu.VMEM((2, 512, D), BF),
            pltpu.VMEM((blocks, nc, 512 // nc, D), BF),
            pltpu.VMEM((4, blocks, 512 // nc, D // 2), BF),
            pltpu.VMEM(rows + (cols,), BF),
            pltpu.SemaphoreType.DMA((32,)),
            pltpu.SemaphoreType.DMA((32,)),
            pltpu.SemaphoreType.DMA((24,)),
        ],
        compiler_params=pltpu.CompilerParams(
            collective_id=4, has_side_effects=True, vmem_limit_bytes=62 << 20
        ),
        name="feed_forward",
    )(attended, out_full, up_full, down_part, tokens, cotangent, gains, wq_rows)


def backward_kernel(
    nz,
    nc,
    qkv_ref,
    o_ref,
    lse_ref,
    att_ref,
    cnt_ref,
    term_out_ref,
    term_up_ref,
    down_ref,
    down_y_ref,
    down_x_ref,
    x_ref,
    early_ref,
    late_out,
    heads_out,
    grad,
    heads,
    qkv,
    o_all,
    x_all,
    dq_ref,
    row_ref,
    weight_ref,
    own_ref,
    far_y,
    far_x,
    near_in,
    far_in,
    mine_ref,
    mine_in_ref,
    zpart_ref,
    zsend_ref,
    znext_ref,
    late_ref,
    lpart_ref,
    lsend_ref,
    lnext_ref,
    send,
    recv,
    local_sems,
):
    me_z, me_c, me_t = (lax.axis_index(a) for a in ("fsdp", "context", "tensor"))
    images, local_len = att_ref.shape[:2]
    x_c, y_c, far_c = me_c ^ 1, me_c ^ 2, me_c ^ 3
    x_near, y_near = {"context": x_c}, {"context": y_c}
    z_peers = [{"fsdp": lax.rem(me_z + k, nz)} for k in range(1, nz)]
    c_peers = [{"context": me_c ^ k} for k in range(1, nc)]
    left, right = pl.ds(0, D // 2), pl.ds(D // 2, D // 2)
    ups, downs = term_up_ref.shape[0], down_ref.shape[0]
    terms = [(term_out_ref, 0)] + [(term_up_ref, j) for j in range(ups)]
    local = Local(local_sems)
    held = [
        [local.start(a.at[i], b.at[i]) for a, b in ((qkv_ref, qkv), (o_ref, o_all))]
        for i in range(images)
    ]
    x_in = [local.start(x_ref.at[i], x_all.at[i % 2]) for i in range(2)]
    own_in, far_own = [], []
    for index, (ref, block) in enumerate(terms):
        own_in.append(local.start(ref.at[block, me_c], own_ref.at[index]))
        far_own.append(local.start(ref.at[block, y_c, :, :, left], far_y.at[index]))
        far_own.append(local.start(ref.at[block, x_c, :, :, right], far_x.at[index]))
    mine_in = local.start(down_ref, mine_ref)
    greet(z_peers + c_peers)
    moves = Moves(send, recv)
    sent = []

    def go(*args, **kw):
        move = moves.make(*args, **kw)
        move.start()
        sent.append(move)
        return move

    grad_in = []

    def send_grad(i):
        here = grad.at[i, span(me_c * local_len, local_len)]
        grad_in.append(
            [local.start(att_ref.at[i, :, span(me_c * 128, 128)], here)]
            + [
                go(att_ref.at[i, :, span((me_c ^ k) * 128, 128)], here, c_peers[k - 1])
                for k in range(1, nc)
            ]
        )

    near = []

    def send_term(index):
        ref, block = terms[index]
        near.append(
            [
                go(ref.at[block, x_c, :, :, left], near_in.at[index, 0], x_near),
                go(ref.at[block, far_c, :, :, left], near_in.at[index, 1], x_near),
                go(ref.at[block, y_c, :, :, right], near_in.at[index, 2], y_near),
                go(ref.at[block, far_c, :, :, right], near_in.at[index, 3], y_near),
            ]
        )

    send_grad(0)
    send_term(0)
    send_term(1)
    send_grad(1)
    send_grad(2)
    down_far = [
        go(down_y_ref, mine_in_ref.at[0], y_near),
        go(down_x_ref, mine_in_ref.at[1], x_near),
    ]
    send_term(2)
    z_pair, z_next = {"fsdp": me_z ^ 1}, {"fsdp": me_z ^ 2}

    def halve(ref, low, count, at):
        blocks = pl.ds(low, count)
        return [
            go(ref.at[blocks, me_z ^ 1], zpart_ref.at[0, pl.ds(at, count)], z_pair),
            go(ref.at[blocks, me_z ^ 3], zpart_ref.at[1, pl.ds(at, count)], z_pair),
        ]

    def halve_on(moves_in, own, count, at):
        for move in moves_in:
            move.wait_recv()
        for block in range(count):
            zsend_ref[at + block] = own(block) + zpart_ref[1, at + block]
        blocks = pl.ds(at, count)
        return go(zsend_ref.at[blocks], znext_ref.at[blocks], z_next)

    first = lax.broadcasted_iota(jnp.int32, (local_len, 128), 1) < HD
    place = lax.broadcasted_iota(jnp.int32, (local_len, 128), 0)
    weight_ref[...] = jnp.zeros_like(weight_ref)
    far_moves = []

    def sum_step(index):
        for move in near[index]:
            move.wait_recv()
        local.wait(own_in[index])
        local.wait(far_own[2 * index])
        local.wait(far_own[2 * index + 1])
        far_y[index] += near_in[index, 1]
        first_far = go(far_y.at[index], far_in.at[index, 0], y_near)
        far_x[index] += near_in[index, 3]
        far_moves.append((first_far, go(far_x.at[index], far_in.at[index, 1], x_near)))

    def sum_end(index):
        for move in far_moves[index]:
            move.wait_recv()
        own_ref[index, :, :, left] += near_in[index, 0] + far_in[index, 0]
        own_ref[index, :, :, right] += near_in[index, 2] + far_in[index, 1]

    for i in range(images):
        for copy in held[i]:
            local.wait(copy)
        local.wait(grad_in[i][0])
        for move in grad_in[i][1:]:
            move.wait_recv()
        prod = (grad[i].astype(F32) * o_all[i].astype(F32)).T
        for head in range(2):
            row_ref[8 * head : 8 * head + 8, :] = jnp.broadcast_to(
                jnp.sum(prod[HD * head : HD * (head + 1)], axis=0, keepdims=True),
                (8, prod.shape[1]),
            )
        dq_ref[...] = jnp.zeros_like(dq_ref)
        real = cnt_ref[i : i + 1, :]

        def attend(chunk):
            rows = span(chunk * local_len, local_len)
            q = qkv[i, :, 0:128]
            k = qkv[i, rows, 128:256] * SCALE
            v = qkv[i, rows, 256:384]
            do = grad[i]
            live = (place + chunk * local_len < real)[:, 0:1]
            dks, dvs = [], []
            for head in range(2):
                mask = first if head == 0 else jnp.logical_not(first)
                kh = jnp.where(mask, k, jnp.zeros_like(k))
                vh = jnp.where(mask, v, jnp.zeros_like(v))
                lse = lse_ref[i, 8 * head : 8 * head + 1, :]
                delta = row_ref[8 * head : 8 * head + 1, :]
                prob = jnp.where(live, jnp.exp(dot_nt(kh, q) - lse), 0.0)
                ds = (prob * (dot_nt(vh, do) - delta)).astype(BF)
                dvs.append(dot_nn(prob.astype(BF), do))
                dks.append(dot_nn(ds, q) * SCALE)
                dq_ref[...] += dot_tn(ds, kh)
            heads[i, rows, 128:256] = jnp.where(first, dks[0], dks[1]).astype(BF)
            heads[i, rows, 256:384] = jnp.where(first, dvs[0], dvs[1]).astype(BF)

        pl.loop(0, nc // 2)(attend)
        if i == 2:
            sum_step(2)
            sum_end(0)
            sum_end(1)
            group_a = halve(own_ref, 0, 2, 0)
        pl.loop(nc // 2, nc)(attend)
        heads[i, :, 0:128] = dq_ref[...].astype(BF)
        if i == 0:
            sum_step(0)
            sum_step(1)
            send_term(3)
        if i == 1:
            send_term(4)
            local.wait(mine_in)
            for move in down_far:
                move.wait_recv()
            mine_ref[:, :, :, left] += mine_in_ref[0]
            mine_ref[:, :, :, right] += mine_in_ref[1]
            down_in = halve(mine_ref, 0, downs, len(terms))
        if i == 2:
            sum_step(3)
            down_next = halve_on(down_in, lambda b: mine_ref[b, me_z ^ 2], downs, len(terms))
            sum_step(4)
        local.wait(x_in[i])

        @pl.loop(0, nc)
        def _(chunk):
            rows = span(chunk * local_len, local_len)
            weight_ref[...] += dot_tn(heads[i, rows], x_all[i % 2, rows])

        local.start(heads.at[i], heads_out.at[i])
        if i + 2 < images:
            x_in.append(local.start(x_ref.at[i + 2], x_all.at[i % 2]))
    sub = late_ref.shape[2]
    for z in range(nz):
        for j in range(LATE):
            late_ref[z, j] = weight_ref[pl.ds(j * 128 + z * sub, sub)].astype(BF)
    late_in = [
        go(late_ref.at[me_z ^ 1], lpart_ref.at[0], z_pair),
        go(late_ref.at[me_z ^ 3], lpart_ref.at[1], z_pair),
    ]
    a_next = halve_on(group_a, lambda b: own_ref[b, me_z ^ 2], 2, 0)
    for index in range(2, len(terms)):
        sum_end(index)
    group_b = halve(own_ref, 2, len(terms) - 2, 2)
    next_in = [down_next, a_next]
    for move in late_in:
        move.wait_recv()
    lsend_ref[...] = late_ref[me_z ^ 2] + lpart_ref[1]
    late_next = go(lsend_ref, lnext_ref, z_next)
    next_in.append(
        halve_on(group_b, lambda b: own_ref[2 + b, me_z ^ 2], len(terms) - 2, 2)
    )
    late_next.wait_recv()
    total = late_ref[me_z].astype(F32) + lpart_ref[0].astype(F32) + lnext_ref[...].astype(F32)
    late_out[...] = total.astype(BF)
    for move in next_in:
        move.wait_recv()
    for block in range(EARLY):
        if block < len(terms):
            total = own_ref[block, me_z].astype(F32)
        else:
            total = mine_ref[block - len(terms), me_z].astype(F32)
        total = total + zpart_ref[0, block].astype(F32) + znext_ref[block].astype(F32)
        early_ref[block] = total.astype(BF)
    local.finish()
    for move in sent:
        move.wait_send()


def backward_attention(
    qkv, o_heads, lse, grad_att, counts, term_out, term_up, down, down_y, down_x, x_all, nz, nc
):
    images, seq = qkv.shape[:2]
    local_len = seq // nc
    sub = term_up.shape[3]
    terms = 1 + term_up.shape[0]
    any_ = pl.BlockSpec(memory_space=pl.ANY)
    vmem = pl.BlockSpec(memory_space=pltpu.VMEM)
    return pl.pallas_call(
        functools.partial(backward_kernel, nz, nc),
        out_shape=(
            jax.ShapeDtypeStruct((EARLY, sub, D), BF),
            jax.ShapeDtypeStruct((LATE, sub, D), BF),
            jax.ShapeDtypeStruct((images, seq, 384), BF),
        ),
        in_specs=[
            any_,
            any_,
            vmem,
            any_,
            vmem,
            any_,
            any_,
            any_,
            any_,
            any_,
            any_,
        ],
        out_specs=(vmem, vmem, any_),
        scratch_shapes=[
            pltpu.VMEM((images, seq, 128), BF),
            pltpu.VMEM((images, seq, 384), BF),
            pltpu.VMEM((images, seq, 384), BF),
            pltpu.VMEM((images, seq, 128), BF),
            pltpu.VMEM((2, seq, D), BF),
            pltpu.VMEM((seq, 128), F32),
            pltpu.VMEM((16, seq), F32),
            pltpu.VMEM((384, D), F32),
            pltpu.VMEM((terms, nz, sub, D), BF),
            pltpu.VMEM((terms, nz, sub, D // 2), BF),
            pltpu.VMEM((terms, nz, sub, D // 2), BF),
            pltpu.VMEM((terms, 4, nz, sub, D // 2), BF),
            pltpu.VMEM((terms, 2, nz, sub, D // 2), BF),
            pltpu.VMEM((EARLY - terms, nz, sub, D), BF),
            pltpu.VMEM((2, EARLY - terms, nz, sub, D // 2), BF),
            pltpu.VMEM((2, EARLY, sub, D), BF),
            pltpu.VMEM((EARLY, sub, D), BF),
            pltpu.VMEM((EARLY, sub, D), BF),
            pltpu.VMEM((nz, LATE, sub, D), BF),
            pltpu.VMEM((2, LATE, sub, D), BF),
            pltpu.VMEM((LATE, sub, D), BF),
            pltpu.VMEM((LATE, sub, D), BF),
            pltpu.SemaphoreType.DMA((256,)),
            pltpu.SemaphoreType.DMA((256,)),
            pltpu.SemaphoreType.DMA((64,)),
        ],
        compiler_params=pltpu.CompilerParams(
            collective_id=2, has_side_effects=True, vmem_limit_bytes=61 << 20
        ),
        name="backward_attention",
    )(
        qkv,
        o_heads,
        lse,
        grad_att,
        counts,
        term_out,
        term_up,
        down,
        down_y,
        down_x,
        x_all,
    )


def tail_kernel(
    nz,
    nc,
    token_count,
    slot_blocks,
    early_hbm,
    late_hbm,
    heads_ref,
    wq_own_ref,
    wq_ref,
    tokens_ref,
    mid_ref,
    gain_hbm,
    gains_hbm,
    rl_ref,
    rr_ref,
    sl_ref,
    sr_ref,
    ms_ref,
    tokens_out,
    gain_out,
    grad_hbm,
    left_hbm,
    right_hbm,
    weight_hbm,
    early_ref,
    late_ref,
    gain_ref,
    gains_ref,
    grad_out,
    left_out,
    right_out,
    tok,
    wq,
    x_buf,
    mid_buf,
    part,
    part_in,
    rl,
    rr,
    sl,
    sr,
    ms,
    update,
    square,
    square_in,
    gain_sum,
    gain_in,
    place_ref,
    g_ref,
    l_ref,
    g_all,
    send,
    recv,
    local_sems,
):
    me_z, me_c, me_t = (lax.axis_index(a) for a in ("fsdp", "context", "tensor"))
    images, local_len = tokens_ref.shape[:2]
    slots = g_ref.shape[0]
    x_c, y_c, far_c = me_c ^ 1, me_c ^ 2, me_c ^ 3
    core, x_near, y_near = {"tensor": 1 - me_t}, {"context": x_c}, {"context": y_c}
    above, below = {"fsdp": me_z + 1}, {"fsdp": me_z - 1}
    c_peers = [{"context": me_c ^ k} for k in range(1, nc)]
    group = [
        {"fsdp": me_z ^ (k // 2), "tensor": me_t ^ (k % 2)} for k in range(1, 2 * nz)
    ]
    rows_group = [(me_z ^ (k // nc), me_c ^ (k % nc)) for k in range(1, nz * nc)]
    others = [{"fsdp": z, "context": c} for z, c in rows_group[nc - 1 :] ]
    diagonal = [d for k, d in enumerate(others) if (k + nc) % nc]
    left, right = pl.ds(0, D // 2), pl.ds(D // 2, D // 2)
    local = Local(local_sems)
    small_in = [
        local.start(a, b)
        for a, b in (
            (early_hbm, early_ref),
            (late_hbm, late_ref),
            (gain_hbm, gain_ref),
            (gains_hbm, gains_ref),
        )
    ]
    width = wq.shape[1] // nc
    wq_in = [local.start(wq_own_ref, wq.at[:, span(me_c * width, width)])] + [
        local.start(wq_ref.at[:, span(m * width, width)], wq.at[:, span(m * width, width)])
        for m in (x_c, y_c, far_c)
    ]
    x_in = [local.start(tokens_ref.at[i], x_buf.at[i]) for i in range(images)]
    mid_in = [local.start(mid_ref.at[i], mid_buf.at[i]) for i in range(images)]
    state_in = [
        local.start(a, b) for a, b in ((rl_ref, rl), (sl_ref, sl), (sr_ref, sr), (ms_ref, ms))
    ]
    rr_in = [local.start(rr_ref.at[0], rr)]
    barrier = pltpu.get_barrier_semaphore()
    for device in group + c_peers + diagonal:
        pl.semaphore_signal(
            barrier, inc=1, device_id=device, device_id_type=pl.DeviceIdType.MESH
        )
    for copy in small_in:
        local.wait(copy)
    for slot in range(NBLK):
        block = jnp.clip(slot_blocks[slot] - LATE, 0, EARLY - 1)
        place_ref[slot] = early_ref[block]
    l_ref[:, me_t, me_c, me_z] = late_ref[...]
    for slot in range(slots):
        g_ref[slot, me_t, me_c, me_z] = place_ref[me_c * slots + slot]
    pl.semaphore_wait(barrier, len(group + c_peers + diagonal))
    moves = Moves(send, recv)
    sent = []

    def go(*args, **kw):
        move = moves.make(*args, **kw)
        move.start()
        sent.append(move)
        return move

    placed = []
    for k in range(1, nc):
        theirs = place_ref.at[pl.ds((me_c ^ k) * slots, slots)]
        placed.append(go(theirs, g_ref.at[:, me_t, me_c, me_z], c_peers[k - 1]))

    swapped = []

    def swap(piece, cond=None):
        swapped.append(go(piece, piece, core, cond=cond, recv_cond=cond))

    def along_fsdp(at):
        own = at(me_z)
        return [
            go(own, own, above, cond=me_z < nz - 1, recv_cond=me_z > 0),
            go(own, own, below, cond=me_z > 0, recv_cond=me_z < nz - 1),
        ]

    def onward(at, last, hop):
        up_z, down_z = me_z - hop, me_z + hop
        last[0].wait_recv()
        up = down = None
        if hop < nz - 1:
            piece = at(up_z)
            cond = jnp.logical_and(me_z < nz - 1, up_z >= 0)
            up = go(piece, piece, above, cond=cond, recv_cond=up_z - 1 >= 0)
        last[1].wait_recv()
        if hop < nz - 1:
            piece = at(down_z)
            cond = jnp.logical_and(me_z > 0, down_z <= nz - 1)
            down = go(piece, piece, below, cond=cond, recv_cond=down_z + 1 <= nz - 1)
        return [up, down], [(up_z, up_z >= 0), (down_z, down_z <= nz - 1)]

    def late_at(member):
        return lambda z: l_ref.at[:, me_t, member, z]

    def slot_at(slot):
        return lambda z: g_ref.at[slot, me_t, :, z]

    late_line = along_fsdp(late_at(me_c))
    tok_in = []

    def send_tok(i):
        there = tok.at[i, :, span(me_c * 384, 384)]
        tok_in.append(
            [local.start(heads_ref.at[i, span(me_c * local_len, local_len)], there)]
            + [
                go(
                    heads_ref.at[i, span((me_c ^ k) * local_len, local_len)],
                    there,
                    c_peers[k - 1],
                )
                for k in range(1, nc)
            ]
        )
    lines = []

    def slot_line(slot):
        lines.append(along_fsdp(slot_at(slot)))

    def late_on(hop):
        nonlocal late_line
        late_line, _ = onward(late_at(me_c), late_line, hop)

    send_tok(0)
    send_tok(1)
    late_on(1)
    for move in placed:
        move.wait_recv()
    late_on(2)
    for slot in range(slots):
        slot_line(slot)
    swap(g_ref.at[:, me_t, :, me_z])
    late_on(3)
    late_own = l_ref.at[:, me_t, me_c]
    near = [go(late_own, late_own, x_near), go(late_own, late_own, y_near)]
    swap(late_own)

    part_moves = []
    gain_out[...] = jnp.zeros_like(gain_out)
    square[...] = jnp.zeros_like(square)

    def project(i):
        local.wait(tok_in[i][0])
        for move in tok_in[i][1:]:
            move.wait_recv()
        part[i] = dot_nt(tok[i], wq[...]).astype(BF)
        part_moves.append(go(part.at[i], part_in.at[i], core))

    def norm_backward(i):
        part_moves[i].wait_recv()
        local.wait(x_in[i])
        local.wait(mid_in[i])

        @pl.loop(0, 2)
        def _(step):
            rows = span(step * (local_len // 2), local_len // 2)
            value = x_buf[i, rows]
            centred = value - jnp.mean(value, axis=-1, keepdims=True)
            inv_std = lax.rsqrt(jnp.mean(centred * centred, axis=-1, keepdims=True) + 1e-06)
            normed = centred * inv_std
            grad = part[i, rows].astype(F32) + part_in[i, rows].astype(F32)
            scaled = grad * gain_ref[...]
            inner = (
                scaled
                - jnp.mean(scaled, axis=-1, keepdims=True)
                - normed * jnp.mean(scaled * normed, axis=-1, keepdims=True)
            )
            mid_buf[i, rows] += inner * inv_std
            gain_out[0:1, :] += jnp.sum(grad * normed, axis=0, keepdims=True)

        local.start(mid_buf.at[i], tokens_out.at[i])

    def slots_on(hop):
        for slot in range(slots):
            lines[slot], here = onward(slot_at(slot), lines[slot], hop)
        for z, cond in here:
            swap(g_ref.at[:, me_t, :, z], cond)

    slots_on(1)
    near[0].wait_recv()
    piece = l_ref.at[:, me_t, x_c, :, :, left]
    far = [go(piece, piece, y_near)]
    near[1].wait_recv()
    piece = l_ref.at[:, me_t, y_c, :, :, right]
    far.append(go(piece, piece, x_near))
    send_tok(2)
    swap(l_ref.at[:, me_t, x_c])
    swap(l_ref.at[:, me_t, y_c])
    for copy in wq_in:
        local.wait(copy)
    project(0)
    norm_backward(0)
    slots_on(2)
    for move in far:
        move.wait_recv()
    swap(l_ref.at[:, me_t, far_c])
    project(1)
    norm_backward(1)
    last = []
    for slot in range(slots):
        _, here = onward(slot_at(slot), lines[slot], 3)
        last.append([])
        for z, cond in here:
            piece = g_ref.at[slot, me_t, :, z]
            last[slot].append(go(piece, piece, core, cond=cond, recv_cond=cond))
    project(2)
    for move in swapped:
        move.wait_recv()
    for copy in state_in:
        local.wait(copy)
    offset = me_t * (D // 2) + me_z * rl.shape[1]
    mine = span(offset, rl.shape[1])

    def step(slot):
        for move in last[slot]:
            move.wait_recv()
        block = slot_blocks[me_c * slots + slot]
        late = l_ref[jnp.clip(block, 0, LATE - 1)]
        g_all[...] = jnp.where(block < LATE, late, g_ref[slot]).reshape(D, D)
        rows = g_all[mine, :]
        grad_out[slot] = rows.astype(F32)
        left_out[slot] = 0.5 * sl[slot] + 0.5 / token_count * dot_nt(rows, g_all[...])
        right_out[slot] = 0.5 * sr[slot] + 0.5 / token_count * dot_tn(g_all[:, mine], g_all[...])
        for a, b in ((grad_out, grad_hbm), (left_out, left_hbm), (right_out, right_hbm)):
            local.start(a.at[slot], b.at[slot])
        inner = dot_nn(rl[slot].astype(BF), g_all[...]).astype(BF)
        local.wait(rr_in[slot])
        update[slot] = dot_nn(inner, rr[...].astype(BF))
        if slot + 1 < slots:
            rr_in.append(local.start(rr_ref.at[slot + 1], rr))
        total = jnp.sum(update[slot] * update[slot], axis=0, keepdims=True)
        total = jnp.sum(total, axis=1, keepdims=True)
        square[slot : slot + 1, :] = jnp.broadcast_to(total, (1, 128))

    step(0)
    norm_backward(2)
    gain_sum[...] = gains_ref[...]
    gain_sum[0:1, :] = gain_out[0:1, :]
    gain_moves = []
    for k, (z, c) in enumerate(rows_group):
        theirs = span((z * nc + c) // 2 * 128, 128)
        gain_moves.append(
            go(gain_sum.at[:, theirs], gain_in.at[k], {"fsdp": z, "context": c})
        )
    for slot in range(1, slots):
        step(slot)
    square_moves = [
        go(square, square_in.at[k], group[k]) for k in range(len(group))
    ]
    for move in square_moves:
        move.wait_recv()
    for slot in range(slots):
        total = square[slot : slot + 1, 0:1]
        for k in range(len(group)):
            total = total + square_in[k, slot : slot + 1, 0:1]
        ms[slot] -= lax.rsqrt(total / (D * D) + 1e-06) * update[slot]
        local.start(ms.at[slot], weight_hbm.at[slot])
    total = gain_sum[:, span((me_z * nc + me_c) // 2 * 128, 128)]
    for k, move in enumerate(gain_moves):
        move.wait_recv()
        total = total + gain_in[k]
    gain_out[:, 0:128] = total
    local.finish()
    for move in sent:
        move.wait_send()


def tail(
    block_of,
    early,
    late,
    grad_heads,
    wq,
    wq_all,
    tokens,
    grad_middle,
    gain,
    gain_terms,
    root_left,
    root_right,
    stat_left,
    stat_right,
    master,
    token_count,
    nz,
    nc,
    nt,
):
    images, local_len = tokens.shape[:2]
    sub = early.shape[1]
    slots, row_count = root_left.shape[:2]
    any_ = pl.BlockSpec(memory_space=pl.ANY)
    vmem = pl.BlockSpec(memory_space=pltpu.VMEM)
    state = jax.ShapeDtypeStruct((slots, row_count, D), F32)
    shape = (slots, nt, nc, nz, sub, D)
    return pl.pallas_call(
        functools.partial(tail_kernel, nz, nc, token_count),
        out_shape=(
            jax.ShapeDtypeStruct((images, local_len, D), F32),
            jax.ShapeDtypeStruct((8, D), F32),
            state,
            state,
            state,
            state,
        ),
        in_specs=[pl.BlockSpec(memory_space=pltpu.SMEM)] + [any_] * 14,
        out_specs=(any_, vmem, any_, any_, any_, any_),
        scratch_shapes=[
            pltpu.VMEM((EARLY, sub, D), BF),
            pltpu.VMEM((LATE, sub, D), BF),
            pltpu.VMEM((1, D), F32),
            pltpu.VMEM((8, D), F32),
            pltpu.VMEM((slots, row_count, D), F32),
            pltpu.VMEM((slots, row_count, D), F32),
            pltpu.VMEM((slots, row_count, D), F32),
            pltpu.VMEM((images, local_len, nc * 384), BF),
            pltpu.VMEM((D, nc * 384), BF),
            pltpu.VMEM((images, local_len, D), F32),
            pltpu.VMEM((images, local_len, D), F32),
            pltpu.VMEM((images, local_len, D), BF),
            pltpu.VMEM((images, local_len, D), BF),
            pltpu.VMEM((slots, row_count, D), F32),
            pltpu.VMEM((D, D), F32),
            pltpu.VMEM((slots, row_count, D), F32),
            pltpu.VMEM((slots, row_count, D), F32),
            pltpu.VMEM((slots, row_count, D), F32),
            pltpu.VMEM((slots, row_count, D), F32),
            pltpu.VMEM((8, 128), F32),
            pltpu.VMEM((2 * nz - 1, 8, 128), F32),
            pltpu.VMEM((8, D), F32),
            pltpu.VMEM((nz * nc - 1, 8, 128), F32),
            pltpu.VMEM((NBLK, sub, D), BF),
            pltpu.VMEM(shape, BF),
            pltpu.VMEM((LATE, nt, nc, nz, sub, D), BF),
            pltpu.VMEM((D, D), BF),
            pltpu.SemaphoreType.DMA((160,)),
            pltpu.SemaphoreType.DMA((160,)),
            pltpu.SemaphoreType.DMA((48,)),
        ],
        compiler_params=pltpu.CompilerParams(
            collective_id=3, has_side_effects=True, vmem_limit_bytes=61 << 20
        ),
        name="tail",
    )(
        block_of,
        early,
        late,
        grad_heads,
        wq,
        wq_all,
        tokens,
        grad_middle,
        gain,
        gain_terms,
        root_left,
        root_right,
        stat_left,
        stat_right,
        master,
    )


def xor_permute(value, axis, step):
    size = lax.axis_size(axis)
    return lax.ppermute(value, axis, [(j, j ^ step) for j in range(size)])


def xor_order(pieces, index):
    bit = 1
    while bit < len(pieces):
        odd = (index & bit) > 0
        pieces = [jnp.where(odd, pieces[j ^ bit], pieces[j]) for j in range(len(pieces))]
        bit *= 2
    return pieces


def sum_tensor(value):
    low = lax.optimization_barrier(value.astype(BF))
    return low.astype(F32) + xor_permute(low, "tensor", 1).astype(F32)


def gather_fsdp(value):
    size = lax.axis_size("fsdp")
    if size > 4:
        return lax.all_gather(value, "fsdp", axis=0, tiled=False)
    pieces = [value] + [
        lax.ppermute(value, "fsdp", [(j, (j - k) % size) for j in range(size)])
        for k in range(1, size)
    ]
    doubled = jnp.stack(pieces + pieces[:-1])
    start = lax.rem(size - lax.axis_index("fsdp"), size)
    return lax.dynamic_slice_in_dim(doubled, start, size, 0)


def sum_fsdp(value):
    size = lax.axis_size("fsdp")
    if size > 4:
        return lax.psum(value, "fsdp")
    total = value
    for k in range(1, size):
        total = total + lax.ppermute(value, "fsdp", [(j, (j - k) % size) for j in range(size)])
    return total


def grad_gather_plain(block_of, early, late, nz, nc):
    me_c, me_t = (lax.axis_index(a) for a in ("context", "tensor"))
    sub = early.shape[1]
    half_width = nc * nz * sub
    slot_count = NBLK // nc
    slots_of = block_of.reshape(nc, slot_count)

    def slots_for(k):
        blocks = lax.dynamic_index_in_dim(slots_of, me_c ^ k, 0, keepdims=False)
        return early[jnp.clip(blocks - LATE, 0, EARLY - 1)]

    placed = [slots_for(0)] + [xor_permute(slots_for(k), "context", k) for k in range(1, nc)]
    placed = jnp.stack(xor_order(placed, me_c), axis=1)
    placed = lax.all_gather(placed, "fsdp", axis=2, tiled=False)
    placed = placed.reshape(slot_count, half_width, D)
    placed_other = xor_permute(placed, "tensor", 1)
    both = jnp.stack([placed, placed_other], axis=1)
    early_full = jnp.where(me_t > 0, both[:, ::-1], both).reshape(slot_count, D, D)

    late = late.reshape(-1, D)
    late = lax.psum_scatter(late, "fsdp", scatter_dimension=0, tiled=True)
    late = lax.all_gather(late, ("context", "fsdp"), axis=0, tiled=True)
    late = jnp.swapaxes(late.reshape(nc * nz, LATE, sub, D), 0, 1).reshape(LATE, half_width, D)
    late_other = xor_permute(late, "tensor", 1)
    both = jnp.stack([late, late_other], axis=1)
    late_full = jnp.where(me_t > 0, both[:, ::-1], both).reshape(LATE, D, D)

    mine = lax.dynamic_index_in_dim(slots_of, me_c, 0, keepdims=False)
    return jnp.where(
        (mine < LATE)[:, None, None], late_full[jnp.clip(mine, 0, LATE - 1)], early_full
    )


def to_natural(value, me_t, half_len):
    parts = value.reshape((-1, half_len) + value.shape[1:])
    return jnp.where(me_t > 0, parts[::-1], parts).reshape(value.shape)


def forward_plain(tokens, gain, key_mask, w_qkv, w_out, w_up, w_down):
    images, local_len = tokens.shape[:2]
    nc, nt = (lax.axis_size(a) for a in ("context", "tensor"))
    me_c, me_t = (lax.axis_index(a) for a in ("context", "tensor"))
    cols = w_qkv.shape[2] // nc
    half_len = local_len // nt
    wq_part = lax.dynamic_slice_in_dim(w_qkv, me_c * cols, cols, 2)
    wq = gather_fsdp(wq_part).reshape(D, 3 * cols)

    def two_stage(weight, member_axis, fsdp_axis):
        width = weight.shape[member_axis] // nc
        part = lax.dynamic_slice_in_dim(weight, me_c * width, width, member_axis)
        part = lax.all_gather(part, "fsdp", axis=fsdp_axis, tiled=True)
        return lax.all_gather(part, "context", axis=member_axis, tiled=True)

    out_full = two_stage(w_out, 0, 1)
    up_full = two_stage(w_up, 1, 0)
    down_full = two_stage(w_down, 0, 1)

    counts = jnp.sum(key_mask, axis=1)
    real = counts
    for k in range(1, nc):
        real = real + xor_permute(counts, "context", k)
    position = (
        (me_c ^ jnp.arange(nc))[:, None, None] * local_len
        + (me_t ^ jnp.arange(nt))[None, :, None] * half_len
        + jnp.arange(half_len)[None, None, :]
    ).reshape(-1)
    live = position[None, :] < real[:, None]
    bias = jnp.where(live, 0.0, -1e30).astype(F32)
    live_col = jnp.broadcast_to(live[:, :, None].astype(F32), (images, SEQ, 128))

    normed1, inv_std1, pre_norm1 = norm_fwd(tokens, gain)
    normed1_low = pre_norm1.astype(BF)

    x_all, qkv, out_heads, log_sums, attended = [], [], [], [], []
    for i in range(images):
        mine = lax.dynamic_slice_in_dim(normed1_low[i], me_t * half_len, half_len, 0)
        held = jnp.stack([mine] + [xor_permute(mine, "context", k) for k in range(1, nc)])
        other = xor_permute(held, "tensor", 1)
        x_i = jnp.stack([held, other], axis=1).reshape(SEQ, D)
        qkv_i = dot_nn(x_i, wq).astype(BF)
        o_i, lse_i = attn_fwd(qkv_i, bias[i][None])
        chunks = o_i.reshape(nc, local_len, 2 * HD)
        moved = [to_natural(chunks[0], me_t, half_len)] + [
            to_natural(xor_permute(chunks[k], "context", k), me_t, half_len) for k in range(1, nc)
        ]
        attended.append(jnp.concatenate(xor_order(moved, me_c), axis=-1))
        x_all.append(x_i)
        qkv.append(qkv_i)
        out_heads.append(o_i)
        log_sums.append(lse_i)
    attended = jnp.stack(attended)
    return (
        jnp.stack(x_all),
        jnp.stack(qkv),
        jnp.stack(out_heads),
        jnp.stack(log_sums),
        attended,
        live_col,
        wq,
        out_full,
        up_full,
        down_full,
        normed1,
        inv_std1,
    )


def backward_plain(qkv, out_heads, log_sums, grad_att, live_col, early, wq):
    images, local_len = grad_att.shape[:2]
    nz, nc, nt = (lax.axis_size(a) for a in ("fsdp", "context", "tensor"))
    me_c, me_t = (lax.axis_index(a) for a in ("context", "tensor"))
    cols = grad_att.shape[2] // nc
    half_len = local_len // nt
    sub = early.shape[2]
    grad_heads = []
    grad_tok = []
    for i in range(images):
        pieces = [grad_att[i, :, j * cols : (j + 1) * cols] for j in range(nc)]
        pieces = [to_natural(p, me_t, half_len) for p in xor_order(pieces, me_c)]
        grad_i = jnp.concatenate(
            [pieces[0]] + [xor_permute(pieces[k], "context", k) for k in range(1, nc)]
        )
        g_i = attn_bwd(qkv[i], grad_i, out_heads[i], log_sums[i], live_col[i])
        chunks = g_i.reshape(nc, local_len, 3 * cols)
        moved = [to_natural(chunks[0], me_t, half_len)] + [
            to_natural(xor_permute(chunks[k], "context", k), me_t, half_len) for k in range(1, nc)
        ]
        grad_tok.append(jnp.stack(xor_order(moved, me_c), axis=1))
        grad_heads.append(g_i)
    grad_tok = jnp.stack(grad_tok)
    wq_all = lax.all_gather(wq, "context", axis=0, tiled=False)
    grad_n1 = sum_tensor(
        jnp.einsum("isjc,jdc->isd", grad_tok, wq_all, preferred_element_type=F32)
    )
    early = lax.psum_scatter(
        jnp.swapaxes(early, 0, 1).reshape(-1, D),
        "fsdp",
        scatter_dimension=0,
        tiled=True,
    ).reshape(EARLY, sub, D)
    return jnp.stack(grad_heads), grad_n1, early


def per_device(
    tokens,
    cotangent,
    gains,
    w_qkv,
    w_out,
    w_up,
    w_down,
    key_mask,
    owner,
    stat_left,
    stat_right,
    root_left,
    root_right,
    master,
    gain_state,
):
    images, local_len = tokens.shape[:2]
    tok_rows = images * local_len
    nz, nc, nt = (lax.axis_size(a) for a in ("fsdp", "context", "tensor"))
    me_z, me_c, me_t = (lax.axis_index(a) for a in ("fsdp", "context", "tensor"))
    half_width = w_qkv.shape[2]
    hidden = w_up.shape[1]
    up_blocks = hidden // half_width
    cols = half_width // nc
    fast = nz == 4 and nc == 4 and nt == 2 and images == 3
    if fast:
        wq_rows = jnp.swapaxes(w_qkv.reshape(-1, 3, nc, cols), 1, 2).reshape(-1, nc * 3 * cols)
        counts = jnp.pad(jnp.sum(key_mask, axis=1), (0, 8 - images))
        counts = jnp.broadcast_to(counts[:, None], (8, 128))
        (
            x_all,
            qkv,
            out_heads,
            log_sums,
            attended,
            counts,
            wq,
            out_full,
            up_full,
            down_part,
        ) = forward_attention(
            tokens, gains[0:1], counts, wq_rows, w_out, w_up, w_down, nz, nc
        )
    else:
        (
            x_all,
            qkv,
            out_heads,
            log_sums,
            attended,
            live_col,
            wq,
            out_full,
            up_full,
            down_full,
            normed1,
            inv_std1,
        ) = forward_plain(tokens, gains[0], key_mask, w_qkv, w_out, w_up, w_down)

    sub = half_width // nc // nz
    onehot = (owner[:, None] == jnp.arange(NBLK, dtype=jnp.int32)[None, :]).astype(jnp.int32)
    block_of = jnp.sum(onehot * jnp.arange(NBLK, dtype=jnp.int32)[:, None], axis=0)

    if fast:
        (
            output,
            grad_middle,
            grad_att,
            term_out,
            term_up,
            down,
            down_y,
            down_x,
            wq_all,
            gain_terms,
        ) = feed_forward(
            attended, out_full, up_full, down_part, tokens, cotangent, gains, wq_rows, nz, nc
        )
        term_out = term_out.reshape(1, nc, nz, sub, D)
        term_up = term_up.reshape(-1, nc, nz, sub, D)
        down = down.reshape(-1, nz, sub, D)
        down_y = down_y.reshape(-1, nz, sub, D // 2)
        down_x = down_x.reshape(-1, nz, sub, D // 2)
    else:
        branch_attn = sum_tensor(
            jnp.einsum("ish,hd->isd", attended, out_full, preferred_element_type=F32)
        )
        middle = tokens + gains[2] * branch_attn
        normed2, inv_std2, pre_norm2 = norm_fwd(middle, gains[1])
        normed2_low = pre_norm2.astype(BF)
        pre_act = jnp.einsum("isd,df->isf", normed2_low, up_full, preferred_element_type=F32)
        act_val, act_slope = gelu_parts(pre_act)
        act_low = act_val.astype(BF)
        branch_mlp = sum_tensor(
            jnp.einsum("isf,fd->isd", act_low, down_full, preferred_element_type=F32)
        )
        output = middle + gains[3] * branch_mlp

        grad_mlp = (gains[3] * cotangent).astype(BF)
        grad_hidden = jnp.einsum("isd,fd->isf", grad_mlp, down_full, preferred_element_type=F32)
        grad_pre = (grad_hidden * act_slope).astype(BF)
        grad_n2 = sum_tensor(
            jnp.einsum("isf,df->isd", grad_pre, up_full, preferred_element_type=F32)
        )
        middle_part, grad_gain2 = norm_back(grad_n2, gains[1], normed2, inv_std2)
        grad_middle = cotangent + middle_part
        grad_branch = (gains[2] * grad_middle).astype(BF)
        grad_att = jnp.einsum(
            "isd,hd->ish", grad_branch, out_full, preferred_element_type=F32
        ).astype(BF)

        def early_term(left, right):
            term = dot_tn(left.reshape(tok_rows, -1), right.reshape(tok_rows, D)).astype(BF)
            return term.reshape(-1, nc, nz, sub, D)

        def early_sum(term):
            return lax.psum_scatter(
                jnp.swapaxes(term, 0, 1).reshape(-1, D), "context", scatter_dimension=0, tiled=True
            ).reshape(-1, nz, sub, D)

        term_out = early_term(attended, grad_branch)
        term_up = early_term(grad_pre, normed2_low)
        down = early_sum(early_term(act_low, grad_mlp))
        grad_gain3 = jnp.sum(grad_middle * branch_attn, axis=(0, 1))
        grad_gain4 = jnp.sum(cotangent * branch_mlp, axis=(0, 1))
        blank = jnp.zeros_like(grad_gain2)
        gain_terms = jnp.stack([blank, grad_gain2, grad_gain3, grad_gain4] + [blank] * 4, axis=0)
    tokens_all = images * nz * SEQ
    if fast:
        early, late, grad_heads = backward_attention(
            qkv, out_heads, log_sums, grad_att, counts, term_out, term_up, down, down_y, down_x, x_all, nz, nc
        )
        grad_tokens, gain_sum, grad_mine, left_new, right_new, weight_new = tail(
            block_of,
            early,
            late,
            grad_heads,
            wq,
            wq_all,
            tokens,
            grad_middle,
            gains[0:1],
            gain_terms,
            root_left[:, 0],
            root_right,
            stat_left[:, 0],
            stat_right[:, 0],
            master[:, 0],
            tokens_all,
            nz,
            nc,
            nt,
        )
    else:
        early = jnp.concatenate([early_sum(term_out), early_sum(term_up), down], axis=0)
        grad_heads, grad_n1, early = backward_plain(
            qkv, out_heads, log_sums, grad_att, live_col, early, wq
        )
        term_qkv = jnp.einsum("isk,isd->kd", grad_heads, x_all, preferred_element_type=F32)
        late = jnp.swapaxes(term_qkv.astype(BF).reshape(LATE, nz, sub, D), 0, 1)
        grad_full = grad_gather_plain(block_of, early, late, nz, nc)
        input_part, grad_gain1 = norm_back(grad_n1, gains[0], normed1, inv_std1)
        grad_tokens = grad_middle + input_part
        row_count = half_width // nz
        row_offset = me_t * half_width + me_z * row_count
        grad_mine = lax.dynamic_slice_in_dim(grad_full, row_offset, row_count, 1)
        left_new = 0.5 * stat_left[:, 0] + 0.5 / tokens_all * jnp.einsum(
            "sra,sba->srb", grad_mine, grad_full, preferred_element_type=F32
        )
        grad_cols = lax.dynamic_slice_in_dim(grad_full, row_offset, row_count, 2)
        right_new = 0.5 * stat_right[:, 0] + 0.5 / tokens_all * jnp.einsum(
            "sar,sab->srb", grad_cols, grad_full, preferred_element_type=F32
        )
        inner_prod = jnp.einsum(
            "sra,sab->srb", root_left[:, 0].astype(BF), grad_full, preferred_element_type=F32
        ).astype(BF)
        update = jnp.einsum(
            "srb,sbc->src", inner_prod, root_right.astype(BF), preferred_element_type=F32
        )
        square_sum = jnp.sum(update * update, axis=(1, 2))
        square_sum = sum_fsdp(square_sum + xor_permute(square_sum, "tensor", 1))
        factor = lax.rsqrt(square_sum / (D * D) + 1e-06)
        weight_new = master[:, 0] - factor[:, None, None] * update

        gain_terms = gain_terms[:4].at[0].set(grad_gain1)
        gain_sum = gain_terms
        step = 1
        while step < nc:
            gain_sum = gain_sum + xor_permute(gain_sum, "context", step)
            step *= 2
        gain_sum = sum_fsdp(gain_sum)

    share_width = gain_state.shape[1]
    gain_index = lax.axis_index(("fsdp", "context"))
    if fast:
        at = lax.rem(gain_index * share_width, 128)
        gain_grad = lax.dynamic_slice(gain_sum, (0, at), (4, share_width))
    else:
        gain_grad = lax.dynamic_slice_in_dim(
            gain_sum, gain_index * share_width, share_width, 1
        )
    gain_mine = lax.dynamic_slice_in_dim(gains, gain_index * share_width, share_width, 1)
    state_new = 0.5 * gain_state + 0.5 * gain_grad * gain_grad / tokens_all
    gain_new = gain_mine - 0.1 * gain_grad * lax.rsqrt(tokens_all * state_new)
    return (
        output,
        grad_tokens,
        grad_mine.astype(F32)[:, None],
        left_new[:, None],
        right_new[:, None],
        weight_new[:, None],
        gain_grad,
        state_new,
        gain_new,
    )


def solution(mesh):
    return jax.shard_map(
        per_device,
        mesh=mesh,
        in_specs=(
            P("fsdp", "context", None),
            P("fsdp", "context", None),
            P(),
            P("fsdp", None, "tensor"),
            P("tensor", "fsdp"),
            P("fsdp", "tensor"),
            P("tensor", "fsdp"),
            P("fsdp", "context"),
            P(),
            P("context", "tensor", "fsdp", None),
            P("context", "tensor", "fsdp", None),
            P("context", "tensor", "fsdp", None),
            P("context", None, None),
            P("context", "tensor", "fsdp", None),
            P(None, ("fsdp", "context")),
        ),
        out_specs=(
            P("fsdp", "context", None),
            P("fsdp", "context", None),
            P("context", "tensor", "fsdp", None),
            P("context", "tensor", "fsdp", None),
            P("context", "tensor", "fsdp", None),
            P("context", "tensor", "fsdp", None),
            P(None, ("fsdp", "context")),
            P(None, ("fsdp", "context")),
            P(None, ("fsdp", "context")),
        ),
        check_vma=False,
    )
```

```python
import functools

import jax
import jax.numpy as jnp
from jax import lax
from jax.experimental import pallas as pl
from jax.experimental.pallas import tpu as pltpu
from jax.sharding import PartitionSpec as P

D = 1024
HD = 64
SEQ = 1408
NBLK = 12
LATE = 3
EARLY = NBLK - LATE
BF = jnp.bfloat16
F32 = jnp.float32
SCALE = HD ** (-0.5)


def norm_fwd(field_in, gain_vec):
    centred = field_in - jnp.mean(field_in, axis=-1, keepdims=True)
    inv_std = lax.rsqrt(jnp.mean(centred * centred, axis=-1, keepdims=True) + 1e-06)
    normed = centred * inv_std
    return (normed, inv_std, normed * gain_vec)


def norm_back(grad_out, gain_vec, normed, inv_std):
    scaled = grad_out * gain_vec
    inner_sum = (
        scaled
        - jnp.mean(scaled, axis=-1, keepdims=True)
        - normed * jnp.mean(scaled * normed, axis=-1, keepdims=True)
    )
    return (inner_sum * inv_std, jnp.sum(grad_out * normed, axis=(0, 1)))


def gelu_parts(field_in):
    normal_cdf = 0.5 * (1.0 + lax.erf(field_in * 0.7071067811865476))
    normal_pdf = jnp.exp(-0.5 * field_in * field_in) * 0.3989422804014327
    return (field_in * normal_cdf, normal_cdf + field_in * normal_pdf)


def dot_nt(a, b):
    return lax.dot_general(a, b, (((1,), (1,)), ((), ())), preferred_element_type=F32)


def dot_tn(a, b):
    return lax.dot_general(a, b, (((0,), (0,)), ((), ())), preferred_element_type=F32)


def dot_nn(a, b):
    return lax.dot_general(a, b, (((1,), (0,)), ((), ())), preferred_element_type=F32)


def attn_fwd_kernel(q_ref, k_ref, v_ref, bias_ref, o_ref, lse_ref):
    q = q_ref[...] * SCALE
    k = k_ref[...]
    v = v_ref[...]
    bias = bias_ref[...]
    first = lax.broadcasted_iota(jnp.int32, q.shape, 1) < HD
    outs, sums = [], []
    for head in range(2):
        mask = first if head == 0 else jnp.logical_not(first)
        scores = dot_nt(jnp.where(mask, q, jnp.zeros_like(q)), k) + bias
        peak = jnp.max(scores, axis=-1, keepdims=True)
        expo = jnp.exp(scores - peak)
        total = jnp.sum(expo, axis=-1, keepdims=True)
        outs.append(dot_nn(expo.astype(BF), v) / total)
        sums.append(peak + jnp.log(total))
    o_ref[...] = jnp.where(first, outs[0], outs[1]).astype(BF)
    lse_ref[...] = jnp.where(first, sums[0], sums[1])


def attn_fwd(qkv, bias_row):
    rows = qkv.shape[0]
    bq = rows // 4
    return pl.pallas_call(
        attn_fwd_kernel,
        grid=(rows // bq,),
        out_shape=(
            jax.ShapeDtypeStruct((rows, 128), BF),
            jax.ShapeDtypeStruct((rows, 128), F32),
        ),
        in_specs=[
            pl.BlockSpec((bq, 128), lambda i: (i, 0)),
            pl.BlockSpec((rows, 128), lambda i: (0, 1)),
            pl.BlockSpec((rows, 128), lambda i: (0, 2)),
            pl.BlockSpec((1, rows), lambda i: (0, 0)),
        ],
        out_specs=(
            pl.BlockSpec((bq, 128), lambda i: (i, 0)),
            pl.BlockSpec((bq, 128), lambda i: (i, 0)),
        ),
        compiler_params=pltpu.CompilerParams(vmem_limit_bytes=40 << 20),
        cost_estimate=pl.CostEstimate(
            flops=4 * rows * rows * 512, bytes_accessed=rows * 2048, transcendentals=2 * rows * rows
        ),
        name="attn_fwd",
    )(qkv, qkv, qkv, bias_row)


def attn_bwd_kernel(q_ref, k_ref, v_ref, do_ref, o_ref, lse_ref, live_ref, out_ref, dq_ref, row_ref):
    step = pl.program_id(0)
    chunk = k_ref.shape[0]

    @pl.when(step == 0)
    def _():
        row_ref[0:128, :] = lse_ref[...].T
        prod = do_ref[...].astype(F32) * o_ref[...].astype(F32)
        prod_t = prod.T
        row_ref[128:136, :] = jnp.broadcast_to(
            jnp.sum(prod_t[0:HD], axis=0, keepdims=True), (8, prod_t.shape[1])
        )
        row_ref[136:144, :] = jnp.broadcast_to(
            jnp.sum(prod_t[HD:128], axis=0, keepdims=True), (8, prod_t.shape[1])
        )
        dq_ref[...] = jnp.zeros_like(dq_ref)

    q = q_ref[...]
    k = k_ref[...] * SCALE
    v = v_ref[...]
    do = do_ref[...]
    live = live_ref[:, 0:1] > 0
    first = lax.broadcasted_iota(jnp.int32, k.shape, 1) < HD
    dks, dvs = [], []
    for head in range(2):
        mask = first if head == 0 else jnp.logical_not(first)
        kh = jnp.where(mask, k, jnp.zeros_like(k))
        vh = jnp.where(mask, v, jnp.zeros_like(v))
        lse = row_ref[64 * head : 64 * head + 1, :]
        delta = row_ref[128 + 8 * head : 129 + 8 * head, :]
        prob = jnp.where(live, jnp.exp(dot_nt(kh, q) - lse), 0.0)
        ds = (prob * (dot_nt(vh, do) - delta)).astype(BF)
        dvs.append(dot_nn(prob.astype(BF), do))
        dks.append(dot_nn(ds, q) * SCALE)
        dq_ref[...] += dot_tn(ds, kh)
    at = pl.ds(pl.multiple_of(step * chunk, chunk), chunk)
    out_ref[at, 128:256] = jnp.where(first, dks[0], dks[1]).astype(BF)
    out_ref[at, 256:384] = jnp.where(first, dvs[0], dvs[1]).astype(BF)

    @pl.when(step == pl.num_programs(0) - 1)
    def _():
        out_ref[:, 0:128] = dq_ref[...].astype(BF)


def attn_bwd(qkv, grad, out, lse, live_col):
    rows = qkv.shape[0]
    chunk = rows // 4
    return pl.pallas_call(
        attn_bwd_kernel,
        grid=(rows // chunk,),
        out_shape=jax.ShapeDtypeStruct((rows, 384), BF),
        in_specs=[
            pl.BlockSpec((rows, 128), lambda i: (0, 0)),
            pl.BlockSpec((chunk, 128), lambda i: (i, 1)),
            pl.BlockSpec((chunk, 128), lambda i: (i, 2)),
            pl.BlockSpec((rows, 128), lambda i: (0, 0)),
            pl.BlockSpec((rows, 128), lambda i: (0, 0)),
            pl.BlockSpec((rows, 128), lambda i: (0, 0)),
            pl.BlockSpec((chunk, 128), lambda i: (i, 0)),
        ],
        out_specs=pl.BlockSpec((rows, 384), lambda i: (0, 0)),
        scratch_shapes=[pltpu.VMEM((rows, 128), F32), pltpu.VMEM((144, rows), F32)],
        compiler_params=pltpu.CompilerParams(vmem_limit_bytes=50 << 20),
        cost_estimate=pl.CostEstimate(
            flops=10 * rows * rows * 512, bytes_accessed=rows * 4096, transcendentals=2 * rows * rows
        ),
        name="attn_bwd",
    )(qkv, qkv, qkv, grad, out, lse, live_col)


class Moves:
    def __init__(self, send_sems, recv_sems):
        self.send_sems, self.recv_sems, self.count = send_sems, recv_sems, 0

    def make(self, src, dst, device, cond=None, recv_cond=None):
        index = self.count
        self.count += 1
        return Move(self, index, src, dst, device, cond, recv_cond)


class Move:
    def __init__(self, moves, index, src, dst, device, cond, recv_cond):
        self.args = (src, dst, moves.send_sems.at[index], moves.recv_sems.at[index])
        self.device, self.cond, self.recv_cond = device, cond, recv_cond

    def copy(self):
        return pltpu.make_async_remote_copy(
            *self.args, device_id=self.device, device_id_type=pl.DeviceIdType.MESH
        )

    def when(self, cond, act):
        if cond is None:
            act()
        else:
            pl.when(cond)(act)

    def start(self):
        self.when(self.cond, lambda: self.copy().start())

    def wait_recv(self):
        self.when(self.recv_cond, lambda: self.copy().wait_recv())

    def wait_send(self):
        self.when(self.cond, lambda: self.copy().wait_send())


def greet(devices):
    barrier = pltpu.get_barrier_semaphore()
    for device in devices:
        pl.semaphore_signal(
            barrier, inc=1, device_id=device, device_id_type=pl.DeviceIdType.MESH
        )
    pl.semaphore_wait(barrier, len(devices))


def span(start, size):
    return pl.ds(pl.multiple_of(start, size & -size), size)


class Local:
    def __init__(self, sems):
        self.sems, self.count, self.open = sems, 0, []

    def start(self, src, dst):
        copy = pltpu.make_async_copy(src, dst, self.sems.at[self.count])
        self.count += 1
        copy.start()
        self.open.append(copy)
        return copy

    def wait(self, copy):
        copy.wait()
        self.open = [c for c in self.open if c is not copy]

    def finish(self):
        for copy in self.open:
            copy.wait()
        self.open = []


def spread_plane(go, ref_of, me_c, cond=None):
    own = ref_of(me_c, None)
    return [go(own, own, {"context": me_c ^ 1}), go(own, own, {"context": me_c ^ 2})]


def spread_plane_on(go, ref_of, me_c, near):
    near[0].wait_recv()
    piece = ref_of(me_c ^ 1, 0)
    first = go(piece, piece, {"context": me_c ^ 2})
    near[1].wait_recv()
    piece = ref_of(me_c ^ 2, 1)
    second = go(piece, piece, {"context": me_c ^ 1})
    return [first, second]


def forward_kernel(
    nz,
    nc,
    tokens_ref,
    gain_ref,
    count_ref,
    wq_ref,
    wout_ref,
    wup_ref,
    wdown_ref,
    x_out,
    qkv_out,
    o_out,
    lse_out,
    att_out,
    cnt_out,
    wq_out,
    out_full,
    up_full,
    down_part,
    tok,
    x_all,
    qkv,
    o_all,
    lse_all,
    wq,
    counts,
    stage_up,
    stage_out,
    stage_down,
    send,
    recv,
    local_sems,
):
    me_z, me_c, me_t = (lax.axis_index(a) for a in ("fsdp", "context", "tensor"))
    images, local_len = att_out.shape[:2]
    half = local_len // 2
    seq = x_all.shape[1]
    core = {"tensor": 1 - me_t}
    z_peers = [{"fsdp": lax.rem(me_z + k, nz)} for k in range(1, nz)]
    c_peers = [{"context": me_c ^ k} for k in range(1, nc)]
    local = Local(local_sems)
    token_in = [
        local.start(tokens_ref.at[i, span(me_t * half, half)], tok.at[i]) for i in range(images)
    ]
    depth = wq_ref.shape[0]
    hid, depth_o = wup_ref.shape[1] // nc, wout_ref.shape[1]
    staged = [
        local.start(wup_ref.at[:, span(me_c * hid, hid)], stage_up),
        local.start(wout_ref, stage_out),
        local.start(wdown_ref.at[span(me_c * hid, hid)], stage_down),
    ]
    wq_part = wq_ref.at[:, span(me_c * 384, 384)]
    wq_own = local.start(wq_part, wq.at[span(me_z * depth, depth)])
    greet(z_peers + c_peers + [core])
    moves = Moves(send, recv)
    sent = []

    def go(*args, **kw):
        move = moves.make(*args, **kw)
        move.start()
        sent.append(move)
        return move

    wq_in = [go(wq_part, wq.at[span(me_z * depth, depth)], peer) for peer in z_peers]
    counts[me_c] = count_ref[...]
    count_in = [go(count_ref, counts.at[me_c], peer) for peer in c_peers]

    def to_line(index, src, dst):
        local.wait(staged[index])
        local_copy = local.start(src, dst)
        return [local_copy] + [go(src, dst, peer) for peer in z_peers]


    def x_piece(i):
        def at(member, part):
            rows = span(member * local_len + me_t * half, half)
            if part is None:
                return x_all.at[i, rows]
            return x_all.at[i, rows, pl.ds(part * (D // 2), D // 2)]

        return at

    swaps = [[] for _ in range(images)]
    near, far = [], []

    def swap(i, member, part=None):
        piece = x_piece(i)(member, part)
        swaps[i].append(go(piece, piece, core))

    def normalize(i):
        local.wait(token_in[i])
        value = tok[i]
        centred = value - jnp.mean(value, axis=-1, keepdims=True)
        inv_std = lax.rsqrt(jnp.mean(centred * centred, axis=-1, keepdims=True) + 1e-06)
        x_all[i, span(me_c * local_len + me_t * half, half)] = (
            centred * inv_std * gain_ref[0:1, :]
        ).astype(BF)

    def send_near(i):
        near.append(spread_plane(go, x_piece(i), me_c))
        swap(i, me_c)

    def send_far(i):
        far.append(spread_plane_on(go, x_piece(i), me_c, near[i]))
        swap(i, me_c ^ 1)
        swap(i, me_c ^ 2)

    normalize(0)
    send_near(0)
    normalize(1)
    send_near(1)
    normalize(2)
    send_far(0)
    send_near(2)
    local.wait(wq_own)
    for move in wq_in:
        move.wait_recv()
    up_in = to_line(
        0,
        stage_up,
        up_full.at[span(me_z * depth, depth), span(me_c * hid, hid)],
    )
    local.start(wq, wq_out)
    for move in count_in:
        move.wait_recv()
    total = counts[0]
    for k in range(1, nc):
        total = total + counts[k]
    cnt_out[...] = total

    first = lax.broadcasted_iota(jnp.int32, (local_len, 128), 1) < HD
    place = lax.broadcasted_iota(jnp.int32, (1, seq), 1)

    def up_piece(k):
        start = lax.rem(me_z - k + nz, nz) * depth

        def at(member, part):
            columns = span(member * hid, hid)
            if part is None:
                return up_full.at[span(start, depth), columns]
            return up_full.at[span(start + part * (depth // 2), depth // 2), columns]

        return at

    up_near, up_far = [], []

    def up_step(k):
        if k == 0:
            local.wait(up_in[0])
        else:
            up_in[k].wait_recv()
        up_near.append(spread_plane(go, up_piece(k), me_c))

    def up_step_on(k):
        up_far.extend(spread_plane_on(go, up_piece(k), me_c, up_near[k]))

    att_in = []
    for i in range(images):
        for part in range(2):
            far[i][part].wait_recv()
            swap(i, me_c ^ 3, part)
        for move in swaps[i]:
            move.wait_recv()
        local.start(x_all.at[i], x_out.at[i])

        @pl.loop(0, nc)
        def _(chunk):
            rows = span(chunk * local_len, local_len)
            qkv[i, rows] = dot_nn(x_all[i, rows], wq[...]).astype(BF)

        local.start(qkv.at[i], qkv_out.at[i])
        if i == 0:
            send_far(1)
        bias = jnp.where(place < cnt_out[i : i + 1, 0:1], 0.0, -1e30)
        def attend(chunk):
            rows = span(chunk * local_len, local_len)
            q = qkv[i, rows, 0:128] * SCALE
            k = qkv[i, :, 128:256]
            v = qkv[i, :, 256:384]
            outs, sums = [], []
            for head in range(2):
                mask = first if head == 0 else jnp.logical_not(first)
                scores = dot_nt(jnp.where(mask, q, jnp.zeros_like(q)), k) + bias
                peak = jnp.max(scores, axis=-1, keepdims=True)
                expo = jnp.exp(scores - peak)
                norm = jnp.sum(expo, axis=-1, keepdims=True)
                outs.append(dot_nn(expo.astype(BF), v) / norm)
                sums.append(peak + jnp.log(norm))
            o_all[i, rows] = jnp.where(first, outs[0], outs[1]).astype(BF)
            lse_all[rows] = jnp.where(first, sums[0], sums[1])

        if i == 2:
            up_step_on(0)
            up_step_on(1)
        pl.loop(0, nc)(attend)
        if i == 0:
            send_far(2)
            up_step(0)

        mine = att_out.at[i, :, span(me_c * 128, 128)]
        for k in range(1, nc):
            att_in.append(
                go(o_all.at[i, span((me_c ^ k) * local_len, local_len)], mine, c_peers[k - 1])
            )
        local.start(o_all.at[i, span(me_c * local_len, local_len)], mine)
        local.start(o_all.at[i], o_out.at[i])
        sums_t = lse_all[...].T
        for head in range(2):
            lse_out[i, 8 * head : 8 * head + 8, :] = jnp.broadcast_to(
                sums_t[HD * head : HD * head + 1], (8, seq)
            )
        if i == 0:
            up_step(1)
            out_in = to_line(1, stage_out, out_full.at[:, span(me_z * depth_o, depth_o)])
        if i == 1:
            up_step(2)
            up_step(3)
            down_in = to_line(
                2,
                stage_down,
                down_part.at[:, span(me_z * depth_o, depth_o)],
            )
    up_step_on(2)
    up_step_on(3)
    for move in up_far:
        move.wait_recv()
    for move in att_in:
        move.wait_recv()
    for move in out_in[1:] + down_in[1:]:
        move.wait_recv()
    local.finish()
    for move in sent:
        move.wait_send()


def forward_attention(tokens, gain, counts, wq_part, w_out, w_up, w_down, nz, nc):
    images, local_len = tokens.shape[:2]
    seq = nc * local_len
    cols, hid = w_out.shape[0], w_up.shape[1]
    any_ = pl.BlockSpec(memory_space=pl.ANY)
    vmem = pl.BlockSpec(memory_space=pltpu.VMEM)
    return pl.pallas_call(
        functools.partial(forward_kernel, nz, nc),
        out_shape=(
            jax.ShapeDtypeStruct((images, seq, D), BF),
            jax.ShapeDtypeStruct((images, seq, 384), BF),
            jax.ShapeDtypeStruct((images, seq, 128), BF),
            jax.ShapeDtypeStruct((images, 16, seq), F32),
            jax.ShapeDtypeStruct((images, local_len, cols), BF),
            jax.ShapeDtypeStruct((8, 128), jnp.int32),
            jax.ShapeDtypeStruct((D, 384), BF),
            jax.ShapeDtypeStruct((cols, D), BF),
            jax.ShapeDtypeStruct((D, hid), BF),
            jax.ShapeDtypeStruct((hid // nc, D), BF),
        ),
        in_specs=[any_, vmem, vmem, any_, any_, any_, any_],
        out_specs=(any_, any_, any_, vmem, any_, vmem, any_, any_, any_, any_),
        scratch_shapes=[
            pltpu.VMEM((images, local_len // 2, D), F32),
            pltpu.VMEM((images, seq, D), BF),
            pltpu.VMEM((images, seq, 384), BF),
            pltpu.VMEM((images, seq, 128), BF),
            pltpu.VMEM((seq, 128), F32),
            pltpu.VMEM((D, 384), BF),
            pltpu.VMEM((nc, 8, 128), jnp.int32),
            pltpu.VMEM((w_up.shape[0], hid // nc), BF),
            pltpu.VMEM(w_out.shape, BF),
            pltpu.VMEM((hid // nc, w_down.shape[1]), BF),
            pltpu.SemaphoreType.DMA((96,)),
            pltpu.SemaphoreType.DMA((96,)),
            pltpu.SemaphoreType.DMA((32,)),
        ],
        compiler_params=pltpu.CompilerParams(
            collective_id=1, has_side_effects=True, vmem_limit_bytes=56 << 20
        ),
        name="forward_attention",
    )(tokens, gain, counts, wq_part, w_out, w_up, w_down)


def feed_forward_kernel(
    nz,
    nc,
    att_ref,
    wout_ref,
    wup_ref,
    wdown_ref,
    tokens_ref,
    cot_ref,
    gains_ref,
    wq_ref,
    output_out,
    mid_out,
    gatt_out,
    tout_out,
    tup_out,
    own_out,
    fary_out,
    farx_out,
    wq_out,
    gain_out,
    att,
    wout,
    wup,
    wdown,
    tok,
    cot,
    normed_low,
    act,
    slope,
    low,
    first_own,
    first_in,
    second_own,
    second_in,
    third_in,
    stage,
    term,
    near_in,
    gatt,
    send,
    recv,
    local_sems,
):
    me_z, me_c, me_t = (lax.axis_index(a) for a in ("fsdp", "context", "tensor"))
    z_peers = [{"fsdp": lax.rem(me_z + k, nz)} for k in range(1, nz)]
    images, local_len = tok.shape[:2]
    hid = wdown_ref.shape[0]
    x_c, y_c, far_c = me_c ^ 1, me_c ^ 2, me_c ^ 3
    core, x_near, y_near = {"tensor": 1 - me_t}, {"context": x_c}, {"context": y_c}
    left, right = pl.ds(0, D // 2), pl.ds(D // 2, D // 2)
    half = local_len // 2
    local = Local(local_sems)
    att_in = [local.start(att_ref, att), local.start(wout_ref, wout)]
    cot_in = local.start(cot_ref, cot)
    tok_in = local.start(tokens_ref, tok)
    up_in = local.start(wup_ref, wup)

    def down_piece(member, part):
        rows = span(member * hid, hid)
        return wdown.at[rows] if part is None else wdown.at[rows, pl.ds(part * (D // 2), D // 2)]

    down_own = local.start(wdown_ref, down_piece(me_c, None))
    greet([core, x_near, y_near] + z_peers)
    moves = Moves(send, recv)
    sent = []

    def go(*args, **kw):
        move = moves.make(*args, **kw)
        move.start()
        sent.append(move)
        return move

    down_near = [
        go(wdown_ref.at[:, columns], down_piece(me_c, part), device)
        for part, columns, device in (
            (0, left, x_near),
            (1, right, y_near),
            (1, right, x_near),
            (0, left, y_near),
        )
    ]
    depth = wq_ref.shape[0]
    wq_in = []
    for k in range(1, nc):
        columns = span((me_c ^ k) * 384, 384)
        there = wq_out.at[span(me_z * depth, depth), columns]
        wq_in += [go(wq_ref.at[:, columns], there, peer) for peer in z_peers]
    for copy in att_in:
        local.wait(copy)

    @pl.loop(0, images)
    def _(i):
        first_own[i] = dot_nn(att[i], wout[...]).astype(BF)

    first = go(first_own, first_in, core)
    local.wait(cot_in)

    @pl.loop(0, images)
    def _(i):
        low[i] = (gains_ref[3:4, :] * cot[i]).astype(BF)

    local.wait(tok_in)
    first.wait_recv()

    @pl.loop(0, 2 * images)
    def _(step):
        i, rows = step // 2, span(lax.rem(step, 2) * half, half)
        branch = first_own[i, rows].astype(F32) + first_in[i, rows].astype(F32)
        value = tok[i, rows] + gains_ref[2:3, :] * branch
        tok[i, rows] = value
        centred = value - jnp.mean(value, axis=-1, keepdims=True)
        inv_std = lax.rsqrt(jnp.mean(centred * centred, axis=-1, keepdims=True) + 1e-06)
        normed_low[i, rows] = (centred * inv_std * gains_ref[1:2, :]).astype(BF)

    local.wait(up_in)
    width = 512

    @pl.loop(0, images)
    def _(i):
        @pl.loop(0, wup.shape[1] // width)
        def _(step):
            cols = span(step * width, width)
            value = dot_nn(normed_low[i], wup[:, cols])
            cdf = 0.5 * (1.0 + lax.erf(value * 0.7071067811865476))
            pdf = jnp.exp(-0.5 * value * value) * 0.3989422804014327
            act[i, :, cols] = (value * cdf).astype(BF)
            slope[i, :, cols] = (cdf + value * pdf).astype(BF)

    down_near[0].wait_recv()
    x_piece = down_piece(x_c, 0)
    down_far = [go(x_piece, x_piece, y_near)]
    down_near[1].wait_recv()
    y_piece = down_piece(y_c, 1)
    down_far.append(go(y_piece, y_piece, x_near))
    blocks = term.shape[0]
    chunk_rows = term.shape[2]

    @pl.loop(0, blocks)
    def _(j):
        cols = span(j * width, width)
        total = jnp.zeros((width, D), F32)
        for i in range(images):
            total += dot_tn(act[i, :, cols], low[i])
        for c in range(nc):
            term[j, c] = total[c * chunk_rows : (c + 1) * chunk_rows].astype(BF)

    near = [
        go(term.at[:, x_c, :, left], near_in.at[0], x_near),
        go(term.at[:, far_c, :, left], near_in.at[1], x_near),
        go(term.at[:, y_c, :, right], near_in.at[2], y_near),
        go(term.at[:, far_c, :, right], near_in.at[3], y_near),
    ]
    local.wait(down_own)
    for move in down_near[2:]:
        move.wait_recv()

    def back_down(member):
        columns = span(member * hid, hid)

        @pl.loop(0, images)
        def _(i):
            value = dot_nt(low[i], wdown[columns, :]) * slope[i, :, columns].astype(F32)
            slope[i, :, columns] = value.astype(BF)

    copies = []

    def up_term(k):
        if k >= 2:
            local.wait(copies[k - 2])
        cols = span((me_c ^ k) * width, width)
        total = jnp.zeros((width, D), F32)
        for i in range(images):
            total += dot_tn(slope[i, :, cols], normed_low[i])
        stage[k % 2] = total.astype(BF)
        copies.append(local.start(stage.at[k % 2], tup_out.at[cols]))

    @pl.loop(0, 3)
    def _(k):
        back_down(me_c ^ k)

    for k in range(3):
        up_term(k)
    for move in down_far:
        move.wait_recv()
    back_down(far_c)

    @pl.loop(0, images)
    def _(i):
        second_own[i] = dot_nn(act[i], wdown[...]).astype(BF)

    second = go(second_own, second_in, core)
    first.wait_send()
    sent.remove(first)
    gain_out[...] = jnp.zeros_like(gain_out)

    @pl.loop(0, 2 * images)
    def _(step):
        i, rows = step // 2, span(lax.rem(step, 2) * half, half)
        branch = first_own[i, rows].astype(F32) + first_in[i, rows].astype(F32)
        first_in[i, rows] = branch.astype(BF)

    @pl.loop(0, images)
    def _(i):
        first_own[i] = dot_nt(slope[i], wup[...]).astype(BF)

    third = go(first_own, third_in, core)

    up_term(3)
    second.wait_recv()
    third.wait_recv()

    @pl.loop(0, 2 * images)
    def _(step):
        i, rows = step // 2, span(lax.rem(step, 2) * half, half)
        value = tok[i, rows]
        centred = value - jnp.mean(value, axis=-1, keepdims=True)
        inv_std = lax.rsqrt(jnp.mean(centred * centred, axis=-1, keepdims=True) + 1e-06)
        normed = centred * inv_std
        branch = second_own[i, rows].astype(F32) + second_in[i, rows].astype(F32)
        tok[i, rows] = value + gains_ref[3:4, :] * branch
        cotangent = cot[i, rows]
        gain_out[3:4, :] += jnp.sum(cotangent * branch, axis=0, keepdims=True)
        grad = first_own[i, rows].astype(F32) + third_in[i, rows].astype(F32)
        gain_out[1:2, :] += jnp.sum(grad * normed, axis=0, keepdims=True)
        scaled = grad * gains_ref[1:2, :]
        inner = (
            scaled
            - jnp.mean(scaled, axis=-1, keepdims=True)
            - normed * jnp.mean(scaled * normed, axis=-1, keepdims=True)
        )
        grad = cotangent + inner * inv_std
        cot[i, rows] = grad
        gain_out[2:3, :] += jnp.sum(grad * first_in[i, rows].astype(F32), axis=0, keepdims=True)
        low[i, rows] = (gains_ref[2:3, :] * grad).astype(BF)

    local.start(tok, output_out)
    local.start(cot, mid_out)

    @pl.loop(0, images)
    def _(i):
        gatt[i] = dot_nt(low[i], wout[...]).astype(BF)

    local.start(gatt, gatt_out)
    total = jnp.zeros((att.shape[2], D), F32)
    for i in range(images):
        total += dot_tn(att[i], low[i])
    for copy in copies[-2:]:
        local.wait(copy)
    stage[0] = total.astype(BF)
    local.start(stage.at[0], tout_out)
    for move in near:
        move.wait_recv()
    for move in near:
        move.wait_send()
        sent.remove(move)
    term[:, me_c, :, left] += near_in[0]
    term[:, me_c, :, right] += near_in[2]
    term[:, y_c, :, left] += near_in[1]
    term[:, x_c, :, right] += near_in[3]
    for move in wq_in:
        move.wait_recv()
    local.start(term.at[:, me_c], own_out)
    local.start(term.at[:, y_c, :, left], fary_out)
    local.start(term.at[:, x_c, :, right], farx_out)
    local.finish()
    for move in sent:
        move.wait_send()


def feed_forward(attended, out_full, up_full, down_part, tokens, cotangent, gains, wq_rows, nz, nc):
    images, local_len = tokens.shape[:2]
    cols, hid = out_full.shape[0], up_full.shape[1]
    blocks = hid // 512
    piece = (blocks, 512 // nc)
    any_ = pl.BlockSpec(memory_space=pl.ANY)
    vmem = pl.BlockSpec(memory_space=pltpu.VMEM)
    rows = (images, local_len)
    return pl.pallas_call(
        functools.partial(feed_forward_kernel, nz, nc),
        out_shape=(
            jax.ShapeDtypeStruct(rows + (D,), F32),
            jax.ShapeDtypeStruct(rows + (D,), F32),
            jax.ShapeDtypeStruct(rows + (cols,), BF),
            jax.ShapeDtypeStruct((cols, D), BF),
            jax.ShapeDtypeStruct((hid, D), BF),
            jax.ShapeDtypeStruct(piece + (D,), BF),
            jax.ShapeDtypeStruct(piece + (D // 2,), BF),
            jax.ShapeDtypeStruct(piece + (D // 2,), BF),
            jax.ShapeDtypeStruct((D, nc * 384), BF),
            jax.ShapeDtypeStruct((8, D), F32),
        ),
        in_specs=[any_] * 6 + [vmem, any_],
        out_specs=(any_,) * 9 + (vmem,),
        scratch_shapes=[
            pltpu.VMEM(rows + (cols,), BF),
            pltpu.VMEM((cols, D), BF),
            pltpu.VMEM((D, hid), BF),
            pltpu.VMEM((hid, D), BF),
            pltpu.VMEM(rows + (D,), F32),
            pltpu.VMEM(rows + (D,), F32),
            pltpu.VMEM(rows + (D,), BF),
            pltpu.VMEM(rows + (hid,), BF),
            pltpu.VMEM(rows + (hid,), BF),
            pltpu.VMEM(rows + (D,), BF),
            pltpu.VMEM(rows + (D,), BF),
            pltpu.VMEM(rows + (D,), BF),
            pltpu.VMEM(rows + (D,), BF),
            pltpu.VMEM(rows + (D,), BF),
            pltpu.VMEM(rows + (D,), BF),
            pltpu.VMEM((2, 512, D), BF),
            pltpu.VMEM((blocks, nc, 512 // nc, D), BF),
            pltpu.VMEM((4, blocks, 512 // nc, D // 2), BF),
            pltpu.VMEM(rows + (cols,), BF),
            pltpu.SemaphoreType.DMA((32,)),
            pltpu.SemaphoreType.DMA((32,)),
            pltpu.SemaphoreType.DMA((24,)),
        ],
        compiler_params=pltpu.CompilerParams(
            collective_id=4, has_side_effects=True, vmem_limit_bytes=62 << 20
        ),
        name="feed_forward",
    )(attended, out_full, up_full, down_part, tokens, cotangent, gains, wq_rows)


def backward_kernel(
    nz,
    nc,
    qkv_ref,
    o_ref,
    lse_ref,
    att_ref,
    cnt_ref,
    term_out_ref,
    term_up_ref,
    down_ref,
    down_y_ref,
    down_x_ref,
    x_ref,
    early_ref,
    late_out,
    heads_out,
    grad,
    heads,
    qkv,
    o_all,
    x_all,
    dq_ref,
    row_ref,
    weight_ref,
    own_ref,
    far_y,
    far_x,
    near_in,
    far_in,
    mine_ref,
    mine_in_ref,
    zpart_ref,
    zsend_ref,
    znext_ref,
    late_ref,
    lpart_ref,
    lsend_ref,
    lnext_ref,
    send,
    recv,
    local_sems,
):
    me_z, me_c, me_t = (lax.axis_index(a) for a in ("fsdp", "context", "tensor"))
    images, local_len = att_ref.shape[:2]
    x_c, y_c, far_c = me_c ^ 1, me_c ^ 2, me_c ^ 3
    x_near, y_near = {"context": x_c}, {"context": y_c}
    z_peers = [{"fsdp": lax.rem(me_z + k, nz)} for k in range(1, nz)]
    c_peers = [{"context": me_c ^ k} for k in range(1, nc)]
    left, right = pl.ds(0, D // 2), pl.ds(D // 2, D // 2)
    ups, downs = term_up_ref.shape[0], down_ref.shape[0]
    terms = [(term_out_ref, 0)] + [(term_up_ref, j) for j in range(ups)]
    local = Local(local_sems)
    held = [
        [local.start(a.at[i], b.at[i]) for a, b in ((qkv_ref, qkv), (o_ref, o_all))]
        for i in range(images)
    ]
    x_in = [local.start(x_ref.at[i], x_all.at[i % 2]) for i in range(2)]
    own_in, far_own = [], []
    for index, (ref, block) in enumerate(terms):
        own_in.append(local.start(ref.at[block, me_c], own_ref.at[index]))
        far_own.append(local.start(ref.at[block, y_c, :, :, left], far_y.at[index]))
        far_own.append(local.start(ref.at[block, x_c, :, :, right], far_x.at[index]))
    mine_in = local.start(down_ref, mine_ref)
    greet(z_peers + c_peers)
    moves = Moves(send, recv)
    sent = []

    def go(*args, **kw):
        move = moves.make(*args, **kw)
        move.start()
        sent.append(move)
        return move

    grad_in = []

    def send_grad(i):
        here = grad.at[i, span(me_c * local_len, local_len)]
        grad_in.append(
            [local.start(att_ref.at[i, :, span(me_c * 128, 128)], here)]
            + [
                go(att_ref.at[i, :, span((me_c ^ k) * 128, 128)], here, c_peers[k - 1])
                for k in range(1, nc)
            ]
        )

    near = []

    def send_term(index):
        ref, block = terms[index]
        near.append(
            [
                go(ref.at[block, x_c, :, :, left], near_in.at[index, 0], x_near),
                go(ref.at[block, far_c, :, :, left], near_in.at[index, 1], x_near),
                go(ref.at[block, y_c, :, :, right], near_in.at[index, 2], y_near),
                go(ref.at[block, far_c, :, :, right], near_in.at[index, 3], y_near),
            ]
        )

    send_grad(0)
    down_far = [
        go(down_y_ref, mine_in_ref.at[0], y_near),
        go(down_x_ref, mine_in_ref.at[1], x_near),
    ]
    send_grad(1)
    send_term(0)
    send_term(1)
    send_grad(2)
    send_term(2)
    z_pair, z_next = {"fsdp": me_z ^ 1}, {"fsdp": me_z ^ 2}

    def halve(ref, low, count, at):
        blocks = pl.ds(low, count)
        return [
            go(ref.at[blocks, me_z ^ 1], zpart_ref.at[0, pl.ds(at, count)], z_pair),
            go(ref.at[blocks, me_z ^ 3], zpart_ref.at[1, pl.ds(at, count)], z_pair),
        ]

    def halve_on(moves_in, own, count, at):
        for move in moves_in:
            move.wait_recv()
        for block in range(count):
            zsend_ref[at + block] = own(block) + zpart_ref[1, at + block]
        blocks = pl.ds(at, count)
        return go(zsend_ref.at[blocks], znext_ref.at[blocks], z_next)

    first = lax.broadcasted_iota(jnp.int32, (local_len, 128), 1) < HD
    place = lax.broadcasted_iota(jnp.int32, (local_len, 128), 0)
    weight_ref[...] = jnp.zeros_like(weight_ref)
    far_moves = []

    def sum_step(index):
        for move in near[index]:
            move.wait_recv()
        local.wait(own_in[index])
        local.wait(far_own[2 * index])
        local.wait(far_own[2 * index + 1])
        far_y[index] += near_in[index, 1]
        first_far = go(far_y.at[index], far_in.at[index, 0], y_near)
        far_x[index] += near_in[index, 3]
        far_moves.append((first_far, go(far_x.at[index], far_in.at[index, 1], x_near)))

    def sum_end(index):
        for move in far_moves[index]:
            move.wait_recv()
        own_ref[index, :, :, left] += near_in[index, 0] + far_in[index, 0]
        own_ref[index, :, :, right] += near_in[index, 2] + far_in[index, 1]

    for i in range(images):
        for copy in held[i]:
            local.wait(copy)
        local.wait(grad_in[i][0])
        for move in grad_in[i][1:]:
            move.wait_recv()
        prod = (grad[i].astype(F32) * o_all[i].astype(F32)).T
        for head in range(2):
            row_ref[8 * head : 8 * head + 8, :] = jnp.broadcast_to(
                jnp.sum(prod[HD * head : HD * (head + 1)], axis=0, keepdims=True),
                (8, prod.shape[1]),
            )
        dq_ref[...] = jnp.zeros_like(dq_ref)
        real = cnt_ref[i : i + 1, :]

        def attend(chunk):
            rows = span(chunk * local_len, local_len)
            q = qkv[i, :, 0:128]
            k = qkv[i, rows, 128:256] * SCALE
            v = qkv[i, rows, 256:384]
            do = grad[i]
            live = (place + chunk * local_len < real)[:, 0:1]
            dks, dvs = [], []
            for head in range(2):
                mask = first if head == 0 else jnp.logical_not(first)
                kh = jnp.where(mask, k, jnp.zeros_like(k))
                vh = jnp.where(mask, v, jnp.zeros_like(v))
                lse = lse_ref[i, 8 * head : 8 * head + 1, :]
                delta = row_ref[8 * head : 8 * head + 1, :]
                prob = jnp.where(live, jnp.exp(dot_nt(kh, q) - lse), 0.0)
                ds = (prob * (dot_nt(vh, do) - delta)).astype(BF)
                dvs.append(dot_nn(prob.astype(BF), do))
                dks.append(dot_nn(ds, q) * SCALE)
                dq_ref[...] += dot_tn(ds, kh)
            heads[i, rows, 128:256] = jnp.where(first, dks[0], dks[1]).astype(BF)
            heads[i, rows, 256:384] = jnp.where(first, dvs[0], dvs[1]).astype(BF)

        if i < 2:
            pl.loop(0, nc)(attend)
        if i == 2:
            pl.loop(0, nc // 2)(attend)
            sum_step(2)
            sum_end(0)
            sum_end(1)
            group_a = halve(own_ref, 0, 2, 0)
            pl.loop(nc // 2, nc)(attend)
        heads[i, :, 0:128] = dq_ref[...].astype(BF)
        if i == 0:
            local.wait(mine_in)
            for move in down_far:
                move.wait_recv()
            mine_ref[:, :, :, left] += mine_in_ref[0]
            mine_ref[:, :, :, right] += mine_in_ref[1]
            down_in = halve(mine_ref, 0, downs, len(terms))
        if i == 1:
            sum_step(0)
            sum_step(1)
            for index in range(3, len(terms)):
                send_term(index)
            down_next = halve_on(down_in, lambda b: mine_ref[b, me_z ^ 2], downs, len(terms))
        if i == 2:
            for index in range(3, len(terms)):
                sum_step(index)
        local.wait(x_in[i])

        @pl.loop(0, nc)
        def _(chunk):
            rows = span(chunk * local_len, local_len)
            weight_ref[...] += dot_tn(heads[i, rows], x_all[i % 2, rows])

        local.start(heads.at[i], heads_out.at[i])
        if i + 2 < images:
            x_in.append(local.start(x_ref.at[i + 2], x_all.at[i % 2]))
    sub = late_ref.shape[2]
    for z in range(nz):
        for j in range(LATE):
            late_ref[z, j] = weight_ref[pl.ds(j * 128 + z * sub, sub)].astype(BF)
    late_in = [
        go(late_ref.at[me_z ^ 1], lpart_ref.at[0], z_pair),
        go(late_ref.at[me_z ^ 3], lpart_ref.at[1], z_pair),
    ]
    a_next = halve_on(group_a, lambda b: own_ref[b, me_z ^ 2], 2, 0)
    for index in range(2, len(terms)):
        sum_end(index)
    group_b = halve(own_ref, 2, len(terms) - 2, 2)
    next_in = [down_next, a_next]
    for move in late_in:
        move.wait_recv()
    lsend_ref[...] = late_ref[me_z ^ 2] + lpart_ref[1]
    late_next = go(lsend_ref, lnext_ref, z_next)
    next_in.append(
        halve_on(group_b, lambda b: own_ref[2 + b, me_z ^ 2], len(terms) - 2, 2)
    )
    late_next.wait_recv()
    total = late_ref[me_z].astype(F32) + lpart_ref[0].astype(F32) + lnext_ref[...].astype(F32)
    late_out[...] = total.astype(BF)
    for move in next_in:
        move.wait_recv()
    for block in range(EARLY):
        if block < len(terms):
            total = own_ref[block, me_z].astype(F32)
        else:
            total = mine_ref[block - len(terms), me_z].astype(F32)
        total = total + zpart_ref[0, block].astype(F32) + znext_ref[block].astype(F32)
        early_ref[block] = total.astype(BF)
    local.finish()
    for move in sent:
        move.wait_send()


def backward_attention(
    qkv, o_heads, lse, grad_att, counts, term_out, term_up, down, down_y, down_x, x_all, nz, nc
):
    images, seq = qkv.shape[:2]
    local_len = seq // nc
    sub = term_up.shape[3]
    terms = 1 + term_up.shape[0]
    any_ = pl.BlockSpec(memory_space=pl.ANY)
    vmem = pl.BlockSpec(memory_space=pltpu.VMEM)
    return pl.pallas_call(
        functools.partial(backward_kernel, nz, nc),
        out_shape=(
            jax.ShapeDtypeStruct((EARLY, sub, D), BF),
            jax.ShapeDtypeStruct((LATE, sub, D), BF),
            jax.ShapeDtypeStruct((images, seq, 384), BF),
        ),
        in_specs=[
            any_,
            any_,
            vmem,
            any_,
            vmem,
            any_,
            any_,
            any_,
            any_,
            any_,
            any_,
        ],
        out_specs=(vmem, vmem, any_),
        scratch_shapes=[
            pltpu.VMEM((images, seq, 128), BF),
            pltpu.VMEM((images, seq, 384), BF),
            pltpu.VMEM((images, seq, 384), BF),
            pltpu.VMEM((images, seq, 128), BF),
            pltpu.VMEM((2, seq, D), BF),
            pltpu.VMEM((seq, 128), F32),
            pltpu.VMEM((16, seq), F32),
            pltpu.VMEM((384, D), F32),
            pltpu.VMEM((terms, nz, sub, D), BF),
            pltpu.VMEM((terms, nz, sub, D // 2), BF),
            pltpu.VMEM((terms, nz, sub, D // 2), BF),
            pltpu.VMEM((terms, 4, nz, sub, D // 2), BF),
            pltpu.VMEM((terms, 2, nz, sub, D // 2), BF),
            pltpu.VMEM((EARLY - terms, nz, sub, D), BF),
            pltpu.VMEM((2, EARLY - terms, nz, sub, D // 2), BF),
            pltpu.VMEM((2, EARLY, sub, D), BF),
            pltpu.VMEM((EARLY, sub, D), BF),
            pltpu.VMEM((EARLY, sub, D), BF),
            pltpu.VMEM((nz, LATE, sub, D), BF),
            pltpu.VMEM((2, LATE, sub, D), BF),
            pltpu.VMEM((LATE, sub, D), BF),
            pltpu.VMEM((LATE, sub, D), BF),
            pltpu.SemaphoreType.DMA((256,)),
            pltpu.SemaphoreType.DMA((256,)),
            pltpu.SemaphoreType.DMA((64,)),
        ],
        compiler_params=pltpu.CompilerParams(
            collective_id=2, has_side_effects=True, vmem_limit_bytes=61 << 20
        ),
        name="backward_attention",
    )(
        qkv,
        o_heads,
        lse,
        grad_att,
        counts,
        term_out,
        term_up,
        down,
        down_y,
        down_x,
        x_all,
    )


def tail_kernel(
    nz,
    nc,
    token_count,
    slot_blocks,
    early_hbm,
    late_hbm,
    heads_ref,
    wq_own_ref,
    wq_rows_ref,
    wq_ref,
    tokens_ref,
    mid_ref,
    gain_hbm,
    gains_hbm,
    rl_ref,
    rr_ref,
    sl_ref,
    sr_ref,
    ms_ref,
    tokens_out,
    gain_out,
    grad_hbm,
    left_hbm,
    right_hbm,
    weight_hbm,
    early_ref,
    late_ref,
    gain_ref,
    gains_ref,
    grad_out,
    left_out,
    right_out,
    tok,
    wq,
    x_buf,
    mid_buf,
    part,
    part_in,
    rl,
    rr,
    sl,
    sr,
    ms,
    update,
    square,
    square_in,
    gain_sum,
    gain_in,
    place_ref,
    g_ref,
    l_ref,
    g_all,
    send,
    recv,
    local_sems,
):
    me_z, me_c, me_t = (lax.axis_index(a) for a in ("fsdp", "context", "tensor"))
    images, local_len = tokens_ref.shape[:2]
    slots = g_ref.shape[0]
    x_c, y_c, far_c = me_c ^ 1, me_c ^ 2, me_c ^ 3
    core, x_near, y_near = {"tensor": 1 - me_t}, {"context": x_c}, {"context": y_c}
    above, below = {"fsdp": me_z + 1}, {"fsdp": me_z - 1}
    c_peers = [{"context": me_c ^ k} for k in range(1, nc)]
    group = [
        {"fsdp": me_z ^ (k // 2), "tensor": me_t ^ (k % 2)} for k in range(1, 2 * nz)
    ]
    rows_group = [(me_z ^ (k // nc), me_c ^ (k % nc)) for k in range(1, nz * nc)]
    others = [{"fsdp": z, "context": c} for z, c in rows_group[nc - 1 :] ]
    diagonal = [d for k, d in enumerate(others) if (k + nc) % nc]
    left, right = pl.ds(0, D // 2), pl.ds(D // 2, D // 2)
    local = Local(local_sems)
    small_in = [
        local.start(a, b)
        for a, b in (
            (early_hbm, early_ref),
            (late_hbm, late_ref),
            (gain_hbm, gain_ref),
            (gains_hbm, gains_ref),
        )
    ]
    width = wq.shape[1] // nc
    depth = wq_rows_ref.shape[0]
    wq_in = [local.start(wq_own_ref, wq.at[:, span(me_c * width, width)])]
    for m in (x_c, y_c, far_c):
        columns = span(m * width, width)
        wq_in.append(
            local.start(wq_rows_ref.at[:, columns], wq.at[span(me_z * depth, depth), columns])
        )
        for k in range(1, nz):
            at = (span(lax.rem(me_z + k, nz) * depth, depth), columns)
            wq_in.append(local.start(wq_ref.at[at], wq.at[at]))
    x_in = [local.start(tokens_ref.at[i], x_buf.at[i]) for i in range(images)]
    mid_in = [local.start(mid_ref.at[i], mid_buf.at[i]) for i in range(images)]
    state_in = [
        local.start(a, b) for a, b in ((rl_ref, rl), (sl_ref, sl), (sr_ref, sr), (ms_ref, ms))
    ]
    rr_in = [local.start(rr_ref.at[0], rr)]
    barrier = pltpu.get_barrier_semaphore()
    for device in group + c_peers + diagonal:
        pl.semaphore_signal(
            barrier, inc=1, device_id=device, device_id_type=pl.DeviceIdType.MESH
        )
    for copy in small_in:
        local.wait(copy)
    for slot in range(NBLK):
        block = jnp.clip(slot_blocks[slot] - LATE, 0, EARLY - 1)
        place_ref[slot] = early_ref[block]
    l_ref[:, me_t, me_c, me_z] = late_ref[...]
    for slot in range(slots):
        g_ref[slot, me_t, me_c, me_z] = place_ref[me_c * slots + slot]
    pl.semaphore_wait(barrier, len(group + c_peers + diagonal))
    moves = Moves(send, recv)
    sent = []

    def go(*args, **kw):
        move = moves.make(*args, **kw)
        move.start()
        sent.append(move)
        return move

    placed = []
    for k in range(1, nc):
        theirs = place_ref.at[pl.ds((me_c ^ k) * slots, slots)]
        placed.append(go(theirs, g_ref.at[:, me_t, me_c, me_z], c_peers[k - 1]))

    swapped = []

    def swap(piece, cond=None):
        swapped.append(go(piece, piece, core, cond=cond, recv_cond=cond))

    def along_fsdp(at):
        own = at(me_z)
        return [
            go(own, own, above, cond=me_z < nz - 1, recv_cond=me_z > 0),
            go(own, own, below, cond=me_z > 0, recv_cond=me_z < nz - 1),
        ]

    def onward(at, last, hop):
        up_z, down_z = me_z - hop, me_z + hop
        last[0].wait_recv()
        up = down = None
        if hop < nz - 1:
            piece = at(up_z)
            cond = jnp.logical_and(me_z < nz - 1, up_z >= 0)
            up = go(piece, piece, above, cond=cond, recv_cond=up_z - 1 >= 0)
        last[1].wait_recv()
        if hop < nz - 1:
            piece = at(down_z)
            cond = jnp.logical_and(me_z > 0, down_z <= nz - 1)
            down = go(piece, piece, below, cond=cond, recv_cond=down_z + 1 <= nz - 1)
        return [up, down], [(up_z, up_z >= 0), (down_z, down_z <= nz - 1)]

    def late_at(member):
        return lambda z: l_ref.at[:, me_t, member, z]

    def slot_at(slot):
        return lambda z: g_ref.at[slot, me_t, :, z]

    late_line = along_fsdp(late_at(me_c))
    tok_in = []

    def send_tok(i):
        there = tok.at[i, :, span(me_c * 384, 384)]
        tok_in.append(
            [local.start(heads_ref.at[i, span(me_c * local_len, local_len)], there)]
            + [
                go(
                    heads_ref.at[i, span((me_c ^ k) * local_len, local_len)],
                    there,
                    c_peers[k - 1],
                )
                for k in range(1, nc)
            ]
        )
    lines = []

    def slot_line(slot):
        lines.append(along_fsdp(slot_at(slot)))

    def late_on(hop):
        nonlocal late_line
        late_line, _ = onward(late_at(me_c), late_line, hop)

    send_tok(0)
    send_tok(1)
    late_on(1)
    for move in placed:
        move.wait_recv()
    late_on(2)
    for slot in range(slots):
        slot_line(slot)
    swap(g_ref.at[:, me_t, :, me_z])
    late_on(3)
    late_own = l_ref.at[:, me_t, me_c]
    near = [go(late_own, late_own, x_near), go(late_own, late_own, y_near)]
    swap(late_own)

    part_moves = []
    gain_out[...] = jnp.zeros_like(gain_out)
    square[...] = jnp.zeros_like(square)

    def project(i):
        local.wait(tok_in[i][0])
        for move in tok_in[i][1:]:
            move.wait_recv()
        part[i] = dot_nt(tok[i], wq[...]).astype(BF)
        part_moves.append(go(part.at[i], part_in.at[i], core))

    def norm_backward(i):
        part_moves[i].wait_recv()
        local.wait(x_in[i])
        local.wait(mid_in[i])

        @pl.loop(0, 2)
        def _(step):
            rows = span(step * (local_len // 2), local_len // 2)
            value = x_buf[i, rows]
            centred = value - jnp.mean(value, axis=-1, keepdims=True)
            inv_std = lax.rsqrt(jnp.mean(centred * centred, axis=-1, keepdims=True) + 1e-06)
            normed = centred * inv_std
            grad = part[i, rows].astype(F32) + part_in[i, rows].astype(F32)
            scaled = grad * gain_ref[0:1, :]
            inner = (
                scaled
                - jnp.mean(scaled, axis=-1, keepdims=True)
                - normed * jnp.mean(scaled * normed, axis=-1, keepdims=True)
            )
            mid_buf[i, rows] += inner * inv_std
            gain_out[0:1, :] += jnp.sum(grad * normed, axis=0, keepdims=True)

        local.start(mid_buf.at[i], tokens_out.at[i])

    def slots_on(hop):
        for slot in range(slots):
            lines[slot], here = onward(slot_at(slot), lines[slot], hop)
        for z, cond in here:
            swap(g_ref.at[:, me_t, :, z], cond)

    slots_on(1)
    near[0].wait_recv()
    piece = l_ref.at[:, me_t, x_c, :, :, left]
    far = [go(piece, piece, y_near)]
    near[1].wait_recv()
    piece = l_ref.at[:, me_t, y_c, :, :, right]
    far.append(go(piece, piece, x_near))
    send_tok(2)
    swap(l_ref.at[:, me_t, x_c])
    swap(l_ref.at[:, me_t, y_c])
    for copy in wq_in:
        local.wait(copy)
    project(0)
    norm_backward(0)
    slots_on(2)
    for move in far:
        move.wait_recv()
    swap(l_ref.at[:, me_t, far_c])
    project(1)
    norm_backward(1)
    last = []
    for slot in range(slots):
        _, here = onward(slot_at(slot), lines[slot], 3)
        last.append([])
        for z, cond in here:
            piece = g_ref.at[slot, me_t, :, z]
            last[slot].append(go(piece, piece, core, cond=cond, recv_cond=cond))
    project(2)
    for move in swapped:
        move.wait_recv()
    for copy in state_in:
        local.wait(copy)
    offset = me_t * (D // 2) + me_z * rl.shape[1]
    mine = span(offset, rl.shape[1])

    def step(slot):
        for move in last[slot]:
            move.wait_recv()
        block = slot_blocks[me_c * slots + slot]
        late = l_ref[jnp.clip(block, 0, LATE - 1)]
        g_all[...] = jnp.where(block < LATE, late, g_ref[slot]).reshape(D, D)
        rows = g_all[mine, :]
        grad_out[slot] = rows.astype(F32)
        left_out[slot] = 0.5 * sl[slot] + 0.5 / token_count * dot_nt(rows, g_all[...])
        right_out[slot] = 0.5 * sr[slot] + 0.5 / token_count * dot_tn(g_all[:, mine], g_all[...])
        for a, b in ((grad_out, grad_hbm), (left_out, left_hbm), (right_out, right_hbm)):
            local.start(a.at[slot], b.at[slot])
        inner = dot_nn(rl[slot].astype(BF), g_all[...]).astype(BF)
        local.wait(rr_in[slot])
        update[slot] = dot_nn(inner, rr[...].astype(BF))
        if slot + 1 < slots:
            rr_in.append(local.start(rr_ref.at[slot + 1], rr))
        total = jnp.sum(update[slot] * update[slot], axis=0, keepdims=True)
        total = jnp.sum(total, axis=1, keepdims=True)
        square[slot : slot + 1, :] = jnp.broadcast_to(total, (1, 128))

    step(0)
    norm_backward(2)
    gain_sum[...] = gains_ref[...]
    gain_sum[0:1, :] = gain_out[0:1, :]
    gain_moves = []
    for k, (z, c) in enumerate(rows_group):
        theirs = span((z * nc + c) // 2 * 128, 128)
        gain_moves.append(
            go(gain_sum.at[:, theirs], gain_in.at[k], {"fsdp": z, "context": c})
        )
    for slot in range(1, slots):
        step(slot)
    square_moves = [
        go(square, square_in.at[k], group[k]) for k in range(len(group))
    ]
    for move in square_moves:
        move.wait_recv()
    for slot in range(slots):
        total = square[slot : slot + 1, 0:1]
        for k in range(len(group)):
            total = total + square_in[k, slot : slot + 1, 0:1]
        ms[slot] -= lax.rsqrt(total / (D * D) + 1e-06) * update[slot]
        local.start(ms.at[slot], weight_hbm.at[slot])
    total = gain_sum[:, span((me_z * nc + me_c) // 2 * 128, 128)]
    for k, move in enumerate(gain_moves):
        move.wait_recv()
        total = total + gain_in[k]
    gain_out[:, 0:128] = total
    local.finish()
    for move in sent:
        move.wait_send()


def tail(
    block_of,
    early,
    late,
    grad_heads,
    wq,
    wq_rows,
    wq_all,
    tokens,
    grad_middle,
    gain,
    gain_terms,
    root_left,
    root_right,
    stat_left,
    stat_right,
    master,
    token_count,
    nz,
    nc,
    nt,
):
    images, local_len = tokens.shape[:2]
    sub = early.shape[1]
    slots, row_count = root_left.shape[:2]
    any_ = pl.BlockSpec(memory_space=pl.ANY)
    vmem = pl.BlockSpec(memory_space=pltpu.VMEM)
    state = jax.ShapeDtypeStruct((slots, row_count, D), F32)
    shape = (slots, nt, nc, nz, sub, D)
    return pl.pallas_call(
        functools.partial(tail_kernel, nz, nc, token_count),
        out_shape=(
            jax.ShapeDtypeStruct((images, local_len, D), F32),
            jax.ShapeDtypeStruct((8, D), F32),
            state,
            state,
            state,
            state,
        ),
        in_specs=[pl.BlockSpec(memory_space=pltpu.SMEM)] + [any_] * 15,
        out_specs=(any_, vmem, any_, any_, any_, any_),
        scratch_shapes=[
            pltpu.VMEM((EARLY, sub, D), BF),
            pltpu.VMEM((LATE, sub, D), BF),
            pltpu.VMEM((4, D), F32),
            pltpu.VMEM((8, D), F32),
            pltpu.VMEM((slots, row_count, D), F32),
            pltpu.VMEM((slots, row_count, D), F32),
            pltpu.VMEM((slots, row_count, D), F32),
            pltpu.VMEM((images, local_len, nc * 384), BF),
            pltpu.VMEM((D, nc * 384), BF),
            pltpu.VMEM((images, local_len, D), F32),
            pltpu.VMEM((images, local_len, D), F32),
            pltpu.VMEM((images, local_len, D), BF),
            pltpu.VMEM((images, local_len, D), BF),
            pltpu.VMEM((slots, row_count, D), F32),
            pltpu.VMEM((D, D), F32),
            pltpu.VMEM((slots, row_count, D), F32),
            pltpu.VMEM((slots, row_count, D), F32),
            pltpu.VMEM((slots, row_count, D), F32),
            pltpu.VMEM((slots, row_count, D), F32),
            pltpu.VMEM((8, 128), F32),
            pltpu.VMEM((2 * nz - 1, 8, 128), F32),
            pltpu.VMEM((8, D), F32),
            pltpu.VMEM((nz * nc - 1, 8, 128), F32),
            pltpu.VMEM((NBLK, sub, D), BF),
            pltpu.VMEM(shape, BF),
            pltpu.VMEM((LATE, nt, nc, nz, sub, D), BF),
            pltpu.VMEM((D, D), BF),
            pltpu.SemaphoreType.DMA((160,)),
            pltpu.SemaphoreType.DMA((160,)),
            pltpu.SemaphoreType.DMA((64,)),
        ],
        compiler_params=pltpu.CompilerParams(
            collective_id=3, has_side_effects=True, vmem_limit_bytes=61 << 20
        ),
        name="tail",
    )(
        block_of,
        early,
        late,
        grad_heads,
        wq,
        wq_rows,
        wq_all,
        tokens,
        grad_middle,
        gain,
        gain_terms,
        root_left,
        root_right,
        stat_left,
        stat_right,
        master,
    )


def finish_kernel(count, *refs):
    ins, outs, bufs = refs[:count], refs[count : 2 * count], refs[2 * count : 3 * count]
    in_sems, out_sems = refs[3 * count :]
    pieces = [(i, k) for i in range(ins[0].shape[0]) for k in range(count)]
    loads, stores = [], []
    for n, (i, k) in enumerate(pieces):
        loads.append(pltpu.make_async_copy(ins[k].at[i], bufs[k].at[i], in_sems.at[n]))
        loads[-1].start()
    for n, (i, k) in enumerate(pieces):
        loads[n].wait()
        stores.append(pltpu.make_async_copy(bufs[k].at[i], outs[k].at[i], out_sems.at[n]))
        stores[-1].start()
    for store in stores:
        store.wait()


def finish(arrays):
    any_ = pl.BlockSpec(memory_space=pl.ANY)
    count = len(arrays)
    pieces = count * arrays[0].shape[0]
    size = sum(a.size * a.dtype.itemsize for a in arrays)
    return pl.pallas_call(
        functools.partial(finish_kernel, count),
        out_shape=tuple(jax.ShapeDtypeStruct(a.shape, a.dtype) for a in arrays),
        in_specs=[any_] * count,
        out_specs=(any_,) * count,
        scratch_shapes=[pltpu.VMEM(a.shape, a.dtype) for a in arrays]
        + [pltpu.SemaphoreType.DMA((pieces,)), pltpu.SemaphoreType.DMA((pieces,))],
        compiler_params=pltpu.CompilerParams(vmem_limit_bytes=62 << 20),
        cost_estimate=pl.CostEstimate(flops=0, bytes_accessed=2 * size, transcendentals=0),
        name="finish",
    )(*arrays)


def xor_permute(value, axis, step):
    size = lax.axis_size(axis)
    return lax.ppermute(value, axis, [(j, j ^ step) for j in range(size)])


def xor_order(pieces, index):
    bit = 1
    while bit < len(pieces):
        odd = (index & bit) > 0
        pieces = [jnp.where(odd, pieces[j ^ bit], pieces[j]) for j in range(len(pieces))]
        bit *= 2
    return pieces


def sum_tensor(value):
    low = lax.optimization_barrier(value.astype(BF))
    return low.astype(F32) + xor_permute(low, "tensor", 1).astype(F32)


def gather_fsdp(value):
    size = lax.axis_size("fsdp")
    if size > 4:
        return lax.all_gather(value, "fsdp", axis=0, tiled=False)
    pieces = [value] + [
        lax.ppermute(value, "fsdp", [(j, (j - k) % size) for j in range(size)])
        for k in range(1, size)
    ]
    doubled = jnp.stack(pieces + pieces[:-1])
    start = lax.rem(size - lax.axis_index("fsdp"), size)
    return lax.dynamic_slice_in_dim(doubled, start, size, 0)


def sum_fsdp(value):
    size = lax.axis_size("fsdp")
    if size > 4:
        return lax.psum(value, "fsdp")
    total = value
    for k in range(1, size):
        total = total + lax.ppermute(value, "fsdp", [(j, (j - k) % size) for j in range(size)])
    return total


def grad_gather_plain(block_of, early, late, nz, nc):
    me_c, me_t = (lax.axis_index(a) for a in ("context", "tensor"))
    sub = early.shape[1]
    half_width = nc * nz * sub
    slot_count = NBLK // nc
    slots_of = block_of.reshape(nc, slot_count)

    def slots_for(k):
        blocks = lax.dynamic_index_in_dim(slots_of, me_c ^ k, 0, keepdims=False)
        return early[jnp.clip(blocks - LATE, 0, EARLY - 1)]

    placed = [slots_for(0)] + [xor_permute(slots_for(k), "context", k) for k in range(1, nc)]
    placed = jnp.stack(xor_order(placed, me_c), axis=1)
    placed = lax.all_gather(placed, "fsdp", axis=2, tiled=False)
    placed = placed.reshape(slot_count, half_width, D)
    placed_other = xor_permute(placed, "tensor", 1)
    both = jnp.stack([placed, placed_other], axis=1)
    early_full = jnp.where(me_t > 0, both[:, ::-1], both).reshape(slot_count, D, D)

    late = late.reshape(-1, D)
    late = lax.psum_scatter(late, "fsdp", scatter_dimension=0, tiled=True)
    late = lax.all_gather(late, ("context", "fsdp"), axis=0, tiled=True)
    late = jnp.swapaxes(late.reshape(nc * nz, LATE, sub, D), 0, 1).reshape(LATE, half_width, D)
    late_other = xor_permute(late, "tensor", 1)
    both = jnp.stack([late, late_other], axis=1)
    late_full = jnp.where(me_t > 0, both[:, ::-1], both).reshape(LATE, D, D)

    mine = lax.dynamic_index_in_dim(slots_of, me_c, 0, keepdims=False)
    return jnp.where(
        (mine < LATE)[:, None, None], late_full[jnp.clip(mine, 0, LATE - 1)], early_full
    )


def to_natural(value, me_t, half_len):
    parts = value.reshape((-1, half_len) + value.shape[1:])
    return jnp.where(me_t > 0, parts[::-1], parts).reshape(value.shape)


def forward_plain(tokens, gain, key_mask, w_qkv, w_out, w_up, w_down):
    images, local_len = tokens.shape[:2]
    nc, nt = (lax.axis_size(a) for a in ("context", "tensor"))
    me_c, me_t = (lax.axis_index(a) for a in ("context", "tensor"))
    cols = w_qkv.shape[2] // nc
    half_len = local_len // nt
    wq_part = lax.dynamic_slice_in_dim(w_qkv, me_c * cols, cols, 2)
    wq = gather_fsdp(wq_part).reshape(D, 3 * cols)

    def two_stage(weight, member_axis, fsdp_axis):
        width = weight.shape[member_axis] // nc
        part = lax.dynamic_slice_in_dim(weight, me_c * width, width, member_axis)
        part = lax.all_gather(part, "fsdp", axis=fsdp_axis, tiled=True)
        return lax.all_gather(part, "context", axis=member_axis, tiled=True)

    out_full = two_stage(w_out, 0, 1)
    up_full = two_stage(w_up, 1, 0)
    down_full = two_stage(w_down, 0, 1)

    counts = jnp.sum(key_mask, axis=1)
    real = counts
    for k in range(1, nc):
        real = real + xor_permute(counts, "context", k)
    position = (
        (me_c ^ jnp.arange(nc))[:, None, None] * local_len
        + (me_t ^ jnp.arange(nt))[None, :, None] * half_len
        + jnp.arange(half_len)[None, None, :]
    ).reshape(-1)
    live = position[None, :] < real[:, None]
    bias = jnp.where(live, 0.0, -1e30).astype(F32)
    live_col = jnp.broadcast_to(live[:, :, None].astype(F32), (images, SEQ, 128))

    normed1, inv_std1, pre_norm1 = norm_fwd(tokens, gain)
    normed1_low = pre_norm1.astype(BF)

    x_all, qkv, out_heads, log_sums, attended = [], [], [], [], []
    for i in range(images):
        mine = lax.dynamic_slice_in_dim(normed1_low[i], me_t * half_len, half_len, 0)
        held = jnp.stack([mine] + [xor_permute(mine, "context", k) for k in range(1, nc)])
        other = xor_permute(held, "tensor", 1)
        x_i = jnp.stack([held, other], axis=1).reshape(SEQ, D)
        qkv_i = dot_nn(x_i, wq).astype(BF)
        o_i, lse_i = attn_fwd(qkv_i, bias[i][None])
        chunks = o_i.reshape(nc, local_len, 2 * HD)
        moved = [to_natural(chunks[0], me_t, half_len)] + [
            to_natural(xor_permute(chunks[k], "context", k), me_t, half_len) for k in range(1, nc)
        ]
        attended.append(jnp.concatenate(xor_order(moved, me_c), axis=-1))
        x_all.append(x_i)
        qkv.append(qkv_i)
        out_heads.append(o_i)
        log_sums.append(lse_i)
    attended = jnp.stack(attended)
    return (
        jnp.stack(x_all),
        jnp.stack(qkv),
        jnp.stack(out_heads),
        jnp.stack(log_sums),
        attended,
        live_col,
        wq,
        out_full,
        up_full,
        down_full,
        normed1,
        inv_std1,
    )


def backward_plain(qkv, out_heads, log_sums, grad_att, live_col, early, wq):
    images, local_len = grad_att.shape[:2]
    nz, nc, nt = (lax.axis_size(a) for a in ("fsdp", "context", "tensor"))
    me_c, me_t = (lax.axis_index(a) for a in ("context", "tensor"))
    cols = grad_att.shape[2] // nc
    half_len = local_len // nt
    sub = early.shape[2]
    grad_heads = []
    grad_tok = []
    for i in range(images):
        pieces = [grad_att[i, :, j * cols : (j + 1) * cols] for j in range(nc)]
        pieces = [to_natural(p, me_t, half_len) for p in xor_order(pieces, me_c)]
        grad_i = jnp.concatenate(
            [pieces[0]] + [xor_permute(pieces[k], "context", k) for k in range(1, nc)]
        )
        g_i = attn_bwd(qkv[i], grad_i, out_heads[i], log_sums[i], live_col[i])
        chunks = g_i.reshape(nc, local_len, 3 * cols)
        moved = [to_natural(chunks[0], me_t, half_len)] + [
            to_natural(xor_permute(chunks[k], "context", k), me_t, half_len) for k in range(1, nc)
        ]
        grad_tok.append(jnp.stack(xor_order(moved, me_c), axis=1))
        grad_heads.append(g_i)
    grad_tok = jnp.stack(grad_tok)
    wq_all = lax.all_gather(wq, "context", axis=0, tiled=False)
    grad_n1 = sum_tensor(
        jnp.einsum("isjc,jdc->isd", grad_tok, wq_all, preferred_element_type=F32)
    )
    early = lax.psum_scatter(
        jnp.swapaxes(early, 0, 1).reshape(-1, D),
        "fsdp",
        scatter_dimension=0,
        tiled=True,
    ).reshape(EARLY, sub, D)
    return jnp.stack(grad_heads), grad_n1, early


def per_device(
    tokens,
    cotangent,
    gains,
    w_qkv,
    w_out,
    w_up,
    w_down,
    key_mask,
    owner,
    stat_left,
    stat_right,
    root_left,
    root_right,
    master,
    gain_state,
):
    images, local_len = tokens.shape[:2]
    tok_rows = images * local_len
    nz, nc, nt = (lax.axis_size(a) for a in ("fsdp", "context", "tensor"))
    me_z, me_c, me_t = (lax.axis_index(a) for a in ("fsdp", "context", "tensor"))
    half_width = w_qkv.shape[2]
    hidden = w_up.shape[1]
    up_blocks = hidden // half_width
    cols = half_width // nc
    fast = nz == 4 and nc == 4 and nt == 2 and images == 3
    if fast:
        wq_rows = jnp.swapaxes(w_qkv.reshape(-1, 3, nc, cols), 1, 2).reshape(-1, nc * 3 * cols)
        counts = jnp.pad(jnp.sum(key_mask, axis=1), (0, 8 - images))
        counts = jnp.broadcast_to(counts[:, None], (8, 128))
        (
            x_all,
            qkv,
            out_heads,
            log_sums,
            attended,
            counts,
            wq,
            out_full,
            up_full,
            down_part,
        ) = forward_attention(
            tokens, gains, counts, wq_rows, w_out, w_up, w_down, nz, nc
        )
    else:
        (
            x_all,
            qkv,
            out_heads,
            log_sums,
            attended,
            live_col,
            wq,
            out_full,
            up_full,
            down_full,
            normed1,
            inv_std1,
        ) = forward_plain(tokens, gains[0], key_mask, w_qkv, w_out, w_up, w_down)

    sub = half_width // nc // nz
    onehot = (owner[:, None] == jnp.arange(NBLK, dtype=jnp.int32)[None, :]).astype(jnp.int32)
    block_of = jnp.sum(onehot * jnp.arange(NBLK, dtype=jnp.int32)[:, None], axis=0)

    if fast:
        (
            output,
            grad_middle,
            grad_att,
            term_out,
            term_up,
            down,
            down_y,
            down_x,
            wq_all,
            gain_terms,
        ) = feed_forward(
            attended, out_full, up_full, down_part, tokens, cotangent, gains, wq_rows, nz, nc
        )
        term_out = term_out.reshape(1, nc, nz, sub, D)
        term_up = term_up.reshape(-1, nc, nz, sub, D)
        down = down.reshape(-1, nz, sub, D)
        down_y = down_y.reshape(-1, nz, sub, D // 2)
        down_x = down_x.reshape(-1, nz, sub, D // 2)
    else:
        branch_attn = sum_tensor(
            jnp.einsum("ish,hd->isd", attended, out_full, preferred_element_type=F32)
        )
        middle = tokens + gains[2] * branch_attn
        normed2, inv_std2, pre_norm2 = norm_fwd(middle, gains[1])
        normed2_low = pre_norm2.astype(BF)
        pre_act = jnp.einsum("isd,df->isf", normed2_low, up_full, preferred_element_type=F32)
        act_val, act_slope = gelu_parts(pre_act)
        act_low = act_val.astype(BF)
        branch_mlp = sum_tensor(
            jnp.einsum("isf,fd->isd", act_low, down_full, preferred_element_type=F32)
        )
        output = middle + gains[3] * branch_mlp

        grad_mlp = (gains[3] * cotangent).astype(BF)
        grad_hidden = jnp.einsum("isd,fd->isf", grad_mlp, down_full, preferred_element_type=F32)
        grad_pre = (grad_hidden * act_slope).astype(BF)
        grad_n2 = sum_tensor(
            jnp.einsum("isf,df->isd", grad_pre, up_full, preferred_element_type=F32)
        )
        middle_part, grad_gain2 = norm_back(grad_n2, gains[1], normed2, inv_std2)
        grad_middle = cotangent + middle_part
        grad_branch = (gains[2] * grad_middle).astype(BF)
        grad_att = jnp.einsum(
            "isd,hd->ish", grad_branch, out_full, preferred_element_type=F32
        ).astype(BF)

        def early_term(left, right):
            term = dot_tn(left.reshape(tok_rows, -1), right.reshape(tok_rows, D)).astype(BF)
            return term.reshape(-1, nc, nz, sub, D)

        def early_sum(term):
            return lax.psum_scatter(
                jnp.swapaxes(term, 0, 1).reshape(-1, D), "context", scatter_dimension=0, tiled=True
            ).reshape(-1, nz, sub, D)

        term_out = early_term(attended, grad_branch)
        term_up = early_term(grad_pre, normed2_low)
        down = early_sum(early_term(act_low, grad_mlp))
        grad_gain3 = jnp.sum(grad_middle * branch_attn, axis=(0, 1))
        grad_gain4 = jnp.sum(cotangent * branch_mlp, axis=(0, 1))
        blank = jnp.zeros_like(grad_gain2)
        gain_terms = jnp.stack([blank, grad_gain2, grad_gain3, grad_gain4] + [blank] * 4, axis=0)
    tokens_all = images * nz * SEQ
    if fast:
        early, late, grad_heads = backward_attention(
            qkv, out_heads, log_sums, grad_att, counts, term_out, term_up, down, down_y, down_x, x_all, nz, nc
        )
        grad_tokens, gain_sum, grad_mine, left_new, right_new, weight_new = tail(
            block_of,
            early,
            late,
            grad_heads,
            wq,
            wq_rows,
            wq_all,
            tokens,
            grad_middle,
            gains,
            gain_terms,
            root_left[:, 0],
            root_right,
            stat_left[:, 0],
            stat_right[:, 0],
            master[:, 0],
            tokens_all,
            nz,
            nc,
            nt,
        )
        output, grad_tokens, grad_mine, left_new, right_new, weight_new = finish(
            (output, grad_tokens, grad_mine, left_new, right_new, weight_new)
        )
    else:
        early = jnp.concatenate([early_sum(term_out), early_sum(term_up), down], axis=0)
        grad_heads, grad_n1, early = backward_plain(
            qkv, out_heads, log_sums, grad_att, live_col, early, wq
        )
        term_qkv = jnp.einsum("isk,isd->kd", grad_heads, x_all, preferred_element_type=F32)
        late = jnp.swapaxes(term_qkv.astype(BF).reshape(LATE, nz, sub, D), 0, 1)
        grad_full = grad_gather_plain(block_of, early, late, nz, nc)
        input_part, grad_gain1 = norm_back(grad_n1, gains[0], normed1, inv_std1)
        grad_tokens = grad_middle + input_part
        row_count = half_width // nz
        row_offset = me_t * half_width + me_z * row_count
        grad_mine = lax.dynamic_slice_in_dim(grad_full, row_offset, row_count, 1)
        left_new = 0.5 * stat_left[:, 0] + 0.5 / tokens_all * jnp.einsum(
            "sra,sba->srb", grad_mine, grad_full, preferred_element_type=F32
        )
        grad_cols = lax.dynamic_slice_in_dim(grad_full, row_offset, row_count, 2)
        right_new = 0.5 * stat_right[:, 0] + 0.5 / tokens_all * jnp.einsum(
            "sar,sab->srb", grad_cols, grad_full, preferred_element_type=F32
        )
        inner_prod = jnp.einsum(
            "sra,sab->srb", root_left[:, 0].astype(BF), grad_full, preferred_element_type=F32
        ).astype(BF)
        update = jnp.einsum(
            "srb,sbc->src", inner_prod, root_right.astype(BF), preferred_element_type=F32
        )
        square_sum = jnp.sum(update * update, axis=(1, 2))
        square_sum = sum_fsdp(square_sum + xor_permute(square_sum, "tensor", 1))
        factor = lax.rsqrt(square_sum / (D * D) + 1e-06)
        weight_new = master[:, 0] - factor[:, None, None] * update

        gain_terms = gain_terms[:4].at[0].set(grad_gain1)
        gain_sum = gain_terms
        step = 1
        while step < nc:
            gain_sum = gain_sum + xor_permute(gain_sum, "context", step)
            step *= 2
        gain_sum = sum_fsdp(gain_sum)

    share_width = gain_state.shape[1]
    gain_index = lax.axis_index(("fsdp", "context"))
    if fast:
        at = lax.rem(gain_index * share_width, 128)
        gain_grad = lax.dynamic_slice(gain_sum, (0, at), (4, share_width))
    else:
        gain_grad = lax.dynamic_slice_in_dim(
            gain_sum, gain_index * share_width, share_width, 1
        )
    gain_mine = lax.dynamic_slice_in_dim(gains, gain_index * share_width, share_width, 1)
    state_new = 0.5 * gain_state + 0.5 * gain_grad * gain_grad / tokens_all
    gain_new = gain_mine - 0.1 * gain_grad * lax.rsqrt(tokens_all * state_new)
    return (
        output,
        grad_tokens,
        grad_mine.astype(F32)[:, None],
        left_new[:, None],
        right_new[:, None],
        weight_new[:, None],
        gain_grad,
        state_new,
        gain_new,
    )


def solution(mesh):
    return jax.shard_map(
        per_device,
        mesh=mesh,
        in_specs=(
            P("fsdp", "context", None),
            P("fsdp", "context", None),
            P(),
            P("fsdp", None, "tensor"),
            P("tensor", "fsdp"),
            P("fsdp", "tensor"),
            P("tensor", "fsdp"),
            P("fsdp", "context"),
            P(),
            P("context", "tensor", "fsdp", None),
            P("context", "tensor", "fsdp", None),
            P("context", "tensor", "fsdp", None),
            P("context", None, None),
            P("context", "tensor", "fsdp", None),
            P(None, ("fsdp", "context")),
        ),
        out_specs=(
            P("fsdp", "context", None),
            P("fsdp", "context", None),
            P("context", "tensor", "fsdp", None),
            P("context", "tensor", "fsdp", None),
            P("context", "tensor", "fsdp", None),
            P("context", "tensor", "fsdp", None),
            P(None, ("fsdp", "context")),
            P(None, ("fsdp", "context")),
            P(None, ("fsdp", "context")),
        ),
        check_vma=False,
    )
```

```python
import functools

import jax
import jax.numpy as jnp
from jax import lax
from jax.experimental import pallas as pl
from jax.experimental.pallas import tpu as pltpu
from jax.sharding import PartitionSpec as P

D = 1024
HD = 64
SEQ = 1408
NBLK = 12
LATE = 3
EARLY = NBLK - LATE
BF = jnp.bfloat16
F32 = jnp.float32
SCALE = HD ** (-0.5)


def norm_fwd(field_in, gain_vec):
    centred = field_in - jnp.mean(field_in, axis=-1, keepdims=True)
    inv_std = lax.rsqrt(jnp.mean(centred * centred, axis=-1, keepdims=True) + 1e-06)
    normed = centred * inv_std
    return (normed, inv_std, normed * gain_vec)


def norm_back(grad_out, gain_vec, normed, inv_std):
    scaled = grad_out * gain_vec
    inner_sum = (
        scaled
        - jnp.mean(scaled, axis=-1, keepdims=True)
        - normed * jnp.mean(scaled * normed, axis=-1, keepdims=True)
    )
    return (inner_sum * inv_std, jnp.sum(grad_out * normed, axis=(0, 1)))


def gelu_parts(field_in):
    normal_cdf = 0.5 * (1.0 + lax.erf(field_in * 0.7071067811865476))
    normal_pdf = jnp.exp(-0.5 * field_in * field_in) * 0.3989422804014327
    return (field_in * normal_cdf, normal_cdf + field_in * normal_pdf)


def dot_nt(a, b):
    return lax.dot_general(a, b, (((1,), (1,)), ((), ())), preferred_element_type=F32)


def dot_tn(a, b):
    return lax.dot_general(a, b, (((0,), (0,)), ((), ())), preferred_element_type=F32)


def dot_nn(a, b):
    return lax.dot_general(a, b, (((1,), (0,)), ((), ())), preferred_element_type=F32)


def attn_fwd_kernel(q_ref, k_ref, v_ref, bias_ref, o_ref, lse_ref):
    q = q_ref[...] * SCALE
    k = k_ref[...]
    v = v_ref[...]
    bias = bias_ref[...]
    first = lax.broadcasted_iota(jnp.int32, q.shape, 1) < HD
    outs, sums = [], []
    for head in range(2):
        mask = first if head == 0 else jnp.logical_not(first)
        scores = dot_nt(jnp.where(mask, q, jnp.zeros_like(q)), k) + bias
        peak = jnp.max(scores, axis=-1, keepdims=True)
        expo = jnp.exp(scores - peak)
        total = jnp.sum(expo, axis=-1, keepdims=True)
        outs.append(dot_nn(expo.astype(BF), v) / total)
        sums.append(peak + jnp.log(total))
    o_ref[...] = jnp.where(first, outs[0], outs[1]).astype(BF)
    lse_ref[...] = jnp.where(first, sums[0], sums[1])


def attn_fwd(qkv, bias_row):
    rows = qkv.shape[0]
    bq = rows // 4
    return pl.pallas_call(
        attn_fwd_kernel,
        grid=(rows // bq,),
        out_shape=(
            jax.ShapeDtypeStruct((rows, 128), BF),
            jax.ShapeDtypeStruct((rows, 128), F32),
        ),
        in_specs=[
            pl.BlockSpec((bq, 128), lambda i: (i, 0)),
            pl.BlockSpec((rows, 128), lambda i: (0, 1)),
            pl.BlockSpec((rows, 128), lambda i: (0, 2)),
            pl.BlockSpec((1, rows), lambda i: (0, 0)),
        ],
        out_specs=(
            pl.BlockSpec((bq, 128), lambda i: (i, 0)),
            pl.BlockSpec((bq, 128), lambda i: (i, 0)),
        ),
        compiler_params=pltpu.CompilerParams(vmem_limit_bytes=40 << 20),
        cost_estimate=pl.CostEstimate(
            flops=4 * rows * rows * 512, bytes_accessed=rows * 2048, transcendentals=2 * rows * rows
        ),
        name="attn_fwd",
    )(qkv, qkv, qkv, bias_row)


def attn_bwd_kernel(q_ref, k_ref, v_ref, do_ref, o_ref, lse_ref, live_ref, out_ref, dq_ref, row_ref):
    step = pl.program_id(0)
    chunk = k_ref.shape[0]

    @pl.when(step == 0)
    def _():
        row_ref[0:128, :] = lse_ref[...].T
        prod = do_ref[...].astype(F32) * o_ref[...].astype(F32)
        prod_t = prod.T
        row_ref[128:136, :] = jnp.broadcast_to(
            jnp.sum(prod_t[0:HD], axis=0, keepdims=True), (8, prod_t.shape[1])
        )
        row_ref[136:144, :] = jnp.broadcast_to(
            jnp.sum(prod_t[HD:128], axis=0, keepdims=True), (8, prod_t.shape[1])
        )
        dq_ref[...] = jnp.zeros_like(dq_ref)

    q = q_ref[...]
    k = k_ref[...] * SCALE
    v = v_ref[...]
    do = do_ref[...]
    live = live_ref[:, 0:1] > 0
    first = lax.broadcasted_iota(jnp.int32, k.shape, 1) < HD
    dks, dvs = [], []
    for head in range(2):
        mask = first if head == 0 else jnp.logical_not(first)
        kh = jnp.where(mask, k, jnp.zeros_like(k))
        vh = jnp.where(mask, v, jnp.zeros_like(v))
        lse = row_ref[64 * head : 64 * head + 1, :]
        delta = row_ref[128 + 8 * head : 129 + 8 * head, :]
        prob = jnp.where(live, jnp.exp(dot_nt(kh, q) - lse), 0.0)
        ds = (prob * (dot_nt(vh, do) - delta)).astype(BF)
        dvs.append(dot_nn(prob.astype(BF), do))
        dks.append(dot_nn(ds, q) * SCALE)
        dq_ref[...] += dot_tn(ds, kh)
    at = pl.ds(pl.multiple_of(step * chunk, chunk), chunk)
    out_ref[at, 128:256] = jnp.where(first, dks[0], dks[1]).astype(BF)
    out_ref[at, 256:384] = jnp.where(first, dvs[0], dvs[1]).astype(BF)

    @pl.when(step == pl.num_programs(0) - 1)
    def _():
        out_ref[:, 0:128] = dq_ref[...].astype(BF)


def attn_bwd(qkv, grad, out, lse, live_col):
    rows = qkv.shape[0]
    chunk = rows // 4
    return pl.pallas_call(
        attn_bwd_kernel,
        grid=(rows // chunk,),
        out_shape=jax.ShapeDtypeStruct((rows, 384), BF),
        in_specs=[
            pl.BlockSpec((rows, 128), lambda i: (0, 0)),
            pl.BlockSpec((chunk, 128), lambda i: (i, 1)),
            pl.BlockSpec((chunk, 128), lambda i: (i, 2)),
            pl.BlockSpec((rows, 128), lambda i: (0, 0)),
            pl.BlockSpec((rows, 128), lambda i: (0, 0)),
            pl.BlockSpec((rows, 128), lambda i: (0, 0)),
            pl.BlockSpec((chunk, 128), lambda i: (i, 0)),
        ],
        out_specs=pl.BlockSpec((rows, 384), lambda i: (0, 0)),
        scratch_shapes=[pltpu.VMEM((rows, 128), F32), pltpu.VMEM((144, rows), F32)],
        compiler_params=pltpu.CompilerParams(vmem_limit_bytes=50 << 20),
        cost_estimate=pl.CostEstimate(
            flops=10 * rows * rows * 512, bytes_accessed=rows * 4096, transcendentals=2 * rows * rows
        ),
        name="attn_bwd",
    )(qkv, qkv, qkv, grad, out, lse, live_col)


class Moves:
    def __init__(self, send_sems, recv_sems):
        self.send_sems, self.recv_sems, self.count = send_sems, recv_sems, 0

    def make(self, src, dst, device, cond=None, recv_cond=None):
        index = self.count
        self.count += 1
        return Move(self, index, src, dst, device, cond, recv_cond)


class Move:
    def __init__(self, moves, index, src, dst, device, cond, recv_cond):
        self.args = (src, dst, moves.send_sems.at[index], moves.recv_sems.at[index])
        self.device, self.cond, self.recv_cond = device, cond, recv_cond

    def copy(self):
        return pltpu.make_async_remote_copy(
            *self.args, device_id=self.device, device_id_type=pl.DeviceIdType.MESH
        )

    def when(self, cond, act):
        if cond is None:
            act()
        else:
            pl.when(cond)(act)

    def start(self):
        self.when(self.cond, lambda: self.copy().start())

    def wait_recv(self):
        self.when(self.recv_cond, lambda: self.copy().wait_recv())

    def wait_send(self):
        self.when(self.cond, lambda: self.copy().wait_send())


def greet(devices):
    barrier = pltpu.get_barrier_semaphore()
    for device in devices:
        pl.semaphore_signal(
            barrier, inc=1, device_id=device, device_id_type=pl.DeviceIdType.MESH
        )
    pl.semaphore_wait(barrier, len(devices))


def span(start, size):
    return pl.ds(pl.multiple_of(start, size & -size), size)


class Local:
    def __init__(self, sems):
        self.sems, self.count, self.open = sems, 0, []

    def start(self, src, dst):
        copy = pltpu.make_async_copy(src, dst, self.sems.at[self.count])
        self.count += 1
        copy.start()
        self.open.append(copy)
        return copy

    def wait(self, copy):
        copy.wait()
        self.open = [c for c in self.open if c is not copy]

    def finish(self):
        for copy in self.open:
            copy.wait()
        self.open = []


def spread_plane(go, ref_of, me_c, cond=None):
    own = ref_of(me_c, None)
    return [go(own, own, {"context": me_c ^ 1}), go(own, own, {"context": me_c ^ 2})]


def spread_plane_on(go, ref_of, me_c, near):
    near[0].wait_recv()
    piece = ref_of(me_c ^ 1, 0)
    first = go(piece, piece, {"context": me_c ^ 2})
    near[1].wait_recv()
    piece = ref_of(me_c ^ 2, 1)
    second = go(piece, piece, {"context": me_c ^ 1})
    return [first, second]


def forward_kernel(
    nz,
    nc,
    tokens_ref,
    gain_ref,
    count_ref,
    wq_ref,
    wout_ref,
    wup_ref,
    wdown_ref,
    x_out,
    qkv_out,
    o_out,
    lse_out,
    att_out,
    cnt_out,
    wq_out,
    out_full,
    up_full,
    down_part,
    tok,
    x_all,
    qkv,
    o_all,
    lse_all,
    wq,
    counts,
    stage_up,
    stage_out,
    stage_down,
    send,
    recv,
    local_sems,
):
    me_z, me_c, me_t = (lax.axis_index(a) for a in ("fsdp", "context", "tensor"))
    images, local_len = att_out.shape[0], att_out.shape[2]
    half = local_len // 2
    seq = x_all.shape[1]
    core = {"tensor": 1 - me_t}
    z_peers = [{"fsdp": lax.rem(me_z + k, nz)} for k in range(1, nz)]
    c_peers = [{"context": me_c ^ k} for k in range(1, nc)]
    local = Local(local_sems)
    token_in = [
        local.start(tokens_ref.at[i, span(me_t * half, half)], tok.at[i]) for i in range(images)
    ]
    depth = wq_ref.shape[0]
    hid = wup_ref.shape[1] // nc
    staged = [
        local.start(wup_ref.at[:, span(me_c * hid, hid)], stage_up),
        local.start(wout_ref, stage_out),
        local.start(wdown_ref.at[span(me_c * hid, hid)], stage_down),
    ]
    wq_part = wq_ref.at[:, span(me_c * 384, 384)]
    wq_own = local.start(wq_part, wq.at[span(me_z * depth, depth)])
    greet(z_peers + c_peers + [core])
    moves = Moves(send, recv)
    sent = []

    def go(*args, **kw):
        move = moves.make(*args, **kw)
        move.start()
        sent.append(move)
        return move

    wq_in = [go(wq_part, wq.at[span(me_z * depth, depth)], peer) for peer in z_peers]
    counts[me_c] = count_ref[...]
    count_in = [go(count_ref, counts.at[me_c], peer) for peer in c_peers]

    def to_line(index, src, dst):
        local.wait(staged[index])
        local_copy = local.start(src, dst)
        return [local_copy] + [go(src, dst, peer) for peer in z_peers]


    def x_piece(i):
        def at(member, part):
            rows = span(member * local_len + me_t * half, half)
            if part is None:
                return x_all.at[i, rows]
            return x_all.at[i, rows, pl.ds(part * (D // 2), D // 2)]

        return at

    swaps = [[] for _ in range(images)]
    near, far = [], []

    def swap(i, member, part=None):
        piece = x_piece(i)(member, part)
        swaps[i].append(go(piece, piece, core))

    def normalize(i):
        local.wait(token_in[i])
        value = tok[i]
        centred = value - jnp.mean(value, axis=-1, keepdims=True)
        inv_std = lax.rsqrt(jnp.mean(centred * centred, axis=-1, keepdims=True) + 1e-06)
        x_all[i, span(me_c * local_len + me_t * half, half)] = (
            centred * inv_std * gain_ref[0:1, :]
        ).astype(BF)

    def send_near(i):
        near.append(spread_plane(go, x_piece(i), me_c))
        swap(i, me_c)

    def send_far(i):
        far.append(spread_plane_on(go, x_piece(i), me_c, near[i]))
        swap(i, me_c ^ 1)
        swap(i, me_c ^ 2)

    normalize(0)
    send_near(0)
    normalize(1)
    send_near(1)
    normalize(2)
    send_far(0)
    send_near(2)
    local.wait(wq_own)
    for move in wq_in:
        move.wait_recv()
    up_in = to_line(
        0,
        stage_up,
        up_full.at[me_c, span(me_z * depth, depth)],
    )
    local.start(wq, wq_out)
    for move in count_in:
        move.wait_recv()
    total = counts[0]
    for k in range(1, nc):
        total = total + counts[k]
    cnt_out[...] = total

    first = lax.broadcasted_iota(jnp.int32, (local_len, 128), 1) < HD
    place = lax.broadcasted_iota(jnp.int32, (1, seq), 1)

    def up_piece(k):
        start = lax.rem(me_z - k + nz, nz) * depth

        def at(member, part):
            if part is None:
                return up_full.at[member, span(start, depth)]
            return up_full.at[member, span(start + part * (depth // 2), depth // 2)]

        return at

    up_near, up_far = [], []

    def up_step(k):
        if k == 0:
            local.wait(up_in[0])
        else:
            up_in[k].wait_recv()
        up_near.append(spread_plane(go, up_piece(k), me_c))

    def up_step_on(k):
        up_far.extend(spread_plane_on(go, up_piece(k), me_c, up_near[k]))

    att_in = []
    for i in range(images):
        for part in range(2):
            far[i][part].wait_recv()
            swap(i, me_c ^ 3, part)
        for move in swaps[i]:
            move.wait_recv()
        local.start(x_all.at[i], x_out.at[i])

        @pl.loop(0, nc)
        def _(chunk):
            rows = span(chunk * local_len, local_len)
            qkv[i, rows] = dot_nn(x_all[i, rows], wq[...]).astype(BF)

        local.start(qkv.at[i], qkv_out.at[i])
        if i == 0:
            send_far(1)
        bias = jnp.where(place < cnt_out[i : i + 1, 0:1], 0.0, -1e30)
        def attend(chunk):
            rows = span(chunk * local_len, local_len)
            q = qkv[i, rows, 0:128] * SCALE
            k = qkv[i, :, 128:256]
            v = qkv[i, :, 256:384]
            outs, sums = [], []
            for head in range(2):
                mask = first if head == 0 else jnp.logical_not(first)
                scores = dot_nt(jnp.where(mask, q, jnp.zeros_like(q)), k) + bias
                peak = jnp.max(scores, axis=-1, keepdims=True)
                expo = jnp.exp(scores - peak)
                norm = jnp.sum(expo, axis=-1, keepdims=True)
                outs.append(dot_nn(expo.astype(BF), v) / norm)
                sums.append(peak + jnp.log(norm))
            o_all[i, rows] = jnp.where(first, outs[0], outs[1]).astype(BF)
            lse_all[rows] = jnp.where(first, sums[0], sums[1])

        if i == 2:
            up_step_on(0)
            up_step_on(1)
        pl.loop(0, nc)(attend)
        if i == 0:
            send_far(2)
            up_step(0)

        mine = att_out.at[i, me_c]
        for k in range(1, nc):
            att_in.append(
                go(o_all.at[i, span((me_c ^ k) * local_len, local_len)], mine, c_peers[k - 1])
            )
        local.start(o_all.at[i, span(me_c * local_len, local_len)], mine)
        local.start(o_all.at[i], o_out.at[i])
        sums_t = lse_all[...].T
        for head in range(2):
            lse_out[i, 8 * head : 8 * head + 8, :] = jnp.broadcast_to(
                sums_t[HD * head : HD * head + 1], (8, seq)
            )
        if i == 0:
            up_step(1)
            out_in = to_line(1, stage_out, out_full.at[me_z])
        if i == 1:
            up_step(2)
            up_step(3)
            down_in = to_line(
                2,
                stage_down,
                down_part.at[me_z],
            )
    up_step_on(2)
    up_step_on(3)
    for move in up_far:
        move.wait_recv()
    for move in att_in:
        move.wait_recv()
    for move in out_in[1:] + down_in[1:]:
        move.wait_recv()
    local.finish()
    for move in sent:
        move.wait_send()


def forward_attention(tokens, gain, counts, wq_part, w_out, w_up, w_down, nz, nc):
    images, local_len = tokens.shape[:2]
    seq = nc * local_len
    cols, hid = w_out.shape[0], w_up.shape[1]
    any_ = pl.BlockSpec(memory_space=pl.ANY)
    vmem = pl.BlockSpec(memory_space=pltpu.VMEM)
    return pl.pallas_call(
        functools.partial(forward_kernel, nz, nc),
        out_shape=(
            jax.ShapeDtypeStruct((images, seq, D), BF),
            jax.ShapeDtypeStruct((images, seq, 384), BF),
            jax.ShapeDtypeStruct((images, seq, 128), BF),
            jax.ShapeDtypeStruct((images, 16, seq), F32),
            jax.ShapeDtypeStruct((images, nc, local_len, cols // nc), BF),
            jax.ShapeDtypeStruct((8, 128), jnp.int32),
            jax.ShapeDtypeStruct((D, 384), BF),
            jax.ShapeDtypeStruct((nz, cols, D // nz), BF),
            jax.ShapeDtypeStruct((nc, D, hid // nc), BF),
            jax.ShapeDtypeStruct((nz, hid // nc, D // nz), BF),
        ),
        in_specs=[any_, vmem, vmem, any_, any_, any_, any_],
        out_specs=(any_, any_, any_, vmem, any_, vmem, any_, any_, any_, any_),
        scratch_shapes=[
            pltpu.VMEM((images, local_len // 2, D), F32),
            pltpu.VMEM((images, seq, D), BF),
            pltpu.VMEM((images, seq, 384), BF),
            pltpu.VMEM((images, seq, 128), BF),
            pltpu.VMEM((seq, 128), F32),
            pltpu.VMEM((D, 384), BF),
            pltpu.VMEM((nc, 8, 128), jnp.int32),
            pltpu.VMEM((w_up.shape[0], hid // nc), BF),
            pltpu.VMEM(w_out.shape, BF),
            pltpu.VMEM((hid // nc, w_down.shape[1]), BF),
            pltpu.SemaphoreType.DMA((96,)),
            pltpu.SemaphoreType.DMA((96,)),
            pltpu.SemaphoreType.DMA((32,)),
        ],
        compiler_params=pltpu.CompilerParams(
            collective_id=1, has_side_effects=True, vmem_limit_bytes=56 << 20
        ),
        name="forward_attention",
    )(tokens, gain, counts, wq_part, w_out, w_up, w_down)


def feed_forward_kernel(
    nz,
    nc,
    att_ref,
    wout_ref,
    wup_ref,
    wdown_ref,
    tokens_ref,
    cot_ref,
    gains_ref,
    wq_ref,
    output_out,
    mid_out,
    gatt_out,
    tout_out,
    tup_out,
    own_out,
    fary_out,
    farx_out,
    wq_out,
    gain_out,
    att,
    wout,
    wup,
    wdown,
    tok,
    cot,
    normed_low,
    act,
    slope,
    low,
    first_own,
    first_in,
    second_own,
    second_in,
    third_in,
    stage,
    term,
    near_in,
    gatt,
    send,
    recv,
    local_sems,
):
    me_z, me_c, me_t = (lax.axis_index(a) for a in ("fsdp", "context", "tensor"))
    z_peers = [{"fsdp": lax.rem(me_z + k, nz)} for k in range(1, nz)]
    images, local_len = tok.shape[:2]
    hid = wdown_ref.shape[1]
    depth_o = wdown_ref.shape[2]
    x_c, y_c, far_c = me_c ^ 1, me_c ^ 2, me_c ^ 3
    core, x_near, y_near = {"tensor": 1 - me_t}, {"context": x_c}, {"context": y_c}
    left, right = pl.ds(0, D // 2), pl.ds(D // 2, D // 2)
    half = local_len // 2
    local = Local(local_sems)
    down_own = [
        local.start(wdown_ref.at[z], wdown.at[span(me_c * hid, hid), pl.ds(z * depth_o, depth_o)])
        for z in range(nz)
    ]
    att_in = [
        local.start(att_ref.at[:, c], att.at[:, :, pl.ds(c * 128, 128)]) for c in range(nc)
    ] + [local.start(wout_ref.at[z], wout.at[:, pl.ds(z * depth_o, depth_o)]) for z in range(nz)]
    cot_in = local.start(cot_ref, cot)
    tok_in = local.start(tokens_ref, tok)
    up_in = [
        local.start(wup_ref.at[c], wup.at[:, pl.ds(c * hid, hid)]) for c in range(nc)
    ]

    def down_piece(member, part):
        rows = span(member * hid, hid)
        return wdown.at[rows] if part is None else wdown.at[rows, pl.ds(part * (D // 2), D // 2)]

    greet([core, x_near, y_near] + z_peers)
    for copy in down_own:
        local.wait(copy)
    moves = Moves(send, recv)
    sent = []

    def go(*args, **kw):
        move = moves.make(*args, **kw)
        move.start()
        sent.append(move)
        return move

    down_near = [
        go(down_piece(me_c, part), down_piece(me_c, part), device)
        for part, device in (
            (0, x_near),
            (1, y_near),
            (1, x_near),
            (0, y_near),
        )
    ]
    depth = wq_ref.shape[0]
    wq_in = []
    for k in range(1, nc):
        columns = span((me_c ^ k) * 384, 384)
        there = wq_out.at[span(me_z * depth, depth), columns]
        wq_in += [go(wq_ref.at[:, columns], there, peer) for peer in z_peers]
    for copy in att_in:
        local.wait(copy)

    @pl.loop(0, images)
    def _(i):
        first_own[i] = dot_nn(att[i], wout[...]).astype(BF)

    first = go(first_own, first_in, core)
    local.wait(cot_in)

    @pl.loop(0, images)
    def _(i):
        low[i] = (gains_ref[3:4, :] * cot[i]).astype(BF)

    local.wait(tok_in)
    first.wait_recv()

    @pl.loop(0, 2 * images)
    def _(step):
        i, rows = step // 2, span(lax.rem(step, 2) * half, half)
        branch = first_own[i, rows].astype(F32) + first_in[i, rows].astype(F32)
        value = tok[i, rows] + gains_ref[2:3, :] * branch
        tok[i, rows] = value
        centred = value - jnp.mean(value, axis=-1, keepdims=True)
        inv_std = lax.rsqrt(jnp.mean(centred * centred, axis=-1, keepdims=True) + 1e-06)
        normed_low[i, rows] = (centred * inv_std * gains_ref[1:2, :]).astype(BF)

    for copy in up_in:
        local.wait(copy)
    width = 512

    @pl.loop(0, images)
    def _(i):
        @pl.loop(0, wup.shape[1] // width)
        def _(step):
            cols = span(step * width, width)
            value = dot_nn(normed_low[i], wup[:, cols])
            cdf = 0.5 * (1.0 + lax.erf(value * 0.7071067811865476))
            pdf = jnp.exp(-0.5 * value * value) * 0.3989422804014327
            act[i, :, cols] = (value * cdf).astype(BF)
            slope[i, :, cols] = (cdf + value * pdf).astype(BF)

    down_near[0].wait_recv()
    x_piece = down_piece(x_c, 0)
    down_far = [go(x_piece, x_piece, y_near)]
    down_near[1].wait_recv()
    y_piece = down_piece(y_c, 1)
    down_far.append(go(y_piece, y_piece, x_near))
    blocks = term.shape[0]
    chunk_rows = term.shape[2]

    @pl.loop(0, blocks)
    def _(j):
        cols = span(j * width, width)
        total = jnp.zeros((width, D), F32)
        for i in range(images):
            total += dot_tn(act[i, :, cols], low[i])
        for c in range(nc):
            term[j, c] = total[c * chunk_rows : (c + 1) * chunk_rows].astype(BF)

    near = [
        go(term.at[:, x_c, :, left], near_in.at[0], x_near),
        go(term.at[:, far_c, :, left], near_in.at[1], x_near),
        go(term.at[:, y_c, :, right], near_in.at[2], y_near),
        go(term.at[:, far_c, :, right], near_in.at[3], y_near),
    ]
    for move in down_near[2:]:
        move.wait_recv()

    def back_down(member):
        columns = span(member * hid, hid)

        @pl.loop(0, images)
        def _(i):
            value = dot_nt(low[i], wdown[columns, :]) * slope[i, :, columns].astype(F32)
            slope[i, :, columns] = value.astype(BF)

    copies = []

    def up_term(k):
        if k >= 2:
            local.wait(copies[k - 2])
        cols = span((me_c ^ k) * width, width)
        total = jnp.zeros((width, D), F32)
        for i in range(images):
            total += dot_tn(slope[i, :, cols], normed_low[i])
        stage[k % 2] = total.astype(BF)
        copies.append(local.start(stage.at[k % 2], tup_out.at[cols]))

    @pl.loop(0, 3)
    def _(k):
        back_down(me_c ^ k)

    for k in range(3):
        up_term(k)
    for move in down_far:
        move.wait_recv()
    back_down(far_c)

    @pl.loop(0, images)
    def _(i):
        second_own[i] = dot_nn(act[i], wdown[...]).astype(BF)

    second = go(second_own, second_in, core)
    first.wait_send()
    sent.remove(first)
    gain_out[...] = jnp.zeros_like(gain_out)

    @pl.loop(0, 2 * images)
    def _(step):
        i, rows = step // 2, span(lax.rem(step, 2) * half, half)
        branch = first_own[i, rows].astype(F32) + first_in[i, rows].astype(F32)
        first_in[i, rows] = branch.astype(BF)

    @pl.loop(0, images)
    def _(i):
        first_own[i] = dot_nt(slope[i], wup[...]).astype(BF)

    third = go(first_own, third_in, core)

    up_term(3)
    second.wait_recv()
    third.wait_recv()

    @pl.loop(0, 2 * images)
    def _(step):
        i, rows = step // 2, span(lax.rem(step, 2) * half, half)
        value = tok[i, rows]
        centred = value - jnp.mean(value, axis=-1, keepdims=True)
        inv_std = lax.rsqrt(jnp.mean(centred * centred, axis=-1, keepdims=True) + 1e-06)
        normed = centred * inv_std
        branch = second_own[i, rows].astype(F32) + second_in[i, rows].astype(F32)
        tok[i, rows] = value + gains_ref[3:4, :] * branch
        cotangent = cot[i, rows]
        gain_out[3:4, :] += jnp.sum(cotangent * branch, axis=0, keepdims=True)
        grad = first_own[i, rows].astype(F32) + third_in[i, rows].astype(F32)
        gain_out[1:2, :] += jnp.sum(grad * normed, axis=0, keepdims=True)
        scaled = grad * gains_ref[1:2, :]
        inner = (
            scaled
            - jnp.mean(scaled, axis=-1, keepdims=True)
            - normed * jnp.mean(scaled * normed, axis=-1, keepdims=True)
        )
        grad = cotangent + inner * inv_std
        cot[i, rows] = grad
        gain_out[2:3, :] += jnp.sum(grad * first_in[i, rows].astype(F32), axis=0, keepdims=True)
        low[i, rows] = (gains_ref[2:3, :] * grad).astype(BF)

    local.start(tok, output_out)
    local.start(cot, mid_out)

    @pl.loop(0, images)
    def _(i):
        gatt[i] = dot_nt(low[i], wout[...]).astype(BF)

    for c in range(nc):
        local.start(gatt.at[:, :, pl.ds(c * 128, 128)], gatt_out.at[:, c])
    total = jnp.zeros((att.shape[2], D), F32)
    for i in range(images):
        total += dot_tn(att[i], low[i])
    for copy in copies[-2:]:
        local.wait(copy)
    stage[0] = total.astype(BF)
    local.start(stage.at[0], tout_out)
    for move in near:
        move.wait_recv()
    for move in near:
        move.wait_send()
        sent.remove(move)
    term[:, me_c, :, left] += near_in[0]
    term[:, me_c, :, right] += near_in[2]
    term[:, y_c, :, left] += near_in[1]
    term[:, x_c, :, right] += near_in[3]
    for move in wq_in:
        move.wait_recv()
    local.start(term.at[:, me_c], own_out)
    local.start(term.at[:, y_c, :, left], fary_out)
    local.start(term.at[:, x_c, :, right], farx_out)
    local.finish()
    for move in sent:
        move.wait_send()


def feed_forward(attended, out_full, up_full, down_part, tokens, cotangent, gains, wq_rows, nz, nc):
    images, local_len = tokens.shape[:2]
    cols, hid = out_full.shape[1], nc * up_full.shape[2]
    blocks = hid // 512
    piece = (blocks, 512 // nc)
    any_ = pl.BlockSpec(memory_space=pl.ANY)
    vmem = pl.BlockSpec(memory_space=pltpu.VMEM)
    rows = (images, local_len)
    return pl.pallas_call(
        functools.partial(feed_forward_kernel, nz, nc),
        out_shape=(
            jax.ShapeDtypeStruct(rows + (D,), F32),
            jax.ShapeDtypeStruct(rows + (D,), F32),
            jax.ShapeDtypeStruct((images, nc, local_len, cols // nc), BF),
            jax.ShapeDtypeStruct((cols, D), BF),
            jax.ShapeDtypeStruct((hid, D), BF),
            jax.ShapeDtypeStruct(piece + (D,), BF),
            jax.ShapeDtypeStruct(piece + (D // 2,), BF),
            jax.ShapeDtypeStruct(piece + (D // 2,), BF),
            jax.ShapeDtypeStruct((D, nc * 384), BF),
            jax.ShapeDtypeStruct((8, D), F32),
        ),
        in_specs=[any_] * 6 + [vmem, any_],
        out_specs=(any_,) * 9 + (vmem,),
        scratch_shapes=[
            pltpu.VMEM(rows + (cols,), BF),
            pltpu.VMEM((cols, D), BF),
            pltpu.VMEM((D, hid), BF),
            pltpu.VMEM((hid, D), BF),
            pltpu.VMEM(rows + (D,), F32),
            pltpu.VMEM(rows + (D,), F32),
            pltpu.VMEM(rows + (D,), BF),
            pltpu.VMEM(rows + (hid,), BF),
            pltpu.VMEM(rows + (hid,), BF),
            pltpu.VMEM(rows + (D,), BF),
            pltpu.VMEM(rows + (D,), BF),
            pltpu.VMEM(rows + (D,), BF),
            pltpu.VMEM(rows + (D,), BF),
            pltpu.VMEM(rows + (D,), BF),
            pltpu.VMEM(rows + (D,), BF),
            pltpu.VMEM((2, 512, D), BF),
            pltpu.VMEM((blocks, nc, 512 // nc, D), BF),
            pltpu.VMEM((4, blocks, 512 // nc, D // 2), BF),
            pltpu.VMEM(rows + (cols,), BF),
            pltpu.SemaphoreType.DMA((32,)),
            pltpu.SemaphoreType.DMA((32,)),
            pltpu.SemaphoreType.DMA((48,)),
        ],
        compiler_params=pltpu.CompilerParams(
            collective_id=4, has_side_effects=True, vmem_limit_bytes=62 << 20
        ),
        name="feed_forward",
    )(attended, out_full, up_full, down_part, tokens, cotangent, gains, wq_rows)


def backward_kernel(
    nz,
    nc,
    qkv_ref,
    o_ref,
    lse_ref,
    att_ref,
    cnt_ref,
    term_out_ref,
    term_up_ref,
    down_ref,
    down_y_ref,
    down_x_ref,
    x_ref,
    early_out,
    late_hbm,
    heads_out,
    grad,
    heads,
    qkv,
    o_all,
    x_all,
    dq_ref,
    row_ref,
    weight_ref,
    own_ref,
    far_y,
    far_x,
    near_in,
    far_in,
    mine_ref,
    mine_in_ref,
    zpart_ref,
    zsend_ref,
    znext_ref,
    late_ref,
    lpart_ref,
    lsend_ref,
    lnext_ref,
    early_ref,
    late_out,
    send,
    recv,
    local_sems,
):
    me_z, me_c, me_t = (lax.axis_index(a) for a in ("fsdp", "context", "tensor"))
    images, local_len = att_ref.shape[0], att_ref.shape[2]
    x_c, y_c, far_c = me_c ^ 1, me_c ^ 2, me_c ^ 3
    x_near, y_near = {"context": x_c}, {"context": y_c}
    z_peers = [{"fsdp": lax.rem(me_z + k, nz)} for k in range(1, nz)]
    c_peers = [{"context": me_c ^ k} for k in range(1, nc)]
    left, right = pl.ds(0, D // 2), pl.ds(D // 2, D // 2)
    ups, downs = term_up_ref.shape[0], down_ref.shape[0]
    terms = [(term_out_ref, 0)] + [(term_up_ref, j) for j in range(ups)]
    local = Local(local_sems)
    greet(z_peers + c_peers)
    moves = Moves(send, recv)
    sent = []

    def go(*args, **kw):
        move = moves.make(*args, **kw)
        move.start()
        sent.append(move)
        return move

    grad_in = []

    def send_grad(i):
        here = grad.at[i, span(me_c * local_len, local_len)]
        grad_in.append(
            [local.start(att_ref.at[i, me_c], here)]
            + [
                go(att_ref.at[i, me_c ^ k], here, c_peers[k - 1])
                for k in range(1, nc)
            ]
        )

    near = []

    def send_term(index):
        ref, block = terms[index]
        near.append(
            [
                go(ref.at[block, x_c, :, :, left], near_in.at[index, 0], x_near),
                go(ref.at[block, far_c, :, :, left], near_in.at[index, 1], x_near),
                go(ref.at[block, y_c, :, :, right], near_in.at[index, 2], y_near),
                go(ref.at[block, far_c, :, :, right], near_in.at[index, 3], y_near),
            ]
        )

    send_grad(0)
    held = [
        [local.start(a.at[i], b.at[i]) for a, b in ((qkv_ref, qkv), (o_ref, o_all))]
        for i in range(images)
    ]
    x_in = [local.start(x_ref.at[i], x_all.at[i % 2]) for i in range(2)]
    own_in, far_own = [], []
    for index, (ref, block) in enumerate(terms):
        own_in.append(local.start(ref.at[block, me_c], own_ref.at[index]))
        far_own.append(local.start(ref.at[block, y_c, :, :, left], far_y.at[index]))
        far_own.append(local.start(ref.at[block, x_c, :, :, right], far_x.at[index]))
    mine_in = local.start(down_ref, mine_ref)
    down_far = [
        go(down_y_ref, mine_in_ref.at[0], y_near),
        go(down_x_ref, mine_in_ref.at[1], x_near),
    ]
    send_grad(1)
    send_term(0)
    send_term(1)
    send_grad(2)
    send_term(2)
    z_pair, z_next = {"fsdp": me_z ^ 1}, {"fsdp": me_z ^ 2}

    def halve(ref, low, count, at):
        blocks = pl.ds(low, count)
        return [
            go(ref.at[blocks, me_z ^ 1], zpart_ref.at[0, pl.ds(at, count)], z_pair),
            go(ref.at[blocks, me_z ^ 3], zpart_ref.at[1, pl.ds(at, count)], z_pair),
        ]

    def halve_on(moves_in, own, count, at):
        for move in moves_in:
            move.wait_recv()
        for block in range(count):
            zsend_ref[at + block] = own(block) + zpart_ref[1, at + block]
        blocks = pl.ds(at, count)
        return go(zsend_ref.at[blocks], znext_ref.at[blocks], z_next)

    first = lax.broadcasted_iota(jnp.int32, (local_len, 128), 1) < HD
    place = lax.broadcasted_iota(jnp.int32, (local_len, 128), 0)
    weight_ref[...] = jnp.zeros_like(weight_ref)
    far_moves = []

    def sum_step(index):
        for move in near[index]:
            move.wait_recv()
        local.wait(own_in[index])
        local.wait(far_own[2 * index])
        local.wait(far_own[2 * index + 1])
        far_y[index] += near_in[index, 1]
        first_far = go(far_y.at[index], far_in.at[index, 0], y_near)
        far_x[index] += near_in[index, 3]
        far_moves.append((first_far, go(far_x.at[index], far_in.at[index, 1], x_near)))

    def sum_end(index):
        for move in far_moves[index]:
            move.wait_recv()
        own_ref[index, :, :, left] += near_in[index, 0] + far_in[index, 0]
        own_ref[index, :, :, right] += near_in[index, 2] + far_in[index, 1]

    for i in range(images):
        for copy in held[i]:
            local.wait(copy)
        local.wait(grad_in[i][0])
        for move in grad_in[i][1:]:
            move.wait_recv()
        prod = (grad[i].astype(F32) * o_all[i].astype(F32)).T
        for head in range(2):
            row_ref[8 * head : 8 * head + 8, :] = jnp.broadcast_to(
                jnp.sum(prod[HD * head : HD * (head + 1)], axis=0, keepdims=True),
                (8, prod.shape[1]),
            )
        dq_ref[...] = jnp.zeros_like(dq_ref)
        real = cnt_ref[i : i + 1, :]

        def attend(chunk):
            rows = span(chunk * local_len, local_len)
            q = qkv[i, :, 0:128]
            k = qkv[i, rows, 128:256] * SCALE
            v = qkv[i, rows, 256:384]
            do = grad[i]
            live = (place + chunk * local_len < real)[:, 0:1]
            dks, dvs = [], []
            for head in range(2):
                mask = first if head == 0 else jnp.logical_not(first)
                kh = jnp.where(mask, k, jnp.zeros_like(k))
                vh = jnp.where(mask, v, jnp.zeros_like(v))
                lse = lse_ref[i, 8 * head : 8 * head + 1, :]
                delta = row_ref[8 * head : 8 * head + 1, :]
                prob = jnp.where(live, jnp.exp(dot_nt(kh, q) - lse), 0.0)
                ds = (prob * (dot_nt(vh, do) - delta)).astype(BF)
                dvs.append(dot_nn(prob.astype(BF), do))
                dks.append(dot_nn(ds, q) * SCALE)
                dq_ref[...] += dot_tn(ds, kh)
            heads[i, rows, 128:256] = jnp.where(first, dks[0], dks[1]).astype(BF)
            heads[i, rows, 256:384] = jnp.where(first, dvs[0], dvs[1]).astype(BF)

        if i < 2:
            pl.loop(0, nc)(attend)
        if i == 2:
            pl.loop(0, nc // 2)(attend)
            sum_step(2)
            sum_end(0)
            sum_end(1)
            group_a = halve(own_ref, 0, 2, 0)
            pl.loop(nc // 2, nc)(attend)
        heads[i, :, 0:128] = dq_ref[...].astype(BF)
        if i == 0:
            local.wait(mine_in)
            for move in down_far:
                move.wait_recv()
            mine_ref[:, :, :, left] += mine_in_ref[0]
            mine_ref[:, :, :, right] += mine_in_ref[1]
            down_in = halve(mine_ref, 0, downs, len(terms))
        if i == 1:
            sum_step(0)
            sum_step(1)
            for index in range(3, len(terms)):
                send_term(index)
            down_next = halve_on(down_in, lambda b: mine_ref[b, me_z ^ 2], downs, len(terms))
        if i == 2:
            for index in range(3, len(terms)):
                sum_step(index)
            sum_end(2)
            group_m = halve(own_ref, 2, 1, 2)
        local.wait(x_in[i])

        @pl.loop(0, nc)
        def _(chunk):
            rows = span(chunk * local_len, local_len)
            weight_ref[...] += dot_tn(heads[i, rows], x_all[i % 2, rows])

        local.start(heads.at[i], heads_out.at[i])
        if i + 2 < images:
            x_in.append(local.start(x_ref.at[i + 2], x_all.at[i % 2]))
    sub = late_ref.shape[2]
    for z in range(nz):
        for j in range(LATE):
            late_ref[z, j] = weight_ref[pl.ds(j * 128 + z * sub, sub)].astype(BF)
    late_in = [
        go(late_ref.at[me_z ^ 1], lpart_ref.at[0], z_pair),
        go(late_ref.at[me_z ^ 3], lpart_ref.at[1], z_pair),
    ]
    a_next = halve_on(group_a, lambda b: own_ref[b, me_z ^ 2], 2, 0)
    for index in range(3, len(terms)):
        sum_end(index)
    group_b = halve(own_ref, 3, len(terms) - 3, 3)
    m_next = halve_on(group_m, lambda b: own_ref[2, me_z ^ 2], 1, 2)
    next_in = [down_next, a_next, m_next]
    for move in late_in:
        move.wait_recv()
    lsend_ref[...] = late_ref[me_z ^ 2] + lpart_ref[1]
    late_next = go(lsend_ref, lnext_ref, z_next)
    next_in.append(
        halve_on(group_b, lambda b: own_ref[3 + b, me_z ^ 2], len(terms) - 3, 3)
    )
    late_next.wait_recv()
    total = late_ref[me_z].astype(F32) + lpart_ref[0].astype(F32) + lnext_ref[...].astype(F32)
    late_out[...] = total.astype(BF)
    local.start(late_out, late_hbm)
    for move in next_in:
        move.wait_recv()
    for block in range(EARLY):
        if block < len(terms):
            total = own_ref[block, me_z].astype(F32)
        else:
            total = mine_ref[block - len(terms), me_z].astype(F32)
        total = total + zpart_ref[0, block].astype(F32) + znext_ref[block].astype(F32)
        early_ref[block] = total.astype(BF)
    local.start(early_ref, early_out)
    local.finish()
    for move in sent:
        move.wait_send()


def backward_attention(
    qkv, o_heads, lse, grad_att, counts, term_out, term_up, down, down_y, down_x, x_all, nz, nc
):
    images, seq = qkv.shape[:2]
    local_len = seq // nc
    sub = term_up.shape[3]
    terms = 1 + term_up.shape[0]
    any_ = pl.BlockSpec(memory_space=pl.ANY)
    vmem = pl.BlockSpec(memory_space=pltpu.VMEM)
    return pl.pallas_call(
        functools.partial(backward_kernel, nz, nc),
        out_shape=(
            jax.ShapeDtypeStruct((EARLY, sub, D), BF),
            jax.ShapeDtypeStruct((LATE, sub, D), BF),
            jax.ShapeDtypeStruct((images, seq, 384), BF),
        ),
        in_specs=[
            any_,
            any_,
            vmem,
            any_,
            vmem,
            any_,
            any_,
            any_,
            any_,
            any_,
            any_,
        ],
        out_specs=(any_, any_, any_),
        scratch_shapes=[
            pltpu.VMEM((images, seq, 128), BF),
            pltpu.VMEM((images, seq, 384), BF),
            pltpu.VMEM((images, seq, 384), BF),
            pltpu.VMEM((images, seq, 128), BF),
            pltpu.VMEM((2, seq, D), BF),
            pltpu.VMEM((seq, 128), F32),
            pltpu.VMEM((16, seq), F32),
            pltpu.VMEM((384, D), F32),
            pltpu.VMEM((terms, nz, sub, D), BF),
            pltpu.VMEM((terms, nz, sub, D // 2), BF),
            pltpu.VMEM((terms, nz, sub, D // 2), BF),
            pltpu.VMEM((terms, 4, nz, sub, D // 2), BF),
            pltpu.VMEM((terms, 2, nz, sub, D // 2), BF),
            pltpu.VMEM((EARLY - terms, nz, sub, D), BF),
            pltpu.VMEM((2, EARLY - terms, nz, sub, D // 2), BF),
            pltpu.VMEM((2, EARLY, sub, D), BF),
            pltpu.VMEM((EARLY, sub, D), BF),
            pltpu.VMEM((EARLY, sub, D), BF),
            pltpu.VMEM((nz, LATE, sub, D), BF),
            pltpu.VMEM((2, LATE, sub, D), BF),
            pltpu.VMEM((LATE, sub, D), BF),
            pltpu.VMEM((LATE, sub, D), BF),
            pltpu.VMEM((EARLY, sub, D), BF),
            pltpu.VMEM((LATE, sub, D), BF),
            pltpu.SemaphoreType.DMA((256,)),
            pltpu.SemaphoreType.DMA((256,)),
            pltpu.SemaphoreType.DMA((64,)),
        ],
        compiler_params=pltpu.CompilerParams(
            collective_id=2, has_side_effects=True, vmem_limit_bytes=61 << 20
        ),
        name="backward_attention",
    )(
        qkv,
        o_heads,
        lse,
        grad_att,
        counts,
        term_out,
        term_up,
        down,
        down_y,
        down_x,
        x_all,
    )


def tail_kernel(
    nz,
    nc,
    token_count,
    slot_blocks,
    early_hbm,
    late_hbm,
    heads_ref,
    wq_own_ref,
    wq_rows_ref,
    wq_ref,
    tokens_ref,
    mid_ref,
    gain_hbm,
    gains_hbm,
    rl_ref,
    rr_ref,
    sl_ref,
    sr_ref,
    ms_ref,
    tokens_out,
    gain_out,
    grad_hbm,
    left_hbm,
    right_hbm,
    weight_hbm,
    early_ref,
    late_ref,
    gain_ref,
    gains_ref,
    grad_out,
    left_out,
    right_out,
    tok,
    wq,
    x_buf,
    mid_buf,
    part,
    part_in,
    rl,
    rr,
    sl,
    sr,
    ms,
    update,
    square,
    square_in,
    gain_sum,
    gain_in,
    place_ref,
    g_ref,
    l_ref,
    g_all,
    send,
    recv,
    local_sems,
):
    me_z, me_c, me_t = (lax.axis_index(a) for a in ("fsdp", "context", "tensor"))
    images, local_len = tokens_ref.shape[:2]
    slots = g_ref.shape[0]
    x_c, y_c, far_c = me_c ^ 1, me_c ^ 2, me_c ^ 3
    core, x_near, y_near = {"tensor": 1 - me_t}, {"context": x_c}, {"context": y_c}
    above, below = {"fsdp": me_z + 1}, {"fsdp": me_z - 1}
    c_peers = [{"context": me_c ^ k} for k in range(1, nc)]
    group = [
        {"fsdp": me_z ^ (k // 2), "tensor": me_t ^ (k % 2)} for k in range(1, 2 * nz)
    ]
    rows_group = [(me_z ^ (k // nc), me_c ^ (k % nc)) for k in range(1, nz * nc)]
    others = [{"fsdp": z, "context": c} for z, c in rows_group[nc - 1 :] ]
    diagonal = [d for k, d in enumerate(others) if (k + nc) % nc]
    left, right = pl.ds(0, D // 2), pl.ds(D // 2, D // 2)
    local = Local(local_sems)
    small_in = [
        local.start(a, b)
        for a, b in (
            (early_hbm, early_ref),
            (late_hbm, late_ref),
            (gain_hbm, gain_ref),
            (gains_hbm, gains_ref),
        )
    ]
    barrier = pltpu.get_barrier_semaphore()
    for device in group + c_peers + diagonal:
        pl.semaphore_signal(
            barrier, inc=1, device_id=device, device_id_type=pl.DeviceIdType.MESH
        )
    for copy in small_in:
        local.wait(copy)
    for slot in range(NBLK):
        block = jnp.clip(slot_blocks[slot] - LATE, 0, EARLY - 1)
        place_ref[slot] = early_ref[block]
    l_ref[:, me_t, me_c, me_z] = late_ref[...]
    for slot in range(slots):
        g_ref[slot, me_t, me_c, me_z] = place_ref[me_c * slots + slot]
    pl.semaphore_wait(barrier, len(group + c_peers + diagonal))
    moves = Moves(send, recv)
    sent = []

    def go(*args, **kw):
        move = moves.make(*args, **kw)
        move.start()
        sent.append(move)
        return move

    placed = []
    for k in range(1, nc):
        theirs = place_ref.at[pl.ds((me_c ^ k) * slots, slots)]
        placed.append(go(theirs, g_ref.at[:, me_t, me_c, me_z], c_peers[k - 1]))

    swapped = []

    def swap(piece, cond=None):
        swapped.append(go(piece, piece, core, cond=cond, recv_cond=cond))

    def along_fsdp(at):
        own = at(me_z)
        return [
            go(own, own, above, cond=me_z < nz - 1, recv_cond=me_z > 0),
            go(own, own, below, cond=me_z > 0, recv_cond=me_z < nz - 1),
        ]

    def onward(at, last, hop):
        up_z, down_z = me_z - hop, me_z + hop
        last[0].wait_recv()
        up = down = None
        if hop < nz - 1:
            piece = at(up_z)
            cond = jnp.logical_and(me_z < nz - 1, up_z >= 0)
            up = go(piece, piece, above, cond=cond, recv_cond=up_z - 1 >= 0)
        last[1].wait_recv()
        if hop < nz - 1:
            piece = at(down_z)
            cond = jnp.logical_and(me_z > 0, down_z <= nz - 1)
            down = go(piece, piece, below, cond=cond, recv_cond=down_z + 1 <= nz - 1)
        return [up, down], [(up_z, up_z >= 0), (down_z, down_z <= nz - 1)]

    def late_at(member):
        return lambda z: l_ref.at[:, me_t, member, z]

    def slot_at(slot):
        return lambda z: g_ref.at[slot, me_t, :, z]

    late_line = along_fsdp(late_at(me_c))
    tok_in = []

    def send_tok(i):
        there = tok.at[i, :, span(me_c * 384, 384)]
        tok_in.append(
            [local.start(heads_ref.at[i, span(me_c * local_len, local_len)], there)]
            + [
                go(
                    heads_ref.at[i, span((me_c ^ k) * local_len, local_len)],
                    there,
                    c_peers[k - 1],
                )
                for k in range(1, nc)
            ]
        )
    lines = []

    def slot_line(slot):
        lines.append(along_fsdp(slot_at(slot)))

    def late_on(hop):
        nonlocal late_line
        late_line, _ = onward(late_at(me_c), late_line, hop)

    send_tok(0)
    send_tok(1)
    width = wq.shape[1] // nc
    depth = wq_rows_ref.shape[0]
    wq_in = [local.start(wq_own_ref, wq.at[:, span(me_c * width, width)])]
    for m in (x_c, y_c, far_c):
        columns = span(m * width, width)
        wq_in.append(
            local.start(wq_rows_ref.at[:, columns], wq.at[span(me_z * depth, depth), columns])
        )
        for k in range(1, nz):
            at = (span(lax.rem(me_z + k, nz) * depth, depth), columns)
            wq_in.append(local.start(wq_ref.at[at], wq.at[at]))
    x_in = [local.start(tokens_ref.at[i], x_buf.at[i]) for i in range(images)]
    mid_in = [local.start(mid_ref.at[i], mid_buf.at[i]) for i in range(images)]
    state_in = [
        local.start(a, b) for a, b in ((rl_ref, rl), (sl_ref, sl), (sr_ref, sr), (ms_ref, ms))
    ]
    rr_in = [local.start(rr_ref.at[0], rr)]
    late_on(1)
    for move in placed:
        move.wait_recv()
    late_on(2)
    for slot in range(slots):
        slot_line(slot)
    swap(g_ref.at[:, me_t, :, me_z])
    late_on(3)
    late_own = l_ref.at[:, me_t, me_c]
    near = [go(late_own, late_own, x_near), go(late_own, late_own, y_near)]
    swap(late_own)

    part_moves = []
    gain_out[...] = jnp.zeros_like(gain_out)
    square[...] = jnp.zeros_like(square)

    def project(i):
        local.wait(tok_in[i][0])
        for move in tok_in[i][1:]:
            move.wait_recv()
        part[i] = dot_nt(tok[i], wq[...]).astype(BF)
        part_moves.append(go(part.at[i], part_in.at[i], core))

    def norm_backward(i):
        part_moves[i].wait_recv()
        local.wait(x_in[i])
        local.wait(mid_in[i])

        @pl.loop(0, 2)
        def _(step):
            rows = span(step * (local_len // 2), local_len // 2)
            value = x_buf[i, rows]
            centred = value - jnp.mean(value, axis=-1, keepdims=True)
            inv_std = lax.rsqrt(jnp.mean(centred * centred, axis=-1, keepdims=True) + 1e-06)
            normed = centred * inv_std
            grad = part[i, rows].astype(F32) + part_in[i, rows].astype(F32)
            scaled = grad * gain_ref[0:1, :]
            inner = (
                scaled
                - jnp.mean(scaled, axis=-1, keepdims=True)
                - normed * jnp.mean(scaled * normed, axis=-1, keepdims=True)
            )
            mid_buf[i, rows] += inner * inv_std
            gain_out[0:1, :] += jnp.sum(grad * normed, axis=0, keepdims=True)

        local.start(mid_buf.at[i], tokens_out.at[i])

    def slots_on(hop):
        for slot in range(slots):
            lines[slot], here = onward(slot_at(slot), lines[slot], hop)
        for z, cond in here:
            swap(g_ref.at[:, me_t, :, z], cond)

    slots_on(1)
    slots_on(2)
    near[0].wait_recv()
    piece = l_ref.at[:, me_t, x_c, :, :, left]
    far = [go(piece, piece, y_near)]
    near[1].wait_recv()
    piece = l_ref.at[:, me_t, y_c, :, :, right]
    far.append(go(piece, piece, x_near))
    send_tok(2)
    swap(l_ref.at[:, me_t, x_c])
    swap(l_ref.at[:, me_t, y_c])
    for copy in wq_in:
        local.wait(copy)
    project(0)
    norm_backward(0)
    for move in far:
        move.wait_recv()
    swap(l_ref.at[:, me_t, far_c])
    project(1)
    norm_backward(1)
    last = []
    for slot in range(slots):
        _, here = onward(slot_at(slot), lines[slot], 3)
        last.append([])
        for z, cond in here:
            piece = g_ref.at[slot, me_t, :, z]
            last[slot].append(go(piece, piece, core, cond=cond, recv_cond=cond))
    for move in swapped:
        move.wait_recv()
    for copy in state_in:
        local.wait(copy)
    offset = me_t * (D // 2) + me_z * rl.shape[1]
    mine = span(offset, rl.shape[1])

    def step(slot):
        for move in last[slot]:
            move.wait_recv()
        block = slot_blocks[me_c * slots + slot]
        late = l_ref[jnp.clip(block, 0, LATE - 1)]
        g_all[...] = jnp.where(block < LATE, late, g_ref[slot]).reshape(D, D)
        rows = g_all[mine, :]
        grad_out[slot] = rows.astype(F32)
        left_out[slot] = 0.5 * sl[slot] + 0.5 / token_count * dot_nt(rows, g_all[...])
        right_out[slot] = 0.5 * sr[slot] + 0.5 / token_count * dot_tn(g_all[:, mine], g_all[...])
        for a, b in ((grad_out, grad_hbm), (left_out, left_hbm), (right_out, right_hbm)):
            local.start(a.at[slot], b.at[slot])
        inner = dot_nn(rl[slot].astype(BF), g_all[...]).astype(BF)
        local.wait(rr_in[slot])
        update[slot] = dot_nn(inner, rr[...].astype(BF))
        if slot + 1 < slots:
            rr_in.append(local.start(rr_ref.at[slot + 1], rr))
        total = jnp.sum(update[slot] * update[slot], axis=0, keepdims=True)
        total = jnp.sum(total, axis=1, keepdims=True)
        square[slot : slot + 1, :] = jnp.broadcast_to(total, (1, 128))

    step(0)
    step(1)
    project(2)
    step(2)
    square_moves = [
        go(square, square_in.at[k], group[k]) for k in range(len(group))
    ]
    norm_backward(2)
    gain_sum[...] = gains_ref[...]
    gain_sum[0:1, :] = gain_out[0:1, :]
    gain_moves = []
    for k, (z, c) in enumerate(rows_group):
        theirs = span((z * nc + c) // 2 * 128, 128)
        gain_moves.append(
            go(gain_sum.at[:, theirs], gain_in.at[k], {"fsdp": z, "context": c})
        )
    for move in square_moves:
        move.wait_recv()
    for slot in range(slots):
        total = square[slot : slot + 1, 0:1]
        for k in range(len(group)):
            total = total + square_in[k, slot : slot + 1, 0:1]
        ms[slot] -= lax.rsqrt(total / (D * D) + 1e-06) * update[slot]
        local.start(ms.at[slot], weight_hbm.at[slot])
    total = gain_sum[:, span((me_z * nc + me_c) // 2 * 128, 128)]
    for k, move in enumerate(gain_moves):
        move.wait_recv()
        total = total + gain_in[k]
    gain_out[:, 0:128] = total
    local.finish()
    for move in sent:
        move.wait_send()


def tail(
    block_of,
    early,
    late,
    grad_heads,
    wq,
    wq_rows,
    wq_all,
    tokens,
    grad_middle,
    gain,
    gain_terms,
    root_left,
    root_right,
    stat_left,
    stat_right,
    master,
    token_count,
    nz,
    nc,
    nt,
):
    images, local_len = tokens.shape[:2]
    sub = early.shape[1]
    slots, row_count = root_left.shape[:2]
    any_ = pl.BlockSpec(memory_space=pl.ANY)
    vmem = pl.BlockSpec(memory_space=pltpu.VMEM)
    state = jax.ShapeDtypeStruct((slots, row_count, D), F32)
    shape = (slots, nt, nc, nz, sub, D)
    return pl.pallas_call(
        functools.partial(tail_kernel, nz, nc, token_count),
        out_shape=(
            jax.ShapeDtypeStruct((images, local_len, D), F32),
            jax.ShapeDtypeStruct((8, D), F32),
            state,
            state,
            state,
            state,
        ),
        in_specs=[pl.BlockSpec(memory_space=pltpu.SMEM)] + [any_] * 15,
        out_specs=(any_, vmem, any_, any_, any_, any_),
        scratch_shapes=[
            pltpu.VMEM((EARLY, sub, D), BF),
            pltpu.VMEM((LATE, sub, D), BF),
            pltpu.VMEM((4, D), F32),
            pltpu.VMEM((8, D), F32),
            pltpu.VMEM((slots, row_count, D), F32),
            pltpu.VMEM((slots, row_count, D), F32),
            pltpu.VMEM((slots, row_count, D), F32),
            pltpu.VMEM((images, local_len, nc * 384), BF),
            pltpu.VMEM((D, nc * 384), BF),
            pltpu.VMEM((images, local_len, D), F32),
            pltpu.VMEM((images, local_len, D), F32),
            pltpu.VMEM((images, local_len, D), BF),
            pltpu.VMEM((images, local_len, D), BF),
            pltpu.VMEM((slots, row_count, D), F32),
            pltpu.VMEM((D, D), F32),
            pltpu.VMEM((slots, row_count, D), F32),
            pltpu.VMEM((slots, row_count, D), F32),
            pltpu.VMEM((slots, row_count, D), F32),
            pltpu.VMEM((slots, row_count, D), F32),
            pltpu.VMEM((8, 128), F32),
            pltpu.VMEM((2 * nz - 1, 8, 128), F32),
            pltpu.VMEM((8, D), F32),
            pltpu.VMEM((nz * nc - 1, 8, 128), F32),
            pltpu.VMEM((NBLK, sub, D), BF),
            pltpu.VMEM(shape, BF),
            pltpu.VMEM((LATE, nt, nc, nz, sub, D), BF),
            pltpu.VMEM((D, D), BF),
            pltpu.SemaphoreType.DMA((160,)),
            pltpu.SemaphoreType.DMA((160,)),
            pltpu.SemaphoreType.DMA((64,)),
        ],
        compiler_params=pltpu.CompilerParams(
            collective_id=3, has_side_effects=True, vmem_limit_bytes=61 << 20
        ),
        name="tail",
    )(
        block_of,
        early,
        late,
        grad_heads,
        wq,
        wq_rows,
        wq_all,
        tokens,
        grad_middle,
        gain,
        gain_terms,
        root_left,
        root_right,
        stat_left,
        stat_right,
        master,
    )


def finish_kernel(count, *refs):
    ins, outs, bufs = refs[:count], refs[count : 2 * count], refs[2 * count : 3 * count]
    in_sems, out_sems = refs[3 * count :]
    pieces = [(i, k) for i in range(ins[0].shape[0]) for k in range(count)]
    loads, stores = [], []
    for n, (i, k) in enumerate(pieces):
        loads.append(pltpu.make_async_copy(ins[k].at[i], bufs[k].at[i], in_sems.at[n]))
        loads[-1].start()
    for n, (i, k) in enumerate(pieces):
        loads[n].wait()
        stores.append(pltpu.make_async_copy(bufs[k].at[i], outs[k].at[i], out_sems.at[n]))
        stores[-1].start()
    for store in stores:
        store.wait()


def finish(arrays):
    any_ = pl.BlockSpec(memory_space=pl.ANY)
    count = len(arrays)
    pieces = count * arrays[0].shape[0]
    size = sum(a.size * a.dtype.itemsize for a in arrays)
    return pl.pallas_call(
        functools.partial(finish_kernel, count),
        out_shape=tuple(jax.ShapeDtypeStruct(a.shape, a.dtype) for a in arrays),
        in_specs=[any_] * count,
        out_specs=(any_,) * count,
        scratch_shapes=[pltpu.VMEM(a.shape, a.dtype) for a in arrays]
        + [pltpu.SemaphoreType.DMA((pieces,)), pltpu.SemaphoreType.DMA((pieces,))],
        compiler_params=pltpu.CompilerParams(vmem_limit_bytes=62 << 20),
        cost_estimate=pl.CostEstimate(flops=0, bytes_accessed=2 * size, transcendentals=0),
        name="finish",
    )(*arrays)


def xor_permute(value, axis, step):
    size = lax.axis_size(axis)
    return lax.ppermute(value, axis, [(j, j ^ step) for j in range(size)])


def xor_order(pieces, index):
    bit = 1
    while bit < len(pieces):
        odd = (index & bit) > 0
        pieces = [jnp.where(odd, pieces[j ^ bit], pieces[j]) for j in range(len(pieces))]
        bit *= 2
    return pieces


def sum_tensor(value):
    low = lax.optimization_barrier(value.astype(BF))
    return low.astype(F32) + xor_permute(low, "tensor", 1).astype(F32)


def gather_fsdp(value):
    size = lax.axis_size("fsdp")
    if size > 4:
        return lax.all_gather(value, "fsdp", axis=0, tiled=False)
    pieces = [value] + [
        lax.ppermute(value, "fsdp", [(j, (j - k) % size) for j in range(size)])
        for k in range(1, size)
    ]
    doubled = jnp.stack(pieces + pieces[:-1])
    start = lax.rem(size - lax.axis_index("fsdp"), size)
    return lax.dynamic_slice_in_dim(doubled, start, size, 0)


def sum_fsdp(value):
    size = lax.axis_size("fsdp")
    if size > 4:
        return lax.psum(value, "fsdp")
    total = value
    for k in range(1, size):
        total = total + lax.ppermute(value, "fsdp", [(j, (j - k) % size) for j in range(size)])
    return total


def grad_gather_plain(block_of, early, late, nz, nc):
    me_c, me_t = (lax.axis_index(a) for a in ("context", "tensor"))
    sub = early.shape[1]
    half_width = nc * nz * sub
    slot_count = NBLK // nc
    slots_of = block_of.reshape(nc, slot_count)

    def slots_for(k):
        blocks = lax.dynamic_index_in_dim(slots_of, me_c ^ k, 0, keepdims=False)
        return early[jnp.clip(blocks - LATE, 0, EARLY - 1)]

    placed = [slots_for(0)] + [xor_permute(slots_for(k), "context", k) for k in range(1, nc)]
    placed = jnp.stack(xor_order(placed, me_c), axis=1)
    placed = lax.all_gather(placed, "fsdp", axis=2, tiled=False)
    placed = placed.reshape(slot_count, half_width, D)
    placed_other = xor_permute(placed, "tensor", 1)
    both = jnp.stack([placed, placed_other], axis=1)
    early_full = jnp.where(me_t > 0, both[:, ::-1], both).reshape(slot_count, D, D)

    late = late.reshape(-1, D)
    late = lax.psum_scatter(late, "fsdp", scatter_dimension=0, tiled=True)
    late = lax.all_gather(late, ("context", "fsdp"), axis=0, tiled=True)
    late = jnp.swapaxes(late.reshape(nc * nz, LATE, sub, D), 0, 1).reshape(LATE, half_width, D)
    late_other = xor_permute(late, "tensor", 1)
    both = jnp.stack([late, late_other], axis=1)
    late_full = jnp.where(me_t > 0, both[:, ::-1], both).reshape(LATE, D, D)

    mine = lax.dynamic_index_in_dim(slots_of, me_c, 0, keepdims=False)
    return jnp.where(
        (mine < LATE)[:, None, None], late_full[jnp.clip(mine, 0, LATE - 1)], early_full
    )


def to_natural(value, me_t, half_len):
    parts = value.reshape((-1, half_len) + value.shape[1:])
    return jnp.where(me_t > 0, parts[::-1], parts).reshape(value.shape)


def forward_plain(tokens, gain, key_mask, w_qkv, w_out, w_up, w_down):
    images, local_len = tokens.shape[:2]
    nc, nt = (lax.axis_size(a) for a in ("context", "tensor"))
    me_c, me_t = (lax.axis_index(a) for a in ("context", "tensor"))
    cols = w_qkv.shape[2] // nc
    half_len = local_len // nt
    wq_part = lax.dynamic_slice_in_dim(w_qkv, me_c * cols, cols, 2)
    wq = gather_fsdp(wq_part).reshape(D, 3 * cols)

    def two_stage(weight, member_axis, fsdp_axis):
        width = weight.shape[member_axis] // nc
        part = lax.dynamic_slice_in_dim(weight, me_c * width, width, member_axis)
        part = lax.all_gather(part, "fsdp", axis=fsdp_axis, tiled=True)
        return lax.all_gather(part, "context", axis=member_axis, tiled=True)

    out_full = two_stage(w_out, 0, 1)
    up_full = two_stage(w_up, 1, 0)
    down_full = two_stage(w_down, 0, 1)

    counts = jnp.sum(key_mask, axis=1)
    real = counts
    for k in range(1, nc):
        real = real + xor_permute(counts, "context", k)
    position = (
        (me_c ^ jnp.arange(nc))[:, None, None] * local_len
        + (me_t ^ jnp.arange(nt))[None, :, None] * half_len
        + jnp.arange(half_len)[None, None, :]
    ).reshape(-1)
    live = position[None, :] < real[:, None]
    bias = jnp.where(live, 0.0, -1e30).astype(F32)
    live_col = jnp.broadcast_to(live[:, :, None].astype(F32), (images, SEQ, 128))

    normed1, inv_std1, pre_norm1 = norm_fwd(tokens, gain)
    normed1_low = pre_norm1.astype(BF)

    x_all, qkv, out_heads, log_sums, attended = [], [], [], [], []
    for i in range(images):
        mine = lax.dynamic_slice_in_dim(normed1_low[i], me_t * half_len, half_len, 0)
        held = jnp.stack([mine] + [xor_permute(mine, "context", k) for k in range(1, nc)])
        other = xor_permute(held, "tensor", 1)
        x_i = jnp.stack([held, other], axis=1).reshape(SEQ, D)
        qkv_i = dot_nn(x_i, wq).astype(BF)
        o_i, lse_i = attn_fwd(qkv_i, bias[i][None])
        chunks = o_i.reshape(nc, local_len, 2 * HD)
        moved = [to_natural(chunks[0], me_t, half_len)] + [
            to_natural(xor_permute(chunks[k], "context", k), me_t, half_len) for k in range(1, nc)
        ]
        attended.append(jnp.concatenate(xor_order(moved, me_c), axis=-1))
        x_all.append(x_i)
        qkv.append(qkv_i)
        out_heads.append(o_i)
        log_sums.append(lse_i)
    attended = jnp.stack(attended)
    return (
        jnp.stack(x_all),
        jnp.stack(qkv),
        jnp.stack(out_heads),
        jnp.stack(log_sums),
        attended,
        live_col,
        wq,
        out_full,
        up_full,
        down_full,
        normed1,
        inv_std1,
    )


def backward_plain(qkv, out_heads, log_sums, grad_att, live_col, early, wq):
    images, local_len = grad_att.shape[:2]
    nz, nc, nt = (lax.axis_size(a) for a in ("fsdp", "context", "tensor"))
    me_c, me_t = (lax.axis_index(a) for a in ("context", "tensor"))
    cols = grad_att.shape[2] // nc
    half_len = local_len // nt
    sub = early.shape[2]
    grad_heads = []
    grad_tok = []
    for i in range(images):
        pieces = [grad_att[i, :, j * cols : (j + 1) * cols] for j in range(nc)]
        pieces = [to_natural(p, me_t, half_len) for p in xor_order(pieces, me_c)]
        grad_i = jnp.concatenate(
            [pieces[0]] + [xor_permute(pieces[k], "context", k) for k in range(1, nc)]
        )
        g_i = attn_bwd(qkv[i], grad_i, out_heads[i], log_sums[i], live_col[i])
        chunks = g_i.reshape(nc, local_len, 3 * cols)
        moved = [to_natural(chunks[0], me_t, half_len)] + [
            to_natural(xor_permute(chunks[k], "context", k), me_t, half_len) for k in range(1, nc)
        ]
        grad_tok.append(jnp.stack(xor_order(moved, me_c), axis=1))
        grad_heads.append(g_i)
    grad_tok = jnp.stack(grad_tok)
    wq_all = lax.all_gather(wq, "context", axis=0, tiled=False)
    grad_n1 = sum_tensor(
        jnp.einsum("isjc,jdc->isd", grad_tok, wq_all, preferred_element_type=F32)
    )
    early = lax.psum_scatter(
        jnp.swapaxes(early, 0, 1).reshape(-1, D),
        "fsdp",
        scatter_dimension=0,
        tiled=True,
    ).reshape(EARLY, sub, D)
    return jnp.stack(grad_heads), grad_n1, early


def per_device(
    tokens,
    cotangent,
    gains,
    w_qkv,
    w_out,
    w_up,
    w_down,
    key_mask,
    owner,
    stat_left,
    stat_right,
    root_left,
    root_right,
    master,
    gain_state,
):
    images, local_len = tokens.shape[:2]
    tok_rows = images * local_len
    nz, nc, nt = (lax.axis_size(a) for a in ("fsdp", "context", "tensor"))
    me_z, me_c, me_t = (lax.axis_index(a) for a in ("fsdp", "context", "tensor"))
    half_width = w_qkv.shape[2]
    hidden = w_up.shape[1]
    up_blocks = hidden // half_width
    cols = half_width // nc
    fast = nz == 4 and nc == 4 and nt == 2 and images == 3
    if fast:
        wq_rows = jnp.swapaxes(w_qkv.reshape(-1, 3, nc, cols), 1, 2).reshape(-1, nc * 3 * cols)
        counts = jnp.pad(jnp.sum(key_mask, axis=1), (0, 8 - images))
        counts = jnp.broadcast_to(counts[:, None], (8, 128))
        (
            x_all,
            qkv,
            out_heads,
            log_sums,
            attended,
            counts,
            wq,
            out_full,
            up_full,
            down_part,
        ) = forward_attention(
            tokens, gains, counts, wq_rows, w_out, w_up, w_down, nz, nc
        )
    else:
        (
            x_all,
            qkv,
            out_heads,
            log_sums,
            attended,
            live_col,
            wq,
            out_full,
            up_full,
            down_full,
            normed1,
            inv_std1,
        ) = forward_plain(tokens, gains[0], key_mask, w_qkv, w_out, w_up, w_down)

    sub = half_width // nc // nz
    onehot = (owner[:, None] == jnp.arange(NBLK, dtype=jnp.int32)[None, :]).astype(jnp.int32)
    block_of = jnp.sum(onehot * jnp.arange(NBLK, dtype=jnp.int32)[:, None], axis=0)

    if fast:
        (
            output,
            grad_middle,
            grad_att,
            term_out,
            term_up,
            down,
            down_y,
            down_x,
            wq_all,
            gain_terms,
        ) = feed_forward(
            attended, out_full, up_full, down_part, tokens, cotangent, gains, wq_rows, nz, nc
        )
        term_out, block_of = lax.optimization_barrier((term_out, block_of))
        term_out = term_out.reshape(1, nc, nz, sub, D)
        term_up = term_up.reshape(-1, nc, nz, sub, D)
        down = down.reshape(-1, nz, sub, D)
        down_y = down_y.reshape(-1, nz, sub, D // 2)
        down_x = down_x.reshape(-1, nz, sub, D // 2)
    else:
        branch_attn = sum_tensor(
            jnp.einsum("ish,hd->isd", attended, out_full, preferred_element_type=F32)
        )
        middle = tokens + gains[2] * branch_attn
        normed2, inv_std2, pre_norm2 = norm_fwd(middle, gains[1])
        normed2_low = pre_norm2.astype(BF)
        pre_act = jnp.einsum("isd,df->isf", normed2_low, up_full, preferred_element_type=F32)
        act_val, act_slope = gelu_parts(pre_act)
        act_low = act_val.astype(BF)
        branch_mlp = sum_tensor(
            jnp.einsum("isf,fd->isd", act_low, down_full, preferred_element_type=F32)
        )
        output = middle + gains[3] * branch_mlp

        grad_mlp = (gains[3] * cotangent).astype(BF)
        grad_hidden = jnp.einsum("isd,fd->isf", grad_mlp, down_full, preferred_element_type=F32)
        grad_pre = (grad_hidden * act_slope).astype(BF)
        grad_n2 = sum_tensor(
            jnp.einsum("isf,df->isd", grad_pre, up_full, preferred_element_type=F32)
        )
        middle_part, grad_gain2 = norm_back(grad_n2, gains[1], normed2, inv_std2)
        grad_middle = cotangent + middle_part
        grad_branch = (gains[2] * grad_middle).astype(BF)
        grad_att = jnp.einsum(
            "isd,hd->ish", grad_branch, out_full, preferred_element_type=F32
        ).astype(BF)

        def early_term(left, right):
            term = dot_tn(left.reshape(tok_rows, -1), right.reshape(tok_rows, D)).astype(BF)
            return term.reshape(-1, nc, nz, sub, D)

        def early_sum(term):
            return lax.psum_scatter(
                jnp.swapaxes(term, 0, 1).reshape(-1, D), "context", scatter_dimension=0, tiled=True
            ).reshape(-1, nz, sub, D)

        term_out = early_term(attended, grad_branch)
        term_up = early_term(grad_pre, normed2_low)
        down = early_sum(early_term(act_low, grad_mlp))
        grad_gain3 = jnp.sum(grad_middle * branch_attn, axis=(0, 1))
        grad_gain4 = jnp.sum(cotangent * branch_mlp, axis=(0, 1))
        blank = jnp.zeros_like(grad_gain2)
        gain_terms = jnp.stack([blank, grad_gain2, grad_gain3, grad_gain4] + [blank] * 4, axis=0)
    tokens_all = images * nz * SEQ
    if fast:
        early, late, grad_heads = backward_attention(
            qkv, out_heads, log_sums, grad_att, counts, term_out, term_up, down, down_y, down_x, x_all, nz, nc
        )
        grad_tokens, gain_sum, grad_mine, left_new, right_new, weight_new = tail(
            block_of,
            early,
            late,
            grad_heads,
            wq,
            wq_rows,
            wq_all,
            tokens,
            grad_middle,
            gains,
            gain_terms,
            root_left[:, 0],
            root_right,
            stat_left[:, 0],
            stat_right[:, 0],
            master[:, 0],
            tokens_all,
            nz,
            nc,
            nt,
        )
        output, grad_tokens, grad_mine, left_new, right_new, weight_new = finish(
            (output, grad_tokens, grad_mine, left_new, right_new, weight_new)
        )
    else:
        early = jnp.concatenate([early_sum(term_out), early_sum(term_up), down], axis=0)
        grad_heads, grad_n1, early = backward_plain(
            qkv, out_heads, log_sums, grad_att, live_col, early, wq
        )
        term_qkv = jnp.einsum("isk,isd->kd", grad_heads, x_all, preferred_element_type=F32)
        late = jnp.swapaxes(term_qkv.astype(BF).reshape(LATE, nz, sub, D), 0, 1)
        grad_full = grad_gather_plain(block_of, early, late, nz, nc)
        input_part, grad_gain1 = norm_back(grad_n1, gains[0], normed1, inv_std1)
        grad_tokens = grad_middle + input_part
        row_count = half_width // nz
        row_offset = me_t * half_width + me_z * row_count
        grad_mine = lax.dynamic_slice_in_dim(grad_full, row_offset, row_count, 1)
        left_new = 0.5 * stat_left[:, 0] + 0.5 / tokens_all * jnp.einsum(
            "sra,sba->srb", grad_mine, grad_full, preferred_element_type=F32
        )
        grad_cols = lax.dynamic_slice_in_dim(grad_full, row_offset, row_count, 2)
        right_new = 0.5 * stat_right[:, 0] + 0.5 / tokens_all * jnp.einsum(
            "sar,sab->srb", grad_cols, grad_full, preferred_element_type=F32
        )
        inner_prod = jnp.einsum(
            "sra,sab->srb", root_left[:, 0].astype(BF), grad_full, preferred_element_type=F32
        ).astype(BF)
        update = jnp.einsum(
            "srb,sbc->src", inner_prod, root_right.astype(BF), preferred_element_type=F32
        )
        square_sum = jnp.sum(update * update, axis=(1, 2))
        square_sum = sum_fsdp(square_sum + xor_permute(square_sum, "tensor", 1))
        factor = lax.rsqrt(square_sum / (D * D) + 1e-06)
        weight_new = master[:, 0] - factor[:, None, None] * update

        gain_terms = gain_terms[:4].at[0].set(grad_gain1)
        gain_sum = gain_terms
        step = 1
        while step < nc:
            gain_sum = gain_sum + xor_permute(gain_sum, "context", step)
            step *= 2
        gain_sum = sum_fsdp(gain_sum)

    share_width = gain_state.shape[1]
    gain_index = lax.axis_index(("fsdp", "context"))
    if fast:
        at = lax.rem(gain_index * share_width, 128)
        gain_grad = lax.dynamic_slice(gain_sum, (0, at), (4, share_width))
    else:
        gain_grad = lax.dynamic_slice_in_dim(
            gain_sum, gain_index * share_width, share_width, 1
        )
    gain_mine = lax.dynamic_slice_in_dim(gains, gain_index * share_width, share_width, 1)
    state_new = 0.5 * gain_state + 0.5 * gain_grad * gain_grad / tokens_all
    gain_new = gain_mine - 0.1 * gain_grad * lax.rsqrt(tokens_all * state_new)
    return (
        output,
        grad_tokens,
        grad_mine.astype(F32)[:, None],
        left_new[:, None],
        right_new[:, None],
        weight_new[:, None],
        gain_grad,
        state_new,
        gain_new,
    )


def solution(mesh):
    return jax.shard_map(
        per_device,
        mesh=mesh,
        in_specs=(
            P("fsdp", "context", None),
            P("fsdp", "context", None),
            P(),
            P("fsdp", None, "tensor"),
            P("tensor", "fsdp"),
            P("fsdp", "tensor"),
            P("tensor", "fsdp"),
            P("fsdp", "context"),
            P(),
            P("context", "tensor", "fsdp", None),
            P("context", "tensor", "fsdp", None),
            P("context", "tensor", "fsdp", None),
            P("context", None, None),
            P("context", "tensor", "fsdp", None),
            P(None, ("fsdp", "context")),
        ),
        out_specs=(
            P("fsdp", "context", None),
            P("fsdp", "context", None),
            P("context", "tensor", "fsdp", None),
            P("context", "tensor", "fsdp", None),
            P("context", "tensor", "fsdp", None),
            P("context", "tensor", "fsdp", None),
            P(None, ("fsdp", "context")),
            P(None, ("fsdp", "context")),
            P(None, ("fsdp", "context")),
        ),
        check_vma=False,
    )
```

```python
import functools

import jax
import jax.numpy as jnp
from jax import lax
from jax.experimental import pallas as pl
from jax.experimental.pallas import tpu as pltpu
from jax.sharding import PartitionSpec as P

D = 1024
HD = 64
SEQ = 1408
NBLK = 12
LATE = 3
EARLY = NBLK - LATE
BF = jnp.bfloat16
F32 = jnp.float32
SCALE = HD ** (-0.5)


def norm_fwd(field_in, gain_vec):
    centred = field_in - jnp.mean(field_in, axis=-1, keepdims=True)
    inv_std = lax.rsqrt(jnp.mean(centred * centred, axis=-1, keepdims=True) + 1e-06)
    normed = centred * inv_std
    return (normed, inv_std, normed * gain_vec)


def norm_back(grad_out, gain_vec, normed, inv_std):
    scaled = grad_out * gain_vec
    inner_sum = (
        scaled
        - jnp.mean(scaled, axis=-1, keepdims=True)
        - normed * jnp.mean(scaled * normed, axis=-1, keepdims=True)
    )
    return (inner_sum * inv_std, jnp.sum(grad_out * normed, axis=(0, 1)))


def gelu_parts(field_in):
    normal_cdf = 0.5 * (1.0 + lax.erf(field_in * 0.7071067811865476))
    normal_pdf = jnp.exp(-0.5 * field_in * field_in) * 0.3989422804014327
    return (field_in * normal_cdf, normal_cdf + field_in * normal_pdf)


def dot_nt(a, b):
    return lax.dot_general(a, b, (((1,), (1,)), ((), ())), preferred_element_type=F32)


def dot_tn(a, b):
    return lax.dot_general(a, b, (((0,), (0,)), ((), ())), preferred_element_type=F32)


def dot_nn(a, b):
    return lax.dot_general(a, b, (((1,), (0,)), ((), ())), preferred_element_type=F32)


def attn_fwd_kernel(q_ref, k_ref, v_ref, bias_ref, o_ref, lse_ref):
    q = q_ref[...] * SCALE
    k = k_ref[...]
    v = v_ref[...]
    bias = bias_ref[...]
    first = lax.broadcasted_iota(jnp.int32, q.shape, 1) < HD
    outs, sums = [], []
    for head in range(2):
        mask = first if head == 0 else jnp.logical_not(first)
        scores = dot_nt(jnp.where(mask, q, jnp.zeros_like(q)), k) + bias
        peak = jnp.max(scores, axis=-1, keepdims=True)
        expo = jnp.exp(scores - peak)
        total = jnp.sum(expo, axis=-1, keepdims=True)
        outs.append(dot_nn(expo.astype(BF), v) / total)
        sums.append(peak + jnp.log(total))
    o_ref[...] = jnp.where(first, outs[0], outs[1]).astype(BF)
    lse_ref[...] = jnp.where(first, sums[0], sums[1])


def attn_fwd(qkv, bias_row):
    rows = qkv.shape[0]
    bq = rows // 4
    return pl.pallas_call(
        attn_fwd_kernel,
        grid=(rows // bq,),
        out_shape=(
            jax.ShapeDtypeStruct((rows, 128), BF),
            jax.ShapeDtypeStruct((rows, 128), F32),
        ),
        in_specs=[
            pl.BlockSpec((bq, 128), lambda i: (i, 0)),
            pl.BlockSpec((rows, 128), lambda i: (0, 1)),
            pl.BlockSpec((rows, 128), lambda i: (0, 2)),
            pl.BlockSpec((1, rows), lambda i: (0, 0)),
        ],
        out_specs=(
            pl.BlockSpec((bq, 128), lambda i: (i, 0)),
            pl.BlockSpec((bq, 128), lambda i: (i, 0)),
        ),
        compiler_params=pltpu.CompilerParams(vmem_limit_bytes=40 << 20),
        cost_estimate=pl.CostEstimate(
            flops=4 * rows * rows * 512, bytes_accessed=rows * 2048, transcendentals=2 * rows * rows
        ),
        name="attn_fwd",
    )(qkv, qkv, qkv, bias_row)


def attn_bwd_kernel(q_ref, k_ref, v_ref, do_ref, o_ref, lse_ref, live_ref, out_ref, dq_ref, row_ref):
    step = pl.program_id(0)
    chunk = k_ref.shape[0]

    @pl.when(step == 0)
    def _():
        row_ref[0:128, :] = lse_ref[...].T
        prod = do_ref[...].astype(F32) * o_ref[...].astype(F32)
        prod_t = prod.T
        row_ref[128:136, :] = jnp.broadcast_to(
            jnp.sum(prod_t[0:HD], axis=0, keepdims=True), (8, prod_t.shape[1])
        )
        row_ref[136:144, :] = jnp.broadcast_to(
            jnp.sum(prod_t[HD:128], axis=0, keepdims=True), (8, prod_t.shape[1])
        )
        dq_ref[...] = jnp.zeros_like(dq_ref)

    q = q_ref[...]
    k = k_ref[...] * SCALE
    v = v_ref[...]
    do = do_ref[...]
    live = live_ref[:, 0:1] > 0
    first = lax.broadcasted_iota(jnp.int32, k.shape, 1) < HD
    dks, dvs = [], []
    for head in range(2):
        mask = first if head == 0 else jnp.logical_not(first)
        kh = jnp.where(mask, k, jnp.zeros_like(k))
        vh = jnp.where(mask, v, jnp.zeros_like(v))
        lse = row_ref[64 * head : 64 * head + 1, :]
        delta = row_ref[128 + 8 * head : 129 + 8 * head, :]
        prob = jnp.where(live, jnp.exp(dot_nt(kh, q) - lse), 0.0)
        ds = (prob * (dot_nt(vh, do) - delta)).astype(BF)
        dvs.append(dot_nn(prob.astype(BF), do))
        dks.append(dot_nn(ds, q) * SCALE)
        dq_ref[...] += dot_tn(ds, kh)
    at = pl.ds(pl.multiple_of(step * chunk, chunk), chunk)
    out_ref[at, 128:256] = jnp.where(first, dks[0], dks[1]).astype(BF)
    out_ref[at, 256:384] = jnp.where(first, dvs[0], dvs[1]).astype(BF)

    @pl.when(step == pl.num_programs(0) - 1)
    def _():
        out_ref[:, 0:128] = dq_ref[...].astype(BF)


def attn_bwd(qkv, grad, out, lse, live_col):
    rows = qkv.shape[0]
    chunk = rows // 4
    return pl.pallas_call(
        attn_bwd_kernel,
        grid=(rows // chunk,),
        out_shape=jax.ShapeDtypeStruct((rows, 384), BF),
        in_specs=[
            pl.BlockSpec((rows, 128), lambda i: (0, 0)),
            pl.BlockSpec((chunk, 128), lambda i: (i, 1)),
            pl.BlockSpec((chunk, 128), lambda i: (i, 2)),
            pl.BlockSpec((rows, 128), lambda i: (0, 0)),
            pl.BlockSpec((rows, 128), lambda i: (0, 0)),
            pl.BlockSpec((rows, 128), lambda i: (0, 0)),
            pl.BlockSpec((chunk, 128), lambda i: (i, 0)),
        ],
        out_specs=pl.BlockSpec((rows, 384), lambda i: (0, 0)),
        scratch_shapes=[pltpu.VMEM((rows, 128), F32), pltpu.VMEM((144, rows), F32)],
        compiler_params=pltpu.CompilerParams(vmem_limit_bytes=50 << 20),
        cost_estimate=pl.CostEstimate(
            flops=10 * rows * rows * 512, bytes_accessed=rows * 4096, transcendentals=2 * rows * rows
        ),
        name="attn_bwd",
    )(qkv, qkv, qkv, grad, out, lse, live_col)


class Moves:
    def __init__(self, send_sems, recv_sems):
        self.send_sems, self.recv_sems, self.count = send_sems, recv_sems, 0

    def make(self, src, dst, device, cond=None, recv_cond=None):
        index = self.count
        self.count += 1
        return Move(self, index, src, dst, device, cond, recv_cond)


class Move:
    def __init__(self, moves, index, src, dst, device, cond, recv_cond):
        self.args = (src, dst, moves.send_sems.at[index], moves.recv_sems.at[index])
        self.device, self.cond, self.recv_cond = device, cond, recv_cond

    def copy(self):
        return pltpu.make_async_remote_copy(
            *self.args, device_id=self.device, device_id_type=pl.DeviceIdType.MESH
        )

    def when(self, cond, act):
        if cond is None:
            act()
        else:
            pl.when(cond)(act)

    def start(self):
        self.when(self.cond, lambda: self.copy().start())

    def wait_recv(self):
        self.when(self.recv_cond, lambda: self.copy().wait_recv())

    def wait_send(self):
        self.when(self.cond, lambda: self.copy().wait_send())


def greet(devices):
    barrier = pltpu.get_barrier_semaphore()
    for device in devices:
        pl.semaphore_signal(
            barrier, inc=1, device_id=device, device_id_type=pl.DeviceIdType.MESH
        )
    pl.semaphore_wait(barrier, len(devices))


def span(start, size):
    return pl.ds(pl.multiple_of(start, size & -size), size)


class Local:
    def __init__(self, sems):
        self.sems, self.count, self.open = sems, 0, []

    def start(self, src, dst):
        copy = pltpu.make_async_copy(src, dst, self.sems.at[self.count])
        self.count += 1
        copy.start()
        self.open.append(copy)
        return copy

    def wait(self, copy):
        copy.wait()
        self.open = [c for c in self.open if c is not copy]

    def finish(self):
        for copy in self.open:
            copy.wait()
        self.open = []


def spread_plane(go, ref_of, me_c, cond=None):
    own = ref_of(me_c, None)
    return [go(own, own, {"context": me_c ^ 1}), go(own, own, {"context": me_c ^ 2})]


def spread_plane_on(go, ref_of, me_c, near):
    near[0].wait_recv()
    piece = ref_of(me_c ^ 1, 0)
    first = go(piece, piece, {"context": me_c ^ 2})
    near[1].wait_recv()
    piece = ref_of(me_c ^ 2, 1)
    second = go(piece, piece, {"context": me_c ^ 1})
    return [first, second]


def forward_kernel(
    nz,
    nc,
    tokens_ref,
    gain_ref,
    count_ref,
    wq_ref,
    wout_ref,
    wup_ref,
    wdown_ref,
    x_out,
    qkv_out,
    o_out,
    lse_out,
    att_out,
    cnt_out,
    wq_out,
    out_full,
    up_full,
    down_part,
    tok,
    x_all,
    qkv,
    o_all,
    lse_all,
    wq,
    counts,
    stage_up,
    stage_out,
    stage_down,
    send,
    recv,
    local_sems,
):
    me_z, me_c, me_t = (lax.axis_index(a) for a in ("fsdp", "context", "tensor"))
    images, local_len = att_out.shape[0], att_out.shape[2]
    half = local_len // 2
    seq = x_all.shape[1]
    core = {"tensor": 1 - me_t}
    z_peers = [{"fsdp": lax.rem(me_z + k, nz)} for k in range(1, nz)]
    c_peers = [{"context": me_c ^ k} for k in range(1, nc)]
    local = Local(local_sems)
    token_in = [
        local.start(tokens_ref.at[i, span(me_t * half, half)], tok.at[i]) for i in range(images)
    ]
    depth = wq_ref.shape[0]
    hid = wup_ref.shape[1] // nc
    staged = [
        local.start(wup_ref.at[:, span(me_c * hid, hid)], stage_up),
        local.start(wout_ref, stage_out),
        local.start(wdown_ref.at[span(me_c * hid, hid)], stage_down),
    ]
    wq_part = wq_ref.at[:, span(me_c * 384, 384)]
    wq_own = local.start(wq_part, wq.at[span(me_z * depth, depth)])
    greet(z_peers + c_peers + [core])
    moves = Moves(send, recv)
    sent = []

    def go(*args, **kw):
        move = moves.make(*args, **kw)
        move.start()
        sent.append(move)
        return move

    wq_in = [go(wq_part, wq.at[span(me_z * depth, depth)], peer) for peer in z_peers]
    counts[me_c] = count_ref[...]
    count_in = [go(count_ref, counts.at[me_c], peer) for peer in c_peers]

    def to_line(index, src, dst):
        local.wait(staged[index])
        local_copy = local.start(src, dst)
        return [local_copy] + [go(src, dst, peer) for peer in z_peers]


    def x_piece(i):
        def at(member, part):
            rows = span(member * local_len + me_t * half, half)
            if part is None:
                return x_all.at[i, rows]
            return x_all.at[i, rows, pl.ds(part * (D // 2), D // 2)]

        return at

    swaps = [[] for _ in range(images)]
    near, far = [], []

    def swap(i, member, part=None):
        piece = x_piece(i)(member, part)
        swaps[i].append(go(piece, piece, core))

    def normalize(i):
        local.wait(token_in[i])
        value = tok[i]
        centred = value - jnp.mean(value, axis=-1, keepdims=True)
        inv_std = lax.rsqrt(jnp.mean(centred * centred, axis=-1, keepdims=True) + 1e-06)
        x_all[i, span(me_c * local_len + me_t * half, half)] = (
            centred * inv_std * gain_ref[0:1, :]
        ).astype(BF)

    def send_near(i):
        near.append(spread_plane(go, x_piece(i), me_c))
        swap(i, me_c)

    def send_far(i):
        far.append(spread_plane_on(go, x_piece(i), me_c, near[i]))
        swap(i, me_c ^ 1)
        swap(i, me_c ^ 2)

    normalize(0)
    send_near(0)
    normalize(1)
    send_near(1)
    normalize(2)
    send_far(0)
    send_near(2)
    local.wait(wq_own)
    for move in wq_in:
        move.wait_recv()
    up_in = to_line(
        0,
        stage_up,
        up_full.at[me_c, span(me_z * depth, depth)],
    )
    local.start(wq, wq_out)
    for move in count_in:
        move.wait_recv()
    total = counts[0]
    for k in range(1, nc):
        total = total + counts[k]
    cnt_out[...] = total

    first = lax.broadcasted_iota(jnp.int32, (local_len, 128), 1) < HD
    place = lax.broadcasted_iota(jnp.int32, (1, seq), 1)

    def up_piece(k):
        start = lax.rem(me_z - k + nz, nz) * depth

        def at(member, part):
            if part is None:
                return up_full.at[member, span(start, depth)]
            return up_full.at[member, span(start + part * (depth // 2), depth // 2)]

        return at

    up_near, up_far = [], []

    def up_step(k):
        if k == 0:
            local.wait(up_in[0])
        else:
            up_in[k].wait_recv()
        up_near.append(spread_plane(go, up_piece(k), me_c))

    def up_step_on(k):
        up_far.extend(spread_plane_on(go, up_piece(k), me_c, up_near[k]))

    att_in = []
    for i in range(images):
        for part in range(2):
            far[i][part].wait_recv()
            swap(i, me_c ^ 3, part)
        for move in swaps[i]:
            move.wait_recv()
        local.start(x_all.at[i], x_out.at[i])

        @pl.loop(0, nc)
        def _(chunk):
            rows = span(chunk * local_len, local_len)
            qkv[i, rows] = dot_nn(x_all[i, rows], wq[...]).astype(BF)

        local.start(qkv.at[i], qkv_out.at[i])
        if i == 0:
            send_far(1)
        bias = jnp.where(place < cnt_out[i : i + 1, 0:1], 0.0, -1e30)
        def attend(chunk):
            rows = span(chunk * local_len, local_len)
            q = qkv[i, rows, 0:128] * SCALE
            k = qkv[i, :, 128:256]
            v = qkv[i, :, 256:384]
            outs, sums = [], []
            for head in range(2):
                mask = first if head == 0 else jnp.logical_not(first)
                scores = dot_nt(jnp.where(mask, q, jnp.zeros_like(q)), k) + bias
                peak = jnp.max(scores, axis=-1, keepdims=True)
                expo = jnp.exp(scores - peak)
                norm = jnp.sum(expo, axis=-1, keepdims=True)
                outs.append(dot_nn(expo.astype(BF), v) / norm)
                sums.append(peak + jnp.log(norm))
            o_all[i, rows] = jnp.where(first, outs[0], outs[1]).astype(BF)
            lse_all[rows] = jnp.where(first, sums[0], sums[1])

        if i == 2:
            up_step_on(0)
            up_step_on(1)
        pl.loop(0, nc)(attend)
        if i == 0:
            send_far(2)
            up_step(0)

        mine = att_out.at[i, me_c]
        for k in range(1, nc):
            att_in.append(
                go(o_all.at[i, span((me_c ^ k) * local_len, local_len)], mine, c_peers[k - 1])
            )
        local.start(o_all.at[i, span(me_c * local_len, local_len)], mine)
        local.start(o_all.at[i], o_out.at[i])
        sums_t = lse_all[...].T
        for head in range(2):
            lse_out[i, 8 * head : 8 * head + 8, :] = jnp.broadcast_to(
                sums_t[HD * head : HD * head + 1], (8, seq)
            )
        if i == 0:
            up_step(1)
            out_in = to_line(1, stage_out, out_full.at[me_z])
        if i == 1:
            up_step(2)
            up_step(3)
            down_in = to_line(
                2,
                stage_down,
                down_part.at[me_z],
            )
    up_step_on(2)
    up_step_on(3)
    for move in up_far:
        move.wait_recv()
    for move in att_in:
        move.wait_recv()
    for move in out_in[1:] + down_in[1:]:
        move.wait_recv()
    local.finish()
    for move in sent:
        move.wait_send()


def forward_attention(tokens, gain, counts, wq_part, w_out, w_up, w_down, nz, nc):
    images, local_len = tokens.shape[:2]
    seq = nc * local_len
    cols, hid = w_out.shape[0], w_up.shape[1]
    any_ = pl.BlockSpec(memory_space=pl.ANY)
    vmem = pl.BlockSpec(memory_space=pltpu.VMEM)
    return pl.pallas_call(
        functools.partial(forward_kernel, nz, nc),
        out_shape=(
            jax.ShapeDtypeStruct((images, seq, D), BF),
            jax.ShapeDtypeStruct((images, seq, 384), BF),
            jax.ShapeDtypeStruct((images, seq, 128), BF),
            jax.ShapeDtypeStruct((images, 16, seq), F32),
            jax.ShapeDtypeStruct((images, nc, local_len, cols // nc), BF),
            jax.ShapeDtypeStruct((8, 128), jnp.int32),
            jax.ShapeDtypeStruct((D, 384), BF),
            jax.ShapeDtypeStruct((nz, cols, D // nz), BF),
            jax.ShapeDtypeStruct((nc, D, hid // nc), BF),
            jax.ShapeDtypeStruct((nz, hid // nc, D // nz), BF),
        ),
        in_specs=[any_, vmem, vmem, any_, any_, any_, any_],
        out_specs=(any_, any_, any_, vmem, any_, vmem, any_, any_, any_, any_),
        scratch_shapes=[
            pltpu.VMEM((images, local_len // 2, D), F32),
            pltpu.VMEM((images, seq, D), BF),
            pltpu.VMEM((images, seq, 384), BF),
            pltpu.VMEM((images, seq, 128), BF),
            pltpu.VMEM((seq, 128), F32),
            pltpu.VMEM((D, 384), BF),
            pltpu.VMEM((nc, 8, 128), jnp.int32),
            pltpu.VMEM((w_up.shape[0], hid // nc), BF),
            pltpu.VMEM(w_out.shape, BF),
            pltpu.VMEM((hid // nc, w_down.shape[1]), BF),
            pltpu.SemaphoreType.DMA((96,)),
            pltpu.SemaphoreType.DMA((96,)),
            pltpu.SemaphoreType.DMA((32,)),
        ],
        compiler_params=pltpu.CompilerParams(
            collective_id=1, has_side_effects=True, vmem_limit_bytes=56 << 20
        ),
        name="forward_attention",
    )(tokens, gain, counts, wq_part, w_out, w_up, w_down)


def feed_forward_kernel(
    nz,
    nc,
    att_ref,
    wout_ref,
    wup_ref,
    wdown_ref,
    tokens_ref,
    cot_ref,
    gains_ref,
    wq_ref,
    output_out,
    mid_out,
    gatt_out,
    tout_out,
    tup_out,
    own_out,
    fary_out,
    farx_out,
    wq_out,
    gain_out,
    att,
    wout,
    wup,
    wdown,
    tok,
    cot,
    normed_low,
    act,
    slope,
    low,
    first_own,
    first_in,
    second_own,
    second_in,
    third_in,
    stage,
    term,
    near_in,
    gatt,
    send,
    recv,
    local_sems,
):
    me_z, me_c, me_t = (lax.axis_index(a) for a in ("fsdp", "context", "tensor"))
    z_peers = [{"fsdp": lax.rem(me_z + k, nz)} for k in range(1, nz)]
    images, local_len = tok.shape[:2]
    hid = wdown_ref.shape[1]
    depth_o = wdown_ref.shape[2]
    x_c, y_c, far_c = me_c ^ 1, me_c ^ 2, me_c ^ 3
    core, x_near, y_near = {"tensor": 1 - me_t}, {"context": x_c}, {"context": y_c}
    left, right = pl.ds(0, D // 2), pl.ds(D // 2, D // 2)
    half = local_len // 2
    local = Local(local_sems)
    down_own = [
        local.start(wdown_ref.at[z], wdown.at[span(me_c * hid, hid), pl.ds(z * depth_o, depth_o)])
        for z in range(nz)
    ]
    att_in = [
        local.start(att_ref.at[:, c], att.at[:, :, pl.ds(c * 128, 128)]) for c in range(nc)
    ] + [local.start(wout_ref.at[z], wout.at[:, pl.ds(z * depth_o, depth_o)]) for z in range(nz)]
    cot_in = local.start(cot_ref, cot)
    tok_in = local.start(tokens_ref, tok)
    up_in = [
        local.start(wup_ref.at[c], wup.at[:, pl.ds(c * hid, hid)]) for c in range(nc)
    ]

    def down_piece(member, part):
        rows = span(member * hid, hid)
        return wdown.at[rows] if part is None else wdown.at[rows, pl.ds(part * (D // 2), D // 2)]

    greet([core, x_near, y_near] + z_peers)
    for copy in down_own:
        local.wait(copy)
    moves = Moves(send, recv)
    sent = []

    def go(*args, **kw):
        move = moves.make(*args, **kw)
        move.start()
        sent.append(move)
        return move

    down_near = [
        go(down_piece(me_c, part), down_piece(me_c, part), device)
        for part, device in (
            (0, x_near),
            (1, y_near),
            (1, x_near),
            (0, y_near),
        )
    ]
    depth = wq_ref.shape[0]
    wq_in = []
    for k in range(1, nc):
        columns = span((me_c ^ k) * 384, 384)
        there = wq_out.at[span(me_z * depth, depth), columns]
        wq_in += [go(wq_ref.at[:, columns], there, peer) for peer in z_peers]
    for copy in att_in:
        local.wait(copy)

    @pl.loop(0, images)
    def _(i):
        first_own[i] = dot_nn(att[i], wout[...]).astype(BF)

    first = go(first_own, first_in, core)
    local.wait(cot_in)

    @pl.loop(0, images)
    def _(i):
        low[i] = (gains_ref[3:4, :] * cot[i]).astype(BF)

    local.wait(tok_in)
    first.wait_recv()

    @pl.loop(0, 2 * images)
    def _(step):
        i, rows = step // 2, span(lax.rem(step, 2) * half, half)
        branch = first_own[i, rows].astype(F32) + first_in[i, rows].astype(F32)
        value = tok[i, rows] + gains_ref[2:3, :] * branch
        tok[i, rows] = value
        centred = value - jnp.mean(value, axis=-1, keepdims=True)
        inv_std = lax.rsqrt(jnp.mean(centred * centred, axis=-1, keepdims=True) + 1e-06)
        normed_low[i, rows] = (centred * inv_std * gains_ref[1:2, :]).astype(BF)

    for copy in up_in:
        local.wait(copy)
    width = 512

    @pl.loop(0, images)
    def _(i):
        @pl.loop(0, wup.shape[1] // width)
        def _(step):
            cols = span(step * width, width)
            value = dot_nn(normed_low[i], wup[:, cols])
            cdf = 0.5 * (1.0 + lax.erf(value * 0.7071067811865476))
            pdf = jnp.exp(-0.5 * value * value) * 0.3989422804014327
            act[i, :, cols] = (value * cdf).astype(BF)
            slope[i, :, cols] = (cdf + value * pdf).astype(BF)

    down_near[0].wait_recv()
    x_piece = down_piece(x_c, 0)
    down_far = [go(x_piece, x_piece, y_near)]
    down_near[1].wait_recv()
    y_piece = down_piece(y_c, 1)
    down_far.append(go(y_piece, y_piece, x_near))
    blocks = term.shape[0]
    chunk_rows = term.shape[2]

    @pl.loop(0, blocks)
    def _(j):
        cols = span(j * width, width)
        total = jnp.zeros((width, D), F32)
        for i in range(images):
            total += dot_tn(act[i, :, cols], low[i])
        for c in range(nc):
            term[j, c] = total[c * chunk_rows : (c + 1) * chunk_rows].astype(BF)

    near = [
        go(term.at[:, x_c, :, left], near_in.at[0], x_near),
        go(term.at[:, far_c, :, left], near_in.at[1], x_near),
        go(term.at[:, y_c, :, right], near_in.at[2], y_near),
        go(term.at[:, far_c, :, right], near_in.at[3], y_near),
    ]
    for move in down_near[2:]:
        move.wait_recv()

    def back_down(member):
        columns = span(member * hid, hid)

        @pl.loop(0, images)
        def _(i):
            value = dot_nt(low[i], wdown[columns, :]) * slope[i, :, columns].astype(F32)
            slope[i, :, columns] = value.astype(BF)

    copies = []

    def up_term(k):
        if k >= 2:
            local.wait(copies[k - 2])
        cols = span((me_c ^ k) * width, width)
        total = jnp.zeros((width, D), F32)
        for i in range(images):
            total += dot_tn(slope[i, :, cols], normed_low[i])
        stage[k % 2] = total.astype(BF)
        copies.append(local.start(stage.at[k % 2], tup_out.at[cols]))

    @pl.loop(0, 3)
    def _(k):
        back_down(me_c ^ k)

    for k in range(3):
        up_term(k)
    for move in down_far:
        move.wait_recv()
    back_down(far_c)

    @pl.loop(0, images)
    def _(i):
        second_own[i] = dot_nn(act[i], wdown[...]).astype(BF)

    second = go(second_own, second_in, core)
    first.wait_send()
    sent.remove(first)
    gain_out[...] = jnp.zeros_like(gain_out)

    @pl.loop(0, 2 * images)
    def _(step):
        i, rows = step // 2, span(lax.rem(step, 2) * half, half)
        branch = first_own[i, rows].astype(F32) + first_in[i, rows].astype(F32)
        first_in[i, rows] = branch.astype(BF)

    @pl.loop(0, images)
    def _(i):
        first_own[i] = dot_nt(slope[i], wup[...]).astype(BF)

    third = go(first_own, third_in, core)

    up_term(3)
    second.wait_recv()
    third.wait_recv()

    @pl.loop(0, 2 * images)
    def _(step):
        i, rows = step // 2, span(lax.rem(step, 2) * half, half)
        value = tok[i, rows]
        centred = value - jnp.mean(value, axis=-1, keepdims=True)
        inv_std = lax.rsqrt(jnp.mean(centred * centred, axis=-1, keepdims=True) + 1e-06)
        normed = centred * inv_std
        branch = second_own[i, rows].astype(F32) + second_in[i, rows].astype(F32)
        tok[i, rows] = value + gains_ref[3:4, :] * branch
        cotangent = cot[i, rows]
        gain_out[3:4, :] += jnp.sum(cotangent * branch, axis=0, keepdims=True)
        grad = first_own[i, rows].astype(F32) + third_in[i, rows].astype(F32)
        gain_out[1:2, :] += jnp.sum(grad * normed, axis=0, keepdims=True)
        scaled = grad * gains_ref[1:2, :]
        inner = (
            scaled
            - jnp.mean(scaled, axis=-1, keepdims=True)
            - normed * jnp.mean(scaled * normed, axis=-1, keepdims=True)
        )
        grad = cotangent + inner * inv_std
        cot[i, rows] = grad
        gain_out[2:3, :] += jnp.sum(grad * first_in[i, rows].astype(F32), axis=0, keepdims=True)
        low[i, rows] = (gains_ref[2:3, :] * grad).astype(BF)

    local.start(tok, output_out)
    local.start(cot, mid_out)

    @pl.loop(0, images)
    def _(i):
        gatt[i] = dot_nt(low[i], wout[...]).astype(BF)

    for c in range(nc):
        local.start(gatt.at[:, :, pl.ds(c * 128, 128)], gatt_out.at[:, c])
    total = jnp.zeros((att.shape[2], D), F32)
    for i in range(images):
        total += dot_tn(att[i], low[i])
    for copy in copies[-2:]:
        local.wait(copy)
    stage[0] = total.astype(BF)
    local.start(stage.at[0], tout_out)
    for move in near:
        move.wait_recv()
    for move in near:
        move.wait_send()
        sent.remove(move)
    term[:, me_c, :, left] += near_in[0]
    term[:, me_c, :, right] += near_in[2]
    term[:, y_c, :, left] += near_in[1]
    term[:, x_c, :, right] += near_in[3]
    for move in wq_in:
        move.wait_recv()
    local.start(term.at[:, me_c], own_out)
    local.start(term.at[:, y_c, :, left], fary_out)
    local.start(term.at[:, x_c, :, right], farx_out)
    local.finish()
    for move in sent:
        move.wait_send()


def feed_forward(attended, out_full, up_full, down_part, tokens, cotangent, gains, wq_rows, nz, nc):
    images, local_len = tokens.shape[:2]
    cols, hid = out_full.shape[1], nc * up_full.shape[2]
    blocks = hid // 512
    piece = (blocks, 512 // nc)
    any_ = pl.BlockSpec(memory_space=pl.ANY)
    vmem = pl.BlockSpec(memory_space=pltpu.VMEM)
    rows = (images, local_len)
    return pl.pallas_call(
        functools.partial(feed_forward_kernel, nz, nc),
        out_shape=(
            jax.ShapeDtypeStruct(rows + (D,), F32),
            jax.ShapeDtypeStruct(rows + (D,), F32),
            jax.ShapeDtypeStruct((images, nc, local_len, cols // nc), BF),
            jax.ShapeDtypeStruct((cols, D), BF),
            jax.ShapeDtypeStruct((hid, D), BF),
            jax.ShapeDtypeStruct(piece + (D,), BF),
            jax.ShapeDtypeStruct(piece + (D // 2,), BF),
            jax.ShapeDtypeStruct(piece + (D // 2,), BF),
            jax.ShapeDtypeStruct((D, nc * 384), BF),
            jax.ShapeDtypeStruct((8, D), F32),
        ),
        in_specs=[any_] * 6 + [vmem, any_],
        out_specs=(any_,) * 9 + (vmem,),
        scratch_shapes=[
            pltpu.VMEM(rows + (cols,), BF),
            pltpu.VMEM((cols, D), BF),
            pltpu.VMEM((D, hid), BF),
            pltpu.VMEM((hid, D), BF),
            pltpu.VMEM(rows + (D,), F32),
            pltpu.VMEM(rows + (D,), F32),
            pltpu.VMEM(rows + (D,), BF),
            pltpu.VMEM(rows + (hid,), BF),
            pltpu.VMEM(rows + (hid,), BF),
            pltpu.VMEM(rows + (D,), BF),
            pltpu.VMEM(rows + (D,), BF),
            pltpu.VMEM(rows + (D,), BF),
            pltpu.VMEM(rows + (D,), BF),
            pltpu.VMEM(rows + (D,), BF),
            pltpu.VMEM(rows + (D,), BF),
            pltpu.VMEM((2, 512, D), BF),
            pltpu.VMEM((blocks, nc, 512 // nc, D), BF),
            pltpu.VMEM((4, blocks, 512 // nc, D // 2), BF),
            pltpu.VMEM(rows + (cols,), BF),
            pltpu.SemaphoreType.DMA((32,)),
            pltpu.SemaphoreType.DMA((32,)),
            pltpu.SemaphoreType.DMA((48,)),
        ],
        compiler_params=pltpu.CompilerParams(
            collective_id=4, has_side_effects=True, vmem_limit_bytes=62 << 20
        ),
        name="feed_forward",
    )(attended, out_full, up_full, down_part, tokens, cotangent, gains, wq_rows)


def backward_kernel(
    nz,
    nc,
    qkv_ref,
    o_ref,
    lse_ref,
    att_ref,
    cnt_ref,
    term_out_ref,
    term_up_ref,
    down_ref,
    down_y_ref,
    down_x_ref,
    x_ref,
    early_out,
    late_hbm,
    heads_out,
    grad,
    heads,
    qkv,
    o_all,
    x_all,
    dq_ref,
    row_ref,
    weight_ref,
    own_ref,
    far_y,
    far_x,
    near_in,
    far_in,
    mine_ref,
    mine_in_ref,
    zpart_ref,
    zsend_ref,
    znext_ref,
    late_ref,
    lpart_ref,
    lsend_ref,
    lnext_ref,
    early_ref,
    late_out,
    send,
    recv,
    local_sems,
):
    me_z, me_c, me_t = (lax.axis_index(a) for a in ("fsdp", "context", "tensor"))
    images, local_len = att_ref.shape[0], att_ref.shape[2]
    x_c, y_c, far_c = me_c ^ 1, me_c ^ 2, me_c ^ 3
    x_near, y_near = {"context": x_c}, {"context": y_c}
    z_peers = [{"fsdp": lax.rem(me_z + k, nz)} for k in range(1, nz)]
    c_peers = [{"context": me_c ^ k} for k in range(1, nc)]
    left, right = pl.ds(0, D // 2), pl.ds(D // 2, D // 2)
    ups, downs = term_up_ref.shape[0], down_ref.shape[0]
    terms = [(term_out_ref, 0)] + [(term_up_ref, j) for j in range(ups)]
    local = Local(local_sems)
    greet(z_peers + c_peers)
    moves = Moves(send, recv)
    sent = []

    def go(*args, **kw):
        move = moves.make(*args, **kw)
        move.start()
        sent.append(move)
        return move

    grad_in = []

    def send_grad(i):
        here = grad.at[i, span(me_c * local_len, local_len)]
        grad_in.append(
            [local.start(att_ref.at[i, me_c], here)]
            + [
                go(att_ref.at[i, me_c ^ k], here, c_peers[k - 1])
                for k in range(1, nc)
            ]
        )

    near = []

    def send_term(index):
        ref, block = terms[index]
        near.append(
            [
                go(ref.at[block, x_c, :, :, left], near_in.at[index, 0], x_near),
                go(ref.at[block, far_c, :, :, left], near_in.at[index, 1], x_near),
                go(ref.at[block, y_c, :, :, right], near_in.at[index, 2], y_near),
                go(ref.at[block, far_c, :, :, right], near_in.at[index, 3], y_near),
            ]
        )

    send_grad(0)
    held = [
        [local.start(a.at[i], b.at[i]) for a, b in ((qkv_ref, qkv), (o_ref, o_all))]
        for i in range(images)
    ]
    x_in = [local.start(x_ref.at[i], x_all.at[i % 2]) for i in range(2)]
    own_in, far_own = [], []
    for index, (ref, block) in enumerate(terms):
        own_in.append(local.start(ref.at[block, me_c], own_ref.at[index]))
        far_own.append(local.start(ref.at[block, y_c, :, :, left], far_y.at[index]))
        far_own.append(local.start(ref.at[block, x_c, :, :, right], far_x.at[index]))
    mine_in = local.start(down_ref, mine_ref)
    down_far = [
        go(down_y_ref, mine_in_ref.at[0], y_near),
        go(down_x_ref, mine_in_ref.at[1], x_near),
    ]
    send_grad(1)
    send_term(0)
    send_term(1)
    send_grad(2)
    send_term(2)
    z_pair, z_next = {"fsdp": me_z ^ 1}, {"fsdp": me_z ^ 2}

    def halve(ref, low, count, at):
        blocks = pl.ds(low, count)
        return [
            go(ref.at[blocks, me_z ^ 1], zpart_ref.at[0, pl.ds(at, count)], z_pair),
            go(ref.at[blocks, me_z ^ 3], zpart_ref.at[1, pl.ds(at, count)], z_pair),
        ]

    def halve_on(moves_in, own, count, at):
        for move in moves_in:
            move.wait_recv()
        for block in range(count):
            zsend_ref[at + block] = own(block) + zpart_ref[1, at + block]
        blocks = pl.ds(at, count)
        return go(zsend_ref.at[blocks], znext_ref.at[blocks], z_next)

    first = lax.broadcasted_iota(jnp.int32, (local_len, 128), 1) < HD
    place = lax.broadcasted_iota(jnp.int32, (local_len, 128), 0)
    weight_ref[...] = jnp.zeros_like(weight_ref)
    far_moves = []

    def sum_step(index):
        for move in near[index]:
            move.wait_recv()
        local.wait(own_in[index])
        local.wait(far_own[2 * index])
        local.wait(far_own[2 * index + 1])
        far_y[index] += near_in[index, 1]
        first_far = go(far_y.at[index], far_in.at[index, 0], y_near)
        far_x[index] += near_in[index, 3]
        far_moves.append((first_far, go(far_x.at[index], far_in.at[index, 1], x_near)))

    def sum_end(index):
        for move in far_moves[index]:
            move.wait_recv()
        own_ref[index, :, :, left] += near_in[index, 0] + far_in[index, 0]
        own_ref[index, :, :, right] += near_in[index, 2] + far_in[index, 1]

    for i in range(images):
        for copy in held[i]:
            local.wait(copy)
        local.wait(grad_in[i][0])
        for move in grad_in[i][1:]:
            move.wait_recv()
        prod = (grad[i].astype(F32) * o_all[i].astype(F32)).T
        for head in range(2):
            row_ref[8 * head : 8 * head + 8, :] = jnp.broadcast_to(
                jnp.sum(prod[HD * head : HD * (head + 1)], axis=0, keepdims=True),
                (8, prod.shape[1]),
            )
        dq_ref[...] = jnp.zeros_like(dq_ref)
        real = cnt_ref[i : i + 1, :]

        def attend(chunk):
            rows = span(chunk * local_len, local_len)
            q = qkv[i, :, 0:128]
            k = qkv[i, rows, 128:256] * SCALE
            v = qkv[i, rows, 256:384]
            do = grad[i]
            live = (place + chunk * local_len < real)[:, 0:1]
            dks, dvs = [], []
            for head in range(2):
                mask = first if head == 0 else jnp.logical_not(first)
                kh = jnp.where(mask, k, jnp.zeros_like(k))
                vh = jnp.where(mask, v, jnp.zeros_like(v))
                lse = lse_ref[i, 8 * head : 8 * head + 1, :]
                delta = row_ref[8 * head : 8 * head + 1, :]
                prob = jnp.where(live, jnp.exp(dot_nt(kh, q) - lse), 0.0)
                ds = (prob * (dot_nt(vh, do) - delta)).astype(BF)
                dvs.append(dot_nn(prob.astype(BF), do))
                dks.append(dot_nn(ds, q) * SCALE)
                dq_ref[...] += dot_tn(ds, kh)
            heads[i, rows, 128:256] = jnp.where(first, dks[0], dks[1]).astype(BF)
            heads[i, rows, 256:384] = jnp.where(first, dvs[0], dvs[1]).astype(BF)

        if i < 2:
            pl.loop(0, nc)(attend)
        if i == 2:
            pl.loop(0, nc // 2)(attend)
            sum_step(2)
            sum_end(0)
            sum_end(1)
            group_a = halve(own_ref, 0, 2, 0)
            pl.loop(nc // 2, nc)(attend)
        heads[i, :, 0:128] = dq_ref[...].astype(BF)
        if i == 0:
            local.wait(mine_in)
            for move in down_far:
                move.wait_recv()
            mine_ref[:, :, :, left] += mine_in_ref[0]
            mine_ref[:, :, :, right] += mine_in_ref[1]
            down_in = halve(mine_ref, 0, downs, len(terms))
        if i == 1:
            sum_step(0)
            sum_step(1)
            for index in range(3, len(terms)):
                send_term(index)
            down_next = halve_on(down_in, lambda b: mine_ref[b, me_z ^ 2], downs, len(terms))
        if i == 2:
            for index in range(3, len(terms)):
                sum_step(index)
            sum_end(2)
            group_m = halve(own_ref, 2, 1, 2)
        local.wait(x_in[i])

        @pl.loop(0, nc)
        def _(chunk):
            rows = span(chunk * local_len, local_len)
            weight_ref[...] += dot_tn(heads[i, rows], x_all[i % 2, rows])

        local.start(heads.at[i], heads_out.at[i])
        if i + 2 < images:
            x_in.append(local.start(x_ref.at[i + 2], x_all.at[i % 2]))
    sub = late_ref.shape[2]
    for z in range(nz):
        for j in range(LATE):
            late_ref[z, j] = weight_ref[pl.ds(j * 128 + z * sub, sub)].astype(BF)
    late_in = [
        go(late_ref.at[me_z ^ 1], lpart_ref.at[0], z_pair),
        go(late_ref.at[me_z ^ 3], lpart_ref.at[1], z_pair),
    ]
    a_next = halve_on(group_a, lambda b: own_ref[b, me_z ^ 2], 2, 0)
    for index in range(3, len(terms)):
        sum_end(index)
    group_b = halve(own_ref, 3, len(terms) - 3, 3)
    m_next = halve_on(group_m, lambda b: own_ref[2, me_z ^ 2], 1, 2)
    next_in = [down_next, a_next, m_next]
    for move in late_in:
        move.wait_recv()
    lsend_ref[...] = late_ref[me_z ^ 2] + lpart_ref[1]
    late_next = go(lsend_ref, lnext_ref, z_next)
    next_in.append(
        halve_on(group_b, lambda b: own_ref[3 + b, me_z ^ 2], len(terms) - 3, 3)
    )
    late_next.wait_recv()
    total = late_ref[me_z].astype(F32) + lpart_ref[0].astype(F32) + lnext_ref[...].astype(F32)
    late_out[...] = total.astype(BF)
    local.start(late_out, late_hbm)
    for move in next_in:
        move.wait_recv()
    for block in range(EARLY):
        if block < len(terms):
            total = own_ref[block, me_z].astype(F32)
        else:
            total = mine_ref[block - len(terms), me_z].astype(F32)
        total = total + zpart_ref[0, block].astype(F32) + znext_ref[block].astype(F32)
        early_ref[block] = total.astype(BF)
    local.start(early_ref, early_out)
    local.finish()
    for move in sent:
        move.wait_send()


def backward_attention(
    qkv, o_heads, lse, grad_att, counts, term_out, term_up, down, down_y, down_x, x_all, nz, nc
):
    images, seq = qkv.shape[:2]
    local_len = seq // nc
    sub = term_up.shape[3]
    terms = 1 + term_up.shape[0]
    any_ = pl.BlockSpec(memory_space=pl.ANY)
    vmem = pl.BlockSpec(memory_space=pltpu.VMEM)
    return pl.pallas_call(
        functools.partial(backward_kernel, nz, nc),
        out_shape=(
            jax.ShapeDtypeStruct((EARLY, sub, D), BF),
            jax.ShapeDtypeStruct((LATE, sub, D), BF),
            jax.ShapeDtypeStruct((images, seq, 384), BF),
        ),
        in_specs=[
            any_,
            any_,
            vmem,
            any_,
            vmem,
            any_,
            any_,
            any_,
            any_,
            any_,
            any_,
        ],
        out_specs=(any_, any_, any_),
        scratch_shapes=[
            pltpu.VMEM((images, seq, 128), BF),
            pltpu.VMEM((images, seq, 384), BF),
            pltpu.VMEM((images, seq, 384), BF),
            pltpu.VMEM((images, seq, 128), BF),
            pltpu.VMEM((2, seq, D), BF),
            pltpu.VMEM((seq, 128), F32),
            pltpu.VMEM((16, seq), F32),
            pltpu.VMEM((384, D), F32),
            pltpu.VMEM((terms, nz, sub, D), BF),
            pltpu.VMEM((terms, nz, sub, D // 2), BF),
            pltpu.VMEM((terms, nz, sub, D // 2), BF),
            pltpu.VMEM((terms, 4, nz, sub, D // 2), BF),
            pltpu.VMEM((terms, 2, nz, sub, D // 2), BF),
            pltpu.VMEM((EARLY - terms, nz, sub, D), BF),
            pltpu.VMEM((2, EARLY - terms, nz, sub, D // 2), BF),
            pltpu.VMEM((2, EARLY, sub, D), BF),
            pltpu.VMEM((EARLY, sub, D), BF),
            pltpu.VMEM((EARLY, sub, D), BF),
            pltpu.VMEM((nz, LATE, sub, D), BF),
            pltpu.VMEM((2, LATE, sub, D), BF),
            pltpu.VMEM((LATE, sub, D), BF),
            pltpu.VMEM((LATE, sub, D), BF),
            pltpu.VMEM((EARLY, sub, D), BF),
            pltpu.VMEM((LATE, sub, D), BF),
            pltpu.SemaphoreType.DMA((256,)),
            pltpu.SemaphoreType.DMA((256,)),
            pltpu.SemaphoreType.DMA((64,)),
        ],
        compiler_params=pltpu.CompilerParams(
            collective_id=2, has_side_effects=True, vmem_limit_bytes=61 << 20
        ),
        name="backward_attention",
    )(
        qkv,
        o_heads,
        lse,
        grad_att,
        counts,
        term_out,
        term_up,
        down,
        down_y,
        down_x,
        x_all,
    )


def tail_kernel(
    nz,
    nc,
    token_count,
    slot_blocks,
    early_hbm,
    late_hbm,
    heads_ref,
    wq_own_ref,
    wq_rows_ref,
    wq_ref,
    tokens_ref,
    mid_ref,
    gain_hbm,
    gains_hbm,
    rl_ref,
    rr_ref,
    sl_ref,
    sr_ref,
    ms_ref,
    tokens_out,
    gain_out,
    grad_hbm,
    left_hbm,
    right_hbm,
    weight_hbm,
    early_ref,
    late_ref,
    gain_ref,
    gains_ref,
    grad_out,
    left_out,
    right_out,
    tok,
    wq,
    x_buf,
    mid_buf,
    part,
    part_in,
    rl,
    rr,
    sl,
    sr,
    ms,
    update,
    square,
    square_in,
    gain_sum,
    gain_in,
    place_ref,
    g_ref,
    l_ref,
    g_all,
    send,
    recv,
    local_sems,
):
    me_z, me_c, me_t = (lax.axis_index(a) for a in ("fsdp", "context", "tensor"))
    images, local_len = tokens_ref.shape[:2]
    slots = g_ref.shape[0]
    x_c, y_c, far_c = me_c ^ 1, me_c ^ 2, me_c ^ 3
    core, x_near, y_near = {"tensor": 1 - me_t}, {"context": x_c}, {"context": y_c}
    above, below = {"fsdp": me_z + 1}, {"fsdp": me_z - 1}
    c_peers = [{"context": me_c ^ k} for k in range(1, nc)]
    group = [
        {"fsdp": me_z ^ (k // 2), "tensor": me_t ^ (k % 2)} for k in range(1, 2 * nz)
    ]
    rows_group = [(me_z ^ (k // nc), me_c ^ (k % nc)) for k in range(1, nz * nc)]
    others = [{"fsdp": z, "context": c} for z, c in rows_group[nc - 1 :] ]
    diagonal = [d for k, d in enumerate(others) if (k + nc) % nc]
    left, right = pl.ds(0, D // 2), pl.ds(D // 2, D // 2)
    local = Local(local_sems)
    small_in = [
        local.start(a, b)
        for a, b in (
            (early_hbm, early_ref),
            (late_hbm, late_ref),
            (gain_hbm, gain_ref),
            (gains_hbm, gains_ref),
        )
    ]
    barrier = pltpu.get_barrier_semaphore()
    for device in group + c_peers + diagonal:
        pl.semaphore_signal(
            barrier, inc=1, device_id=device, device_id_type=pl.DeviceIdType.MESH
        )
    for copy in small_in:
        local.wait(copy)
    for slot in range(NBLK):
        block = jnp.clip(slot_blocks[slot] - LATE, 0, EARLY - 1)
        place_ref[slot] = early_ref[block]
    l_ref[:, me_t, me_c, me_z] = late_ref[...]
    for slot in range(slots):
        g_ref[slot, me_t, me_c, me_z] = place_ref[me_c * slots + slot]
    pl.semaphore_wait(barrier, len(group + c_peers + diagonal))
    moves = Moves(send, recv)
    sent = []

    def go(*args, **kw):
        move = moves.make(*args, **kw)
        move.start()
        sent.append(move)
        return move

    placed = []
    for k in range(1, nc):
        theirs = place_ref.at[pl.ds((me_c ^ k) * slots, slots)]
        placed.append(go(theirs, g_ref.at[:, me_t, me_c, me_z], c_peers[k - 1]))

    swapped = []

    def swap(piece, cond=None):
        swapped.append(go(piece, piece, core, cond=cond, recv_cond=cond))

    def along_fsdp(at):
        own = at(me_z)
        return [
            go(own, own, above, cond=me_z < nz - 1, recv_cond=me_z > 0),
            go(own, own, below, cond=me_z > 0, recv_cond=me_z < nz - 1),
        ]

    def onward(at, last, hop):
        up_z, down_z = me_z - hop, me_z + hop
        last[0].wait_recv()
        up = down = None
        if hop < nz - 1:
            piece = at(up_z)
            cond = jnp.logical_and(me_z < nz - 1, up_z >= 0)
            up = go(piece, piece, above, cond=cond, recv_cond=up_z - 1 >= 0)
        last[1].wait_recv()
        if hop < nz - 1:
            piece = at(down_z)
            cond = jnp.logical_and(me_z > 0, down_z <= nz - 1)
            down = go(piece, piece, below, cond=cond, recv_cond=down_z + 1 <= nz - 1)
        return [up, down], [(up_z, up_z >= 0), (down_z, down_z <= nz - 1)]

    def late_at(member):
        return lambda z: l_ref.at[:, me_t, member, z]

    def member_at(k):
        return lambda z: g_ref.at[:, me_t, me_c ^ k, z]

    late_line = along_fsdp(late_at(me_c))
    lines = [along_fsdp(member_at(0))]
    tok_in = []

    def send_tok(i):
        there = tok.at[i, :, span(me_c * 384, 384)]
        tok_in.append(
            [local.start(heads_ref.at[i, span(me_c * local_len, local_len)], there)]
            + [
                go(
                    heads_ref.at[i, span((me_c ^ k) * local_len, local_len)],
                    there,
                    c_peers[k - 1],
                )
                for k in range(1, nc)
            ]
        )
    def late_on(hop):
        nonlocal late_line
        late_line, _ = onward(late_at(me_c), late_line, hop)

    send_tok(0)
    send_tok(1)
    width = wq.shape[1] // nc
    depth = wq_rows_ref.shape[0]
    wq_in = [local.start(wq_own_ref, wq.at[:, span(me_c * width, width)])]
    for m in (x_c, y_c, far_c):
        columns = span(m * width, width)
        wq_in.append(
            local.start(wq_rows_ref.at[:, columns], wq.at[span(me_z * depth, depth), columns])
        )
        for k in range(1, nz):
            at = (span(lax.rem(me_z + k, nz) * depth, depth), columns)
            wq_in.append(local.start(wq_ref.at[at], wq.at[at]))
    x_in = [local.start(tokens_ref.at[i], x_buf.at[i]) for i in range(images)]
    mid_in = [local.start(mid_ref.at[i], mid_buf.at[i]) for i in range(images)]
    state_in = [
        local.start(a, b) for a, b in ((rl_ref, rl), (sl_ref, sl), (sr_ref, sr), (ms_ref, ms))
    ]
    rr_in = [local.start(rr_ref.at[0], rr)]
    late_on(1)
    for k in range(1, nc):
        placed[k - 1].wait_recv()
        lines.append(along_fsdp(member_at(k)))
        if k == 2:
            late_on(2)
    swap(g_ref.at[:, me_t, :, me_z])
    late_on(3)
    late_own = l_ref.at[:, me_t, me_c]
    near = [go(late_own, late_own, x_near), go(late_own, late_own, y_near)]
    swap(late_own)

    part_moves = []
    gain_out[...] = jnp.zeros_like(gain_out)
    square[...] = jnp.zeros_like(square)

    def project(i):
        local.wait(tok_in[i][0])
        for move in tok_in[i][1:]:
            move.wait_recv()
        part[i] = dot_nt(tok[i], wq[...]).astype(BF)
        part_moves.append(go(part.at[i], part_in.at[i], core))

    def norm_backward(i):
        part_moves[i].wait_recv()
        local.wait(x_in[i])
        local.wait(mid_in[i])

        @pl.loop(0, 2)
        def _(step):
            rows = span(step * (local_len // 2), local_len // 2)
            value = x_buf[i, rows]
            centred = value - jnp.mean(value, axis=-1, keepdims=True)
            inv_std = lax.rsqrt(jnp.mean(centred * centred, axis=-1, keepdims=True) + 1e-06)
            normed = centred * inv_std
            grad = part[i, rows].astype(F32) + part_in[i, rows].astype(F32)
            scaled = grad * gain_ref[0:1, :]
            inner = (
                scaled
                - jnp.mean(scaled, axis=-1, keepdims=True)
                - normed * jnp.mean(scaled * normed, axis=-1, keepdims=True)
            )
            mid_buf[i, rows] += inner * inv_std
            gain_out[0:1, :] += jnp.sum(grad * normed, axis=0, keepdims=True)

        local.start(mid_buf.at[i], tokens_out.at[i])

    def slots_on(hop):
        for k in range(nc):
            lines[k], here = onward(member_at(k), lines[k], hop)
        for z, cond in here:
            swap(g_ref.at[:, me_t, :, z], cond)

    slots_on(1)
    slots_on(2)
    near[0].wait_recv()
    piece = l_ref.at[:, me_t, x_c, :, :, left]
    far = [go(piece, piece, y_near)]
    near[1].wait_recv()
    piece = l_ref.at[:, me_t, y_c, :, :, right]
    far.append(go(piece, piece, x_near))
    send_tok(2)
    swap(l_ref.at[:, me_t, x_c])
    swap(l_ref.at[:, me_t, y_c])
    for copy in wq_in:
        local.wait(copy)
    project(0)
    norm_backward(0)
    for move in far:
        move.wait_recv()
    swap(l_ref.at[:, me_t, far_c])
    project(1)
    norm_backward(1)
    last = []
    for k in range(nc):
        _, here = onward(member_at(k), lines[k], 3)
        for z, cond in here:
            piece = member_at(k)(z)
            last.append(go(piece, piece, core, cond=cond, recv_cond=cond))
    for move in swapped:
        move.wait_recv()
    for copy in state_in:
        local.wait(copy)
    offset = me_t * (D // 2) + me_z * rl.shape[1]
    mine = span(offset, rl.shape[1])

    def step(slot):
        block = slot_blocks[me_c * slots + slot]
        late = l_ref[jnp.clip(block, 0, LATE - 1)]
        g_all[...] = jnp.where(block < LATE, late, g_ref[slot]).reshape(D, D)
        rows = g_all[mine, :]
        grad_out[slot] = rows.astype(F32)
        left_out[slot] = 0.5 * sl[slot] + 0.5 / token_count * dot_nt(rows, g_all[...])
        right_out[slot] = 0.5 * sr[slot] + 0.5 / token_count * dot_tn(g_all[:, mine], g_all[...])
        for a, b in ((grad_out, grad_hbm), (left_out, left_hbm), (right_out, right_hbm)):
            local.start(a.at[slot], b.at[slot])
        inner = dot_nn(rl[slot].astype(BF), g_all[...]).astype(BF)
        local.wait(rr_in[slot])
        update[slot] = dot_nn(inner, rr[...].astype(BF))
        if slot + 1 < slots:
            rr_in.append(local.start(rr_ref.at[slot + 1], rr))
        total = jnp.sum(update[slot] * update[slot], axis=0, keepdims=True)
        total = jnp.sum(total, axis=1, keepdims=True)
        square[slot : slot + 1, :] = jnp.broadcast_to(total, (1, 128))

    for move in last:
        move.wait_recv()
    step(0)
    step(1)
    project(2)
    step(2)
    square_moves = [
        go(square, square_in.at[k], group[k]) for k in range(len(group))
    ]
    norm_backward(2)
    gain_sum[...] = gains_ref[...]
    gain_sum[0:1, :] = gain_out[0:1, :]
    gain_moves = []
    for k, (z, c) in enumerate(rows_group):
        theirs = span((z * nc + c) // 2 * 128, 128)
        gain_moves.append(
            go(gain_sum.at[:, theirs], gain_in.at[k], {"fsdp": z, "context": c})
        )
    for move in square_moves:
        move.wait_recv()
    for slot in range(slots):
        total = square[slot : slot + 1, 0:1]
        for k in range(len(group)):
            total = total + square_in[k, slot : slot + 1, 0:1]
        ms[slot] -= lax.rsqrt(total / (D * D) + 1e-06) * update[slot]
        local.start(ms.at[slot], weight_hbm.at[slot])
    total = gain_sum[:, span((me_z * nc + me_c) // 2 * 128, 128)]
    for k, move in enumerate(gain_moves):
        move.wait_recv()
        total = total + gain_in[k]
    gain_out[:, 0:128] = total
    local.finish()
    for move in sent:
        move.wait_send()


def tail(
    block_of,
    early,
    late,
    grad_heads,
    wq,
    wq_rows,
    wq_all,
    tokens,
    grad_middle,
    gain,
    gain_terms,
    root_left,
    root_right,
    stat_left,
    stat_right,
    master,
    token_count,
    nz,
    nc,
    nt,
):
    images, local_len = tokens.shape[:2]
    sub = early.shape[1]
    slots, row_count = root_left.shape[:2]
    any_ = pl.BlockSpec(memory_space=pl.ANY)
    vmem = pl.BlockSpec(memory_space=pltpu.VMEM)
    state = jax.ShapeDtypeStruct((slots, row_count, D), F32)
    shape = (slots, nt, nc, nz, sub, D)
    return pl.pallas_call(
        functools.partial(tail_kernel, nz, nc, token_count),
        out_shape=(
            jax.ShapeDtypeStruct((images, local_len, D), F32),
            jax.ShapeDtypeStruct((8, D), F32),
            state,
            state,
            state,
            state,
        ),
        in_specs=[pl.BlockSpec(memory_space=pltpu.SMEM)] + [any_] * 15,
        out_specs=(any_, vmem, any_, any_, any_, any_),
        scratch_shapes=[
            pltpu.VMEM((EARLY, sub, D), BF),
            pltpu.VMEM((LATE, sub, D), BF),
            pltpu.VMEM((4, D), F32),
            pltpu.VMEM((8, D), F32),
            pltpu.VMEM((slots, row_count, D), F32),
            pltpu.VMEM((slots, row_count, D), F32),
            pltpu.VMEM((slots, row_count, D), F32),
            pltpu.VMEM((images, local_len, nc * 384), BF),
            pltpu.VMEM((D, nc * 384), BF),
            pltpu.VMEM((images, local_len, D), F32),
            pltpu.VMEM((images, local_len, D), F32),
            pltpu.VMEM((images, local_len, D), BF),
            pltpu.VMEM((images, local_len, D), BF),
            pltpu.VMEM((slots, row_count, D), F32),
            pltpu.VMEM((D, D), F32),
            pltpu.VMEM((slots, row_count, D), F32),
            pltpu.VMEM((slots, row_count, D), F32),
            pltpu.VMEM((slots, row_count, D), F32),
            pltpu.VMEM((slots, row_count, D), F32),
            pltpu.VMEM((8, 128), F32),
            pltpu.VMEM((2 * nz - 1, 8, 128), F32),
            pltpu.VMEM((8, D), F32),
            pltpu.VMEM((nz * nc - 1, 8, 128), F32),
            pltpu.VMEM((NBLK, sub, D), BF),
            pltpu.VMEM(shape, BF),
            pltpu.VMEM((LATE, nt, nc, nz, sub, D), BF),
            pltpu.VMEM((D, D), BF),
            pltpu.SemaphoreType.DMA((160,)),
            pltpu.SemaphoreType.DMA((160,)),
            pltpu.SemaphoreType.DMA((64,)),
        ],
        compiler_params=pltpu.CompilerParams(
            collective_id=3, has_side_effects=True, vmem_limit_bytes=61 << 20
        ),
        name="tail",
    )(
        block_of,
        early,
        late,
        grad_heads,
        wq,
        wq_rows,
        wq_all,
        tokens,
        grad_middle,
        gain,
        gain_terms,
        root_left,
        root_right,
        stat_left,
        stat_right,
        master,
    )


def finish_kernel(count, *refs):
    ins, outs, bufs = refs[:count], refs[count : 2 * count], refs[2 * count : 3 * count]
    in_sems, out_sems = refs[3 * count :]
    pieces = [(i, k) for i in range(ins[0].shape[0]) for k in range(count)]
    loads, stores = [], []
    for n, (i, k) in enumerate(pieces):
        loads.append(pltpu.make_async_copy(ins[k].at[i], bufs[k].at[i], in_sems.at[n]))
        loads[-1].start()
    for n, (i, k) in enumerate(pieces):
        loads[n].wait()
        stores.append(pltpu.make_async_copy(bufs[k].at[i], outs[k].at[i], out_sems.at[n]))
        stores[-1].start()
    for store in stores:
        store.wait()


def finish(arrays):
    any_ = pl.BlockSpec(memory_space=pl.ANY)
    count = len(arrays)
    pieces = count * arrays[0].shape[0]
    size = sum(a.size * a.dtype.itemsize for a in arrays)
    return pl.pallas_call(
        functools.partial(finish_kernel, count),
        out_shape=tuple(jax.ShapeDtypeStruct(a.shape, a.dtype) for a in arrays),
        in_specs=[any_] * count,
        out_specs=(any_,) * count,
        scratch_shapes=[pltpu.VMEM(a.shape, a.dtype) for a in arrays]
        + [pltpu.SemaphoreType.DMA((pieces,)), pltpu.SemaphoreType.DMA((pieces,))],
        compiler_params=pltpu.CompilerParams(vmem_limit_bytes=62 << 20),
        cost_estimate=pl.CostEstimate(flops=0, bytes_accessed=2 * size, transcendentals=0),
        name="finish",
    )(*arrays)


def xor_permute(value, axis, step):
    size = lax.axis_size(axis)
    return lax.ppermute(value, axis, [(j, j ^ step) for j in range(size)])


def xor_order(pieces, index):
    bit = 1
    while bit < len(pieces):
        odd = (index & bit) > 0
        pieces = [jnp.where(odd, pieces[j ^ bit], pieces[j]) for j in range(len(pieces))]
        bit *= 2
    return pieces


def sum_tensor(value):
    low = lax.optimization_barrier(value.astype(BF))
    return low.astype(F32) + xor_permute(low, "tensor", 1).astype(F32)


def gather_fsdp(value):
    size = lax.axis_size("fsdp")
    if size > 4:
        return lax.all_gather(value, "fsdp", axis=0, tiled=False)
    pieces = [value] + [
        lax.ppermute(value, "fsdp", [(j, (j - k) % size) for j in range(size)])
        for k in range(1, size)
    ]
    doubled = jnp.stack(pieces + pieces[:-1])
    start = lax.rem(size - lax.axis_index("fsdp"), size)
    return lax.dynamic_slice_in_dim(doubled, start, size, 0)


def sum_fsdp(value):
    size = lax.axis_size("fsdp")
    if size > 4:
        return lax.psum(value, "fsdp")
    total = value
    for k in range(1, size):
        total = total + lax.ppermute(value, "fsdp", [(j, (j - k) % size) for j in range(size)])
    return total


def grad_gather_plain(block_of, early, late, nz, nc):
    me_c, me_t = (lax.axis_index(a) for a in ("context", "tensor"))
    sub = early.shape[1]
    half_width = nc * nz * sub
    slot_count = NBLK // nc
    slots_of = block_of.reshape(nc, slot_count)

    def slots_for(k):
        blocks = lax.dynamic_index_in_dim(slots_of, me_c ^ k, 0, keepdims=False)
        return early[jnp.clip(blocks - LATE, 0, EARLY - 1)]

    placed = [slots_for(0)] + [xor_permute(slots_for(k), "context", k) for k in range(1, nc)]
    placed = jnp.stack(xor_order(placed, me_c), axis=1)
    placed = lax.all_gather(placed, "fsdp", axis=2, tiled=False)
    placed = placed.reshape(slot_count, half_width, D)
    placed_other = xor_permute(placed, "tensor", 1)
    both = jnp.stack([placed, placed_other], axis=1)
    early_full = jnp.where(me_t > 0, both[:, ::-1], both).reshape(slot_count, D, D)

    late = late.reshape(-1, D)
    late = lax.psum_scatter(late, "fsdp", scatter_dimension=0, tiled=True)
    late = lax.all_gather(late, ("context", "fsdp"), axis=0, tiled=True)
    late = jnp.swapaxes(late.reshape(nc * nz, LATE, sub, D), 0, 1).reshape(LATE, half_width, D)
    late_other = xor_permute(late, "tensor", 1)
    both = jnp.stack([late, late_other], axis=1)
    late_full = jnp.where(me_t > 0, both[:, ::-1], both).reshape(LATE, D, D)

    mine = lax.dynamic_index_in_dim(slots_of, me_c, 0, keepdims=False)
    return jnp.where(
        (mine < LATE)[:, None, None], late_full[jnp.clip(mine, 0, LATE - 1)], early_full
    )


def to_natural(value, me_t, half_len):
    parts = value.reshape((-1, half_len) + value.shape[1:])
    return jnp.where(me_t > 0, parts[::-1], parts).reshape(value.shape)


def forward_plain(tokens, gain, key_mask, w_qkv, w_out, w_up, w_down):
    images, local_len = tokens.shape[:2]
    nc, nt = (lax.axis_size(a) for a in ("context", "tensor"))
    me_c, me_t = (lax.axis_index(a) for a in ("context", "tensor"))
    cols = w_qkv.shape[2] // nc
    half_len = local_len // nt
    wq_part = lax.dynamic_slice_in_dim(w_qkv, me_c * cols, cols, 2)
    wq = gather_fsdp(wq_part).reshape(D, 3 * cols)

    def two_stage(weight, member_axis, fsdp_axis):
        width = weight.shape[member_axis] // nc
        part = lax.dynamic_slice_in_dim(weight, me_c * width, width, member_axis)
        part = lax.all_gather(part, "fsdp", axis=fsdp_axis, tiled=True)
        return lax.all_gather(part, "context", axis=member_axis, tiled=True)

    out_full = two_stage(w_out, 0, 1)
    up_full = two_stage(w_up, 1, 0)
    down_full = two_stage(w_down, 0, 1)

    counts = jnp.sum(key_mask, axis=1)
    real = counts
    for k in range(1, nc):
        real = real + xor_permute(counts, "context", k)
    position = (
        (me_c ^ jnp.arange(nc))[:, None, None] * local_len
        + (me_t ^ jnp.arange(nt))[None, :, None] * half_len
        + jnp.arange(half_len)[None, None, :]
    ).reshape(-1)
    live = position[None, :] < real[:, None]
    bias = jnp.where(live, 0.0, -1e30).astype(F32)
    live_col = jnp.broadcast_to(live[:, :, None].astype(F32), (images, SEQ, 128))

    normed1, inv_std1, pre_norm1 = norm_fwd(tokens, gain)
    normed1_low = pre_norm1.astype(BF)

    x_all, qkv, out_heads, log_sums, attended = [], [], [], [], []
    for i in range(images):
        mine = lax.dynamic_slice_in_dim(normed1_low[i], me_t * half_len, half_len, 0)
        held = jnp.stack([mine] + [xor_permute(mine, "context", k) for k in range(1, nc)])
        other = xor_permute(held, "tensor", 1)
        x_i = jnp.stack([held, other], axis=1).reshape(SEQ, D)
        qkv_i = dot_nn(x_i, wq).astype(BF)
        o_i, lse_i = attn_fwd(qkv_i, bias[i][None])
        chunks = o_i.reshape(nc, local_len, 2 * HD)
        moved = [to_natural(chunks[0], me_t, half_len)] + [
            to_natural(xor_permute(chunks[k], "context", k), me_t, half_len) for k in range(1, nc)
        ]
        attended.append(jnp.concatenate(xor_order(moved, me_c), axis=-1))
        x_all.append(x_i)
        qkv.append(qkv_i)
        out_heads.append(o_i)
        log_sums.append(lse_i)
    attended = jnp.stack(attended)
    return (
        jnp.stack(x_all),
        jnp.stack(qkv),
        jnp.stack(out_heads),
        jnp.stack(log_sums),
        attended,
        live_col,
        wq,
        out_full,
        up_full,
        down_full,
        normed1,
        inv_std1,
    )


def backward_plain(qkv, out_heads, log_sums, grad_att, live_col, early, wq):
    images, local_len = grad_att.shape[:2]
    nz, nc, nt = (lax.axis_size(a) for a in ("fsdp", "context", "tensor"))
    me_c, me_t = (lax.axis_index(a) for a in ("context", "tensor"))
    cols = grad_att.shape[2] // nc
    half_len = local_len // nt
    sub = early.shape[2]
    grad_heads = []
    grad_tok = []
    for i in range(images):
        pieces = [grad_att[i, :, j * cols : (j + 1) * cols] for j in range(nc)]
        pieces = [to_natural(p, me_t, half_len) for p in xor_order(pieces, me_c)]
        grad_i = jnp.concatenate(
            [pieces[0]] + [xor_permute(pieces[k], "context", k) for k in range(1, nc)]
        )
        g_i = attn_bwd(qkv[i], grad_i, out_heads[i], log_sums[i], live_col[i])
        chunks = g_i.reshape(nc, local_len, 3 * cols)
        moved = [to_natural(chunks[0], me_t, half_len)] + [
            to_natural(xor_permute(chunks[k], "context", k), me_t, half_len) for k in range(1, nc)
        ]
        grad_tok.append(jnp.stack(xor_order(moved, me_c), axis=1))
        grad_heads.append(g_i)
    grad_tok = jnp.stack(grad_tok)
    wq_all = lax.all_gather(wq, "context", axis=0, tiled=False)
    grad_n1 = sum_tensor(
        jnp.einsum("isjc,jdc->isd", grad_tok, wq_all, preferred_element_type=F32)
    )
    early = lax.psum_scatter(
        jnp.swapaxes(early, 0, 1).reshape(-1, D),
        "fsdp",
        scatter_dimension=0,
        tiled=True,
    ).reshape(EARLY, sub, D)
    return jnp.stack(grad_heads), grad_n1, early


def per_device(
    tokens,
    cotangent,
    gains,
    w_qkv,
    w_out,
    w_up,
    w_down,
    key_mask,
    owner,
    stat_left,
    stat_right,
    root_left,
    root_right,
    master,
    gain_state,
):
    images, local_len = tokens.shape[:2]
    tok_rows = images * local_len
    nz, nc, nt = (lax.axis_size(a) for a in ("fsdp", "context", "tensor"))
    me_z, me_c, me_t = (lax.axis_index(a) for a in ("fsdp", "context", "tensor"))
    half_width = w_qkv.shape[2]
    hidden = w_up.shape[1]
    up_blocks = hidden // half_width
    cols = half_width // nc
    fast = nz == 4 and nc == 4 and nt == 2 and images == 3
    if fast:
        wq_rows = jnp.swapaxes(w_qkv.reshape(-1, 3, nc, cols), 1, 2).reshape(-1, nc * 3 * cols)
        counts = jnp.pad(jnp.sum(key_mask, axis=1), (0, 8 - images))
        counts = jnp.broadcast_to(counts[:, None], (8, 128))
        (
            x_all,
            qkv,
            out_heads,
            log_sums,
            attended,
            counts,
            wq,
            out_full,
            up_full,
            down_part,
        ) = forward_attention(
            tokens, gains, counts, wq_rows, w_out, w_up, w_down, nz, nc
        )
    else:
        (
            x_all,
            qkv,
            out_heads,
            log_sums,
            attended,
            live_col,
            wq,
            out_full,
            up_full,
            down_full,
            normed1,
            inv_std1,
        ) = forward_plain(tokens, gains[0], key_mask, w_qkv, w_out, w_up, w_down)

    sub = half_width // nc // nz
    onehot = (owner[:, None] == jnp.arange(NBLK, dtype=jnp.int32)[None, :]).astype(jnp.int32)
    block_of = jnp.sum(onehot * jnp.arange(NBLK, dtype=jnp.int32)[:, None], axis=0)

    if fast:
        (
            output,
            grad_middle,
            grad_att,
            term_out,
            term_up,
            down,
            down_y,
            down_x,
            wq_all,
            gain_terms,
        ) = feed_forward(
            attended, out_full, up_full, down_part, tokens, cotangent, gains, wq_rows, nz, nc
        )
        term_out, block_of = lax.optimization_barrier((term_out, block_of))
        term_out = term_out.reshape(1, nc, nz, sub, D)
        term_up = term_up.reshape(-1, nc, nz, sub, D)
        down = down.reshape(-1, nz, sub, D)
        down_y = down_y.reshape(-1, nz, sub, D // 2)
        down_x = down_x.reshape(-1, nz, sub, D // 2)
    else:
        branch_attn = sum_tensor(
            jnp.einsum("ish,hd->isd", attended, out_full, preferred_element_type=F32)
        )
        middle = tokens + gains[2] * branch_attn
        normed2, inv_std2, pre_norm2 = norm_fwd(middle, gains[1])
        normed2_low = pre_norm2.astype(BF)
        pre_act = jnp.einsum("isd,df->isf", normed2_low, up_full, preferred_element_type=F32)
        act_val, act_slope = gelu_parts(pre_act)
        act_low = act_val.astype(BF)
        branch_mlp = sum_tensor(
            jnp.einsum("isf,fd->isd", act_low, down_full, preferred_element_type=F32)
        )
        output = middle + gains[3] * branch_mlp

        grad_mlp = (gains[3] * cotangent).astype(BF)
        grad_hidden = jnp.einsum("isd,fd->isf", grad_mlp, down_full, preferred_element_type=F32)
        grad_pre = (grad_hidden * act_slope).astype(BF)
        grad_n2 = sum_tensor(
            jnp.einsum("isf,df->isd", grad_pre, up_full, preferred_element_type=F32)
        )
        middle_part, grad_gain2 = norm_back(grad_n2, gains[1], normed2, inv_std2)
        grad_middle = cotangent + middle_part
        grad_branch = (gains[2] * grad_middle).astype(BF)
        grad_att = jnp.einsum(
            "isd,hd->ish", grad_branch, out_full, preferred_element_type=F32
        ).astype(BF)

        def early_term(left, right):
            term = dot_tn(left.reshape(tok_rows, -1), right.reshape(tok_rows, D)).astype(BF)
            return term.reshape(-1, nc, nz, sub, D)

        def early_sum(term):
            return lax.psum_scatter(
                jnp.swapaxes(term, 0, 1).reshape(-1, D), "context", scatter_dimension=0, tiled=True
            ).reshape(-1, nz, sub, D)

        term_out = early_term(attended, grad_branch)
        term_up = early_term(grad_pre, normed2_low)
        down = early_sum(early_term(act_low, grad_mlp))
        grad_gain3 = jnp.sum(grad_middle * branch_attn, axis=(0, 1))
        grad_gain4 = jnp.sum(cotangent * branch_mlp, axis=(0, 1))
        blank = jnp.zeros_like(grad_gain2)
        gain_terms = jnp.stack([blank, grad_gain2, grad_gain3, grad_gain4] + [blank] * 4, axis=0)
    tokens_all = images * nz * SEQ
    if fast:
        early, late, grad_heads = backward_attention(
            qkv, out_heads, log_sums, grad_att, counts, term_out, term_up, down, down_y, down_x, x_all, nz, nc
        )
        grad_tokens, gain_sum, grad_mine, left_new, right_new, weight_new = tail(
            block_of,
            early,
            late,
            grad_heads,
            wq,
            wq_rows,
            wq_all,
            tokens,
            grad_middle,
            gains,
            gain_terms,
            root_left[:, 0],
            root_right,
            stat_left[:, 0],
            stat_right[:, 0],
            master[:, 0],
            tokens_all,
            nz,
            nc,
            nt,
        )
        output, grad_tokens, grad_mine, left_new, right_new, weight_new = finish(
            (output, grad_tokens, grad_mine, left_new, right_new, weight_new)
        )
    else:
        early = jnp.concatenate([early_sum(term_out), early_sum(term_up), down], axis=0)
        grad_heads, grad_n1, early = backward_plain(
            qkv, out_heads, log_sums, grad_att, live_col, early, wq
        )
        term_qkv = jnp.einsum("isk,isd->kd", grad_heads, x_all, preferred_element_type=F32)
        late = jnp.swapaxes(term_qkv.astype(BF).reshape(LATE, nz, sub, D), 0, 1)
        grad_full = grad_gather_plain(block_of, early, late, nz, nc)
        input_part, grad_gain1 = norm_back(grad_n1, gains[0], normed1, inv_std1)
        grad_tokens = grad_middle + input_part
        row_count = half_width // nz
        row_offset = me_t * half_width + me_z * row_count
        grad_mine = lax.dynamic_slice_in_dim(grad_full, row_offset, row_count, 1)
        left_new = 0.5 * stat_left[:, 0] + 0.5 / tokens_all * jnp.einsum(
            "sra,sba->srb", grad_mine, grad_full, preferred_element_type=F32
        )
        grad_cols = lax.dynamic_slice_in_dim(grad_full, row_offset, row_count, 2)
        right_new = 0.5 * stat_right[:, 0] + 0.5 / tokens_all * jnp.einsum(
            "sar,sab->srb", grad_cols, grad_full, preferred_element_type=F32
        )
        inner_prod = jnp.einsum(
            "sra,sab->srb", root_left[:, 0].astype(BF), grad_full, preferred_element_type=F32
        ).astype(BF)
        update = jnp.einsum(
            "srb,sbc->src", inner_prod, root_right.astype(BF), preferred_element_type=F32
        )
        square_sum = jnp.sum(update * update, axis=(1, 2))
        square_sum = sum_fsdp(square_sum + xor_permute(square_sum, "tensor", 1))
        factor = lax.rsqrt(square_sum / (D * D) + 1e-06)
        weight_new = master[:, 0] - factor[:, None, None] * update

        gain_terms = gain_terms[:4].at[0].set(grad_gain1)
        gain_sum = gain_terms
        step = 1
        while step < nc:
            gain_sum = gain_sum + xor_permute(gain_sum, "context", step)
            step *= 2
        gain_sum = sum_fsdp(gain_sum)

    share_width = gain_state.shape[1]
    gain_index = lax.axis_index(("fsdp", "context"))
    if fast:
        at = lax.rem(gain_index * share_width, 128)
        gain_grad = lax.dynamic_slice(gain_sum, (0, at), (4, share_width))
    else:
        gain_grad = lax.dynamic_slice_in_dim(
            gain_sum, gain_index * share_width, share_width, 1
        )
    gain_mine = lax.dynamic_slice_in_dim(gains, gain_index * share_width, share_width, 1)
    state_new = 0.5 * gain_state + 0.5 * gain_grad * gain_grad / tokens_all
    gain_new = gain_mine - 0.1 * gain_grad * lax.rsqrt(tokens_all * state_new)
    return (
        output,
        grad_tokens,
        grad_mine.astype(F32)[:, None],
        left_new[:, None],
        right_new[:, None],
        weight_new[:, None],
        gain_grad,
        state_new,
        gain_new,
    )


def solution(mesh):
    return jax.shard_map(
        per_device,
        mesh=mesh,
        in_specs=(
            P("fsdp", "context", None),
            P("fsdp", "context", None),
            P(),
            P("fsdp", None, "tensor"),
            P("tensor", "fsdp"),
            P("fsdp", "tensor"),
            P("tensor", "fsdp"),
            P("fsdp", "context"),
            P(),
            P("context", "tensor", "fsdp", None),
            P("context", "tensor", "fsdp", None),
            P("context", "tensor", "fsdp", None),
            P("context", None, None),
            P("context", "tensor", "fsdp", None),
            P(None, ("fsdp", "context")),
        ),
        out_specs=(
            P("fsdp", "context", None),
            P("fsdp", "context", None),
            P("context", "tensor", "fsdp", None),
            P("context", "tensor", "fsdp", None),
            P("context", "tensor", "fsdp", None),
            P("context", "tensor", "fsdp", None),
            P(None, ("fsdp", "context")),
            P(None, ("fsdp", "context")),
            P(None, ("fsdp", "context")),
        ),
        check_vma=False,
    )
```
